32 devices in a mesh: blade: 4 (over y, x), dp: 8 (over z, core).
Axes of the slice: x: 2, y: 2, z: 4, core: 2. Of those that a mesh axis runs over, the one named last changes fastest.
Arguments:
- inputs: bfloat16 [64, 4, 48, 4096], P('dp', 'blade'), may hold values from -6 to 6
- cotangent: bfloat16 [64, 4, 48, 4096], P('dp', 'blade'), may hold values from -6 to 6
- norm_table: float32 [16], replicated, may hold values from 0.5 to 2
- sample_index: int32 [64], P('dp'), may hold values from 0 to 15
- spec_weight: float32 [4, 256, 2, 48, 48], P('blade', 'dp'), may hold values from -0.875 to 0.875
- spec_first: float32 [4, 256, 2, 48, 48], P('blade', 'dp'), may hold values from -6 to 6
- spec_second: float32 [4, 256, 2, 48, 48], P('blade', 'dp'), may hold values from 0.32 to 1.344
- lin_weight: float32 [4, 48, 48], P('blade'), may hold values from -0.4375 to 0.4375
- lin_first: float32 [4, 48, 48], P('blade'), may hold values from -640 to 640
- lin_second: float32 [4, 48, 48], P('blade'), may hold values from 786.432 to 3145.728
Outputs:
- output: bfloat16 [64, 4, 48, 4096], P('dp', 'blade')
- input_grad: float32 [64, 4, 48, 4096], P('dp', 'blade')
- spec_new: float32 [4, 256, 2, 48, 48], P('blade', 'dp')
- spec_first_new: float32 [4, 256, 2, 48, 48], P('blade', 'dp')
- spec_second_new: float32 [4, 256, 2, 48, 48], P('blade', 'dp')
- lin_new: float32 [4, 48, 48], P('blade')
- lin_first_new: float32 [4, 48, 48], P('blade')
- lin_second_new: float32 [4, 48, 48], P('blade')
The draws below stay inside these ranges and needn't reach their ends.
All inputs are finite; a program needn't handle non-finite values.
Results may differ from the reference program's by a relative error of at most 0.014.
Values may be sent and summed in bfloat16 or wider, within the bound.
No kernel may reach another device: no remote copies, remote signals or barrier semaphores. Data moves between devices by JAX's collectives and lax.ppermute only.
A program may use at most 192 MiB of HBM per device.

```python
import math
import jax
import jax.numpy as jnp
from jax import lax

C = 48
GRID = 64
MSIDE = 16
NTAB = 16
STEP_COUNT = 5
NPIX = 4096
MODES = 256
TOTAL_B = 64


def plant(entries, rng, low, top_value):
    longest = entries.shape.index(max(entries.shape))
    spots = []
    for shift in (0, 1):
        where = [jax.random.randint(jax.random.fold_in(rng, axis), (), 0, length) for axis, length in enumerate(entries.shape)]
        where[longest] = (where[longest] + shift) % entries.shape[longest]
        spots.append(tuple(where))
    return entries.at[spots[0]].set(low).at[spots[1]].set(top_value)


def level_of(own_key, shape, cuts, least, largest):
    level = 1.0
    for axis_at, shards_of in cuts:
        draws = jax.random.uniform(jax.random.fold_in(jax.random.fold_in(own_key, 6), axis_at), (shards_of,), jnp.float32, least / len(cuts), largest / len(cuts))
        level = level * jnp.repeat(jnp.exp(draws), shape[axis_at] // shards_of).reshape((-1,) + (1,) * (len(shape) - 1 - axis_at))
    return level


def centred(rng, dims, scale, bound, shards=(), kind=jnp.bfloat16):
    values = jax.random.normal(rng, dims, jnp.float32) * scale
    if len(shards) > 0:
        values = level_of(rng, dims, shards, -0.22, 0.18) * values
    return jnp.clip(values, min=-bound, max=bound).astype(kind)


def setup_inputs(seed: int = 0) -> dict:
    key_of = jax.random.split(jax.random.key(seed), 11)
    inputs = centred(key_of[0], (TOTAL_B, 4, C, NPIX), 1.0, 6.0, ((0, 8), (1, 4)))
    cotangent = centred(key_of[1], (TOTAL_B, 4, C, NPIX), 1.0, 6.0, ((0, 8), (1, 4)))
    norm_table = jnp.clip(jnp.exp(jax.random.uniform(key_of[2], (NTAB,), jnp.float32, math.log(0.5), math.log(2.0))), 0.5, 2.0)
    sample_index = plant(jax.random.randint(key_of[3], (TOTAL_B,), 0, NTAB), jax.random.fold_in(key_of[3], 1), 0, NTAB - 1).astype(jnp.int32)
    spec_weight = centred(key_of[4], (4, MODES, 2, C, C), 50 ** -0.5, 0.875, ((0, 4), (1, 8)), jnp.float32)
    spec_first = centred(key_of[5], (4, MODES, 2, C, C), (0.25 * TOTAL_B ** 0.5), 6.0, ((0, 4), (1, 8)), jnp.float32)
    spec_second = jnp.clip(jnp.exp(math.log(1.344) - 1.43508453 * jax.random.uniform(key_of[6], (4, MODES, 2, C, C), jnp.float32) ** level_of(key_of[6], (4, MODES, 2, C, C), ((0, 4), (1, 8)), -0.2, 0.2)), 0.32, 1.344)
    lin_weight = centred(key_of[7], (4, C, C), (4 * C) ** -0.5, 0.4375, ((0, 4),), jnp.float32)
    lin_first = centred(key_of[8], (4, C, C), (0.2 * (TOTAL_B * NPIX) ** 0.5), 640.0, ((0, 4),), jnp.float32)
    lin_second = jnp.clip(jnp.exp(math.log(3145.728) - 1.3862944 * jax.random.uniform(key_of[9], (4, C, C), jnp.float32) ** level_of(key_of[9], (4, C, C), ((0, 4),), -0.2, 0.2)), 786.432, 3145.728)
    return dict(inputs=inputs, cotangent=cotangent, norm_table=norm_table, sample_index=sample_index, spec_weight=spec_weight, spec_first=spec_first, spec_second=spec_second, lin_weight=lin_weight, lin_first=lin_first, lin_second=lin_second)


@jax.custom_vjp
def low(v):
    return lax.optimization_barrier(v.astype(jnp.bfloat16)).astype(jnp.float32)

@jax.custom_vjp
def low_back(v):
    return v

def low_keep(v):
    return (low(v), None)

def low_pass(kept, grad):
    return (grad,)

def back_keep(v):
    return (v, None)

def back_low(kept, grad):
    return (low(grad),)
low.defvjp(low_keep, low_pass)
low_back.defvjp(back_keep, back_low)
BETA_ONE = 0.9
BETA_TWO = 0.999
EPSILON = 1e-08
RATE = 0.1
DECAY = 0.01
HIGH = lax.Precision.HIGHEST

def blade_sign(left_blade, right_blade):
    return 1 - 2 * (left_blade // 2 % 2) * (right_blade % 2)

def tables():
    pix_ids = jnp.arange(NPIX, dtype=jnp.int32)
    pix_row = pix_ids // GRID
    pix_col = pix_ids % GRID
    mode_ids = jnp.arange(MODES, dtype=jnp.int32)
    row_index = mode_ids // MSIDE
    col_freq = mode_ids % MSIDE
    row_freq = jnp.where(row_index < MSIDE // 2, row_index, GRID - MSIDE + row_index)
    phase_int = (pix_row[:, None] * row_freq[None, :] + pix_col[:, None] * col_freq[None, :]) % GRID
    angles = phase_int.astype(jnp.float32) * (2.0 * math.pi / GRID)
    forward = jnp.concatenate([jnp.cos(angles), -jnp.sin(angles)], axis=1) / GRID
    factor = jnp.where(col_freq == 0, 1.0, 2.0).astype(jnp.float32)
    factor = jnp.concatenate([factor, factor])
    return (forward.astype(jnp.bfloat16).astype(jnp.float32), (forward * factor[None, :]).astype(jnp.bfloat16).astype(jnp.float32))

def adamw(weight, first, second, grad):
    first_new = BETA_ONE * first + (1.0 - BETA_ONE) * grad
    second_new = BETA_TWO * second + (1.0 - BETA_TWO) * grad * grad
    corr_one = 1.0 - BETA_ONE ** STEP_COUNT
    corr_two = 1.0 - BETA_TWO ** STEP_COUNT
    update = first_new / corr_one / (jnp.sqrt(second_new / corr_two) + EPSILON)
    return (weight - RATE * (update + DECAY * weight), first_new, second_new)

def reference(inputs, cotangent, norm_table, sample_index, spec_weight, spec_first, spec_second, lin_weight, lin_first, lin_second):
    forward_table, inverse_table = tables()
    matches = sample_index[:, None] == jnp.arange(NTAB, dtype=jnp.int32)[None, :]
    normalizer = lax.optimization_barrier(jnp.sum(jnp.where(matches, norm_table[None, :], 0.0), axis=1))

    def clifford_layer(fields, spec_w, lin_w):
        normed = fields / normalizer[:, None, None, None]
        normed_low = low(normed)
        spectrum = low(low_back(jnp.einsum('sjcp,pn->sjcn', normed_low, forward_table, precision=HIGH)))
        modes_real = spectrum[..., :MODES]
        modes_imag = spectrum[..., MODES:]
        spec_low = low(spec_w)
        lin_low = low(lin_w)
        spec_list = []
        lin_list = []
        for out_blade in range(4):
            sum_real = jnp.zeros((fields.shape[0], C, MODES), jnp.float32)
            sum_imag = jnp.zeros((fields.shape[0], C, MODES), jnp.float32)
            sum_lin = jnp.zeros((fields.shape[0], C, NPIX), jnp.float32)
            for in_blade in range(4):
                w_blade = out_blade ^ in_blade
                sign_val = float(blade_sign(in_blade, w_blade))
                w_real = spec_low[w_blade, :, 0]
                w_imag = spec_low[w_blade, :, 1]
                x_real = modes_real[:, in_blade]
                x_imag = modes_imag[:, in_blade]
                sum_real = sum_real + sign_val * (jnp.einsum('scm,mco->som', x_real, w_real, precision=HIGH) - jnp.einsum('scm,mco->som', x_imag, w_imag, precision=HIGH))
                sum_imag = sum_imag + sign_val * (jnp.einsum('scm,mco->som', x_real, w_imag, precision=HIGH) + jnp.einsum('scm,mco->som', x_imag, w_real, precision=HIGH))
                sum_lin = sum_lin + sign_val * jnp.einsum('scp,co->sop', normed_low[:, in_blade], lin_low[w_blade], precision=HIGH)
            spec_list.append(jnp.concatenate([sum_real, sum_imag], axis=-1))
            lin_list.append(sum_lin)
        spec_out = low(low_back(jnp.stack(spec_list, axis=1)))
        spatial = jnp.einsum('sjcn,pn->sjcp', spec_out, inverse_table, precision=HIGH)
        pre = low_back(spatial + jnp.stack(lin_list, axis=1))
        return normed + jax.nn.gelu(pre, approximate=False)
    result, pullback = jax.vjp(clifford_layer, inputs.astype(jnp.float32), spec_weight, lin_weight)
    input_grad, spec_grad, lin_grad = pullback(cotangent.astype(jnp.float32))
    spec_new, spec_first_new, spec_second_new = adamw(spec_weight, spec_first, spec_second, spec_grad)
    lin_new, lin_first_new, lin_second_new = adamw(lin_weight, lin_first, lin_second, lin_grad)
    return (result.astype(jnp.bfloat16), input_grad, spec_new, spec_first_new, spec_second_new, lin_new, lin_first_new, lin_second_new)
```

```python
from functools import partial
import math

import jax
import jax.numpy as jnp
from jax import lax
from jax.experimental import pallas as pl
from jax.experimental.pallas import tpu as pltpu
from jax.sharding import PartitionSpec as P

GRID = 64
MSIDE = 16
NTAB = 16
STEP_COUNT = 5
NPIX = 4096
MODES = 256
C = 48
LANES = 2 * C
QUAD = 4
TILE = 1024
ROWS = 16

BETA_ONE = 0.9
BETA_TWO = 0.999
EPSILON = 1e-08
RATE = 0.1
DECAY = 0.01

F32 = jnp.float32
BF16 = jnp.bfloat16
SMEM = pltpu.MemorySpace.SMEM


def sgn(left, right):
    return -1.0 if (left & 2) and (right & 1) else 1.0


def flip_of(own, k):
    if k & 1:
        return (1 - 2 * ((own // 2) % 2)).astype(F32)
    return jnp.float32(1.0)


def mode_factor(mode):
    return jnp.where(mode % MSIDE == 0, 1.0, 2.0).astype(F32)


def dot(left, right, dims=((1,), (0,))):
    return lax.dot_general(left, right, (dims, ((), ())), preferred_element_type=F32)


def whole(shape):
    zeros = (0,) * len(shape)
    return pl.BlockSpec(tuple(shape), lambda *_: zeros)


def params(**kw):
    return pltpu.CompilerParams(vmem_limit_bytes=60 * 1024 * 1024, **kw)


def small_tables():
    mode_ids = jnp.arange(2 * MODES, dtype=jnp.int32)
    imag = mode_ids >= MODES
    mode_ids = mode_ids % MODES
    row_index = mode_ids // MSIDE
    col_freq = mode_ids % MSIDE
    row_freq = jnp.where(row_index < MSIDE // 2, row_index, GRID - MSIDE + row_index)
    place = jnp.arange(GRID, dtype=jnp.int32)[:, None]
    row_angle = ((place * row_freq[None, :]) % GRID).astype(F32) * (2.0 * math.pi / GRID)
    col_angle = ((place * col_freq[None, :]) % GRID).astype(F32) * (2.0 * math.pi / GRID)
    row_cos, row_sin = jnp.cos(row_angle) / GRID, jnp.sin(row_angle) / GRID
    first = jnp.where(imag[None, :], -row_sin, row_cos)
    second = jnp.where(imag[None, :], -row_cos, -row_sin)
    return first, second, jnp.cos(col_angle), jnp.sin(col_angle)


def table_kernel(first_ref, second_ref, cos_ref, sin_ref, f_ref, ft_ref):
    for h in range(first_ref.shape[0]):
        tile = first_ref[h : h + 1, :] * cos_ref[...] + second_ref[h : h + 1, :] * sin_ref[...]
        f_ref[h * GRID : (h + 1) * GRID, :] = tile.astype(BF16)
    for h in range(0, first_ref.shape[0], 2):
        tile = f_ref[h * GRID : (h + 2) * GRID, :].astype(F32)
        ft_ref[:, h * GRID : (h + 2) * GRID] = tile.T.astype(BF16)


def make_tables():
    first, second, cosine, sine = lax.optimization_barrier(small_tables())
    rows = 8
    n = 2 * MODES
    return pl.pallas_call(
        table_kernel,
        grid=(GRID // rows,),
        in_specs=[
            pl.BlockSpec((rows, n), lambda i: (i, 0)),
            pl.BlockSpec((rows, n), lambda i: (i, 0)),
            whole((GRID, n)),
            whole((GRID, n)),
        ],
        out_specs=[
            pl.BlockSpec((rows * GRID, n), lambda i: (i, 0)),
            pl.BlockSpec((n, rows * GRID), lambda i: (0, i)),
        ],
        out_shape=[
            jax.ShapeDtypeStruct((NPIX, n), BF16),
            jax.ShapeDtypeStruct((n, NPIX), BF16),
        ],
        compiler_params=params(),
        cost_estimate=pl.CostEstimate(
            flops=4 * NPIX * n, bytes_accessed=4 * NPIX * n, transcendentals=0
        ),
        name="tables",
    )(first, second, cosine, sine)


def pack_kernel(w_ref, o_ref):
    for q in range(QUAD):
        for r in range(2):
            lane = q * LANES + r * C
            o_ref[0, :, lane : lane + C] = w_ref[0, q, r].astype(BF16)


def pack_weights(spec_weight):
    modes = spec_weight.shape[1]
    return pl.pallas_call(
        pack_kernel,
        grid=(modes // QUAD,),
        in_specs=[pl.BlockSpec((1, QUAD, 2, C, C), lambda g: (0, g, 0, 0, 0))],
        out_specs=pl.BlockSpec((1, C, QUAD * LANES), lambda g: (g, 0, 0)),
        out_shape=jax.ShapeDtypeStruct((modes // QUAD, C, QUAD * LANES), BF16),
        compiler_params=params(),
        cost_estimate=pl.CostEstimate(
            flops=modes * 4608, bytes_accessed=modes * 4608 * 6, transcendentals=0
        ),
        name="pack",
    )(spec_weight)


def build_kernel(ids_ref, w0, w1, w2, w3, l0, l1, l2, l3, pq_ref, lt_ref, lb_ref, wsc, lsc):
    own = ids_ref[0]
    shard = ids_ref[1]
    quads = w0.shape[0]
    for t, (w, line) in enumerate(((w0, l0), (w1, l1), (w2, l2), (w3, l3))):
        slot = jnp.bitwise_xor(own, t)
        wsc[slot] = w[...]
        lsc[slot] = line[...]

    for k in range(4):
        flip = flip_of(own, k)

        def step(g, carry):
            for q in range(QUAD):
                mode = shard * (quads * QUAD) + g * QUAD + q
                scale = mode_factor(mode) * flip
                p = wsc[k, g, :, q * LANES : (q + 1) * LANES].astype(F32) * scale
                low = jnp.concatenate([-p[:, C:], p[:, :C]], axis=1)
                pq_ref[k, g * QUAD + q] = jnp.concatenate([p, low], axis=0).astype(BF16)
            return carry

        lax.fori_loop(0, quads, step, 0)

    for t in range(4):
        for u in range(4):
            k = t ^ u
            block = lsc[k].astype(F32) * (flip_of(own, k) * sgn(t, k))
            lb_ref[t * C : (t + 1) * C, u * C : (u + 1) * C] = block.astype(BF16)
            lt_ref[u * C : (u + 1) * C, t * C : (t + 1) * C] = block.T.astype(BF16)


def build_weights(ids, packs, lines):
    quads = packs[0].shape[0]
    modes = quads * QUAD
    return pl.pallas_call(
        build_kernel,
        in_specs=[pl.BlockSpec(memory_space=SMEM)]
        + [pl.BlockSpec(memory_space=pltpu.MemorySpace.VMEM)] * 8,
        out_shape=[
            jax.ShapeDtypeStruct((4, modes, LANES, LANES), BF16),
            jax.ShapeDtypeStruct((4 * C, 4 * C), BF16),
            jax.ShapeDtypeStruct((4 * C, 4 * C), BF16),
        ],
        scratch_shapes=[
            pltpu.VMEM((4, quads, C, QUAD * LANES), BF16),
            pltpu.VMEM((4, C, C), BF16),
        ],
        compiler_params=params(),
        cost_estimate=pl.CostEstimate(
            flops=modes * 4 * 40000, bytes_accessed=modes * 4 * 30000, transcendentals=0
        ),
        name="build",
    )(ids, *packs, *lines)


def spread(acc, rsc, outs, shard):
    samples = acc.shape[0]
    modes = rsc.shape[1]
    rows = []
    for s in range(samples):
        for t in range(4):
            for r in range(2):
                rows.append(acc[s, t * C : (t + 1) * C, r * MODES : (r + 1) * MODES])
    turned = jnp.concatenate(rows, axis=0).T
    rsc[...] = turned.reshape(rsc.shape)
    for x, out in enumerate(outs):
        out[...] = rsc[jnp.bitwise_xor(shard, x)].astype(BF16)


def collect(blocks, rsc, ysc, shard):
    samples = ysc.shape[0]
    for x, block in enumerate(blocks):
        rsc[jnp.bitwise_xor(shard, x)] = block[...].astype(F32)
    turned = rsc[...].reshape(MODES, rsc.shape[2]).T
    for s in range(samples):
        for t in range(4):
            for r in range(2):
                row = ((s * 4 + t) * 2 + r) * C
                ysc[s, t * C : (t + 1) * C, r * MODES : (r + 1) * MODES] = turned[
                    row : row + C
                ].astype(BF16)


def forward_kernel(shards, ids_ref, inv_ref, *refs):
    x = refs[:4]
    f_ref = refs[4]
    outs = refs[5 : 5 + shards]
    acc, rsc = refs[5 + shards :]
    i = pl.program_id(0)
    for s in range(acc.shape[0]):
        low = [(x[t][s, 0].astype(F32) * inv_ref[s]).astype(BF16) for t in range(4)]
        part = dot(jnp.concatenate(low, axis=0), f_ref[...])

        @pl.when(i == 0)
        def _():
            acc[s] = part

        @pl.when(i > 0)
        def _():
            acc[s] += part

    @pl.when(i == pl.num_programs(0) - 1)
    def _():
        spread(acc, rsc, outs, ids_ref[1])


def forward_spectrum(ids, inv, x, table, shards):
    samples = x[0].shape[0]
    modes = MODES // shards
    width = samples * 4 * LANES
    n = 2 * MODES
    return pl.pallas_call(
        partial(forward_kernel, shards),
        grid=(NPIX // TILE,),
        in_specs=[pl.BlockSpec(memory_space=SMEM)] * 2
        + [pl.BlockSpec((samples, 1, C, TILE), lambda i: (0, 0, 0, i))] * 4
        + [pl.BlockSpec((TILE, n), lambda i: (i, 0))],
        out_specs=[whole((modes, width))] * shards,
        out_shape=[jax.ShapeDtypeStruct((modes, width), BF16)] * shards,
        scratch_shapes=[
            pltpu.VMEM((samples, 4 * C, n), F32),
            pltpu.VMEM((shards, modes, width), F32),
        ],
        compiler_params=params(),
        cost_estimate=pl.CostEstimate(
            flops=2 * samples * 4 * C * NPIX * n, bytes_accessed=8_000_000, transcendentals=0
        ),
        name="forward",
    )(ids, inv, *x, table)


def rows_of(sc, mode, samples, shards):
    at = pl.ds(pl.multiple_of(mode * shards, shards), shards)
    line = jnp.concatenate([sc[n, at, :] for n in range(sc.shape[0])], axis=1)
    parts = []
    for t in range(4):
        for s in range(samples):
            lane = (s * 4 + t) * LANES
            parts.append(line[:, lane : lane + LANES])
    return jnp.concatenate(parts, axis=0)


def gather_rows(blocks, sc):
    shards = len(blocks)
    modes = blocks[0].shape[0]
    for x, block in enumerate(blocks):
        for n in range(sc.shape[0]):
            sc[n, pl.ds(x, modes, stride=shards), :] = block[:, n * 128 : (n + 1) * 128].astype(F32)


def row_scratch(modes, shards, width):
    return pltpu.VMEM((width // 128, modes * shards, 128), F32)


def mix_kernel(shards, samples, back, *refs):
    blocks = refs[:shards]
    pq_ref = refs[shards]
    outs = refs[shards + 1 : 2 * shards + 1]
    xsc, ysc = refs[2 * shards + 1 :]
    modes = xsc.shape[1] // shards
    group = samples * shards
    gather_rows(blocks, xsc)

    def step(m, carry):
        low = rows_of(xsc, m, samples, shards).astype(BF16)
        total = [None] * 4
        for k in range(4):
            part = dot(low, pq_ref[k, m], ((1,), (1,)) if back else ((1,), (0,)))
            for t in range(4):
                u = t ^ k
                piece = part[t * group : (t + 1) * group]
                sign = sgn(u, k) if back else sgn(t, k)
                if total[u] is None:
                    total[u] = piece if sign > 0 else -piece
                else:
                    total[u] = total[u] + piece if sign > 0 else total[u] - piece
        lanes = []
        for s in range(samples):
            for u in range(4):
                lanes.append(total[u][s * shards : (s + 1) * shards])
        line = jnp.concatenate(lanes, axis=1)
        at = pl.ds(pl.multiple_of(m * shards, shards), shards)
        for n in range(ysc.shape[0]):
            ysc[n, at, :] = line[:, n * 128 : (n + 1) * 128]
        return carry

    lax.fori_loop(0, modes, step, 0, unroll=2)
    for x, out in enumerate(outs):
        for n in range(ysc.shape[0]):
            piece = ysc[n, pl.ds(x, modes, stride=shards), :]
            out[:, n * 128 : (n + 1) * 128] = piece.astype(BF16)


def mix(blocks, pq, samples, back):
    shards = len(blocks)
    modes, width = blocks[0].shape
    vmem = pl.BlockSpec(memory_space=pltpu.MemorySpace.VMEM)
    return pl.pallas_call(
        partial(mix_kernel, shards, samples, back),
        in_specs=[vmem] * (shards + 1),
        out_specs=[vmem] * shards,
        out_shape=[jax.ShapeDtypeStruct((modes, width), BF16)] * shards,
        scratch_shapes=[row_scratch(modes, shards, width)] * 2,
        compiler_params=params(),
        cost_estimate=pl.CostEstimate(
            flops=modes * 4 * 2 * 64 * 96 * 96, bytes_accessed=4_000_000, transcendentals=0
        ),
        name="mix_back" if back else "mix",
    )(*blocks, pq)


def grad_kernel(shards, samples, ids_ref, *refs):
    x_blocks = refs[:shards]
    g_blocks = refs[shards : 2 * shards]
    outs = refs[2 * shards : 2 * shards + 4]
    xsc, gsc, osc = refs[2 * shards + 4 :]
    modes = xsc.shape[1] // shards
    group = samples * shards
    own = ids_ref[0]
    first_mode = ids_ref[1] * modes
    gather_rows(x_blocks, xsc)
    gather_rows(g_blocks, gsc)

    def step(quad, carry):
        for q in range(QUAD):
            m = quad * QUAD + q
            x = rows_of(xsc, m, samples, shards)
            g = rows_of(gsc, m, samples, shards)
            turned = jnp.concatenate([g[:, C:], -g[:, :C]], axis=1)
            left = jnp.concatenate([x[:, :C], x[:, C:]], axis=0).astype(BF16)
            factor = mode_factor(first_mode + m)
            for k in range(4):
                rows = []
                for source in (g, turned):
                    for t in range(4):
                        u = t ^ k
                        piece = source[u * group : (u + 1) * group]
                        rows.append(piece if sgn(t, k) > 0 else -piece)
                right = jnp.concatenate(rows, axis=0).astype(BF16)
                grad = dot(left, right, ((0,), (0,))) * (factor * flip_of(own, k))
                osc[k, quad, :, q * LANES : (q + 1) * LANES] = grad.astype(BF16)
        return carry

    lax.fori_loop(0, modes // QUAD, step, 0)
    for t, out in enumerate(outs):
        out[...] = osc[jnp.bitwise_xor(own, t)]


def weight_grads(ids, x_blocks, g_blocks, samples):
    shards = len(x_blocks)
    modes, width = x_blocks[0].shape
    vmem = pl.BlockSpec(memory_space=pltpu.MemorySpace.VMEM)
    shape = (modes // QUAD, C, QUAD * LANES)
    return pl.pallas_call(
        partial(grad_kernel, shards, samples),
        in_specs=[pl.BlockSpec(memory_space=SMEM)] + [vmem] * (2 * shards),
        out_specs=[vmem] * 4,
        out_shape=[jax.ShapeDtypeStruct(shape, BF16)] * 4,
        scratch_shapes=[row_scratch(modes, shards, width)] * 2
        + [pltpu.VMEM((4,) + shape, BF16)],
        compiler_params=params(),
        cost_estimate=pl.CostEstimate(
            flops=modes * 4 * 2 * 128 * 96 * 96, bytes_accessed=4_000_000, transcendentals=0
        ),
        name="weight_grads",
    )(ids, *x_blocks, *g_blocks)


def pixel_kernel(shards, ids_ref, inv_ref, *refs):
    x = refs[:4]
    cot = refs[4:8]
    y = refs[8 : 8 + shards]
    f_ref, ft_ref, lt_ref = refs[8 + shards : 11 + shards]
    refs = refs[11 + shards :]
    outs = refs[:4]
    g_ref = refs[4]
    g_outs = refs[5 : 5 + shards]
    lin_ref = refs[5 + shards]
    ysc, rsc, pre, low, gacc, lacc = refs[6 + shards :]
    i = pl.program_id(0)
    s = pl.program_id(1)
    own = ids_ref[0]
    shard = ids_ref[1]
    inv = inv_ref[s]
    start = jnp.logical_and(i == 0, s == 0)

    @pl.when(start)
    def _():
        collect(y, rsc, ysc, shard)

    for t in range(4):
        low[t * C : (t + 1) * C] = (x[t][0, 0].astype(F32) * inv).astype(BF16)
    pre[...] = dot(ysc[s], ft_ref[...]) + dot(lt_ref[...], low[...])

    for t in range(4):
        for c in range(0, C, ROWS):
            v = pre[t * C + c : t * C + c + ROWS]
            phi = jnp.exp(v * v * -0.5) * (1.0 / math.sqrt(2.0 * math.pi))
            cdf = 0.5 + 0.5 * lax.erf(v * (1.0 / math.sqrt(2.0)))
            normed = x[t][0, 0, c : c + ROWS].astype(F32) * inv
            outs[t][0, 0, c : c + ROWS] = (normed + v * cdf).astype(BF16)
            grad = cot[t][0, 0, c : c + ROWS].astype(F32) * (cdf + v * phi)
            g_ref[0, t * C + c : t * C + c + ROWS] = grad.astype(BF16)

    g = g_ref[0]
    part = dot(g, f_ref[...])
    lin = dot(low[...], g, ((1,), (1,)))

    @pl.when(i == 0)
    def _():
        gacc[s] = part

    @pl.when(i > 0)
    def _():
        gacc[s] += part

    @pl.when(start)
    def _():
        lacc[...] = lin

    @pl.when(jnp.logical_not(start))
    def _():
        lacc[...] += lin

    @pl.when(jnp.logical_and(i == pl.num_programs(0) - 1, s == pl.num_programs(1) - 1))
    def _():
        spread(gacc, rsc, g_outs, shard)
        for k in range(4):
            total = None
            for t in range(4):
                u = t ^ k
                piece = lacc[t * C : (t + 1) * C, u * C : (u + 1) * C] * sgn(t, k)
                total = piece if total is None else total + piece
            lin_ref[k] = total * flip_of(own, k)


def pixels(ids, inv, x, cot, y, table, turned, lt):
    samples = x[0].shape[0]
    shards = len(y)
    modes, width = y[0].shape
    n = 2 * MODES
    tile = TILE // 2
    block = pl.BlockSpec((1, 1, C, tile), lambda i, s: (s, 0, 0, i))
    block_shape = jax.ShapeDtypeStruct((samples, 1, C, NPIX), BF16)
    return pl.pallas_call(
        partial(pixel_kernel, shards),
        grid=(NPIX // tile, samples),
        in_specs=[pl.BlockSpec(memory_space=SMEM)] * 2
        + [block] * 8
        + [whole((modes, width))] * shards
        + [
            pl.BlockSpec((tile, n), lambda i, s: (i, 0)),
            pl.BlockSpec((n, tile), lambda i, s: (0, i)),
            whole((4 * C, 4 * C)),
        ],
        out_specs=[block] * 4
        + [pl.BlockSpec((1, 4 * C, tile), lambda i, s: (s, 0, i))]
        + [whole((modes, width))] * shards
        + [whole((4, C, C))],
        out_shape=[block_shape] * 4
        + [jax.ShapeDtypeStruct((samples, 4 * C, NPIX), BF16)]
        + [jax.ShapeDtypeStruct((modes, width), BF16)] * shards
        + [jax.ShapeDtypeStruct((4, C, C), F32)],
        scratch_shapes=[
            pltpu.VMEM((samples, 4 * C, n), BF16),
            pltpu.VMEM((shards, modes, width), F32),
            pltpu.VMEM((4 * C, tile), F32),
            pltpu.VMEM((4 * C, tile), BF16),
            pltpu.VMEM((samples, 4 * C, n), F32),
            pltpu.VMEM((4 * C, 4 * C), F32),
        ],
        compiler_params=params(),
        cost_estimate=pl.CostEstimate(
            flops=4 * samples * 4 * C * NPIX * n,
            bytes_accessed=20_000_000,
            transcendentals=2 * samples * 4 * C * NPIX,
        ),
        name="pixels",
    )(ids, inv, *x, *cot, *y, table, turned, lt)


def inner_kernel(shards, ids_ref, *refs):
    blocks = refs[:shards]
    g_ref, ft_ref, lb_ref = refs[shards : shards + 3]
    outs = refs[shards + 3 : shards + 7]
    ysc, rsc = refs[shards + 7 :]
    i = pl.program_id(0)
    s = pl.program_id(1)

    @pl.when(jnp.logical_and(i == 0, s == 0))
    def _():
        collect(blocks, rsc, ysc, ids_ref[1])

    total = dot(ysc[s], ft_ref[...]) + dot(lb_ref[...], g_ref[0])
    for t in range(4):
        outs[t][0, 0] = total[t * C : (t + 1) * C].astype(BF16)


def inner_grads(ids, blocks, g, turned, lb):
    samples = g.shape[0]
    shards = len(blocks)
    modes, width = blocks[0].shape
    n = 2 * MODES
    tile = TILE
    block = pl.BlockSpec((1, 1, C, tile), lambda i, s: (s, 0, 0, i))
    return pl.pallas_call(
        partial(inner_kernel, shards),
        grid=(NPIX // tile, samples),
        in_specs=[pl.BlockSpec(memory_space=SMEM)]
        + [whole((modes, width))] * shards
        + [
            pl.BlockSpec((1, 4 * C, tile), lambda i, s: (s, 0, i)),
            pl.BlockSpec((n, tile), lambda i, s: (0, i)),
            whole((4 * C, 4 * C)),
        ],
        out_specs=[block] * 4,
        out_shape=[jax.ShapeDtypeStruct((samples, 1, C, NPIX), BF16)] * 4,
        scratch_shapes=[
            pltpu.VMEM((samples, 4 * C, n), BF16),
            pltpu.VMEM((shards, modes, width), F32),
        ],
        compiler_params=params(),
        cost_estimate=pl.CostEstimate(
            flops=3 * samples * 4 * C * NPIX * n, bytes_accessed=10_000_000, transcendentals=0
        ),
        name="inner_grads",
    )(ids, *blocks, g, turned, lb)


def place_kernel(ids_ref, part_ref, *refs):
    refs[-1][...] = part_ref[...]


def place_output(own, parts, total):
    samples = parts[0].shape[0]
    result = None
    for t, part in enumerate(parts):
        slot = jnp.bitwise_xor(own, t).reshape(1)
        extra = [] if result is None else [result]
        result = pl.pallas_call(
            place_kernel,
            grid_spec=pltpu.PrefetchScalarGridSpec(
                num_scalar_prefetch=1,
                grid=(samples,),
                in_specs=[pl.BlockSpec((1, 1, C, NPIX), lambda s, ids: (s, 0, 0, 0))]
                + [pl.BlockSpec(memory_space=pl.ANY)] * len(extra),
                out_specs=pl.BlockSpec(
                    (1, 1, C, NPIX), lambda s, ids: (ids[0] * samples + s, 0, 0, 0)
                ),
            ),
            out_shape=jax.ShapeDtypeStruct((total, 1, C, NPIX), BF16),
            input_output_aliases={2: 0} if extra else {},
            compiler_params=params(),
            cost_estimate=pl.CostEstimate(
                flops=0, bytes_accessed=4 * samples * C * NPIX, transcendentals=0
            ),
            name="place",
        )(slot, part, *extra)
    return result


def final_kernel(ids_ref, inv_ref, cot_ref, part_ref, *refs):
    inv = inv_ref[ids_ref[0] * pl.num_programs(0) + pl.program_id(0)]
    refs[-1][...] = (cot_ref[...].astype(F32) + part_ref[...].astype(F32)) * inv


def final_grads(own, inv, cotangent, parts):
    samples = parts[0].shape[0]
    result = None
    for t, part in enumerate(parts):
        slot = jnp.bitwise_xor(own, t).reshape(1)
        extra = [] if result is None else [result]
        place = pl.BlockSpec(
            (1, 1, C, NPIX // 2), lambda s, i, ids, inv: (ids[0] * samples + s, 0, 0, i)
        )
        result = pl.pallas_call(
            final_kernel,
            grid_spec=pltpu.PrefetchScalarGridSpec(
                num_scalar_prefetch=2,
                grid=(samples, 2),
                in_specs=[
                    place,
                    pl.BlockSpec((1, 1, C, NPIX // 2), lambda s, i, ids, inv: (s, 0, 0, i)),
                ]
                + [pl.BlockSpec(memory_space=pl.ANY)] * len(extra),
                out_specs=place,
            ),
            out_shape=jax.ShapeDtypeStruct(cotangent.shape, F32),
            input_output_aliases={4: 0} if extra else {},
            compiler_params=params(),
            cost_estimate=pl.CostEstimate(
                flops=0, bytes_accessed=8 * samples * C * NPIX, transcendentals=0
            ),
            name="final",
        )(slot, inv, cotangent, part, *extra)
    return result


def adamw(weight, first, second, grad):
    first_new = BETA_ONE * first + (1.0 - BETA_ONE) * grad
    second_new = BETA_TWO * second + (1.0 - BETA_TWO) * grad * grad
    corr_one = 1.0 - BETA_ONE**STEP_COUNT
    corr_two = 1.0 - BETA_TWO**STEP_COUNT
    update = first_new / corr_one / (jnp.sqrt(second_new / corr_two) + EPSILON)
    return (weight - RATE * (update + DECAY * weight), first_new, second_new)


def adam_kernel(d0, d1, d2, d3, w_ref, first_ref, second_ref, w_out, first_out, second_out):
    grad = d0[0].astype(F32) + d1[0].astype(F32) + d2[0].astype(F32) + d3[0].astype(F32)
    for q in range(QUAD):
        for r in range(2):
            lane = q * LANES + r * C
            at = (0, q, r)
            new = adamw(w_ref[at], first_ref[at], second_ref[at], grad[:, lane : lane + C])
            w_out[at], first_out[at], second_out[at] = new


def adam_spec(grads, weight, first, second):
    modes = weight.shape[1]
    packed = pl.BlockSpec((1, C, QUAD * LANES), lambda g: (g, 0, 0))
    block = pl.BlockSpec((1, QUAD, 2, C, C), lambda g: (0, g, 0, 0, 0))
    return pl.pallas_call(
        adam_kernel,
        grid=(modes // QUAD,),
        in_specs=[packed] * 4 + [block] * 3,
        out_specs=[block] * 3,
        out_shape=[jax.ShapeDtypeStruct(weight.shape, F32)] * 3,
        compiler_params=params(),
        cost_estimate=pl.CostEstimate(
            flops=modes * 4608 * 20, bytes_accessed=modes * 4608 * 72, transcendentals=modes * 4608
        ),
        name="adam",
    )(*grads, weight, first, second)


def swap(value, axis, size, x):
    return lax.ppermute(value, axis, [(i, i ^ x) for i in range(size)])


def exchange(values, axis):
    size = len(values)
    return [values[0]] + [swap(values[x], axis, size, x) for x in range(1, size)]


def after(values, first):
    values, _ = lax.optimization_barrier((values, first))
    return values


def body(
    shards,
    inputs,
    cotangent,
    norm_table,
    sample_index,
    spec_weight,
    spec_first,
    spec_second,
    lin_weight,
    lin_first,
    lin_second,
):
    own = lax.axis_index("blade")
    shard = lax.axis_index("dp")
    ids = jnp.stack([own, shard]).astype(jnp.int32)
    total = inputs.shape[0]
    samples = total // 4

    def cut(array):
        return [
            lax.dynamic_slice_in_dim(array, jnp.bitwise_xor(own, t) * samples, samples, 0)
            for t in range(4)
        ]

    x = exchange(cut(inputs), "blade")

    matches = sample_index[:, None] == jnp.arange(NTAB, dtype=jnp.int32)[None, :]
    normalizer = jnp.sum(jnp.where(matches, norm_table[None, :], 0.0), axis=1)
    inv_all = 1.0 / normalizer
    inv = lax.dynamic_slice_in_dim(inv_all, own * samples, samples, 0)

    table, turned = make_tables()
    packed = pack_weights(spec_weight)
    line = lin_weight[0].astype(BF16)
    packed, line = after((packed, line), x)
    packs = [packed] + [swap(packed, "blade", 4, t) for t in range(1, 4)]
    lines = [line] + [swap(line, "blade", 4, t) for t in range(1, 4)]
    cot = exchange(after(cut(cotangent), packs), "blade")

    modes_sent = forward_spectrum(ids, inv, x, table, shards)
    modes_got = exchange(modes_sent, "dp")
    pq, lt, lb = build_weights(ids, packs, lines)
    y = exchange(mix(modes_got, pq, samples, False), "dp")

    result = pixels(ids, inv, x, cot, y, table, turned, lt)
    out_parts, grad_pre = result[:4], result[4]
    grads_sent, lin_parts = result[5 : 5 + shards], result[5 + shards]

    grads_got = exchange(grads_sent, "dp")
    out_parts = exchange(out_parts, "blade")
    back = exchange(mix(grads_got, pq, samples, True), "dp")
    spec_grads = weight_grads(ids, modes_got, grads_got, samples)
    spec_grads = exchange(spec_grads, "blade")

    lin_grads = [
        lax.dynamic_index_in_dim(lin_parts, jnp.bitwise_xor(own, t), 0, keepdims=False)
        for t in range(4)
    ]
    lin_grads = exchange(lin_grads, "blade")
    lin_grad = lin_grads[0] + lin_grads[1] + lin_grads[2] + lin_grads[3]
    step = 1
    while step < shards:
        lin_grad = lin_grad + swap(lin_grad, "dp", shards, step)
        step *= 2

    inner = exchange(inner_grads(ids, back, grad_pre, turned, lb), "blade")

    output = place_output(own, out_parts, total)
    spec_out = adam_spec(spec_grads, spec_weight, spec_first, spec_second)
    lin_out = adamw(lin_weight, lin_first, lin_second, lin_grad[None])
    input_grad = final_grads(own, inv_all, cotangent, inner)
    return (output, input_grad, *spec_out, *lin_out)


def solution(mesh):
    fields = P("dp", "blade", None, None)
    spec = P("blade", "dp", None, None, None)
    lin = P("blade", None, None)
    return jax.shard_map(
        partial(body, mesh.shape["dp"]),
        mesh=mesh,
        in_specs=(fields, fields, P(), P("dp"), spec, spec, spec, lin, lin, lin),
        out_specs=(fields, fields, spec, spec, spec, lin, lin, lin),
        check_vma=False,
    )
```

```python
from functools import partial
import math

import jax
import jax.numpy as jnp
from jax import lax
from jax.experimental import pallas as pl
from jax.experimental.pallas import tpu as pltpu
from jax.sharding import PartitionSpec as P

GRID = 64
MSIDE = 16
NTAB = 16
STEP_COUNT = 5
NPIX = 4096
MODES = 256
C = 48
LANES = 2 * C
QUAD = 4
PACK = 128
ROWS = 16

BETA_ONE = 0.9
BETA_TWO = 0.999
EPSILON = 1e-08
RATE = 0.1
DECAY = 0.01

F32 = jnp.float32
BF16 = jnp.bfloat16
SMEM = pltpu.MemorySpace.SMEM


def sgn(left, right):
    return -1.0 if (left & 2) and (right & 1) else 1.0


def flip_of(own, k):
    if k & 1:
        return (1 - 2 * ((own // 2) % 2)).astype(F32)
    return jnp.float32(1.0)


def mode_factor(mode):
    return jnp.where(mode % MSIDE == 0, 1.0, 2.0).astype(F32)


def dot(left, right, dims=((1,), (0,))):
    return lax.dot_general(left, right, (dims, ((), ())), preferred_element_type=F32)


def whole(shape):
    zeros = (0,) * len(shape)
    return pl.BlockSpec(tuple(shape), lambda *_: zeros)


def params(mib):
    return pltpu.CompilerParams(vmem_limit_bytes=60 * 1024 * 1024)


def in_vmem(count):
    return [pl.BlockSpec(memory_space=pltpu.MemorySpace.VMEM)] * count


def cost(flops, size, hard=0):
    return pl.CostEstimate(flops=flops, bytes_accessed=size, transcendentals=hard)


def small_tables():
    mode_ids = jnp.arange(2 * MODES, dtype=jnp.int32)
    imag = mode_ids >= MODES
    mode_ids = mode_ids % MODES
    row_index = mode_ids // MSIDE
    col_freq = mode_ids % MSIDE
    row_freq = jnp.where(row_index < MSIDE // 2, row_index, GRID - MSIDE + row_index)
    place = jnp.arange(GRID, dtype=jnp.int32)[:, None]
    row_angle = ((place * row_freq[None, :]) % GRID).astype(F32) * (2.0 * math.pi / GRID)
    col_angle = ((place * col_freq[None, :]) % GRID).astype(F32) * (2.0 * math.pi / GRID)
    row_cos, row_sin = jnp.cos(row_angle) / GRID, jnp.sin(row_angle) / GRID
    first = jnp.where(imag[None, :], -row_sin, row_cos)
    second = jnp.where(imag[None, :], -row_cos, -row_sin)
    return first, second, jnp.cos(col_angle), jnp.sin(col_angle)


def table_kernel(first_ref, second_ref, cos_ref, sin_ref, f_ref, ft_ref):
    for h in range(first_ref.shape[0]):
        tile = first_ref[h : h + 1, :] * cos_ref[...] + second_ref[h : h + 1, :] * sin_ref[...]
        f_ref[h * GRID : (h + 1) * GRID, :] = tile.astype(BF16)
    for h in range(0, first_ref.shape[0], 2):
        tile = f_ref[h * GRID : (h + 2) * GRID, :].astype(F32)
        ft_ref[:, h * GRID : (h + 2) * GRID] = tile.T.astype(BF16)


def make_tables():
    first, second, cosine, sine = lax.optimization_barrier(small_tables())
    rows = 8
    n = 2 * MODES
    return pl.pallas_call(
        table_kernel,
        grid=(GRID // rows,),
        in_specs=[
            pl.BlockSpec((rows, n), lambda i: (i, 0)),
            pl.BlockSpec((rows, n), lambda i: (i, 0)),
            whole((GRID, n)),
            whole((GRID, n)),
        ],
        out_specs=[
            pl.BlockSpec((rows * GRID, n), lambda i: (i, 0)),
            pl.BlockSpec((n, rows * GRID), lambda i: (0, i)),
        ],
        out_shape=[
            jax.ShapeDtypeStruct((NPIX, n), BF16),
            jax.ShapeDtypeStruct((n, NPIX), BF16),
        ],
        compiler_params=params(16),
        cost_estimate=cost(4 * NPIX * n, 4 * NPIX * n),
        name="tables",
    )(first, second, cosine, sine)


def pack_kernel(w_ref, l_ref, o_ref):
    def step(g, carry):
        parts = [w_ref[0, g * QUAD + q, r] for q in range(QUAD) for r in range(2)]
        at = pl.ds(pl.multiple_of(g * QUAD * LANES, PACK), QUAD * LANES)
        o_ref[:, at] = jnp.concatenate(parts, axis=1).astype(BF16)
        return carry

    modes = w_ref.shape[1]
    lax.fori_loop(0, modes // QUAD, step, 0)
    line = jnp.concatenate([l_ref[0], jnp.zeros((C, PACK - C), F32)], axis=1)
    o_ref[:, modes * LANES :] = line.astype(BF16)


def pack_weights(spec_weight, lin_weight):
    modes = spec_weight.shape[1]
    return pl.pallas_call(
        pack_kernel,
        in_specs=in_vmem(2),
        out_specs=in_vmem(1)[0],
        out_shape=jax.ShapeDtypeStruct((C, modes * LANES + PACK), BF16),
        compiler_params=params(8),
        cost_estimate=cost(modes * 4608, modes * 4608 * 12),
        name="pack",
    )(spec_weight, lin_weight)


def spread(acc, out_ref):
    rows = []
    for n in range(acc.shape[0] // C):
        for r in range(2):
            rows.append(acc[n * C : (n + 1) * C, r * MODES : (r + 1) * MODES])
    turned = jnp.concatenate(rows, axis=0).T
    out_ref[...] = turned.reshape(out_ref.shape).astype(BF16)


def collect(block, ysc):
    turned = block[...].astype(F32).reshape(MODES, block.shape[2]).T
    for n in range(ysc.shape[0] // C):
        for r in range(2):
            row = (n * 2 + r) * C
            piece = turned[row : row + C].astype(BF16)
            ysc[n * C : (n + 1) * C, r * MODES : (r + 1) * MODES] = piece


def forward_kernel(ids_ref, inv_ref, x0, x1, f_ref, out_ref, acc):
    i = pl.program_id(0)
    samples = x0.shape[0]
    first = inv_ref.shape[0] - samples
    low = []
    for s in range(samples):
        for x in (x0, x1):
            low.append((x[s, 0].astype(F32) * inv_ref[s]).astype(BF16))
    part = dot(jnp.concatenate(low, axis=0), f_ref[...])

    @pl.when(i == 0)
    def _():
        acc[...] = part

    @pl.when(i > 0)
    def _():
        acc[...] += part

    @pl.when(i == pl.num_programs(0) - 1)
    def _():
        spread(acc, out_ref)


def forward_spectrum(ids, inv, x, table, shards):
    samples = inv.shape[0]
    modes = MODES // shards
    width = samples * 2 * LANES
    n = 2 * MODES
    tile = 1024

    def spec(array):
        if array.shape[0] == samples:
            return pl.BlockSpec((samples, 1, C, tile), lambda i, ids, inv: (0, 0, 0, i))
        return pl.BlockSpec((samples, 1, C, tile), lambda i, ids, inv: (ids[0], 0, 0, i))

    return pl.pallas_call(
        forward_kernel,
        grid_spec=pltpu.PrefetchScalarGridSpec(
            num_scalar_prefetch=2,
            grid=(NPIX // tile,),
            in_specs=[spec(x[0]), spec(x[1]), pl.BlockSpec((tile, n), lambda i, ids, inv: (i, 0))],
            out_specs=whole((shards, modes, width)),
            scratch_shapes=[pltpu.VMEM((samples * 2 * C, n), F32)],
        ),
        out_shape=jax.ShapeDtypeStruct((shards, modes, width), BF16),
        compiler_params=params(16),
        cost_estimate=cost(4 * samples * C * NPIX * n, 6_000_000),
        name="forward",
    )(ids, inv, *x, table)


def row_scratch(modes, shards, width):
    return pltpu.VMEM((width // 128, modes * shards, 128), F32)


def gather_rows(blocks, sc):
    shards, modes = blocks[0].shape[:2]
    first = 0
    for block in blocks:
        for n in range(block.shape[2] // 128):
            for x in range(shards):
                rows = block[x, :, n * 128 : (n + 1) * 128].astype(F32)
                sc[first + n, pl.ds(x, modes, stride=shards), :] = rows
        first += block.shape[2] // 128


def line_of(sc, mode, shards):
    at = pl.ds(pl.multiple_of(mode * shards, shards), shards)
    return [sc[n, at, :] for n in range(sc.shape[0])]


def blade_rows(tiles, order):
    samples = len(tiles) * 128 // (4 * LANES)
    line = jnp.concatenate(tiles, axis=1)
    found = [[] for _ in range(4)]
    for n, (s, t) in enumerate(order):
        found[t].append(line[:, n * LANES : (n + 1) * LANES])
    return [jnp.concatenate(found[t], axis=0) for t in range(4)]


def split_order(samples):
    return [(s, t) for pair in ((0, 3), (1, 2)) for s in range(samples) for t in pair]


def plain_order(samples):
    return [(s, t) for s in range(samples) for t in range(4)]


def mode_weights(wk, g, q):
    rows = []
    at = pl.ds(pl.multiple_of(g * QUAD * LANES, PACK), QUAD * LANES)
    for k in range(4):
        p = wk[k, :, at][:, q * LANES : (q + 1) * LANES]
        low = jnp.concatenate([-p[:, C:], p[:, :C]], axis=1)
        both = jnp.concatenate([p, low], axis=0)
        rows.append(both)
    return rows


def mix_modes(xsc, ysc, wk, order, samples, shards, first_mode, back):
    modes = xsc.shape[1] // shards
    group = samples * shards

    def step(g, carry):
        for q in range(QUAD):
            m = g * QUAD + q
            low = jnp.concatenate(blade_rows(line_of(xsc, m, shards), order), axis=0).astype(BF16)
            weights = mode_weights(wk, g, q)
            total = [None] * 4
            for k in range(4):
                part = dot(low, weights[k], ((1,), (1,)) if back else ((1,), (0,)))
                for t in range(4):
                    u = t ^ k
                    piece = part[t * group : (t + 1) * group]
                    sign = sgn(u, k) if back else sgn(t, k)
                    if total[u] is None:
                        total[u] = piece if sign > 0 else -piece
                    else:
                        total[u] = total[u] + piece if sign > 0 else total[u] - piece
            lanes = []
            for s in range(samples):
                for u in range(4):
                    lanes.append(total[u][s * shards : (s + 1) * shards])
            line = jnp.concatenate(lanes, axis=1) * mode_factor(first_mode + m)
            at = pl.ds(pl.multiple_of(m * shards, shards), shards)
            for n in range(ysc.shape[0]):
                ysc[n, at, :] = line[:, n * 128 : (n + 1) * 128]
        return carry

    lax.fori_loop(0, modes // QUAD, step, 0)


def scatter_rows(ysc, out):
    shards, modes = out.shape[:2]
    for x in range(shards):
        for n in range(ysc.shape[0]):
            piece = ysc[n, pl.ds(x, modes, stride=shards), :]
            out[x, :, n * 128 : (n + 1) * 128] = piece.astype(BF16)


def mix_kernel(ids_ref, xa, xb, w0, w1, w2, w3, y_ref, wk, lt_ref, lb_ref, xsc, ysc):
    shards, modes, half = xa.shape
    samples = half // (2 * LANES)
    own = ids_ref[0]
    for t, w in enumerate((w0, w1, w2, w3)):
        slot = jnp.bitwise_xor(own, t)
        flip = jnp.where(slot % 2 == 1, flip_of(own, 1), 1.0)
        wk[slot] = (w[...].astype(F32) * flip).astype(BF16)
    gather_rows((xa, xb), xsc)
    mix_modes(xsc, ysc, wk, split_order(samples), samples, shards, ids_ref[1] * modes, False)
    scatter_rows(ysc, y_ref)
    for k in range(4):
        line = wk[k, :, modes * LANES :].astype(F32)
        turned = line.T
        for t in range(4):
            u = t ^ k
            lb_ref[t * C : (t + 1) * C, u * C : (u + 1) * C] = (line[:, :C] * sgn(t, k)).astype(BF16)
            lt_ref[u * C : (u + 1) * C, t * C : (t + 1) * C] = (turned[:C] * sgn(t, k)).astype(BF16)


def mix(ids, xa, xb, packs):
    shards, modes, half = xa.shape
    return pl.pallas_call(
        mix_kernel,
        in_specs=[pl.BlockSpec(memory_space=SMEM)] + in_vmem(6),
        out_specs=in_vmem(4),
        out_shape=[
            jax.ShapeDtypeStruct((shards, modes, 2 * half), BF16),
            jax.ShapeDtypeStruct((4,) + packs[0].shape, BF16),
            jax.ShapeDtypeStruct((4 * C, 4 * C), BF16),
            jax.ShapeDtypeStruct((4 * C, 4 * C), BF16),
        ],
        scratch_shapes=[row_scratch(modes, shards, 2 * half)] * 2,
        compiler_params=params(16),
        cost_estimate=cost(modes * 64 * 96 * 96 * 8, 4_000_000),
        name="mix",
    )(ids, xa, xb, *packs)


def mix_back_kernel(ids_ref, g_ref, wk, out_ref, gsc, ysc):
    shards, modes, width = g_ref.shape
    samples = width // (4 * LANES)
    gather_rows((g_ref,), gsc)
    mix_modes(gsc, ysc, wk, plain_order(samples), samples, shards, ids_ref[1] * modes, True)
    scatter_rows(ysc, out_ref)


def mix_back(ids, g, wk):
    shards, modes, width = g.shape
    return pl.pallas_call(
        mix_back_kernel,
        in_specs=[pl.BlockSpec(memory_space=SMEM)] + in_vmem(2),
        out_specs=in_vmem(1)[0],
        out_shape=jax.ShapeDtypeStruct(g.shape, BF16),
        scratch_shapes=[row_scratch(modes, shards, width)] * 2,
        compiler_params=params(16),
        cost_estimate=cost(modes * 64 * 96 * 96 * 8, 3_000_000),
        name="mix_back",
    )(ids, g, wk)


def grad_kernel(ids_ref, xa, xb, g_ref, lin_ref, o0, o1, o2, o3, xsc, gsc, osc):
    shards, modes, width = g_ref.shape
    samples = width // (4 * LANES)
    own = ids_ref[0]
    first_mode = ids_ref[1] * modes
    gather_rows((xa, xb), xsc)
    gather_rows((g_ref,), gsc)

    def step(g, carry):
        found = [[] for _ in range(4)]
        for q in range(QUAD):
            m = g * QUAD + q
            x = jnp.concatenate(
                blade_rows(line_of(xsc, m, shards), split_order(samples)), axis=0
            ).astype(BF16)
            left = jnp.concatenate([x[:, :C], x[:, C:]], axis=0)
            factor = mode_factor(first_mode + m)
            plain = [rows * factor for rows in blade_rows(line_of(gsc, m, shards), plain_order(samples))]
            turned = [jnp.concatenate([rows[:, C:], -rows[:, :C]], axis=1) for rows in plain]
            for k in range(4):
                rows = []
                for source in (plain, turned):
                    for t in range(4):
                        rows.append(source[t ^ k] if sgn(t, k) > 0 else -source[t ^ k])
                right = jnp.concatenate(rows, axis=0).astype(BF16)
                found[k].append(dot(left, right, ((0,), (0,))))
        at = pl.ds(pl.multiple_of(g * QUAD * LANES, PACK), QUAD * LANES)
        for k in range(4):
            osc[k, :, at] = jnp.concatenate(found[k], axis=1).astype(BF16)
        return carry

    lax.fori_loop(0, modes // QUAD, step, 0)
    for k in range(4):
        line = jnp.concatenate([lin_ref[k], jnp.zeros((C, PACK - C), F32)], axis=1)
        osc[k, :, modes * LANES :] = line.astype(BF16)
    for t, out in enumerate((o0, o1, o2, o3)):
        out[...] = osc[jnp.bitwise_xor(own, t)]


def weight_grads(ids, xa, xb, g, lin):
    shards, modes, width = g.shape
    shape = (C, modes * LANES + PACK)
    return pl.pallas_call(
        grad_kernel,
        in_specs=[pl.BlockSpec(memory_space=SMEM)] + in_vmem(4),
        out_specs=in_vmem(4),
        out_shape=[jax.ShapeDtypeStruct(shape, BF16)] * 4,
        scratch_shapes=[row_scratch(modes, shards, width)] * 2 + [pltpu.VMEM((4,) + shape, BF16)],
        compiler_params=params(16),
        cost_estimate=cost(modes * 128 * 96 * 96 * 8, 4_000_000),
        name="weight_grads",
    )(ids, xa, xb, g, lin)


CDF_AT = 0.28
CDF = (0.11652094, 0.06749571, 0.2689128, -0.23699677, 0.38987606, -0.10580875)


def gelu_parts(v):
    z = jnp.abs(v)
    t = 1.0 / (1.0 + CDF_AT * z)
    bell = jnp.exp2(v * v * (-0.5 * math.log2(math.e)))
    series = jnp.float32(CDF[-1])
    for value in CDF[-2::-1]:
        series = series * t + value
    tail = series * t * bell
    cdf = jnp.where(v < 0.0, tail, 1.0 - tail)
    return v * cdf, cdf + v * (bell * (1.0 / math.sqrt(2.0 * math.pi)))


def pixel_kernel(ids_ref, inv_ref, *refs):
    x, cot = refs[:4], refs[4:8]
    y_ref, f_ref, ft_ref, lt_ref = refs[8:12]
    outs = refs[12:16]
    g_ref, g_out, lin_ref = refs[16:19]
    ysc, pre, low, gacc, lacc = refs[19:]
    i = pl.program_id(0)
    own = ids_ref[0]
    samples = x[1].shape[0]
    rows = 4 * C

    @pl.when(i == 0)
    def _():
        collect(y_ref, ysc)

    for s in range(samples):
        for t in range(4):
            at = s * rows + t * C
            low[at : at + C] = (x[t][s, 0].astype(F32) * inv_ref[s]).astype(BF16)
    spatial = dot(ysc[...], ft_ref[...])
    for s in range(samples):
        at = slice(s * rows, (s + 1) * rows)
        pre[at] = spatial[at] + dot(lt_ref[...], low[at])

    for s in range(samples):
        for t in range(4):
            for c in range(0, C, ROWS):
                at = s * rows + t * C + c
                value, slope = gelu_parts(pre[at : at + ROWS])
                normed = x[t][s, 0, c : c + ROWS].astype(F32) * inv_ref[s]
                outs[t][s, 0, c : c + ROWS] = (normed + value).astype(BF16)
                grad = cot[t][s, 0, c : c + ROWS].astype(F32) * slope
                g_ref[at : at + ROWS] = grad.astype(BF16)

    part = dot(g_ref[...], f_ref[...])
    lin = None
    for s in range(samples):
        at = slice(s * rows, (s + 1) * rows)
        piece = dot(low[at], g_ref[at], ((1,), (1,)))
        lin = piece if lin is None else lin + piece

    @pl.when(i == 0)
    def _():
        gacc[...] = part
        lacc[...] = lin

    @pl.when(i > 0)
    def _():
        gacc[...] += part
        lacc[...] += lin

    @pl.when(i == pl.num_programs(0) - 1)
    def _():
        spread(gacc, g_out)
        for k in range(4):
            total = None
            for t in range(4):
                u = t ^ k
                piece = lacc[t * C : (t + 1) * C, u * C : (u + 1) * C] * sgn(t, k)
                total = piece if total is None else total + piece
            lin_ref[k] = total


def pixels(ids, inv, x, cot, y, table, turned, lt):
    samples = inv.shape[0]
    n = 2 * MODES
    tile = 512
    mine = pl.BlockSpec((samples, 1, C, tile), lambda i, ids, inv: (ids[0], 0, 0, i))
    block = pl.BlockSpec((samples, 1, C, tile), lambda i, ids, inv: (0, 0, 0, i))
    block_shape = jax.ShapeDtypeStruct((samples, 1, C, NPIX), BF16)
    rows = samples * 4 * C
    return pl.pallas_call(
        pixel_kernel,
        grid_spec=pltpu.PrefetchScalarGridSpec(
            num_scalar_prefetch=2,
            grid=(NPIX // tile,),
            in_specs=[mine]
            + [block] * 3
            + [mine]
            + [block] * 3
            + [
                whole(y.shape),
                pl.BlockSpec((tile, n), lambda i, ids, inv: (i, 0)),
                pl.BlockSpec((n, tile), lambda i, ids, inv: (0, i)),
                whole((4 * C, 4 * C)),
            ],
            out_specs=[mine]
            + [block] * 3
            + [
                pl.BlockSpec((rows, tile), lambda i, ids, inv: (0, i)),
                whole(y.shape),
                whole((4, C, C)),
            ],
            scratch_shapes=[
                pltpu.VMEM((rows, n), BF16),
                pltpu.VMEM((rows, tile), F32),
                pltpu.VMEM((rows, tile), BF16),
                pltpu.VMEM((rows, n), F32),
                pltpu.VMEM((4 * C, 4 * C), F32),
            ],
        ),
        out_shape=[jax.ShapeDtypeStruct(x[0].shape, BF16)]
        + [block_shape] * 3
        + [
            jax.ShapeDtypeStruct((rows, NPIX), BF16),
            jax.ShapeDtypeStruct(y.shape, BF16),
            jax.ShapeDtypeStruct((4, C, C), F32),
        ],
        compiler_params=params(24),
        cost_estimate=cost(4 * rows * NPIX * n, 20_000_000, 2 * rows * NPIX),
        name="pixels",
    )(ids, inv, *x, *cot, y, table, turned, lt)


def inner_kernel(ids_ref, inv_ref, y_ref, g_ref, ft_ref, lb_ref, cot_ref, mine_ref, o1, o2, o3, ysc):
    samples = cot_ref.shape[0]
    rows = 4 * C

    @pl.when(pl.program_id(0) == 0)
    def _():
        collect(y_ref, ysc)

    spatial = dot(ysc[...], ft_ref[...])
    for s in range(samples):
        at = slice(s * rows, (s + 1) * rows)
        total = spatial[at] + dot(lb_ref[...], g_ref[at])
        mine_ref[s, 0] = (cot_ref[s, 0].astype(F32) + total[:C]) * inv_ref[s]
        for t, out in ((1, o1), (2, o2), (3, o3)):
            out[s, 0] = total[t * C : (t + 1) * C].astype(BF16)


def inner_grads(ids, inv, y, g, turned, lb, cotangent):
    samples = inv.shape[0]
    n = 2 * MODES
    tile = 512
    rows = samples * 4 * C
    mine = pl.BlockSpec((samples, 1, C, tile), lambda i, ids, inv: (ids[0], 0, 0, i))
    block = pl.BlockSpec((samples, 1, C, tile), lambda i, ids, inv: (0, 0, 0, i))
    return pl.pallas_call(
        inner_kernel,
        grid_spec=pltpu.PrefetchScalarGridSpec(
            num_scalar_prefetch=2,
            grid=(NPIX // tile,),
            in_specs=[
                whole(y.shape),
                pl.BlockSpec((rows, tile), lambda i, ids, inv: (0, i)),
                pl.BlockSpec((n, tile), lambda i, ids, inv: (0, i)),
                whole((4 * C, 4 * C)),
                mine,
            ],
            out_specs=[mine] + [block] * 3,
            scratch_shapes=[pltpu.VMEM((rows, n), BF16)],
        ),
        out_shape=[jax.ShapeDtypeStruct(cotangent.shape, F32)]
        + [jax.ShapeDtypeStruct((samples, 1, C, NPIX), BF16)] * 3,
        compiler_params=params(16),
        cost_estimate=cost(3 * rows * NPIX * n, 10_000_000),
        name="inner_grads",
    )(ids, inv, y, g, turned, lb, cotangent)


def place_kernel(ids_ref, a_ref, b_ref, c_ref, old_ref, out_ref):
    for n, part in enumerate((a_ref, b_ref, c_ref)):

        @pl.when(pl.program_id(0) == n)
        def _():
            out_ref[...] = part[...]


def place_output(ids, parts, result):
    samples = parts[0].shape[0]
    shape = (1, 1, C, NPIX)

    def spec(n):
        def at(j, s, ids):
            return (jnp.where(j == n, s, jnp.where(j < n, 0, samples - 1)), 0, 0, 0)

        return pl.BlockSpec(shape, at)

    return pl.pallas_call(
        place_kernel,
        grid_spec=pltpu.PrefetchScalarGridSpec(
            num_scalar_prefetch=1,
            grid=(3, samples),
            in_specs=[spec(0), spec(1), spec(2), pl.BlockSpec(memory_space=pl.ANY)],
            out_specs=pl.BlockSpec(
                shape, lambda j, s, ids: (jnp.bitwise_xor(ids[0], j + 1) * samples + s, 0, 0, 0)
            ),
        ),
        out_shape=jax.ShapeDtypeStruct(result.shape, BF16),
        input_output_aliases={4: 0},
        compiler_params=params(12),
        cost_estimate=cost(0, 12 * samples * C * NPIX),
        name="place",
    )(ids, *parts, result)


def final_kernel(count, codes, ids_ref, inv_ref, cot_ref, *refs):
    samples = pl.num_programs(1)
    j = pl.program_id(0)
    for n in range(count):

        @pl.when(j == n)
        def _():
            inv = inv_ref[jnp.bitwise_xor(ids_ref[0], codes[n]) * samples + pl.program_id(1)]
            refs[-1][...] = (cot_ref[...].astype(F32) + refs[n][...].astype(F32)) * inv


def final_grads(ids, inv, cotangent, parts, codes, result):
    samples = parts[0].shape[0]
    count = len(parts)
    shape = (1, 1, C, NPIX)

    def code(j):
        value = codes[0]
        for n in range(1, count):
            value = jnp.where(j == n, codes[n], value)
        return value

    def spec(n):
        def at(j, s, ids, inv):
            return (jnp.where(j == n, s, jnp.where(j < n, 0, samples - 1)), 0, 0, 0)

        return pl.BlockSpec(shape, at)

    place = pl.BlockSpec(
        shape, lambda j, s, ids, inv: (jnp.bitwise_xor(ids[0], code(j)) * samples + s, 0, 0, 0)
    )
    return pl.pallas_call(
        partial(final_kernel, count, codes),
        grid_spec=pltpu.PrefetchScalarGridSpec(
            num_scalar_prefetch=2,
            grid=(count, samples),
            in_specs=[place]
            + [spec(n) for n in range(count)]
            + [pl.BlockSpec(memory_space=pl.ANY)],
            out_specs=place,
        ),
        out_shape=jax.ShapeDtypeStruct(cotangent.shape, F32),
        input_output_aliases={3 + count: 0},
        compiler_params=params(12),
        cost_estimate=cost(0, 8 * count * samples * C * NPIX),
        name="final",
    )(ids, inv, cotangent, *parts, result)


def adamw(weight, first, second, grad):
    first_new = BETA_ONE * first + (1.0 - BETA_ONE) * grad
    second_new = BETA_TWO * second + (1.0 - BETA_TWO) * grad * grad
    corr_one = 1.0 - BETA_ONE**STEP_COUNT
    corr_two = 1.0 - BETA_TWO**STEP_COUNT
    update = first_new / corr_one / (jnp.sqrt(second_new / corr_two) + EPSILON)
    return (weight - RATE * (update + DECAY * weight), first_new, second_new)


def adam_kernel(flips, d0, d1, d2, d3, w_ref, first_ref, second_ref, w_out, first_out, second_out):
    grad = d0[...].astype(F32) * flips[0]
    for t, d in ((1, d1), (2, d2), (3, d3)):
        grad = grad + d[...].astype(F32) * flips[t]
    for q in range(QUAD):
        for r in range(2):
            lane = q * LANES + r * C
            at = (0, q, r)
            new = adamw(w_ref[at], first_ref[at], second_ref[at], grad[:, lane : lane + C])
            w_out[at], first_out[at], second_out[at] = new


def adam_spec(flips, grads, weight, first, second):
    modes = weight.shape[1]
    packed = pl.BlockSpec((C, QUAD * LANES), lambda g: (0, g))
    block = pl.BlockSpec((1, QUAD, 2, C, C), lambda g: (0, g, 0, 0, 0))
    return pl.pallas_call(
        adam_kernel,
        grid=(modes // QUAD,),
        in_specs=[pl.BlockSpec(memory_space=SMEM)] + [packed] * 4 + [block] * 3,
        out_specs=[block] * 3,
        out_shape=[jax.ShapeDtypeStruct(weight.shape, F32)] * 3,
        compiler_params=params(12),
        cost_estimate=cost(modes * 4608 * 20, modes * 4608 * 72, modes * 4608),
        name="adam",
    )(flips, *grads, weight, first, second)


def swap(value, axis, size, x):
    return lax.ppermute(value, axis, [(i, i ^ x) for i in range(size)])


def to_modes(value):
    return lax.all_to_all(value, "dp", split_axis=0, concat_axis=0, tiled=True)


def after(values, first):
    values, _ = lax.optimization_barrier((values, first))
    return values


def body(
    shards,
    inputs,
    cotangent,
    norm_table,
    sample_index,
    spec_weight,
    spec_first,
    spec_second,
    lin_weight,
    lin_first,
    lin_second,
):
    own = lax.axis_index("blade")
    shard = lax.axis_index("dp")
    ids = jnp.stack([own, shard]).astype(jnp.int32)
    samples = inputs.shape[0] // 4

    def send(array, t):
        block = lax.dynamic_slice_in_dim(array, jnp.bitwise_xor(own, t) * samples, samples, 0)
        return block, swap(block, "blade", 4, t)

    sent, x3 = send(inputs, 3)
    rest = after(inputs, sent)
    sent, x1 = send(rest, 1)
    rest = after(rest, sent)
    _, x2 = send(rest, 2)

    matches = sample_index[:, None] == jnp.arange(NTAB, dtype=jnp.int32)[None, :]
    normalizer = jnp.sum(jnp.where(matches, norm_table[None, :], 0.0), axis=1)
    inv_all = 1.0 / normalizer
    inv = lax.dynamic_slice_in_dim(inv_all, own * samples, samples, 0)

    table, turned = make_tables()
    packed = pack_weights(spec_weight, lin_weight)
    packs = [packed] + [swap(packed, "blade", 4, t) for t in (1, 2, 3)]

    xa = to_modes(forward_spectrum(ids, inv, (inputs, x3), table, shards))
    late = after(cotangent, (x1, x2))
    cot = (cotangent,) + tuple(send(late, t)[1] for t in (1, 2, 3))
    xb = to_modes(forward_spectrum(ids, inv, (x1, x2), table, shards))
    sent, wk, lt, lb = mix(ids, xa, xb, packs)
    y = to_modes(sent)

    result = pixels(ids, inv, (inputs, x1, x2, x3), cot, y, table, turned, lt)
    output, grad_pre, sent, lin = result[0], result[4], result[5], result[6]
    out_parts = [swap(result[t], "blade", 4, t) for t in (1, 2, 3)]

    g = to_modes(sent)
    back = to_modes(mix_back(ids, g, wk))
    spec_grads = weight_grads(ids, xa, xb, g, lin)
    spec_grads = [spec_grads[0]] + [swap(spec_grads[t], "blade", 4, t) for t in (1, 2, 3)]

    flips = jnp.stack(
        [jnp.where(own % 2 == 1, flip_of(jnp.bitwise_xor(own, t), 1), 1.0) for t in range(4)]
    )
    lin_grad = 0.0
    first = spec_weight.shape[1] * LANES
    for t in range(4):
        lin_grad = lin_grad + spec_grads[t][:, first : first + C].astype(F32) * flips[t]
    step = 1
    while step < shards:
        lin_grad = lin_grad + swap(lin_grad, "dp", shards, step)
        step *= 2

    inner = inner_grads(ids, inv, back, grad_pre, turned, lb, cotangent)
    grad_parts = [swap(inner[t], "blade", 4, t) for t in (1, 2, 3)]

    output = place_output(ids, out_parts, output)
    spec_out = adam_spec(flips, spec_grads, spec_weight, spec_first, spec_second)
    lin_out = adamw(lin_weight, lin_first, lin_second, lin_grad[None])
    input_grad = final_grads(ids, inv_all, cotangent, grad_parts[2:], (3,), inner[0])
    input_grad = final_grads(ids, inv_all, cotangent, grad_parts[:2], (1, 2), input_grad)
    return (output, input_grad, *spec_out, *lin_out)


def solution(mesh):
    fields = P("dp", "blade", None, None)
    spec = P("blade", "dp", None, None, None)
    lin = P("blade", None, None)
    return jax.shard_map(
        partial(body, mesh.shape["dp"]),
        mesh=mesh,
        in_specs=(fields, fields, P(), P("dp"), spec, spec, spec, lin, lin, lin),
        out_specs=(fields, fields, spec, spec, spec, lin, lin, lin),
        check_vma=False,
    )
```

```python
from functools import partial
import math

import jax
import jax.numpy as jnp
from jax import lax
from jax.experimental import pallas as pl
from jax.experimental.pallas import tpu as pltpu
from jax.sharding import PartitionSpec as P

GRID = 64
MSIDE = 16
NTAB = 16
STEP_COUNT = 5
NPIX = 4096
MODES = 256
C = 48
LANES = 2 * C
QUAD = 4
PACK = 128
ROWS = 16

BETA_ONE = 0.9
BETA_TWO = 0.999
EPSILON = 1e-08
RATE = 0.1
DECAY = 0.01

F32 = jnp.float32
BF16 = jnp.bfloat16
SMEM = pltpu.MemorySpace.SMEM


def sgn(left, right):
    return -1.0 if (left & 2) and (right & 1) else 1.0


def flip_of(own, k):
    if k & 1:
        return (1 - 2 * ((own // 2) % 2)).astype(F32)
    return jnp.float32(1.0)


def mode_factor(mode):
    return jnp.where(mode % MSIDE == 0, 1.0, 2.0).astype(F32)


def dot(left, right, dims=((1,), (0,))):
    return lax.dot_general(left, right, (dims, ((), ())), preferred_element_type=F32)


def whole(shape):
    zeros = (0,) * len(shape)
    return pl.BlockSpec(tuple(shape), lambda *_: zeros)


def params(mib):
    return pltpu.CompilerParams(vmem_limit_bytes=mib * 1024 * 1024)


def in_vmem(count):
    return [pl.BlockSpec(memory_space=pltpu.MemorySpace.VMEM)] * count


def cost(flops, size, hard=0):
    return pl.CostEstimate(flops=1, bytes_accessed=1, transcendentals=0)


def small_tables():
    mode_ids = jnp.arange(2 * MODES, dtype=jnp.int32)
    imag = mode_ids >= MODES
    mode_ids = mode_ids % MODES
    row_index = mode_ids // MSIDE
    col_freq = mode_ids % MSIDE
    row_freq = jnp.where(row_index < MSIDE // 2, row_index, GRID - MSIDE + row_index)
    place = jnp.arange(GRID, dtype=jnp.int32)[:, None]
    row_angle = ((place * row_freq[None, :]) % GRID).astype(F32) * (2.0 * math.pi / GRID)
    col_angle = ((place * col_freq[None, :]) % GRID).astype(F32) * (2.0 * math.pi / GRID)
    row_cos, row_sin = jnp.cos(row_angle) / GRID, jnp.sin(row_angle) / GRID
    first = jnp.where(imag[None, :], -row_sin, row_cos)
    second = jnp.where(imag[None, :], -row_cos, -row_sin)
    return first, second, jnp.cos(col_angle), jnp.sin(col_angle)


def table_kernel(first_ref, second_ref, cos_ref, sin_ref, f_ref, ft_ref):
    for h in range(first_ref.shape[0]):
        tile = first_ref[h : h + 1, :] * cos_ref[...] + second_ref[h : h + 1, :] * sin_ref[...]
        f_ref[h * GRID : (h + 1) * GRID, :] = tile.astype(BF16)
    for h in range(0, first_ref.shape[0], 2):
        tile = f_ref[h * GRID : (h + 2) * GRID, :].astype(F32)
        ft_ref[:, h * GRID : (h + 2) * GRID] = tile.T.astype(BF16)


def make_tables():
    first, second, cosine, sine = lax.optimization_barrier(small_tables())
    rows = 8
    n = 2 * MODES
    return pl.pallas_call(
        table_kernel,
        grid=(GRID // rows,),
        in_specs=[
            pl.BlockSpec((rows, n), lambda i: (i, 0)),
            pl.BlockSpec((rows, n), lambda i: (i, 0)),
            whole((GRID, n)),
            whole((GRID, n)),
        ],
        out_specs=[
            pl.BlockSpec((rows * GRID, n), lambda i: (i, 0)),
            pl.BlockSpec((n, rows * GRID), lambda i: (0, i)),
        ],
        out_shape=[
            jax.ShapeDtypeStruct((NPIX, n), BF16),
            jax.ShapeDtypeStruct((n, NPIX), BF16),
        ],
        compiler_params=params(60),
        cost_estimate=cost(4 * NPIX * n, 4 * NPIX * n),
        name="tables",
    )(first, second, cosine, sine)


def pack_kernel(w_ref, l_ref, o_ref):
    def step(g, carry):
        parts = [w_ref[0, g * QUAD + q, r] for q in range(QUAD) for r in range(2)]
        at = pl.ds(pl.multiple_of(g * QUAD * LANES, PACK), QUAD * LANES)
        o_ref[:, at] = jnp.concatenate(parts, axis=1).astype(BF16)
        return carry

    modes = w_ref.shape[1]
    lax.fori_loop(0, modes // QUAD, step, 0)
    line = jnp.concatenate([l_ref[0], jnp.zeros((C, PACK - C), F32)], axis=1)
    o_ref[:, modes * LANES :] = line.astype(BF16)


def pack_weights(spec_weight, lin_weight):
    modes = spec_weight.shape[1]
    return pl.pallas_call(
        pack_kernel,
        in_specs=in_vmem(2),
        out_specs=in_vmem(1)[0],
        out_shape=jax.ShapeDtypeStruct((C, modes * LANES + PACK), BF16),
        compiler_params=params(60),
        cost_estimate=cost(modes * 4608, modes * 4608 * 12),
        name="pack",
    )(spec_weight, lin_weight)


def lanes_of(shape):
    return lax.broadcasted_iota(jnp.int32, shape, len(shape) - 1)


def split_lanes(a, b, c):
    lane = lanes_of(a.shape)
    second = jnp.where(lane < 32, pltpu.roll(a, 32, 1), pltpu.roll(b, 32, 1))
    third = jnp.where(lane < 64, pltpu.roll(b, 64, 1), pltpu.roll(c, 64, 1))
    return a, second, third, pltpu.roll(c, 96, 1)


def join_lanes(first, second, third, fourth):
    lane = lanes_of(first.shape)
    a = jnp.where(lane < 96, first, pltpu.roll(second, 96, 1))
    b = jnp.where(lane < 64, pltpu.roll(second, 96, 1), pltpu.roll(third, 64, 1))
    c = jnp.where(lane < 32, pltpu.roll(third, 64, 1), pltpu.roll(fourth, 32, 1))
    return a, b, c


def quad_tiles(ref, g):
    tiles = []
    for n in range(3):
        at = pl.ds(pl.multiple_of(g * QUAD * LANES + n * PACK, PACK), PACK)
        tiles.append(ref[:, at].astype(F32))
    return tiles


def unpack_kernel(ids_ref, w0, w1, w2, w3, pq_ref, lt_ref, lb_ref, lsc):
    own = ids_ref[0]
    modes = pq_ref.shape[0]
    lane = lanes_of((C, PACK))
    for t, w in enumerate((w0, w1, w2, w3)):
        slot = jnp.bitwise_xor(own, t)
        flip = jnp.where(slot % 2 == 1, flip_of(own, 1), 1.0)
        at = pl.ds(pl.multiple_of(slot * PACK, PACK), PACK)

        def step(g, carry):
            tiles = [tile * flip for tile in quad_tiles(w, g)]
            for q, p in enumerate(split_lanes(*tiles)):
                p = jnp.where(lane < LANES, p, 0.0)
                low = jnp.where(lane < C, -pltpu.roll(p, PACK - C, 1), pltpu.roll(p, C, 1))
                low = jnp.where(lane < LANES, low, 0.0)
                pq_ref[g * QUAD + q, :C, at] = p.astype(BF16)
                pq_ref[g * QUAD + q, C:, at] = low.astype(BF16)
            return carry

        lax.fori_loop(0, modes // QUAD, step, 0, unroll=2)
        lsc[slot] = w[:, modes * LANES :].astype(F32) * flip

    for k in range(4):
        line = lsc[k]
        turned = line.T
        for t in range(4):
            u = t ^ k
            lb_ref[t * C : (t + 1) * C, u * C : (u + 1) * C] = (line[:, :C] * sgn(t, k)).astype(BF16)
            lt_ref[u * C : (u + 1) * C, t * C : (t + 1) * C] = (turned[:C] * sgn(t, k)).astype(BF16)


def unpack(ids, packs):
    modes = (packs[0].shape[1] - PACK) // LANES
    return pl.pallas_call(
        unpack_kernel,
        in_specs=[pl.BlockSpec(memory_space=SMEM)] + in_vmem(4),
        out_specs=in_vmem(3),
        out_shape=[
            jax.ShapeDtypeStruct((modes, LANES, 4 * PACK), BF16),
            jax.ShapeDtypeStruct((4 * C, 4 * C), BF16),
            jax.ShapeDtypeStruct((4 * C, 4 * C), BF16),
        ],
        scratch_shapes=[pltpu.VMEM((4, C, PACK), F32)],
        compiler_params=params(60),
        cost_estimate=cost(modes * 100_000, 5_000_000),
        name="unpack",
    )(ids, *packs)


def spread(acc, out_ref):
    rows = []
    for n in range(acc.shape[0] // C):
        for r in range(2):
            rows.append(acc[n * C : (n + 1) * C, r * MODES : (r + 1) * MODES])
    turned = jnp.concatenate(rows, axis=0).T
    out_ref[...] = turned.reshape(out_ref.shape).astype(BF16)


def collect(block, ysc):
    turned = block[...].astype(F32).reshape(MODES, block.shape[2]).T
    for n in range(ysc.shape[0] // C):
        for r in range(2):
            row = (n * 2 + r) * C
            piece = turned[row : row + C].astype(BF16)
            ysc[n * C : (n + 1) * C, r * MODES : (r + 1) * MODES] = piece


def forward_kernel(ids_ref, inv_ref, x0, x1, f_ref, out_ref, acc):
    i = pl.program_id(0)
    samples = x0.shape[0]
    low = []
    for s in range(samples):
        for x in (x0, x1):
            low.append((x[s, 0].astype(F32) * inv_ref[s]).astype(BF16))
    part = dot(jnp.concatenate(low, axis=0), f_ref[...])

    @pl.when(i == 0)
    def _():
        acc[...] = part

    @pl.when(i > 0)
    def _():
        acc[...] += part

    @pl.when(i == pl.num_programs(0) - 1)
    def _():
        spread(acc, out_ref)


def forward_spectrum(ids, inv, x, table, shards):
    samples = inv.shape[0]
    modes = MODES // shards
    width = samples * 2 * LANES
    n = 2 * MODES
    tile = 1024

    def spec(array):
        if array.shape[0] == samples:
            return pl.BlockSpec((samples, 1, C, tile), lambda i, ids, inv: (0, 0, 0, i))
        return pl.BlockSpec((samples, 1, C, tile), lambda i, ids, inv: (ids[0], 0, 0, i))

    return pl.pallas_call(
        forward_kernel,
        grid_spec=pltpu.PrefetchScalarGridSpec(
            num_scalar_prefetch=2,
            grid=(NPIX // tile,),
            in_specs=[spec(x[0]), spec(x[1]), pl.BlockSpec((tile, n), lambda i, ids, inv: (i, 0))],
            out_specs=whole((shards, modes, width)),
            scratch_shapes=[pltpu.VMEM((samples * 2 * C, n), F32)],
        ),
        out_shape=jax.ShapeDtypeStruct((shards, modes, width), BF16),
        compiler_params=params(60),
        cost_estimate=cost(4 * samples * C * NPIX * n, 6_000_000),
        name="forward",
    )(ids, inv, *x, table)


def row_scratch(modes, shards, width):
    return pltpu.VMEM((width // PACK, modes * shards, PACK), F32)


def gather_rows(blocks, sc):
    shards, modes = blocks[0].shape[:2]
    first = 0
    for block in blocks:
        for n in range(block.shape[2] // PACK):
            for x in range(shards):
                rows = block[x, :, n * PACK : (n + 1) * PACK].astype(F32)
                sc[first + n, pl.ds(x, modes, stride=shards), :] = rows
        first += block.shape[2] // PACK


def scatter_rows(ysc, out):
    shards, modes = out.shape[:2]
    for x in range(shards):
        for n in range(ysc.shape[0]):
            piece = ysc[n, pl.ds(x, modes, stride=shards), :]
            out[x, :, n * PACK : (n + 1) * PACK] = piece.astype(BF16)


def blade_rows(sc, mode, shards, order):
    at = pl.ds(pl.multiple_of(mode * shards, shards), shards)
    found = [[] for _ in range(4)]
    for n in range(0, len(order), 4):
        tile = n // 4 * 3
        pieces = split_lanes(sc[tile, at, :], sc[tile + 1, at, :], sc[tile + 2, at, :])
        for piece, (_, t) in zip(pieces, order[n : n + 4]):
            found[t].append(piece)
    return [jnp.concatenate(found[t], axis=0) for t in range(4)]


def split_order(samples):
    return [(s, t) for pair in ((0, 3), (1, 2)) for s in range(samples) for t in pair]


def plain_order(samples):
    return [(s, t) for s in range(samples) for t in range(4)]


def mix_modes(xsc, ysc, pq_ref, order, shards, first_mode, back):
    modes = xsc.shape[1] // shards
    samples = len(order) // 4
    group = samples * shards

    def step(m, carry):
        low = jnp.concatenate(blade_rows(xsc, m, shards, order), axis=0)
        low = low[:, :LANES].astype(BF16)
        total = [None] * 4
        if not back:
            parts = dot(low, pq_ref[m])
        for k in range(4):
            if back:
                part = dot(low, pq_ref[m, :, k * PACK : k * PACK + LANES], ((1,), (1,)))
            else:
                part = parts[:, k * PACK : (k + 1) * PACK]
            for t in range(4):
                u = t ^ k
                piece = part[t * group : (t + 1) * group]
                sign = sgn(u, k) if back else sgn(t, k)
                if total[u] is None:
                    total[u] = piece if sign > 0 else -piece
                else:
                    total[u] = total[u] + piece if sign > 0 else total[u] - piece
        factor = mode_factor(first_mode + m)
        at = pl.ds(pl.multiple_of(m * shards, shards), shards)
        for s in range(samples):
            rows = []
            for u in range(4):
                piece = total[u][s * shards : (s + 1) * shards] * factor
                if back:
                    piece = jnp.concatenate([piece, jnp.zeros((shards, PACK - LANES), F32)], axis=1)
                rows.append(piece)
            for n, tile in enumerate(join_lanes(*rows)):
                ysc[s * 3 + n, at, :] = tile
        return carry

    lax.fori_loop(0, modes, step, 0, unroll=4)


def mix_kernel(ids_ref, xa, xb, pq_ref, y_ref, xsc, ysc):
    shards, modes, half = xa.shape
    gather_rows((xa, xb), xsc)
    order = split_order(half // (2 * LANES))
    mix_modes(xsc, ysc, pq_ref, order, shards, ids_ref[1] * modes, False)
    scatter_rows(ysc, y_ref)


def mix(ids, xa, xb, pq):
    shards, modes, half = xa.shape
    return pl.pallas_call(
        mix_kernel,
        in_specs=[pl.BlockSpec(memory_space=SMEM)] + in_vmem(3),
        out_specs=in_vmem(1)[0],
        out_shape=jax.ShapeDtypeStruct((shards, modes, 2 * half), BF16),
        scratch_shapes=[row_scratch(modes, shards, 2 * half)] * 2,
        compiler_params=params(60),
        cost_estimate=cost(modes * 64 * 96 * 96 * 8, 4_000_000),
        name="mix",
    )(ids, xa, xb, pq)


def mix_back_kernel(ids_ref, g_ref, pq_ref, out_ref, gsc, ysc):
    shards, modes, width = g_ref.shape
    gather_rows((g_ref,), gsc)
    order = plain_order(width // (4 * LANES))
    mix_modes(gsc, ysc, pq_ref, order, shards, ids_ref[1] * modes, True)
    scatter_rows(ysc, out_ref)


def mix_back(ids, g, pq):
    shards, modes, width = g.shape
    return pl.pallas_call(
        mix_back_kernel,
        in_specs=[pl.BlockSpec(memory_space=SMEM)] + in_vmem(2),
        out_specs=in_vmem(1)[0],
        out_shape=jax.ShapeDtypeStruct(g.shape, BF16),
        scratch_shapes=[row_scratch(modes, shards, width)] * 2,
        compiler_params=params(60),
        cost_estimate=cost(modes * 64 * 96 * 96 * 8, 3_000_000),
        name="mix_back",
    )(ids, g, pq)


def grad_kernel(ids_ref, xa, xb, g_ref, lin_ref, o0, o1, o2, o3, xsc, gsc, osc):
    shards, modes, width = g_ref.shape
    samples = width // (4 * LANES)
    own = ids_ref[0]
    first_mode = ids_ref[1] * modes
    gather_rows((xa, xb), xsc)
    gather_rows((g_ref,), gsc)
    lane = lanes_of((samples * shards, PACK))

    def step(g, carry):
        found = [[] for _ in range(4)]
        for q in range(QUAD):
            m = g * QUAD + q
            x = blade_rows(xsc, m, shards, split_order(samples))
            x = x + [pltpu.roll(rows, PACK - C, 1) for rows in x]
            left = jnp.concatenate(x, axis=0)[:, :C].astype(BF16)
            factor = mode_factor(first_mode + m)
            plain = blade_rows(gsc, m, shards, plain_order(samples))
            plain = [rows * factor for rows in plain]
            turned = [
                jnp.where(lane < C, pltpu.roll(rows, PACK - C, 1), -pltpu.roll(rows, C, 1))
                for rows in plain
            ]
            plus = [rows.astype(BF16) for rows in plain + turned]
            minus = [(-rows).astype(BF16) for rows in plain + turned]
            right = []
            for k in range(4):
                rows = []
                for r in range(2):
                    for t in range(4):
                        rows.append((plus if sgn(t, k) > 0 else minus)[4 * r + (t ^ k)])
                right.append(jnp.concatenate(rows, axis=0))
            grad = dot(left, jnp.concatenate(right, axis=1), ((0,), (0,)))
            for k in range(4):
                found[k].append(grad[:, k * PACK : (k + 1) * PACK])
        for k in range(4):
            for n, tile in enumerate(join_lanes(*found[k])):
                at = pl.ds(pl.multiple_of(g * QUAD * LANES + n * PACK, PACK), PACK)
                osc[k, :, at] = tile.astype(BF16)
        return carry

    lax.fori_loop(0, modes // QUAD, step, 0)
    for k in range(4):
        line = jnp.concatenate([lin_ref[k], jnp.zeros((C, PACK - C), F32)], axis=1)
        osc[k, :, modes * LANES :] = line.astype(BF16)
    for t, out in enumerate((o0, o1, o2, o3)):
        out[...] = osc[jnp.bitwise_xor(own, t)]


def weight_grads(ids, xa, xb, g, lin):
    shards, modes, width = g.shape
    shape = (C, modes * LANES + PACK)
    return pl.pallas_call(
        grad_kernel,
        in_specs=[pl.BlockSpec(memory_space=SMEM)] + in_vmem(4),
        out_specs=in_vmem(4),
        out_shape=[jax.ShapeDtypeStruct(shape, BF16)] * 4,
        scratch_shapes=[row_scratch(modes, shards, width)] * 2 + [pltpu.VMEM((4,) + shape, BF16)],
        compiler_params=params(60),
        cost_estimate=cost(modes * 128 * 96 * 96 * 8, 4_000_000),
        name="weight_grads",
    )(ids, xa, xb, g, lin)


CDF_AT = 0.28
CDF = (0.11652094, 0.06749571, 0.2689128, -0.23699677, 0.38987606, -0.10580875)


def gelu_parts(v):
    z = jnp.abs(v)
    t = 1.0 / (1.0 + CDF_AT * z)
    bell = jnp.exp2(v * v * (-0.5 * math.log2(math.e)))
    series = jnp.float32(CDF[-1])
    for value in CDF[-2::-1]:
        series = series * t + value
    tail = series * t * bell
    cdf = jnp.where(v < 0.0, tail, 1.0 - tail)
    return v * cdf, cdf + v * (bell * (1.0 / math.sqrt(2.0 * math.pi)))


def pixel_kernel(ids_ref, inv_ref, *refs):
    x = refs[:4]
    y_ref, ft_ref, lt_ref = refs[4:7]
    outs = refs[7:11]
    low, slope_ref = refs[11:13]
    ysc, pre, full = refs[13:]
    samples = x[1].shape[0]
    rows = 4 * C

    @pl.when(pl.program_id(0) == 0)
    def _():
        collect(y_ref, ysc)

    for s in range(samples):
        for t in range(4):
            at = s * rows + t * C
            normed = x[t][s, 0].astype(F32) * inv_ref[s]
            full[at : at + C] = normed
            low[at : at + C] = normed.astype(BF16)
    for s in range(samples):
        at = slice(s * rows, (s + 1) * rows)
        pre[at] = dot(ysc[at], ft_ref[...]) + dot(lt_ref[...], low[at])
    for s in range(samples):
        for t in range(4):
            for c in range(0, C, ROWS):
                at = s * rows + t * C + c
                value, slope = gelu_parts(pre[at : at + ROWS])
                outs[t][s, 0, c : c + ROWS] = (full[at : at + ROWS] + value).astype(BF16)
                slope_ref[at : at + ROWS] = slope


def pixels(ids, inv, x, y, turned, lt):
    samples = inv.shape[0]
    n = 2 * MODES
    tile = 512
    mine = pl.BlockSpec((samples, 1, C, tile), lambda i, ids, inv: (ids[0], 0, 0, i))
    block = pl.BlockSpec((samples, 1, C, tile), lambda i, ids, inv: (0, 0, 0, i))
    rows = samples * 4 * C
    flat = pl.BlockSpec((rows, tile), lambda i, ids, inv: (0, i))
    return pl.pallas_call(
        pixel_kernel,
        grid_spec=pltpu.PrefetchScalarGridSpec(
            num_scalar_prefetch=2,
            grid=(NPIX // tile,),
            in_specs=[mine]
            + [block] * 3
            + [
                whole(y.shape),
                pl.BlockSpec((n, tile), lambda i, ids, inv: (0, i)),
                whole((4 * C, 4 * C)),
            ],
            out_specs=[mine] + [block] * 3 + [flat] * 2,
            scratch_shapes=[
                pltpu.VMEM((rows, n), BF16),
                pltpu.VMEM((rows, tile), F32),
                pltpu.VMEM((rows, tile), F32),
            ],
        ),
        out_shape=[jax.ShapeDtypeStruct(x[0].shape, BF16)]
        + [jax.ShapeDtypeStruct((samples, 1, C, NPIX), BF16)] * 3
        + [jax.ShapeDtypeStruct((rows, NPIX), BF16), jax.ShapeDtypeStruct((rows, NPIX), F32)],
        compiler_params=params(60),
        cost_estimate=cost(3 * rows * NPIX * n, 20_000_000, 2 * rows * NPIX),
        name="pixels",
    )(ids, inv, *x, y, turned, lt)


def slope_kernel(ids_ref, *refs):
    cot = refs[:4]
    low, slope, f_ref, g_ref, g_out, lin_ref, gacc, lacc = refs[4:]
    samples = cot[1].shape[0]
    rows = 4 * C
    i = pl.program_id(0)
    for s in range(samples):
        for t in range(4):
            at = s * rows + t * C
            grad = cot[t][s, 0].astype(F32) * slope[at : at + C]
            g_ref[at : at + C] = grad.astype(BF16)
    part = dot(g_ref[...], f_ref[...])
    lin = None
    for s in range(samples):
        at = slice(s * rows, (s + 1) * rows)
        piece = dot(low[at], g_ref[at], ((1,), (1,)))
        lin = piece if lin is None else lin + piece

    @pl.when(i == 0)
    def _():
        gacc[...] = part
        lacc[...] = lin

    @pl.when(i > 0)
    def _():
        gacc[...] += part
        lacc[...] += lin

    @pl.when(i == pl.num_programs(0) - 1)
    def _():
        spread(gacc, g_out)
        for k in range(4):
            total = None
            for t in range(4):
                u = t ^ k
                piece = lacc[t * C : (t + 1) * C, u * C : (u + 1) * C] * sgn(t, k)
                total = piece if total is None else total + piece
            lin_ref[k] = total


def pixel_grads(ids, cot, low, slope, table, spectrum):
    rows = low.shape[0]
    samples = rows // (4 * C)
    n = 2 * MODES
    tile = 512
    mine = pl.BlockSpec((samples, 1, C, tile), lambda i, ids: (ids[0], 0, 0, i))
    block = pl.BlockSpec((samples, 1, C, tile), lambda i, ids: (0, 0, 0, i))
    flat = pl.BlockSpec((rows, tile), lambda i, ids: (0, i))
    return pl.pallas_call(
        slope_kernel,
        grid_spec=pltpu.PrefetchScalarGridSpec(
            num_scalar_prefetch=1,
            grid=(NPIX // tile,),
            in_specs=[mine]
            + [block] * 3
            + [flat] * 2
            + [pl.BlockSpec((tile, n), lambda i, ids: (i, 0))],
            out_specs=[flat, whole(spectrum), whole((4, C, C))],
            scratch_shapes=[pltpu.VMEM((rows, n), F32), pltpu.VMEM((4 * C, 4 * C), F32)],
        ),
        out_shape=[
            jax.ShapeDtypeStruct((rows, NPIX), BF16),
            jax.ShapeDtypeStruct(spectrum, BF16),
            jax.ShapeDtypeStruct((4, C, C), F32),
        ],
        compiler_params=params(60),
        cost_estimate=cost(3 * rows * NPIX * n, 20_000_000),
        name="pixel_grads",
    )(ids, *cot, low, slope, table)


def inner_kernel(ids_ref, inv_ref, y_ref, g_ref, ft_ref, lb_ref, cot_ref, mine_ref, o1, o2, o3, ysc):
    samples = cot_ref.shape[0]
    rows = 4 * C

    @pl.when(pl.program_id(0) == 0)
    def _():
        collect(y_ref, ysc)

    spatial = dot(ysc[...], ft_ref[...])
    for s in range(samples):
        at = slice(s * rows, (s + 1) * rows)
        total = spatial[at] + dot(lb_ref[...], g_ref[at])
        mine_ref[s, 0] = (cot_ref[s, 0].astype(F32) + total[:C]) * inv_ref[s]
        for t, out in ((1, o1), (2, o2), (3, o3)):
            out[s, 0] = total[t * C : (t + 1) * C].astype(BF16)


def inner_grads(ids, inv, y, g, turned, lb, cotangent):
    samples = inv.shape[0]
    n = 2 * MODES
    tile = 1024
    rows = samples * 4 * C
    mine = pl.BlockSpec((samples, 1, C, tile), lambda i, ids, inv: (ids[0], 0, 0, i))
    block = pl.BlockSpec((samples, 1, C, tile), lambda i, ids, inv: (0, 0, 0, i))
    return pl.pallas_call(
        inner_kernel,
        grid_spec=pltpu.PrefetchScalarGridSpec(
            num_scalar_prefetch=2,
            grid=(NPIX // tile,),
            in_specs=[
                whole(y.shape),
                pl.BlockSpec((rows, tile), lambda i, ids, inv: (0, i)),
                pl.BlockSpec((n, tile), lambda i, ids, inv: (0, i)),
                whole((4 * C, 4 * C)),
                mine,
            ],
            out_specs=[mine] + [block] * 3,
            scratch_shapes=[pltpu.VMEM((rows, n), BF16)],
        ),
        out_shape=[jax.ShapeDtypeStruct(cotangent.shape, F32)]
        + [jax.ShapeDtypeStruct((samples, 1, C, NPIX), BF16)] * 3,
        compiler_params=params(60),
        cost_estimate=cost(3 * rows * NPIX * n, 10_000_000),
        name="inner_grads",
    )(ids, inv, y, g, turned, lb, cotangent)


def place_kernel(ids_ref, a_ref, b_ref, c_ref, old_ref, out_ref):
    for n, part in enumerate((a_ref, b_ref, c_ref)):

        @pl.when(pl.program_id(0) == n)
        def _():
            out_ref[...] = part[...]


def place_output(ids, parts, result):
    samples = parts[0].shape[0]
    shape = (1, 1, C, NPIX)

    def spec(n):
        def at(j, s, ids):
            return (jnp.where(j == n, s, jnp.where(j < n, 0, samples - 1)), 0, 0, 0)

        return pl.BlockSpec(shape, at)

    return pl.pallas_call(
        place_kernel,
        grid_spec=pltpu.PrefetchScalarGridSpec(
            num_scalar_prefetch=1,
            grid=(3, samples),
            in_specs=[spec(0), spec(1), spec(2), pl.BlockSpec(memory_space=pl.ANY)],
            out_specs=pl.BlockSpec(
                shape, lambda j, s, ids: (jnp.bitwise_xor(ids[0], j + 1) * samples + s, 0, 0, 0)
            ),
        ),
        out_shape=jax.ShapeDtypeStruct(result.shape, BF16),
        input_output_aliases={4: 0},
        compiler_params=params(12),
        cost_estimate=cost(0, 12 * samples * C * NPIX),
        name="place",
    )(ids, *parts, result)


def final_kernel(count, codes, ids_ref, inv_ref, cot_ref, *refs):
    samples = pl.num_programs(1)
    j = pl.program_id(0)
    for n in range(count):

        @pl.when(j == n)
        def _():
            inv = inv_ref[jnp.bitwise_xor(ids_ref[0], codes[n]) * samples + pl.program_id(1)]
            refs[-1][...] = (cot_ref[...].astype(F32) + refs[n][...].astype(F32)) * inv


def final_grads(ids, inv, cotangent, parts, codes, result):
    samples = parts[0].shape[0]
    count = len(parts)
    shape = (1, 1, C, NPIX)

    def code(j):
        value = codes[0]
        for n in range(1, count):
            value = jnp.where(j == n, codes[n], value)
        return value

    def spec(n):
        def at(j, s, ids, inv):
            return (jnp.where(j == n, s, jnp.where(j < n, 0, samples - 1)), 0, 0, 0)

        return pl.BlockSpec(shape, at)

    place = pl.BlockSpec(
        shape, lambda j, s, ids, inv: (jnp.bitwise_xor(ids[0], code(j)) * samples + s, 0, 0, 0)
    )
    return pl.pallas_call(
        partial(final_kernel, count, codes),
        grid_spec=pltpu.PrefetchScalarGridSpec(
            num_scalar_prefetch=2,
            grid=(count, samples),
            in_specs=[place]
            + [spec(n) for n in range(count)]
            + [pl.BlockSpec(memory_space=pl.ANY)],
            out_specs=place,
        ),
        out_shape=jax.ShapeDtypeStruct(cotangent.shape, F32),
        input_output_aliases={3 + count: 0},
        compiler_params=params(12),
        cost_estimate=cost(0, 8 * count * samples * C * NPIX),
        name="final",
    )(ids, inv, cotangent, *parts, result)


def adamw(weight, first, second, grad):
    first_new = BETA_ONE * first + (1.0 - BETA_ONE) * grad
    second_new = BETA_TWO * second + (1.0 - BETA_TWO) * grad * grad
    corr_one = 1.0 - BETA_ONE**STEP_COUNT
    corr_two = 1.0 - BETA_TWO**STEP_COUNT
    update = first_new / corr_one / (jnp.sqrt(second_new / corr_two) + EPSILON)
    return (weight - RATE * (update + DECAY * weight), first_new, second_new)


def adam_kernel(flips, d0, d1, d2, d3, w_ref, first_ref, second_ref, w_out, first_out, second_out):
    grad = d0[...].astype(F32) * flips[0]
    for t, d in ((1, d1), (2, d2), (3, d3)):
        grad = grad + d[...].astype(F32) * flips[t]
    for q in range(QUAD):
        for r in range(2):
            lane = q * LANES + r * C
            at = (0, q, r)
            new = adamw(w_ref[at], first_ref[at], second_ref[at], grad[:, lane : lane + C])
            w_out[at], first_out[at], second_out[at] = new


def adam_spec(flips, grads, weight, first, second):
    modes = weight.shape[1]
    packed = pl.BlockSpec((C, QUAD * LANES), lambda g: (0, g))
    block = pl.BlockSpec((1, QUAD, 2, C, C), lambda g: (0, g, 0, 0, 0))
    return pl.pallas_call(
        adam_kernel,
        grid=(modes // QUAD,),
        in_specs=[pl.BlockSpec(memory_space=SMEM)] + [packed] * 4 + [block] * 3,
        out_specs=[block] * 3,
        out_shape=[jax.ShapeDtypeStruct(weight.shape, F32)] * 3,
        compiler_params=params(12),
        cost_estimate=cost(modes * 4608 * 20, modes * 4608 * 72, modes * 4608),
        name="adam",
    )(flips, *grads, weight, first, second)


def swap(value, axis, size, x):
    return lax.ppermute(value, axis, [(i, i ^ x) for i in range(size)])


def to_modes(value):
    return lax.all_to_all(value, "dp", split_axis=0, concat_axis=0, tiled=True)


def after(values, first):
    values, _ = lax.optimization_barrier((values, first))
    return values


def body(
    shards,
    inputs,
    cotangent,
    norm_table,
    sample_index,
    spec_weight,
    spec_first,
    spec_second,
    lin_weight,
    lin_first,
    lin_second,
):
    own = lax.axis_index("blade")
    shard = lax.axis_index("dp")
    ids = jnp.stack([own, shard]).astype(jnp.int32)
    samples = inputs.shape[0] // 4

    def send(array, t):
        block = lax.dynamic_slice_in_dim(array, jnp.bitwise_xor(own, t) * samples, samples, 0)
        return block, swap(block, "blade", 4, t)

    sent, x3 = send(inputs, 3)
    rest = after(inputs, sent)
    sent, x1 = send(rest, 1)
    rest = after(rest, sent)
    _, x2 = send(rest, 2)

    matches = sample_index[:, None] == jnp.arange(NTAB, dtype=jnp.int32)[None, :]
    normalizer = jnp.sum(jnp.where(matches, norm_table[None, :], 0.0), axis=1)
    inv_all = 1.0 / normalizer
    inv = lax.dynamic_slice_in_dim(inv_all, own * samples, samples, 0)

    table, turned = make_tables()
    packed = pack_weights(spec_weight, lin_weight)
    packs = [packed] + [swap(packed, "blade", 4, t) for t in (1, 2, 3)]

    x3, packed = after(x3, packed), packed
    xa = to_modes(forward_spectrum(ids, inv, (inputs, x3), table, shards))
    late = after(cotangent, (x1, x2))
    cot = (cotangent,) + tuple(send(late, t)[1] for t in (1, 2, 3))
    xb = to_modes(forward_spectrum(ids, inv, (x1, x2), table, shards))
    pq, lt, lb = unpack(ids, packs)
    y = to_modes(mix(ids, xa, xb, pq))

    result = pixels(ids, inv, (inputs, x1, x2, x3), y, turned, lt)
    output, low, slope = result[0], result[4], result[5]
    out_parts = [swap(result[t], "blade", 4, t) for t in (1, 2, 3)]

    grad_pre, sent, lin = pixel_grads(ids, cot, low, slope, table, y.shape)
    g = to_modes(sent)
    back = to_modes(mix_back(ids, g, pq))
    spec_grads = weight_grads(ids, xa, xb, g, lin)
    spec_grads = [spec_grads[0]] + [swap(spec_grads[t], "blade", 4, t) for t in (1, 2, 3)]

    flips = jnp.stack(
        [jnp.where(own % 2 == 1, flip_of(jnp.bitwise_xor(own, t), 1), 1.0) for t in range(4)]
    )
    lin_grad = 0.0
    first = spec_weight.shape[1] * LANES
    for t in range(4):
        lin_grad = lin_grad + spec_grads[t][:, first : first + C].astype(F32) * flips[t]
    step = 1
    while step < shards:
        lin_grad = lin_grad + swap(lin_grad, "dp", shards, step)
        step *= 2

    inner = inner_grads(ids, inv, back, grad_pre, turned, lb, cotangent)
    inner = after(inner, out_parts)
    grad_parts = [swap(inner[t], "blade", 4, t) for t in (1, 2, 3)]

    output = place_output(ids, out_parts, output)
    spec_out = adam_spec(flips, spec_grads, spec_weight, spec_first, spec_second)
    lin_out = adamw(lin_weight, lin_first, lin_second, lin_grad[None])
    input_grad = final_grads(ids, inv_all, cotangent, grad_parts[2:], (3,), inner[0])
    input_grad = final_grads(ids, inv_all, cotangent, grad_parts[:2], (1, 2), input_grad)
    return (output, input_grad, *spec_out, *lin_out)


def solution(mesh):
    fields = P("dp", "blade", None, None)
    spec = P("blade", "dp", None, None, None)
    lin = P("blade", None, None)
    return jax.shard_map(
        partial(body, mesh.shape["dp"]),
        mesh=mesh,
        in_specs=(fields, fields, P(), P("dp"), spec, spec, spec, lin, lin, lin),
        out_specs=(fields, fields, spec, spec, spec, lin, lin, lin),
        check_vma=False,
    )
```

```python
from functools import partial
import math

import jax
import jax.numpy as jnp
from jax import lax
from jax.experimental import pallas as pl
from jax.experimental.pallas import tpu as pltpu
from jax.sharding import PartitionSpec as P

GRID = 64
MSIDE = 16
NTAB = 16
STEP_COUNT = 5
NPIX = 4096
MODES = 256
C = 48
LANES = 2 * C
QUAD = 4
PACK = 128
ROWS = 16

BETA_ONE = 0.9
BETA_TWO = 0.999
EPSILON = 1e-08
RATE = 0.1
DECAY = 0.01

F32 = jnp.float32
BF16 = jnp.bfloat16
SMEM = pltpu.MemorySpace.SMEM


def sgn(left, right):
    return -1.0 if (left & 2) and (right & 1) else 1.0


def flip_of(own, k):
    if k & 1:
        return (1 - 2 * ((own // 2) % 2)).astype(F32)
    return jnp.float32(1.0)


def mode_factor(mode):
    return jnp.where(mode % MSIDE == 0, 1.0, 2.0).astype(F32)


def dot(left, right, dims=((1,), (0,))):
    return lax.dot_general(left, right, (dims, ((), ())), preferred_element_type=F32)


def whole(shape):
    zeros = (0,) * len(shape)
    return pl.BlockSpec(tuple(shape), lambda *_: zeros)


def params(mib):
    return pltpu.CompilerParams(vmem_limit_bytes=mib * 1024 * 1024)


def fast(shape, kind):
    return pltpu.VMEM(tuple(shape), kind)


def slow(shape, kind):
    return pltpu.HBM(tuple(shape), kind)


def pin(*arrays):
    return [pltpu.with_memory_space_constraint(array, pltpu.VMEM) for array in arrays]


def stay(*arrays):
    return [pltpu.with_memory_space_constraint(array, pltpu.HBM) for array in arrays]


def in_vmem(count):
    return [pl.BlockSpec(memory_space=pltpu.MemorySpace.VMEM)] * count


def cost():
    return pl.CostEstimate(flops=1, bytes_accessed=1, transcendentals=0)


def small_tables():
    mode_ids = jnp.arange(2 * MODES, dtype=jnp.int32)
    imag = mode_ids >= MODES
    mode_ids = mode_ids % MODES
    row_index = mode_ids // MSIDE
    col_freq = mode_ids % MSIDE
    row_freq = jnp.where(row_index < MSIDE // 2, row_index, GRID - MSIDE + row_index)
    place = jnp.arange(GRID, dtype=jnp.int32)[:, None]
    row_angle = ((place * row_freq[None, :]) % GRID).astype(F32) * (2.0 * math.pi / GRID)
    col_angle = ((place * col_freq[None, :]) % GRID).astype(F32) * (2.0 * math.pi / GRID)
    row_cos, row_sin = jnp.cos(row_angle) / GRID, jnp.sin(row_angle) / GRID
    first = jnp.where(imag[None, :], -row_sin, row_cos)
    second = jnp.where(imag[None, :], -row_cos, -row_sin)
    return jnp.stack([first, second, jnp.cos(col_angle), jnp.sin(col_angle)])


def table_rows(row_ref, col_ref, start, stop):
    tiles = []
    for h in range(start, stop):
        tile = row_ref[0, h : h + 1] * col_ref[0] + row_ref[1, h : h + 1] * col_ref[1]
        tiles.append(tile.astype(BF16))
    return jnp.concatenate(tiles, axis=0)


def small_specs(tile):
    n = 2 * MODES
    return [
        pl.BlockSpec((2, tile // GRID, n), lambda i, *_: (0, i, 0)),
        pl.BlockSpec((2, GRID, n), lambda i, *_: (1, 0, 0)),
    ]


def turned_kernel(row_ref, col_ref, ft_ref):
    for h in range(0, row_ref.shape[1], 2):
        tile = table_rows(row_ref, col_ref, h, h + 2)
        ft_ref[:, h * GRID : (h + 2) * GRID] = tile.astype(F32).T.astype(BF16)


def turned_table(small):
    rows = 8
    n = 2 * MODES
    return pl.pallas_call(
        turned_kernel,
        grid=(GRID // rows,),
        in_specs=small_specs(rows * GRID),
        out_specs=pl.BlockSpec((n, rows * GRID), lambda i: (0, i)),
        out_shape=slow((n, NPIX), BF16),
        compiler_params=params(12),
        cost_estimate=cost(),
        name="turned",
    )(*stay(small, small))


def pack_kernel(w_ref, l_ref, o_ref):
    def step(g, carry):
        parts = [w_ref[0, g * QUAD + q, r] for q in range(QUAD) for r in range(2)]
        at = pl.ds(pl.multiple_of(g * QUAD * LANES, PACK), QUAD * LANES)
        o_ref[:, at] = jnp.concatenate(parts, axis=1).astype(BF16)
        return carry

    modes = w_ref.shape[1]
    lax.fori_loop(0, modes // QUAD, step, 0)
    line = jnp.concatenate([l_ref[0], jnp.zeros((C, PACK - C), F32)], axis=1)
    o_ref[:, modes * LANES :] = line.astype(BF16)


def pack_weights(spec_weight, lin_weight):
    modes = spec_weight.shape[1]
    return pl.pallas_call(
        pack_kernel,
        in_specs=in_vmem(2),
        out_specs=in_vmem(1)[0],
        out_shape=jax.ShapeDtypeStruct((C, modes * LANES + PACK), BF16),
        compiler_params=params(12),
        cost_estimate=cost(),
        name="pack",
    )(spec_weight, lin_weight)


def lanes_of(shape):
    return lax.broadcasted_iota(jnp.int32, shape, len(shape) - 1)


def split_lanes(a, b, c):
    lane = lanes_of(a.shape)
    second = jnp.where(lane < 32, pltpu.roll(a, 32, 1), pltpu.roll(b, 32, 1))
    third = jnp.where(lane < 64, pltpu.roll(b, 64, 1), pltpu.roll(c, 64, 1))
    return a, second, third, pltpu.roll(c, 96, 1)


def join_lanes(first, second, third, fourth):
    lane = lanes_of(first.shape)
    a = jnp.where(lane < 96, first, pltpu.roll(second, 96, 1))
    b = jnp.where(lane < 64, pltpu.roll(second, 96, 1), pltpu.roll(third, 64, 1))
    c = jnp.where(lane < 32, pltpu.roll(third, 64, 1), pltpu.roll(fourth, 32, 1))
    return a, b, c


def quad_tiles(ref, g):
    tiles = []
    for n in range(3):
        at = pl.ds(pl.multiple_of(g * QUAD * LANES + n * PACK, PACK), PACK)
        tiles.append(ref[:, at].astype(F32))
    return tiles


def unpack_kernel(ids_ref, w0, w1, w2, w3, pq_ref):
    own = ids_ref[0]
    lane = lanes_of((C, PACK))

    def step(g, carry):
        for t, w in enumerate((w0, w1, w2, w3)):
            slot = jnp.bitwise_xor(own, t)
            flip = jnp.where(slot % 2 == 1, flip_of(own, 1), 1.0)
            at = pl.ds(pl.multiple_of(slot * PACK, PACK), PACK)
            tiles = [tile * flip for tile in quad_tiles(w, g)]
            for q, p in enumerate(split_lanes(*tiles)):
                p = jnp.where(lane < LANES, p, 0.0)
                low = jnp.where(lane < C, -pltpu.roll(p, PACK - C, 1), pltpu.roll(p, C, 1))
                low = jnp.where(lane < LANES, low, 0.0)
                pq_ref[g * QUAD + q, :C, at] = p.astype(BF16)
                pq_ref[g * QUAD + q, C:, at] = low.astype(BF16)
        return carry

    lax.fori_loop(0, pq_ref.shape[0] // QUAD, step, 0)


def unpack(ids, packs):
    modes = (packs[0].shape[1] - PACK) // LANES
    return pl.pallas_call(
        unpack_kernel,
        in_specs=[pl.BlockSpec(memory_space=SMEM)] + in_vmem(4),
        out_specs=in_vmem(1)[0],
        out_shape=fast((modes, LANES, 4 * PACK), BF16),
        compiler_params=params(12),
        cost_estimate=cost(),
        name="unpack",
    )(ids, *packs)


def lines_kernel(ids_ref, w0, w1, w2, w3, lt_ref, lb_ref, lsc):
    own = ids_ref[0]
    for t, w in enumerate((w0, w1, w2, w3)):
        slot = jnp.bitwise_xor(own, t)
        flip = jnp.where(slot % 2 == 1, flip_of(own, 1), 1.0)
        lsc[slot] = w[...].astype(F32) * flip
    for k in range(4):
        line = lsc[k]
        turned = line.T
        for t in range(4):
            u = t ^ k
            lb_ref[t * C : (t + 1) * C, u * C : (u + 1) * C] = (line[:, :C] * sgn(t, k)).astype(BF16)
            lt_ref[u * C : (u + 1) * C, t * C : (t + 1) * C] = (turned[:C] * sgn(t, k)).astype(BF16)


def unpack_lines(ids, packs):
    last = packs[0].shape[1] // PACK - 1
    return pl.pallas_call(
        lines_kernel,
        grid=(1,),
        in_specs=[pl.BlockSpec(memory_space=SMEM)]
        + [pl.BlockSpec((C, PACK), lambda i: (0, last))] * 4,
        out_specs=[whole((4 * C, 4 * C))] * 2,
        out_shape=[fast((4 * C, 4 * C), BF16), slow((4 * C, 4 * C), BF16)],
        scratch_shapes=[pltpu.VMEM((4, C, PACK), F32)],
        compiler_params=params(12),
        cost_estimate=cost(),
        name="lines",
    )(ids, *packs)


def spread(acc, out_ref, scales=None):
    rows = []
    for n in range(acc.shape[0] // C):
        for r in range(2):
            row = acc[n * C : (n + 1) * C, r * MODES : (r + 1) * MODES]
            rows.append(row if scales is None else row * scales[n])
    turned = jnp.concatenate(rows, axis=0).T
    out_ref[...] = turned.reshape(out_ref.shape).astype(BF16)


def collect(block, ysc):
    turned = block[...].astype(F32).reshape(MODES, block.shape[2]).T
    for n in range(ysc.shape[0] // C):
        for r in range(2):
            row = (n * 2 + r) * C
            piece = turned[row : row + C].astype(BF16)
            ysc[n * C : (n + 1) * C, r * MODES : (r + 1) * MODES] = piece


def forward_kernel(ids_ref, inv_ref, x0, x1, row_ref, col_ref, out_ref, acc):
    i = pl.program_id(0)
    samples = x0.shape[0]
    rows = [x[s, 0] for s in range(samples) for x in (x0, x1)]
    table = table_rows(row_ref, col_ref, 0, row_ref.shape[1])
    part = dot(jnp.concatenate(rows, axis=0), table)

    @pl.when(i == 0)
    def _():
        acc[...] = part

    @pl.when(i > 0)
    def _():
        acc[...] += part

    @pl.when(i == pl.num_programs(0) - 1)
    def _():
        spread(acc, out_ref, [inv_ref[s] for s in range(samples) for _ in range(2)])


def forward_spectrum(ids, inv, x, small, shards):
    samples = inv.shape[0]
    modes = MODES // shards
    width = samples * 2 * LANES
    n = 2 * MODES
    tile = 1024

    def spec(array):
        if array.shape[0] == samples:
            return pl.BlockSpec((samples, 1, C, tile), lambda i, ids, inv: (0, 0, 0, i))
        return pl.BlockSpec((samples, 1, C, tile), lambda i, ids, inv: (ids[0], 0, 0, i))

    return pl.pallas_call(
        forward_kernel,
        grid_spec=pltpu.PrefetchScalarGridSpec(
            num_scalar_prefetch=2,
            grid=(NPIX // tile,),
            in_specs=[spec(x[0]), spec(x[1])] + small_specs(tile),
            out_specs=whole((shards, modes, width)),
            scratch_shapes=[pltpu.VMEM((samples * 2 * C, n), F32)],
        ),
        out_shape=slow((shards, modes, width), BF16),
        compiler_params=params(12),
        cost_estimate=cost(),
        name="forward",
    )(ids, inv, *stay(*x), *stay(small, small))


def row_scratch(modes, shards, width):
    return pltpu.VMEM((width // PACK, modes * shards, PACK), F32)


def gather_rows(blocks, sc):
    shards, modes = blocks[0].shape[:2]
    first = 0
    for block in blocks:
        for n in range(block.shape[2] // PACK):
            for x in range(shards):
                rows = block[x, :, n * PACK : (n + 1) * PACK].astype(F32)
                sc[first + n, pl.ds(x, modes, stride=shards), :] = rows
        first += block.shape[2] // PACK


def scatter_rows(ysc, out):
    shards, modes = out.shape[:2]
    for x in range(shards):
        for n in range(ysc.shape[0]):
            piece = ysc[n, pl.ds(x, modes, stride=shards), :]
            out[x, :, n * PACK : (n + 1) * PACK] = piece.astype(BF16)


def blade_rows(sc, mode, shards, order):
    at = pl.ds(pl.multiple_of(mode * shards, shards), shards)
    found = [[] for _ in range(4)]
    for n in range(0, len(order), 4):
        tile = n // 4 * 3
        pieces = split_lanes(sc[tile, at, :], sc[tile + 1, at, :], sc[tile + 2, at, :])
        for piece, (_, t) in zip(pieces, order[n : n + 4]):
            found[t].append(piece)
    return [jnp.concatenate(found[t], axis=0) for t in range(4)]


def split_order(samples):
    return [(s, t) for pair in ((0, 3), (1, 2)) for s in range(samples) for t in pair]


def plain_order(samples):
    return [(s, t) for s in range(samples) for t in range(4)]


def mix_modes(xsc, ysc, pq_ref, order, shards, first_mode, back):
    modes = xsc.shape[1] // shards
    samples = len(order) // 4
    group = samples * shards

    def step(m, carry):
        low = jnp.concatenate(blade_rows(xsc, m, shards, order), axis=0)
        low = low[:, :LANES].astype(BF16)
        total = [None] * 4
        if not back:
            parts = dot(low, pq_ref[m])
        for k in range(4):
            if back:
                part = dot(low, pq_ref[m, :, k * PACK : k * PACK + LANES], ((1,), (1,)))
            else:
                part = parts[:, k * PACK : (k + 1) * PACK]
            for t in range(4):
                u = t ^ k
                piece = part[t * group : (t + 1) * group]
                sign = sgn(u, k) if back else sgn(t, k)
                if total[u] is None:
                    total[u] = piece if sign > 0 else -piece
                else:
                    total[u] = total[u] + piece if sign > 0 else total[u] - piece
        factor = mode_factor(first_mode + m)
        at = pl.ds(pl.multiple_of(m * shards, shards), shards)
        for s in range(samples):
            rows = []
            for u in range(4):
                piece = total[u][s * shards : (s + 1) * shards] * factor
                if back:
                    piece = jnp.concatenate([piece, jnp.zeros((shards, PACK - LANES), F32)], axis=1)
                rows.append(piece)
            for n, tile in enumerate(join_lanes(*rows)):
                ysc[s * 3 + n, at, :] = tile
        return carry

    lax.fori_loop(0, modes, step, 0, unroll=4)


def mix_kernel(ids_ref, xa, xb, pq_ref, y_ref, xsc, ysc):
    shards, modes, half = xa.shape
    gather_rows((xa, xb), xsc)
    order = split_order(half // (2 * LANES))
    mix_modes(xsc, ysc, pq_ref, order, shards, ids_ref[1] * modes, False)
    scatter_rows(ysc, y_ref)


def mix(ids, xa, xb, pq):
    shards, modes, half = xa.shape
    return pl.pallas_call(
        mix_kernel,
        in_specs=[pl.BlockSpec(memory_space=SMEM)] + in_vmem(3),
        out_specs=in_vmem(1)[0],
        out_shape=slow((shards, modes, 2 * half), BF16),
        scratch_shapes=[row_scratch(modes, shards, 2 * half)] * 2,
        compiler_params=params(12),
        cost_estimate=cost(),
        name="mix",
    )(ids, xa, xb, *pin(pq))


def mix_back_kernel(ids_ref, g_ref, pq_ref, out_ref, gsc, ysc):
    shards, modes, width = g_ref.shape
    gather_rows((g_ref,), gsc)
    order = plain_order(width // (4 * LANES))
    mix_modes(gsc, ysc, pq_ref, order, shards, ids_ref[1] * modes, True)
    scatter_rows(ysc, out_ref)


def mix_back(ids, g, pq):
    shards, modes, width = g.shape
    return pl.pallas_call(
        mix_back_kernel,
        in_specs=[pl.BlockSpec(memory_space=SMEM)] + in_vmem(2),
        out_specs=in_vmem(1)[0],
        out_shape=slow(g.shape, BF16),
        scratch_shapes=[row_scratch(modes, shards, width)] * 2,
        compiler_params=params(12),
        cost_estimate=cost(),
        name="mix_back",
    )(ids, g, *pin(pq))


def grad_kernel(ids_ref, xa, xb, g_ref, lin_ref, o0, o1, o2, o3, xsc, gsc, osc):
    shards, modes, width = g_ref.shape
    samples = width // (4 * LANES)
    own = ids_ref[0]
    first_mode = ids_ref[1] * modes
    gather_rows((xa, xb), xsc)
    gather_rows((g_ref,), gsc)
    lane = lanes_of((samples * shards, PACK))

    def step(g, carry):
        found = [[] for _ in range(4)]
        for q in range(QUAD):
            m = g * QUAD + q
            x = blade_rows(xsc, m, shards, split_order(samples))
            x = x + [pltpu.roll(rows, PACK - C, 1) for rows in x]
            left = jnp.concatenate(x, axis=0)[:, :C].astype(BF16)
            factor = mode_factor(first_mode + m)
            plain = blade_rows(gsc, m, shards, plain_order(samples))
            plain = [rows * factor for rows in plain]
            turned = [
                jnp.where(lane < C, pltpu.roll(rows, PACK - C, 1), -pltpu.roll(rows, C, 1))
                for rows in plain
            ]
            plus = [rows.astype(BF16) for rows in plain + turned]
            minus = [(-rows).astype(BF16) for rows in plain + turned]
            right = []
            for k in range(4):
                rows = []
                for r in range(2):
                    for t in range(4):
                        rows.append((plus if sgn(t, k) > 0 else minus)[4 * r + (t ^ k)])
                right.append(jnp.concatenate(rows, axis=0))
            grad = dot(left, jnp.concatenate(right, axis=1), ((0,), (0,)))
            for k in range(4):
                found[k].append(grad[:, k * PACK : (k + 1) * PACK])
        for k in range(4):
            for n, tile in enumerate(join_lanes(*found[k])):
                at = pl.ds(pl.multiple_of(g * QUAD * LANES + n * PACK, PACK), PACK)
                osc[k, :, at] = tile.astype(BF16)
        return carry

    lax.fori_loop(0, modes // QUAD, step, 0)
    for k in range(4):
        line = jnp.concatenate([lin_ref[k], jnp.zeros((C, PACK - C), F32)], axis=1)
        osc[k, :, modes * LANES :] = line.astype(BF16)
    for t, out in enumerate((o0, o1, o2, o3)):
        out[...] = osc[jnp.bitwise_xor(own, t)]


def weight_grads(ids, xa, xb, g, lin):
    shards, modes, width = g.shape
    shape = (C, modes * LANES + PACK)
    return pl.pallas_call(
        grad_kernel,
        in_specs=[pl.BlockSpec(memory_space=SMEM)] + in_vmem(4),
        out_specs=in_vmem(4),
        out_shape=[slow(shape, BF16)] * 4,
        scratch_shapes=[row_scratch(modes, shards, width)] * 2 + [pltpu.VMEM((4,) + shape, BF16)],
        compiler_params=params(12),
        cost_estimate=cost(),
        name="weight_grads",
    )(ids, xa, xb, g, lin)


CDF_AT = 0.28
CDF = (0.11652094, 0.06749571, 0.2689128, -0.23699677, 0.38987606, -0.10580875)
SERIES = [value / CDF_AT ** (i + 1) for i, value in enumerate(CDF)]


def gelu_parts(v):
    z = jnp.abs(v)
    t = 1.0 / (z + 1.0 / CDF_AT)
    bell = jnp.exp2(v * v * (-0.5 * math.log2(math.e)))
    series = jnp.float32(SERIES[-1])
    for value in SERIES[-2::-1]:
        series = series * t + value
    tail = series * t * bell
    cdf = jnp.where(v < 0.0, tail, 1.0 - tail)
    return v * cdf, cdf + v * (bell * (1.0 / math.sqrt(2.0 * math.pi)))


def pixel_kernel(ids_ref, inv_ref, *refs):
    x = refs[:4]
    y_ref, ft_ref, lt_ref = refs[4:7]
    outs = refs[7:11]
    slope_ref = refs[11]
    ysc, pre, lts = refs[12:]
    samples = x[1].shape[0]
    rows = 4 * C

    @pl.when(pl.program_id(0) == 0)
    def _():
        collect(y_ref, ysc)
        for s in range(samples):
            lts[s] = (lt_ref[...].astype(F32) * inv_ref[s]).astype(BF16)

    for s in range(samples):
        at = slice(s * rows, (s + 1) * rows)
        fields = jnp.concatenate([x[t][s, 0] for t in range(4)], axis=0)
        pre[at] = dot(ysc[at], ft_ref[...]) + dot(lts[s], fields)
    for s in range(samples):
        for t in range(4):
            for c in range(0, C, ROWS):
                at = s * rows + t * C + c
                value, slope = gelu_parts(pre[at : at + ROWS])
                normed = x[t][s, 0, c : c + ROWS].astype(F32) * inv_ref[s]
                outs[t][s, 0, c : c + ROWS] = (normed + value).astype(BF16)
                slope_ref[at : at + ROWS] = slope.astype(BF16)


def pixels(ids, inv, x, y, turned, lt):
    samples = inv.shape[0]
    n = 2 * MODES
    tile = 512
    mine = pl.BlockSpec((samples, 1, C, tile), lambda i, ids, inv: (ids[0], 0, 0, i))
    block = pl.BlockSpec((samples, 1, C, tile), lambda i, ids, inv: (0, 0, 0, i))
    rows = samples * 4 * C
    flat = pl.BlockSpec((rows, tile), lambda i, ids, inv: (0, i))
    return pl.pallas_call(
        pixel_kernel,
        grid_spec=pltpu.PrefetchScalarGridSpec(
            num_scalar_prefetch=2,
            grid=(NPIX // tile,),
            in_specs=[mine]
            + [block] * 3
            + [
                whole(y.shape),
                pl.BlockSpec((n, tile), lambda i, ids, inv: (0, i)),
                whole((4 * C, 4 * C)),
            ],
            out_specs=[mine] + [block] * 3 + [flat],
            scratch_shapes=[
                pltpu.VMEM((rows, n), BF16),
                pltpu.VMEM((rows, tile), F32),
                pltpu.VMEM((samples, 4 * C, 4 * C), BF16),
            ],
        ),
        out_shape=[slow(x[0].shape, BF16)]
        + [slow((samples, 1, C, NPIX), BF16)] * 3
        + [fast((rows, NPIX), BF16)],
        compiler_params=params(12),
        cost_estimate=cost(),
        name="pixels",
    )(ids, inv, *stay(*x), y, *stay(turned), *pin(lt))


def slope_kernel(ids_ref, inv_ref, *refs):
    x, cot = refs[:4], refs[4:8]
    slope, row_ref, col_ref, g_ref, g_out, lin_ref, gacc, lacc = refs[8:]
    samples = cot[1].shape[0]
    rows = 4 * C
    i = pl.program_id(0)

    @pl.when(i == 0)
    def _():
        gacc[...] = jnp.zeros_like(gacc)
        lacc[...] = jnp.zeros_like(lacc)

    for s in range(samples):
        for t in range(4):
            at = s * rows + t * C
            grad = cot[t][s, 0].astype(F32) * slope[at : at + C].astype(F32)
            g_ref[at : at + C] = grad.astype(BF16)
    table = table_rows(row_ref, col_ref, 0, row_ref.shape[1])
    for s in range(samples):
        at = slice(s * rows, (s + 1) * rows)
        g = g_ref[at]
        gacc[at] += dot(g, table)
        fields = jnp.concatenate([x[t][s, 0] for t in range(4)], axis=0)
        lacc[...] += dot(fields, g, ((1,), (1,))) * inv_ref[s]

    @pl.when(i == pl.num_programs(0) - 1)
    def _():
        spread(gacc, g_out)
        for k in range(4):
            total = None
            for t in range(4):
                u = t ^ k
                piece = lacc[t * C : (t + 1) * C, u * C : (u + 1) * C] * sgn(t, k)
                total = piece if total is None else total + piece
            lin_ref[k] = total


def pixel_grads(ids, inv, x, cot, slope, small, spectrum):
    rows = slope.shape[0]
    samples = rows // (4 * C)
    n = 2 * MODES
    tile = 1024
    mine = pl.BlockSpec((samples, 1, C, tile), lambda i, ids, inv: (ids[0], 0, 0, i))
    block = pl.BlockSpec((samples, 1, C, tile), lambda i, ids, inv: (0, 0, 0, i))
    flat = pl.BlockSpec((rows, tile), lambda i, ids, inv: (0, i))
    return pl.pallas_call(
        slope_kernel,
        grid_spec=pltpu.PrefetchScalarGridSpec(
            num_scalar_prefetch=2,
            grid=(NPIX // tile,),
            in_specs=([mine] + [block] * 3) * 2
            + [flat]
            + small_specs(tile),
            out_specs=[flat, whole(spectrum), whole((4, C, C))],
            scratch_shapes=[pltpu.VMEM((rows, n), F32), pltpu.VMEM((4 * C, 4 * C), F32)],
        ),
        out_shape=[
            slow((rows, NPIX), BF16),
            slow(spectrum, BF16),
            jax.ShapeDtypeStruct((4, C, C), F32),
        ],
        compiler_params=params(12),
        cost_estimate=cost(),
        name="pixel_grads",
    )(ids, inv, *stay(*x), *stay(*cot), *pin(slope), *stay(small, small))


def inner_kernel(ids_ref, inv_ref, y_ref, g_ref, ft_ref, lb_ref, cot_ref, mine_ref, o1, o2, o3, ysc):
    samples = cot_ref.shape[0]
    rows = 4 * C

    @pl.when(pl.program_id(0) == 0)
    def _():
        collect(y_ref, ysc)

    spatial = dot(ysc[...], ft_ref[...])
    for s in range(samples):
        at = slice(s * rows, (s + 1) * rows)
        total = spatial[at] + dot(lb_ref[...], g_ref[at])
        mine_ref[s, 0] = (cot_ref[s, 0].astype(F32) + total[:C]) * inv_ref[s]
        for t, out in ((1, o1), (2, o2), (3, o3)):
            out[s, 0] = total[t * C : (t + 1) * C].astype(BF16)


def inner_grads(ids, inv, y, g, turned, lb, cotangent):
    samples = inv.shape[0]
    n = 2 * MODES
    tile = 1024
    rows = samples * 4 * C
    mine = pl.BlockSpec((samples, 1, C, tile), lambda i, ids, inv: (ids[0], 0, 0, i))
    block = pl.BlockSpec((samples, 1, C, tile), lambda i, ids, inv: (0, 0, 0, i))
    return pl.pallas_call(
        inner_kernel,
        grid_spec=pltpu.PrefetchScalarGridSpec(
            num_scalar_prefetch=2,
            grid=(NPIX // tile,),
            in_specs=[
                whole(y.shape),
                pl.BlockSpec((rows, tile), lambda i, ids, inv: (0, i)),
                pl.BlockSpec((n, tile), lambda i, ids, inv: (0, i)),
                whole((4 * C, 4 * C)),
                mine,
            ],
            out_specs=[mine] + [block] * 3,
            scratch_shapes=[pltpu.VMEM((rows, n), BF16)],
        ),
        out_shape=[slow(cotangent.shape, F32)] + [slow((samples, 1, C, NPIX), BF16)] * 3,
        compiler_params=params(12),
        cost_estimate=cost(),
        name="inner_grads",
    )(ids, inv, y, *stay(g, turned), lb, *stay(cotangent))


def place_kernel(ids_ref, a_ref, b_ref, c_ref, old_ref, out_ref):
    for n, part in enumerate((a_ref, b_ref, c_ref)):

        @pl.when(pl.program_id(0) == n)
        def _():
            out_ref[...] = part[...]


def place_output(ids, parts, result):
    samples = parts[0].shape[0]
    shape = (1, 1, C, NPIX)

    def spec(n):
        def at(j, s, ids):
            return (jnp.where(j == n, s, jnp.where(j < n, 0, samples - 1)), 0, 0, 0)

        return pl.BlockSpec(shape, at)

    return pl.pallas_call(
        place_kernel,
        grid_spec=pltpu.PrefetchScalarGridSpec(
            num_scalar_prefetch=1,
            grid=(3, samples),
            in_specs=[spec(0), spec(1), spec(2), pl.BlockSpec(memory_space=pl.ANY)],
            out_specs=pl.BlockSpec(
                shape, lambda j, s, ids: (jnp.bitwise_xor(ids[0], j + 1) * samples + s, 0, 0, 0)
            ),
        ),
        out_shape=jax.ShapeDtypeStruct(result.shape, BF16),
        input_output_aliases={4: 0},
        compiler_params=params(12),
        cost_estimate=cost(),
        name="place",
    )(ids, *parts, result)


def final_kernel(count, codes, ids_ref, inv_ref, cot_ref, *refs):
    samples = pl.num_programs(1)
    j = pl.program_id(0)
    for n in range(count):

        @pl.when(j == n)
        def _():
            inv = inv_ref[jnp.bitwise_xor(ids_ref[0], codes[n]) * samples + pl.program_id(1)]
            refs[-1][...] = (cot_ref[...].astype(F32) + refs[n][...].astype(F32)) * inv


def final_grads(ids, inv, cotangent, parts, codes, result):
    samples = parts[0].shape[0]
    count = len(parts)
    shape = (1, 1, C, NPIX)

    def code(j):
        value = codes[0]
        for n in range(1, count):
            value = jnp.where(j == n, codes[n], value)
        return value

    def spec(n):
        def at(j, s, ids, inv):
            return (jnp.where(j == n, s, jnp.where(j < n, 0, samples - 1)), 0, 0, 0)

        return pl.BlockSpec(shape, at)

    place = pl.BlockSpec(
        shape, lambda j, s, ids, inv: (jnp.bitwise_xor(ids[0], code(j)) * samples + s, 0, 0, 0)
    )
    return pl.pallas_call(
        partial(final_kernel, count, codes),
        grid_spec=pltpu.PrefetchScalarGridSpec(
            num_scalar_prefetch=2,
            grid=(count, samples),
            in_specs=[place]
            + [spec(n) for n in range(count)]
            + [pl.BlockSpec(memory_space=pl.ANY)],
            out_specs=place,
        ),
        out_shape=jax.ShapeDtypeStruct(cotangent.shape, F32),
        input_output_aliases={3 + count: 0},
        compiler_params=params(12),
        cost_estimate=cost(),
        name="final",
    )(ids, inv, cotangent, *parts, result)


def adamw(weight, first, second, grad):
    first_new = BETA_ONE * first + (1.0 - BETA_ONE) * grad
    second_new = BETA_TWO * second + (1.0 - BETA_TWO) * grad * grad
    corr_one = 1.0 - BETA_ONE**STEP_COUNT
    corr_two = 1.0 - BETA_TWO**STEP_COUNT
    update = first_new / corr_one / (jnp.sqrt(second_new / corr_two) + EPSILON)
    return (weight - RATE * (update + DECAY * weight), first_new, second_new)


def adam_kernel(flips, d0, d1, d2, d3, w_ref, first_ref, second_ref, w_out, first_out, second_out):
    grad = d0[...].astype(F32) * flips[0]
    for t, d in ((1, d1), (2, d2), (3, d3)):
        grad = grad + d[...].astype(F32) * flips[t]
    for q in range(QUAD):
        for r in range(2):
            lane = q * LANES + r * C
            at = (0, q, r)
            new = adamw(w_ref[at], first_ref[at], second_ref[at], grad[:, lane : lane + C])
            w_out[at], first_out[at], second_out[at] = new


def adam_spec(flips, grads, weight, first, second):
    modes = weight.shape[1]
    packed = pl.BlockSpec((C, QUAD * LANES), lambda g: (0, g))
    block = pl.BlockSpec((1, QUAD, 2, C, C), lambda g: (0, g, 0, 0, 0))
    return pl.pallas_call(
        adam_kernel,
        grid=(modes // QUAD,),
        in_specs=[pl.BlockSpec(memory_space=SMEM)] + [packed] * 4 + [block] * 3,
        out_specs=[block] * 3,
        out_shape=[jax.ShapeDtypeStruct(weight.shape, F32)] * 3,
        compiler_params=params(12),
        cost_estimate=cost(),
        name="adam",
    )(flips, *grads, weight, first, second)


def swap(value, axis, size, x):
    return lax.ppermute(value, axis, [(i, i ^ x) for i in range(size)])


def to_modes(value):
    return lax.all_to_all(value, "dp", split_axis=0, concat_axis=0, tiled=True)


def after(values, first):
    values, _ = lax.optimization_barrier((values, first))
    return values


def body(
    shards,
    inputs,
    cotangent,
    norm_table,
    sample_index,
    spec_weight,
    spec_first,
    spec_second,
    lin_weight,
    lin_first,
    lin_second,
):
    own = lax.axis_index("blade")
    shard = lax.axis_index("dp")
    ids = jnp.stack([own, shard]).astype(jnp.int32)
    samples = inputs.shape[0] // 4

    def cut(array, t):
        return lax.dynamic_slice_in_dim(array, jnp.bitwise_xor(own, t) * samples, samples, 0)

    def send(array, t):
        block = cut(array, t)
        return block, swap(block, "blade", 4, t)

    sent, x3 = send(inputs, 3)
    rest = after(inputs, sent)
    sent, x1 = send(rest, 1)
    rest = after(rest, sent)
    _, x2 = send(rest, 2)

    matches = sample_index[:, None] == jnp.arange(NTAB, dtype=jnp.int32)[None, :]
    normalizer = jnp.sum(jnp.where(matches, norm_table[None, :], 0.0), axis=1)
    inv_all = 1.0 / normalizer
    inv = lax.dynamic_slice_in_dim(inv_all, own * samples, samples, 0)

    small = lax.optimization_barrier(small_tables())
    turned = turned_table(small)
    packed = pack_weights(spec_weight, lin_weight)
    packs = [packed] + [swap(packed, "blade", 4, t) for t in (1, 2, 3)]

    x3 = after(x3, (packed, turned))
    xa = to_modes(forward_spectrum(ids, inv, (inputs, x3), small, shards))
    blocks = after([cut(cotangent, t) for t in (1, 2, 3)], (x1, x2))
    cot = (cotangent,) + tuple(swap(blocks[t - 1], "blade", 4, t) for t in (1, 2, 3))
    xb = to_modes(forward_spectrum(ids, inv, (x1, x2), small, shards))
    mixed = mix(ids, xa, xb, unpack(ids, packs))
    y = to_modes(mixed)
    lt, lb = unpack_lines(after(ids, mixed), packs)

    x = (inputs, x1, x2, x3)
    result = pixels(ids, inv, x, y, turned, lt)
    output, slope = result[0], result[4]
    out_parts = [swap(result[t], "blade", 4, t) for t in (1, 2, 3)]

    grad_pre, sent, lin = pixel_grads(ids, inv, x, cot, slope, small, y.shape)
    g = after(to_modes(sent), out_parts[2])
    mixed = mix_back(ids, g, unpack(after(ids, lin), packs))
    back = to_modes(mixed)
    spec_grads = weight_grads(ids, xa, xb, g, lin)
    spec_grads = [spec_grads[0]] + [swap(spec_grads[t], "blade", 4, t) for t in (1, 2, 3)]

    inner = inner_grads(ids, inv, back, grad_pre, turned, lb, cotangent)
    inner = after(inner, out_parts)
    grad_parts = [swap(inner[t], "blade", 4, t) for t in (1, 2, 3)]

    output = place_output(ids, out_parts, output)
    spec_grads = after(spec_grads, output)
    flips = jnp.stack(
        [jnp.where(own % 2 == 1, flip_of(jnp.bitwise_xor(own, t), 1), 1.0) for t in range(4)]
    )
    lin_grad = 0.0
    first = spec_weight.shape[1] * LANES
    for t in range(4):
        lin_grad = lin_grad + spec_grads[t][:, first : first + C].astype(F32) * flips[t]
    step = 1
    while step < shards:
        lin_grad = lin_grad + swap(lin_grad, "dp", shards, step)
        step *= 2

    spec_out = adam_spec(flips, spec_grads, spec_weight, spec_first, spec_second)
    lin_out = adamw(lin_weight, lin_first, lin_second, lin_grad[None])
    input_grad = final_grads(ids, inv_all, cotangent, grad_parts[2:], (3,), inner[0])
    input_grad = final_grads(ids, inv_all, cotangent, grad_parts[:2], (1, 2), input_grad)
    return (output, input_grad, *spec_out, *lin_out)


def solution(mesh):
    fields = P("dp", "blade", None, None)
    spec = P("blade", "dp", None, None, None)
    lin = P("blade", None, None)
    return jax.shard_map(
        partial(body, mesh.shape["dp"]),
        mesh=mesh,
        in_specs=(fields, fields, P(), P("dp"), spec, spec, spec, lin, lin, lin),
        out_specs=(fields, fields, spec, spec, spec, lin, lin, lin),
        check_vma=False,
    )
```

```python
from functools import partial
import math

import jax
import jax.numpy as jnp
from jax import lax
from jax.experimental import pallas as pl
from jax.experimental.pallas import tpu as pltpu
from jax.sharding import PartitionSpec as P

GRID = 64
MSIDE = 16
NTAB = 16
STEP_COUNT = 5
NPIX = 4096
MODES = 256
C = 48
LANES = 2 * C
QUAD = 4
PACK = 128
ROWS = 16

BETA_ONE = 0.9
BETA_TWO = 0.999
EPSILON = 1e-08
RATE = 0.1
DECAY = 0.01

F32 = jnp.float32
BF16 = jnp.bfloat16
SMEM = pltpu.MemorySpace.SMEM


def sgn(left, right):
    return -1.0 if (left & 2) and (right & 1) else 1.0


def flip_of(own, k):
    if k & 1:
        return (1 - 2 * ((own // 2) % 2)).astype(F32)
    return jnp.float32(1.0)


def mode_factor(mode):
    return jnp.where(mode % MSIDE == 0, 1.0, 2.0).astype(F32)


def dot(left, right, dims=((1,), (0,))):
    return lax.dot_general(left, right, (dims, ((), ())), preferred_element_type=F32)


def whole(shape):
    zeros = (0,) * len(shape)
    return pl.BlockSpec(tuple(shape), lambda *_: zeros)


def params(mib):
    return pltpu.CompilerParams(vmem_limit_bytes=mib * 1024 * 1024)


def fast(shape, kind):
    return pltpu.VMEM(tuple(shape), kind)


def slow(shape, kind):
    return pltpu.HBM(tuple(shape), kind)


def pin(*arrays):
    return [pltpu.with_memory_space_constraint(array, pltpu.VMEM) for array in arrays]


def stay(*arrays):
    return [pltpu.with_memory_space_constraint(array, pltpu.HBM) for array in arrays]


def in_vmem(count):
    return [pl.BlockSpec(memory_space=pltpu.MemorySpace.VMEM)] * count


def cost():
    return pl.CostEstimate(flops=1, bytes_accessed=1, transcendentals=0)


def small_tables():
    mode_ids = jnp.arange(2 * MODES, dtype=jnp.int32)
    imag = mode_ids >= MODES
    mode_ids = mode_ids % MODES
    row_index = mode_ids // MSIDE
    col_freq = mode_ids % MSIDE
    row_freq = jnp.where(row_index < MSIDE // 2, row_index, GRID - MSIDE + row_index)
    place = jnp.arange(GRID, dtype=jnp.int32)[:, None]
    row_angle = ((place * row_freq[None, :]) % GRID).astype(F32) * (2.0 * math.pi / GRID)
    col_angle = ((place * col_freq[None, :]) % GRID).astype(F32) * (2.0 * math.pi / GRID)
    row_cos, row_sin = jnp.cos(row_angle) / GRID, jnp.sin(row_angle) / GRID
    first = jnp.where(imag[None, :], -row_sin, row_cos)
    second = jnp.where(imag[None, :], -row_cos, -row_sin)
    return jnp.stack([first, second, jnp.cos(col_angle), jnp.sin(col_angle)])


def table_rows(row_ref, col_ref, start, stop):
    tiles = []
    for h in range(start, stop):
        tile = row_ref[0, h : h + 1] * col_ref[0] + row_ref[1, h : h + 1] * col_ref[1]
        tiles.append(tile.astype(BF16))
    return jnp.concatenate(tiles, axis=0)


def small_specs(tile):
    n = 2 * MODES
    return [
        pl.BlockSpec((2, tile // GRID, n), lambda i, *_: (0, i, 0)),
        pl.BlockSpec((2, GRID, n), lambda i, *_: (1, 0, 0)),
    ]


def turned_kernel(row_ref, col_ref, ft_ref):
    for h in range(0, row_ref.shape[1], 2):
        tile = table_rows(row_ref, col_ref, h, h + 2)
        ft_ref[:, h * GRID : (h + 2) * GRID] = tile.astype(F32).T.astype(BF16)


def turned_table(small):
    rows = 8
    n = 2 * MODES
    return pl.pallas_call(
        turned_kernel,
        grid=(GRID // rows,),
        in_specs=small_specs(rows * GRID),
        out_specs=pl.BlockSpec((n, rows * GRID), lambda i: (0, i)),
        out_shape=slow((n, NPIX), BF16),
        compiler_params=params(28),
        cost_estimate=cost(),
        name="turned",
    )(*stay(small, small))


def pack_kernel(w_ref, l_ref, o_ref):
    def step(g, carry):
        parts = [w_ref[0, g * QUAD + q, r] for q in range(QUAD) for r in range(2)]
        at = pl.ds(pl.multiple_of(g * QUAD * LANES, PACK), QUAD * LANES)
        o_ref[:, at] = jnp.concatenate(parts, axis=1).astype(BF16)
        return carry

    modes = w_ref.shape[1]
    lax.fori_loop(0, modes // QUAD, step, 0)
    line = jnp.concatenate([l_ref[0], jnp.zeros((C, PACK - C), F32)], axis=1)
    o_ref[:, modes * LANES :] = line.astype(BF16)


def pack_weights(spec_weight, lin_weight):
    modes = spec_weight.shape[1]
    return pl.pallas_call(
        pack_kernel,
        in_specs=in_vmem(2),
        out_specs=in_vmem(1)[0],
        out_shape=jax.ShapeDtypeStruct((C, modes * LANES + PACK), BF16),
        compiler_params=params(28),
        cost_estimate=cost(),
        name="pack",
    )(spec_weight, lin_weight)


def lanes_of(shape):
    return lax.broadcasted_iota(jnp.int32, shape, len(shape) - 1)


def split_lanes(a, b, c):
    lane = lanes_of(a.shape)
    second = jnp.where(lane < 32, pltpu.roll(a, 32, 1), pltpu.roll(b, 32, 1))
    third = jnp.where(lane < 64, pltpu.roll(b, 64, 1), pltpu.roll(c, 64, 1))
    return a, second, third, pltpu.roll(c, 96, 1)


def join_lanes(first, second, third, fourth):
    lane = lanes_of(first.shape)
    a = jnp.where(lane < 96, first, pltpu.roll(second, 96, 1))
    b = jnp.where(lane < 64, pltpu.roll(second, 96, 1), pltpu.roll(third, 64, 1))
    c = jnp.where(lane < 32, pltpu.roll(third, 64, 1), pltpu.roll(fourth, 32, 1))
    return a, b, c


def quad_tiles(ref, g):
    tiles = []
    for n in range(3):
        at = pl.ds(pl.multiple_of(g * QUAD * LANES + n * PACK, PACK), PACK)
        tiles.append(ref[:, at].astype(F32))
    return tiles


def unpack_kernel(ids_ref, w0, w1, w2, w3, pq_ref, *lines):
    own = ids_ref[0]
    modes = pq_ref.shape[0]
    lane = lanes_of((C, PACK))
    flip = flip_of(own, 1)

    def step(g, carry):
        for t, w in enumerate((w0, w1, w2, w3)):
            slot = jnp.bitwise_xor(own, t)
            scale = jnp.where(slot % 2 == 1, flip, 1.0)
            at = pl.ds(pl.multiple_of(slot * PACK, PACK), PACK)
            tiles = [tile * scale for tile in quad_tiles(w, g)]
            for q, p in enumerate(split_lanes(*tiles)):
                p = jnp.where(lane < LANES, p, 0.0)
                low = jnp.where(lane < C, -pltpu.roll(p, PACK - C, 1), pltpu.roll(p, C, 1))
                low = jnp.where(lane < LANES, low, 0.0)
                pq_ref[g * QUAD + q, :C, at] = p.astype(BF16)
                pq_ref[g * QUAD + q, C:, at] = low.astype(BF16)
        return carry

    quads = modes // QUAD
    lax.fori_loop(0, quads, step, 0, unroll=min(4, quads))
    if not lines:
        return
    lt_ref, lb_ref, lsc = lines
    for t, w in enumerate((w0, w1, w2, w3)):
        slot = jnp.bitwise_xor(own, t)
        lsc[slot] = w[:, modes * LANES :].astype(F32) * jnp.where(slot % 2 == 1, flip, 1.0)
    for k in range(4):
        line = lsc[k]
        turned = line.T
        for t in range(4):
            u = t ^ k
            lb_ref[t * C : (t + 1) * C, u * C : (u + 1) * C] = (line[:, :C] * sgn(t, k)).astype(BF16)
            lt_ref[u * C : (u + 1) * C, t * C : (t + 1) * C] = (turned[:C] * sgn(t, k)).astype(BF16)


def unpack(ids, packs, lines):
    modes = (packs[0].shape[1] - PACK) // LANES
    weights = fast((modes, LANES, 4 * PACK), BF16)
    shape = (4 * C, 4 * C)
    result = pl.pallas_call(
        unpack_kernel,
        in_specs=[pl.BlockSpec(memory_space=SMEM)] + in_vmem(4),
        out_specs=in_vmem(3 if lines else 1),
        out_shape=[weights] + ([fast(shape, BF16), slow(shape, BF16)] if lines else []),
        scratch_shapes=[pltpu.VMEM((4, C, PACK), F32)] if lines else [],
        compiler_params=params(28),
        cost_estimate=cost(),
        name="unpack",
    )(ids, *packs)
    return result if lines else result[0]


def spread(acc, out_ref, scales=None):
    rows = []
    for n in range(acc.shape[0] // C):
        for r in range(2):
            row = acc[n * C : (n + 1) * C, r * MODES : (r + 1) * MODES]
            rows.append(row if scales is None else row * scales[n])
    turned = jnp.concatenate(rows, axis=0).T
    out_ref[...] = turned.reshape(out_ref.shape).astype(BF16)


def collect(block, ysc):
    turned = block[...].astype(F32).reshape(MODES, block.shape[2]).T
    for n in range(ysc.shape[0] // C):
        for r in range(2):
            row = (n * 2 + r) * C
            piece = turned[row : row + C].astype(BF16)
            ysc[n * C : (n + 1) * C, r * MODES : (r + 1) * MODES] = piece


def forward_kernel(ids_ref, inv_ref, *refs):
    x = refs[:-4]
    row_ref, col_ref, out_ref, acc = refs[-4:]
    i = pl.program_id(0)
    samples = x[0].shape[0]
    rows = [part[s, 0] for s in range(samples) for part in x]
    table = table_rows(row_ref, col_ref, 0, row_ref.shape[1])
    part = dot(jnp.concatenate(rows, axis=0), table)

    @pl.when(i == 0)
    def _():
        acc[...] = part

    @pl.when(i > 0)
    def _():
        acc[...] += part

    @pl.when(i == pl.num_programs(0) - 1)
    def _():
        spread(acc, out_ref, [inv_ref[s] for s in range(samples) for _ in x])


def forward_spectrum(ids, inv, x, small, shards):
    samples = inv.shape[0]
    modes = MODES // shards
    width = samples * len(x) * LANES
    n = 2 * MODES
    tile = 2048

    def spec(array):
        if array.shape[0] == samples:
            return pl.BlockSpec((samples, 1, C, tile), lambda i, ids, inv: (0, 0, 0, i))
        return pl.BlockSpec((samples, 1, C, tile), lambda i, ids, inv: (ids[0], 0, 0, i))

    return pl.pallas_call(
        forward_kernel,
        grid_spec=pltpu.PrefetchScalarGridSpec(
            num_scalar_prefetch=2,
            grid=(NPIX // tile,),
            in_specs=[spec(part) for part in x] + small_specs(tile),
            out_specs=whole((shards, modes, width)),
            scratch_shapes=[pltpu.VMEM((samples * len(x) * C, n), F32)],
        ),
        out_shape=slow((shards, modes, width), BF16),
        compiler_params=params(28),
        cost_estimate=cost(),
        name="forward",
    )(ids, inv, *stay(*x), *stay(small, small))


def row_scratch(modes, shards, width):
    return pltpu.VMEM((width // PACK, modes * shards, PACK), F32)


def gather_rows(blocks, sc):
    shards, modes = blocks[0].shape[:2]
    first = 0
    for block in blocks:
        for n in range(block.shape[2] // PACK):
            for x in range(shards):
                rows = block[x, :, n * PACK : (n + 1) * PACK].astype(F32)
                sc[first + n, pl.ds(x, modes, stride=shards), :] = rows
        first += block.shape[2] // PACK


def scatter_rows(ysc, out):
    shards, modes = out.shape[:2]
    for x in range(shards):
        for n in range(ysc.shape[0]):
            piece = ysc[n, pl.ds(x, modes, stride=shards), :]
            out[x, :, n * PACK : (n + 1) * PACK] = piece.astype(BF16)


def blade_rows(sc, mode, shards, order):
    at = pl.ds(pl.multiple_of(mode * shards, shards), shards)
    found = [[] for _ in range(4)]
    for n in range(0, len(order), 4):
        tile = n // 4 * 3
        pieces = split_lanes(sc[tile, at, :], sc[tile + 1, at, :], sc[tile + 2, at, :])
        for piece, (_, t) in zip(pieces, order[n : n + 4]):
            found[t].append(piece)
    return [jnp.concatenate(found[t], axis=0) for t in range(4)]


def split_order(samples):
    return [(s, t) for pair in ((0, 3), (1, 2)) for s in range(samples) for t in pair]


def plain_order(samples):
    return [(s, t) for s in range(samples) for t in range(4)]


def mix_modes(xsc, ysc, pq_ref, order, shards, first_mode, back):
    modes = xsc.shape[1] // shards
    samples = len(order) // 4
    group = samples * shards

    def step(m, carry):
        low = jnp.concatenate(blade_rows(xsc, m, shards, order), axis=0)
        low = low[:, :LANES].astype(BF16)
        total = [None] * 4
        if not back:
            parts = dot(low, pq_ref[m])
        for k in range(4):
            if back:
                part = dot(low, pq_ref[m, :, k * PACK : k * PACK + LANES], ((1,), (1,)))
            else:
                part = parts[:, k * PACK : (k + 1) * PACK]
            for t in range(4):
                u = t ^ k
                piece = part[t * group : (t + 1) * group]
                sign = sgn(u, k) if back else sgn(t, k)
                if total[u] is None:
                    total[u] = piece if sign > 0 else -piece
                else:
                    total[u] = total[u] + piece if sign > 0 else total[u] - piece
        factor = mode_factor(first_mode + m)
        at = pl.ds(pl.multiple_of(m * shards, shards), shards)
        for s in range(samples):
            rows = []
            for u in range(4):
                piece = total[u][s * shards : (s + 1) * shards] * factor
                if back:
                    piece = jnp.concatenate([piece, jnp.zeros((shards, PACK - LANES), F32)], axis=1)
                rows.append(piece)
            for n, tile in enumerate(join_lanes(*rows)):
                ysc[s * 3 + n, at, :] = tile
        return carry

    lax.fori_loop(0, modes, step, 0, unroll=min(32, modes))


def mix_kernel(ids_ref, xa, xb, pq_ref, y_ref, xsc, ysc):
    shards, modes, half = xa.shape
    gather_rows((xa, xb), xsc)
    order = split_order(half // (2 * LANES))
    mix_modes(xsc, ysc, pq_ref, order, shards, ids_ref[1] * modes, False)
    scatter_rows(ysc, y_ref)


def mix(ids, xa, xb, pq):
    shards, modes, half = xa.shape
    return pl.pallas_call(
        mix_kernel,
        in_specs=[pl.BlockSpec(memory_space=SMEM)] + in_vmem(3),
        out_specs=in_vmem(1)[0],
        out_shape=slow((shards, modes, 2 * half), BF16),
        scratch_shapes=[row_scratch(modes, shards, 2 * half)] * 2,
        compiler_params=params(28),
        cost_estimate=cost(),
        name="mix",
    )(ids, xa, xb, *pin(pq))


def mix_back_kernel(ids_ref, g_ref, pq_ref, out_ref, gsc, ysc):
    shards, modes, width = g_ref.shape
    gather_rows((g_ref,), gsc)
    order = plain_order(width // (4 * LANES))
    mix_modes(gsc, ysc, pq_ref, order, shards, ids_ref[1] * modes, True)
    scatter_rows(ysc, out_ref)


def mix_back(ids, g, pq):
    shards, modes, width = g.shape
    return pl.pallas_call(
        mix_back_kernel,
        in_specs=[pl.BlockSpec(memory_space=SMEM)] + in_vmem(2),
        out_specs=in_vmem(1)[0],
        out_shape=slow(g.shape, BF16),
        scratch_shapes=[row_scratch(modes, shards, width)] * 2,
        compiler_params=params(28),
        cost_estimate=cost(),
        name="mix_back",
    )(ids, g, *pin(pq))


def grad_kernel(ids_ref, xa, xb, g_ref, lin_ref, o0, o1, o2, o3, xsc, gsc, osc):
    shards, modes, width = g_ref.shape
    samples = width // (4 * LANES)
    own = ids_ref[0]
    first_mode = ids_ref[1] * modes
    gather_rows((xa, xb), xsc)
    gather_rows((g_ref,), gsc)
    lane = lanes_of((samples * shards, PACK))

    def step(g, carry):
        found = [[] for _ in range(4)]
        for q in range(QUAD):
            m = g * QUAD + q
            x = blade_rows(xsc, m, shards, split_order(samples))
            x = x + [pltpu.roll(rows, PACK - C, 1) for rows in x]
            left = jnp.concatenate(x, axis=0)[:, :C].astype(BF16)
            factor = mode_factor(first_mode + m)
            plain = blade_rows(gsc, m, shards, plain_order(samples))
            plain = [rows * factor for rows in plain]
            turned = [
                jnp.where(lane < C, pltpu.roll(rows, PACK - C, 1), -pltpu.roll(rows, C, 1))
                for rows in plain
            ]
            plus = [rows.astype(BF16) for rows in plain + turned]
            minus = [(-rows).astype(BF16) for rows in plain + turned]
            right = []
            for k in range(4):
                rows = []
                for r in range(2):
                    for t in range(4):
                        rows.append((plus if sgn(t, k) > 0 else minus)[4 * r + (t ^ k)])
                right.append(jnp.concatenate(rows, axis=0))
            grad = dot(left, jnp.concatenate(right, axis=1), ((0,), (0,)))
            for k in range(4):
                found[k].append(grad[:, k * PACK : (k + 1) * PACK])
        for k in range(4):
            for n, tile in enumerate(join_lanes(*found[k])):
                at = pl.ds(pl.multiple_of(g * QUAD * LANES + n * PACK, PACK), PACK)
                osc[k, :, at] = tile.astype(BF16)
        return carry

    lax.fori_loop(0, modes // QUAD, step, 0)
    for k in range(4):
        line = jnp.concatenate([lin_ref[k], jnp.zeros((C, PACK - C), F32)], axis=1)
        osc[k, :, modes * LANES :] = line.astype(BF16)
    for t, out in enumerate((o0, o1, o2, o3)):
        out[...] = osc[jnp.bitwise_xor(own, t)]


def weight_grads(ids, xa, xb, g, lin):
    shards, modes, width = g.shape
    shape = (C, modes * LANES + PACK)
    return pl.pallas_call(
        grad_kernel,
        in_specs=[pl.BlockSpec(memory_space=SMEM)] + in_vmem(4),
        out_specs=in_vmem(4),
        out_shape=[slow(shape, BF16)] * 4,
        scratch_shapes=[row_scratch(modes, shards, width)] * 2 + [pltpu.VMEM((4,) + shape, BF16)],
        compiler_params=params(28),
        cost_estimate=cost(),
        name="weight_grads",
    )(ids, xa, xb, g, lin)


CDF_AT = 0.28
CDF = (0.11652094, 0.06749571, 0.2689128, -0.23699677, 0.38987606, -0.10580875)
SERIES = [value / CDF_AT ** (i + 1) for i, value in enumerate(CDF)]


def gelu_parts(v):
    z = jnp.abs(v)
    t = 1.0 / (z + 1.0 / CDF_AT)
    bell = jnp.exp2(v * v * (-0.5 * math.log2(math.e)))
    series = jnp.float32(SERIES[-1])
    for value in SERIES[-2::-1]:
        series = series * t + value
    tail = series * t * bell
    cdf = jnp.where(v < 0.0, tail, 1.0 - tail)
    return v * cdf, cdf + v * (bell * (1.0 / math.sqrt(2.0 * math.pi)))


def pixel_kernel(ids_ref, inv_ref, *refs):
    x = refs[:4]
    y_ref, ft_ref, lt_ref = refs[4:7]
    outs = refs[7:11]
    slope_ref = refs[11]
    ysc, pre, lts = refs[12:]
    samples = x[1].shape[0]
    rows = 4 * C

    @pl.when(pl.program_id(0) == 0)
    def _():
        collect(y_ref, ysc)
        for s in range(samples):
            lts[s] = (lt_ref[...].astype(F32) * inv_ref[s]).astype(BF16)

    for s in range(samples):
        at = slice(s * rows, (s + 1) * rows)
        fields = jnp.concatenate([x[t][s, 0] for t in range(4)], axis=0)
        left = jnp.concatenate([ysc[at], lts[s]], axis=1)
        pre[at] = dot(left, jnp.concatenate([ft_ref[...], fields], axis=0))
    for s in range(samples):
        for t in range(4):
            for c in range(0, C, ROWS):
                at = s * rows + t * C + c
                value, slope = gelu_parts(pre[at : at + ROWS])
                normed = x[t][s, 0, c : c + ROWS].astype(F32) * inv_ref[s]
                outs[t][s, 0, c : c + ROWS] = (normed + value).astype(BF16)
                slope_ref[at : at + ROWS] = slope.astype(BF16)


def pixels(ids, inv, x, y, turned, lt):
    samples = inv.shape[0]
    n = 2 * MODES
    tile = 512
    mine = pl.BlockSpec((samples, 1, C, tile), lambda i, ids, inv: (ids[0], 0, 0, i))
    block = pl.BlockSpec((samples, 1, C, tile), lambda i, ids, inv: (0, 0, 0, i))
    rows = samples * 4 * C
    flat = pl.BlockSpec((rows, tile), lambda i, ids, inv: (0, i))
    return pl.pallas_call(
        pixel_kernel,
        grid_spec=pltpu.PrefetchScalarGridSpec(
            num_scalar_prefetch=2,
            grid=(NPIX // tile,),
            in_specs=[mine]
            + [block] * 3
            + [
                whole(y.shape),
                pl.BlockSpec((n, tile), lambda i, ids, inv: (0, i)),
                whole((4 * C, 4 * C)),
            ],
            out_specs=[mine] + [block] * 3 + [flat],
            scratch_shapes=[
                pltpu.VMEM((rows, n), BF16),
                pltpu.VMEM((rows, tile), F32),
                pltpu.VMEM((samples, 4 * C, 4 * C), BF16),
            ],
        ),
        out_shape=[slow(x[0].shape, BF16)]
        + [slow((samples, 1, C, NPIX), BF16)] * 3
        + [fast((rows, NPIX), BF16)],
        compiler_params=params(28),
        cost_estimate=cost(),
        name="pixels",
    )(ids, inv, *stay(*x), y, *stay(turned), *pin(lt))


def slope_kernel(ids_ref, inv_ref, *refs):
    x, cot = refs[:4], refs[4:8]
    slope, row_ref, col_ref, g_ref, g_out, lin_ref, gacc, lacc = refs[8:]
    samples = cot[1].shape[0]
    rows = 4 * C
    i = pl.program_id(0)

    @pl.when(i == 0)
    def _():
        gacc[...] = jnp.zeros_like(gacc)
        lacc[...] = jnp.zeros_like(lacc)

    for s in range(samples):
        for t in range(4):
            at = s * rows + t * C
            grad = cot[t][s, 0].astype(F32) * slope[at : at + C].astype(F32)
            g_ref[at : at + C] = grad.astype(BF16)
    table = table_rows(row_ref, col_ref, 0, row_ref.shape[1])
    gacc[...] += dot(g_ref[...], table)
    for s in range(samples):
        at = slice(s * rows, (s + 1) * rows)
        g = g_ref[at]
        fields = jnp.concatenate([x[t][s, 0] for t in range(4)], axis=0)
        lacc[...] += dot(fields, g, ((1,), (1,))) * inv_ref[s]

    @pl.when(i == pl.num_programs(0) - 1)
    def _():
        spread(gacc, g_out)
        for k in range(4):
            total = None
            for t in range(4):
                u = t ^ k
                piece = lacc[t * C : (t + 1) * C, u * C : (u + 1) * C] * sgn(t, k)
                total = piece if total is None else total + piece
            lin_ref[k] = total


def pixel_grads(ids, inv, x, cot, slope, small, spectrum):
    rows = slope.shape[0]
    samples = rows // (4 * C)
    n = 2 * MODES
    tile = 2048
    mine = pl.BlockSpec((samples, 1, C, tile), lambda i, ids, inv: (ids[0], 0, 0, i))
    block = pl.BlockSpec((samples, 1, C, tile), lambda i, ids, inv: (0, 0, 0, i))
    flat = pl.BlockSpec((rows, tile), lambda i, ids, inv: (0, i))
    return pl.pallas_call(
        slope_kernel,
        grid_spec=pltpu.PrefetchScalarGridSpec(
            num_scalar_prefetch=2,
            grid=(NPIX // tile,),
            in_specs=([mine] + [block] * 3) * 2
            + [flat]
            + small_specs(tile),
            out_specs=[flat, whole(spectrum), whole((4, C, C))],
            scratch_shapes=[pltpu.VMEM((rows, n), F32), pltpu.VMEM((4 * C, 4 * C), F32)],
        ),
        out_shape=[
            slow((rows, NPIX), BF16),
            slow(spectrum, BF16),
            jax.ShapeDtypeStruct((4, C, C), F32),
        ],
        compiler_params=params(28),
        cost_estimate=cost(),
        name="pixel_grads",
    )(ids, inv, *stay(*x), *stay(*cot), *pin(slope), *stay(small, small))


def inner_kernel(ids_ref, inv_ref, y_ref, g_ref, row_ref, col_ref, lb_ref, cot_ref, mine_ref, *refs):
    o1, o2, o3, ysc = refs
    samples = cot_ref.shape[0]
    rows = 4 * C

    @pl.when(pl.program_id(0) == 0)
    def _():
        collect(y_ref, ysc)

    table = table_rows(row_ref, col_ref, 0, row_ref.shape[1])
    spatial = dot(ysc[...], table, ((1,), (1,)))
    for s in range(samples):
        at = slice(s * rows, (s + 1) * rows)
        total = spatial[at] + dot(lb_ref[...], g_ref[at])
        mine_ref[s, 0] = (cot_ref[s, 0].astype(F32) + total[:C]) * inv_ref[s]
        for t, out in ((1, o1), (2, o2), (3, o3)):
            out[s, 0] = total[t * C : (t + 1) * C].astype(BF16)


def inner_grads(ids, inv, y, g, small, lb, cotangent):
    samples = inv.shape[0]
    n = 2 * MODES
    tile = 2048
    rows = samples * 4 * C
    mine = pl.BlockSpec((samples, 1, C, tile), lambda i, ids, inv: (ids[0], 0, 0, i))
    block = pl.BlockSpec((samples, 1, C, tile), lambda i, ids, inv: (0, 0, 0, i))
    return pl.pallas_call(
        inner_kernel,
        grid_spec=pltpu.PrefetchScalarGridSpec(
            num_scalar_prefetch=2,
            grid=(NPIX // tile,),
            in_specs=[
                whole(y.shape),
                pl.BlockSpec((rows, tile), lambda i, ids, inv: (0, i)),
                *small_specs(tile),
                whole((4 * C, 4 * C)),
                mine,
            ],
            out_specs=[mine] + [block] * 3,
            scratch_shapes=[pltpu.VMEM((rows, n), BF16)],
        ),
        out_shape=[slow(cotangent.shape, F32)] + [slow((samples, 1, C, NPIX), BF16)] * 3,
        compiler_params=params(28),
        cost_estimate=cost(),
        name="inner_grads",
    )(ids, inv, y, *stay(g, small, small), lb, *stay(cotangent))


def place_kernel(ids_ref, a_ref, b_ref, c_ref, old_ref, out_ref):
    for n, part in enumerate((a_ref, b_ref, c_ref)):

        @pl.when(pl.program_id(0) == n)
        def _():
            out_ref[...] = part[...]


def place_output(ids, parts, result):
    samples = parts[0].shape[0]
    shape = (1, 1, C, NPIX)

    def spec(n):
        def at(j, s, ids):
            return (jnp.where(j == n, s, jnp.where(j < n, 0, samples - 1)), 0, 0, 0)

        return pl.BlockSpec(shape, at)

    return pl.pallas_call(
        place_kernel,
        grid_spec=pltpu.PrefetchScalarGridSpec(
            num_scalar_prefetch=1,
            grid=(3, samples),
            in_specs=[spec(0), spec(1), spec(2), pl.BlockSpec(memory_space=pl.ANY)],
            out_specs=pl.BlockSpec(
                shape, lambda j, s, ids: (jnp.bitwise_xor(ids[0], j + 1) * samples + s, 0, 0, 0)
            ),
        ),
        out_shape=jax.ShapeDtypeStruct(result.shape, BF16),
        input_output_aliases={4: 0},
        compiler_params=params(28),
        cost_estimate=cost(),
        name="place",
    )(ids, *parts, result)


def final_kernel(count, codes, ids_ref, inv_ref, cot_ref, *refs):
    samples = pl.num_programs(1)
    j = pl.program_id(0)
    for n in range(count):

        @pl.when(j == n)
        def _():
            inv = inv_ref[jnp.bitwise_xor(ids_ref[0], codes[n]) * samples + pl.program_id(1)]
            refs[-1][...] = (cot_ref[...].astype(F32) + refs[n][...].astype(F32)) * inv


def final_grads(ids, inv, cotangent, parts, codes, result):
    samples = parts[0].shape[0]
    count = len(parts)
    shape = (1, 1, C, NPIX)

    def code(j):
        value = codes[0]
        for n in range(1, count):
            value = jnp.where(j == n, codes[n], value)
        return value

    def spec(n):
        def at(j, s, ids, inv):
            return (jnp.where(j == n, s, jnp.where(j < n, 0, samples - 1)), 0, 0, 0)

        return pl.BlockSpec(shape, at)

    place = pl.BlockSpec(
        shape, lambda j, s, ids, inv: (jnp.bitwise_xor(ids[0], code(j)) * samples + s, 0, 0, 0)
    )
    return pl.pallas_call(
        partial(final_kernel, count, codes),
        grid_spec=pltpu.PrefetchScalarGridSpec(
            num_scalar_prefetch=2,
            grid=(count, samples),
            in_specs=[place]
            + [spec(n) for n in range(count)]
            + [pl.BlockSpec(memory_space=pl.ANY)],
            out_specs=place,
        ),
        out_shape=jax.ShapeDtypeStruct(cotangent.shape, F32),
        input_output_aliases={3 + count: 0},
        compiler_params=params(28),
        cost_estimate=cost(),
        name="final",
    )(ids, inv, cotangent, *parts, result)


def adamw(weight, first, second, grad):
    first_new = BETA_ONE * first + (1.0 - BETA_ONE) * grad
    second_new = BETA_TWO * second + (1.0 - BETA_TWO) * grad * grad
    corr_one = 1.0 - BETA_ONE**STEP_COUNT
    corr_two = 1.0 - BETA_TWO**STEP_COUNT
    update = first_new / corr_one / (jnp.sqrt(second_new / corr_two) + EPSILON)
    return (weight - RATE * (update + DECAY * weight), first_new, second_new)


def adam_kernel(flips, d0, d1, d2, d3, w_ref, first_ref, second_ref, w_out, first_out, second_out):
    grad = d0[...].astype(F32) * flips[0]
    for t, d in ((1, d1), (2, d2), (3, d3)):
        grad = grad + d[...].astype(F32) * flips[t]
    for q in range(QUAD):
        for r in range(2):
            lane = q * LANES + r * C
            at = (0, q, r)
            new = adamw(w_ref[at], first_ref[at], second_ref[at], grad[:, lane : lane + C])
            w_out[at], first_out[at], second_out[at] = new


def adam_spec(flips, grads, weight, first, second):
    modes = weight.shape[1]
    packed = pl.BlockSpec((C, QUAD * LANES), lambda g: (0, g))
    block = pl.BlockSpec((1, QUAD, 2, C, C), lambda g: (0, g, 0, 0, 0))
    return pl.pallas_call(
        adam_kernel,
        grid=(modes // QUAD,),
        in_specs=[pl.BlockSpec(memory_space=SMEM)] + [packed] * 4 + [block] * 3,
        out_specs=[block] * 3,
        out_shape=[jax.ShapeDtypeStruct(weight.shape, F32)] * 3,
        compiler_params=params(28),
        cost_estimate=cost(),
        name="adam",
    )(flips, *grads, weight, first, second)


def swap(value, axis, size, x):
    return lax.ppermute(value, axis, [(i, i ^ x) for i in range(size)])


def to_modes(value):
    return lax.all_to_all(value, "dp", split_axis=0, concat_axis=0, tiled=True)


def after(values, first):
    values, _ = lax.optimization_barrier((values, first))
    return values


def body(
    shards,
    inputs,
    cotangent,
    norm_table,
    sample_index,
    spec_weight,
    spec_first,
    spec_second,
    lin_weight,
    lin_first,
    lin_second,
):
    own = lax.axis_index("blade")
    shard = lax.axis_index("dp")
    ids = jnp.stack([own, shard]).astype(jnp.int32)
    samples = inputs.shape[0] // 4

    def cut(array, t):
        return lax.dynamic_slice_in_dim(array, jnp.bitwise_xor(own, t) * samples, samples, 0)

    def send(array, t):
        block = cut(array, t)
        return block, swap(block, "blade", 4, t)

    sent, x3 = send(inputs, 3)
    rest = after(inputs, sent)
    sent, x1 = send(rest, 1)
    rest = after(rest, sent)
    _, x2 = send(rest, 2)

    matches = sample_index[:, None] == jnp.arange(NTAB, dtype=jnp.int32)[None, :]
    normalizer = jnp.sum(jnp.where(matches, norm_table[None, :], 0.0), axis=1)
    inv_all = 1.0 / normalizer
    inv = lax.dynamic_slice_in_dim(inv_all, own * samples, samples, 0)

    small = lax.optimization_barrier(small_tables())
    turned = turned_table(small)
    packed = pack_weights(spec_weight, lin_weight)
    packs = [packed] + [swap(packed, "blade", 4, t) for t in (1, 2, 3)]

    x3 = after(x3, (packed, turned))
    xa = to_modes(forward_spectrum(ids, inv, (inputs, x3), small, shards))
    blocks = after([cut(cotangent, t) for t in (1, 2, 3)], (x1, x2))
    cot = (cotangent,) + tuple(swap(blocks[t - 1], "blade", 4, t) for t in (1, 2, 3))
    xb = to_modes(forward_spectrum(ids, inv, (x1, x2), small, shards))
    pq, lt, lb = unpack(ids, packs, True)
    y = to_modes(mix(ids, xa, xb, pq))

    x = (inputs, x1, x2, x3)
    result = pixels(ids, inv, x, y, turned, lt)
    output, slope = result[0], result[4]
    last, cot = lax.optimization_barrier((result[3], cot))
    parts = (result[1], result[2], last)
    out_parts = [swap(parts[t - 1], "blade", 4, t) for t in (1, 2, 3)]

    grad_pre, sent, lin = pixel_grads(ids, inv, x, cot, slope, small, y.shape)
    g = after(to_modes(sent), out_parts[2])
    mixed = mix_back(ids, g, unpack(after(ids, lin), packs, False))
    back = to_modes(mixed)
    spec_grads = weight_grads(ids, xa, xb, g, lin)
    spec_grads = [spec_grads[0]] + [swap(spec_grads[t], "blade", 4, t) for t in (1, 2, 3)]

    inner = inner_grads(ids, inv, back, grad_pre, small, lb, cotangent)
    inner = after(inner, out_parts)
    grad_parts = [swap(inner[t], "blade", 4, t) for t in (1, 2, 3)]

    output = place_output(ids, out_parts, output)
    spec_grads = after(spec_grads, output)
    flips = jnp.stack(
        [jnp.where(own % 2 == 1, flip_of(jnp.bitwise_xor(own, t), 1), 1.0) for t in range(4)]
    )
    lin_grad = 0.0
    first = spec_weight.shape[1] * LANES
    for t in range(4):
        lin_grad = lin_grad + spec_grads[t][:, first : first + C].astype(F32) * flips[t]
    step = 1
    while step < shards:
        lin_grad = lin_grad + swap(lin_grad, "dp", shards, step)
        step *= 2

    spec_out = adam_spec(flips, spec_grads, spec_weight, spec_first, spec_second)
    lin_out = adamw(lin_weight, lin_first, lin_second, lin_grad[None])
    input_grad = final_grads(ids, inv_all, cotangent, grad_parts[2:], (3,), inner[0])
    input_grad = final_grads(ids, inv_all, cotangent, grad_parts[:2], (1, 2), input_grad)
    return (output, input_grad, *spec_out, *lin_out)


def solution(mesh):
    fields = P("dp", "blade", None, None)
    spec = P("blade", "dp", None, None, None)
    lin = P("blade", None, None)
    return jax.shard_map(
        partial(body, mesh.shape["dp"]),
        mesh=mesh,
        in_specs=(fields, fields, P(), P("dp"), spec, spec, spec, lin, lin, lin),
        out_specs=(fields, fields, spec, spec, spec, lin, lin, lin),
        check_vma=False,
    )
```

```python
from functools import partial
import math

import jax
import jax.numpy as jnp
from jax import lax
from jax.experimental import pallas as pl
from jax.experimental.pallas import tpu as pltpu
from jax.sharding import PartitionSpec as P

GRID = 64
MSIDE = 16
NTAB = 16
STEP_COUNT = 5
NPIX = 4096
MODES = 256
C = 48
LANES = 2 * C
QUAD = 4
PACK = 128
ROWS = 16

BETA_ONE = 0.9
BETA_TWO = 0.999
EPSILON = 1e-08
RATE = 0.1
DECAY = 0.01

F32 = jnp.float32
BF16 = jnp.bfloat16
SMEM = pltpu.MemorySpace.SMEM


def sgn(left, right):
    return -1.0 if (left & 2) and (right & 1) else 1.0


def flip_of(own, k):
    if k & 1:
        return (1 - 2 * ((own // 2) % 2)).astype(F32)
    return jnp.float32(1.0)


def mode_factor(mode):
    return jnp.where(mode % MSIDE == 0, 1.0, 2.0).astype(F32)


def dot(left, right, dims=((1,), (0,))):
    return lax.dot_general(left, right, (dims, ((), ())), preferred_element_type=F32)


def whole(shape):
    zeros = (0,) * len(shape)
    return pl.BlockSpec(tuple(shape), lambda *_: zeros)


def params(mib):
    return pltpu.CompilerParams(vmem_limit_bytes=mib * 1024 * 1024)


def fast(shape, kind):
    return pltpu.VMEM(tuple(shape), kind)


def slow(shape, kind):
    return pltpu.HBM(tuple(shape), kind)


def pin(*arrays):
    return [pltpu.with_memory_space_constraint(array, pltpu.VMEM) for array in arrays]


def stay(*arrays):
    return [pltpu.with_memory_space_constraint(array, pltpu.HBM) for array in arrays]


def in_vmem(count):
    return [pl.BlockSpec(memory_space=pltpu.MemorySpace.VMEM)] * count


def cost():
    return pl.CostEstimate(flops=1, bytes_accessed=1, transcendentals=0)


def small_tables():
    mode_ids = jnp.arange(2 * MODES, dtype=jnp.int32)
    imag = mode_ids >= MODES
    mode_ids = mode_ids % MODES
    row_index = mode_ids // MSIDE
    col_freq = mode_ids % MSIDE
    row_freq = jnp.where(row_index < MSIDE // 2, row_index, GRID - MSIDE + row_index)
    place = jnp.arange(GRID, dtype=jnp.int32)[:, None]
    row_angle = ((place * row_freq[None, :]) % GRID).astype(F32) * (2.0 * math.pi / GRID)
    col_angle = ((place * col_freq[None, :]) % GRID).astype(F32) * (2.0 * math.pi / GRID)
    row_cos, row_sin = jnp.cos(row_angle) / GRID, jnp.sin(row_angle) / GRID
    first = jnp.where(imag[None, :], -row_sin, row_cos)
    second = jnp.where(imag[None, :], -row_cos, -row_sin)
    return jnp.stack([first, second, jnp.cos(col_angle), jnp.sin(col_angle)])


def table_rows(row_ref, col_ref, start, stop):
    tiles = []
    for h in range(start, stop):
        tile = row_ref[0, h : h + 1] * col_ref[0] + row_ref[1, h : h + 1] * col_ref[1]
        tiles.append(tile.astype(BF16))
    return jnp.concatenate(tiles, axis=0)


def small_specs(tile):
    n = 2 * MODES
    return [
        pl.BlockSpec((2, tile // GRID, n), lambda i, *_: (0, i, 0)),
        pl.BlockSpec((2, GRID, n), lambda i, *_: (1, 0, 0)),
    ]


def turned_kernel(row_ref, col_ref, ft_ref):
    for h in range(0, row_ref.shape[1], 2):
        tile = table_rows(row_ref, col_ref, h, h + 2)
        ft_ref[:, h * GRID : (h + 2) * GRID] = tile.astype(F32).T.astype(BF16)


def turned_table(small):
    rows = 8
    n = 2 * MODES
    return pl.pallas_call(
        turned_kernel,
        grid=(GRID // rows,),
        in_specs=small_specs(rows * GRID),
        out_specs=pl.BlockSpec((n, rows * GRID), lambda i: (0, i)),
        out_shape=slow((n, NPIX), BF16),
        compiler_params=params(28),
        cost_estimate=cost(),
        name="turned",
    )(*stay(small, small))


def pack_kernel(w_ref, l_ref, o_ref):
    def step(g, carry):
        parts = [w_ref[0, g * QUAD + q, r] for q in range(QUAD) for r in range(2)]
        at = pl.ds(pl.multiple_of(g * QUAD * LANES, PACK), QUAD * LANES)
        o_ref[:, at] = jnp.concatenate(parts, axis=1).astype(BF16)
        return carry

    modes = w_ref.shape[1]
    lax.fori_loop(0, modes // QUAD, step, 0)
    line = jnp.concatenate([l_ref[0], jnp.zeros((C, PACK - C), F32)], axis=1)
    o_ref[:, modes * LANES :] = line.astype(BF16)


def pack_weights(spec_weight, lin_weight):
    modes = spec_weight.shape[1]
    return pl.pallas_call(
        pack_kernel,
        in_specs=in_vmem(2),
        out_specs=in_vmem(1)[0],
        out_shape=jax.ShapeDtypeStruct((C, modes * LANES + PACK), BF16),
        compiler_params=params(28),
        cost_estimate=cost(),
        name="pack",
    )(spec_weight, lin_weight)


def lanes_of(shape):
    return lax.broadcasted_iota(jnp.int32, shape, len(shape) - 1)


def split_lanes(a, b, c):
    lane = lanes_of(a.shape)
    second = jnp.where(lane < 32, pltpu.roll(a, 32, 1), pltpu.roll(b, 32, 1))
    third = jnp.where(lane < 64, pltpu.roll(b, 64, 1), pltpu.roll(c, 64, 1))
    return a, second, third, pltpu.roll(c, 96, 1)


def join_lanes(first, second, third, fourth):
    lane = lanes_of(first.shape)
    a = jnp.where(lane < 96, first, pltpu.roll(second, 96, 1))
    b = jnp.where(lane < 64, pltpu.roll(second, 96, 1), pltpu.roll(third, 64, 1))
    c = jnp.where(lane < 32, pltpu.roll(third, 64, 1), pltpu.roll(fourth, 32, 1))
    return a, b, c


def quad_tiles(ref, g):
    tiles = []
    for n in range(3):
        at = pl.ds(pl.multiple_of(g * QUAD * LANES + n * PACK, PACK), PACK)
        tiles.append(ref[:, at].astype(F32))
    return tiles


def unpack_kernel(ids_ref, w0, w1, w2, w3, pq_ref, *lines):
    own = ids_ref[0]
    modes = pq_ref.shape[0]
    lane = lanes_of((C, PACK))
    flip = flip_of(own, 1)

    def step(g, carry):
        for t, w in enumerate((w0, w1, w2, w3)):
            slot = jnp.bitwise_xor(own, t)
            scale = jnp.where(slot % 2 == 1, flip, 1.0)
            at = pl.ds(pl.multiple_of(slot * PACK, PACK), PACK)
            tiles = [tile * scale for tile in quad_tiles(w, g)]
            for q, p in enumerate(split_lanes(*tiles)):
                p = jnp.where(lane < LANES, p, 0.0)
                low = jnp.where(lane < C, -pltpu.roll(p, PACK - C, 1), pltpu.roll(p, C, 1))
                low = jnp.where(lane < LANES, low, 0.0)
                pq_ref[g * QUAD + q, :C, at] = p.astype(BF16)
                pq_ref[g * QUAD + q, C:, at] = low.astype(BF16)
        return carry

    quads = modes // QUAD
    lax.fori_loop(0, quads, step, 0, unroll=min(4, quads))
    if not lines:
        return
    lt_ref, lb_ref, lsc = lines
    for t, w in enumerate((w0, w1, w2, w3)):
        slot = jnp.bitwise_xor(own, t)
        lsc[slot] = w[:, modes * LANES :].astype(F32) * jnp.where(slot % 2 == 1, flip, 1.0)
    for k in range(4):
        line = lsc[k]
        turned = line.T
        for t in range(4):
            u = t ^ k
            lb_ref[t * C : (t + 1) * C, u * C : (u + 1) * C] = (line[:, :C] * sgn(t, k)).astype(BF16)
            lt_ref[u * C : (u + 1) * C, t * C : (t + 1) * C] = (turned[:C] * sgn(t, k)).astype(BF16)


def unpack(ids, packs, lines):
    modes = (packs[0].shape[1] - PACK) // LANES
    weights = fast((modes, LANES, 4 * PACK), BF16)
    shape = (4 * C, 4 * C)
    result = pl.pallas_call(
        unpack_kernel,
        in_specs=[pl.BlockSpec(memory_space=SMEM)] + in_vmem(4),
        out_specs=in_vmem(3 if lines else 1),
        out_shape=[weights] + ([fast(shape, BF16), slow(shape, BF16)] if lines else []),
        scratch_shapes=[pltpu.VMEM((4, C, PACK), F32)] if lines else [],
        compiler_params=params(28),
        cost_estimate=cost(),
        name="unpack",
    )(*stay(ids, *packs))
    return result if lines else result[0]


def spread(acc, out_ref, scales=None):
    rows = []
    for n in range(acc.shape[0] // C):
        for r in range(2):
            row = acc[n * C : (n + 1) * C, r * MODES : (r + 1) * MODES]
            rows.append(row if scales is None else row * scales[n])
    extra = out_ref.shape[2] - len(rows) * C
    if extra:
        rows.append(jnp.zeros((extra, MODES), F32))
    turned = jnp.concatenate(rows, axis=0).T
    out_ref[...] = turned.reshape(out_ref.shape).astype(BF16)


def collect(block, ysc):
    turned = block[...].astype(F32).reshape(MODES, block.shape[2]).T
    for n in range(ysc.shape[0] // C):
        for r in range(2):
            row = (n * 2 + r) * C
            piece = turned[row : row + C].astype(BF16)
            ysc[n * C : (n + 1) * C, r * MODES : (r + 1) * MODES] = piece


def forward_kernel(ids_ref, inv_ref, *refs):
    x = refs[:-4]
    row_ref, col_ref, out_ref, acc = refs[-4:]
    i = pl.program_id(0)
    samples = x[0].shape[0]
    rows = [part[s, 0] for s in range(samples) for part in x]
    table = table_rows(row_ref, col_ref, 0, row_ref.shape[1])
    part = dot(jnp.concatenate(rows, axis=0), table)

    @pl.when(i == 0)
    def _():
        acc[...] = part

    @pl.when(i > 0)
    def _():
        acc[...] += part

    @pl.when(i == pl.num_programs(0) - 1)
    def _():
        spread(acc, out_ref, [inv_ref[s] for s in range(samples) for _ in x])


def forward_spectrum(ids, inv, x, small, shards):
    samples = inv.shape[0]
    modes = MODES // shards
    width = -(-samples * len(x) * LANES // PACK) * PACK
    n = 2 * MODES
    tile = 2048

    def spec(array):
        if array.shape[0] == samples:
            return pl.BlockSpec((samples, 1, C, tile), lambda i, ids, inv: (0, 0, 0, i))
        return pl.BlockSpec((samples, 1, C, tile), lambda i, ids, inv: (ids[0], 0, 0, i))

    return pl.pallas_call(
        forward_kernel,
        grid_spec=pltpu.PrefetchScalarGridSpec(
            num_scalar_prefetch=2,
            grid=(NPIX // tile,),
            in_specs=[spec(part) for part in x] + small_specs(tile),
            out_specs=whole((shards, modes, width)),
            scratch_shapes=[pltpu.VMEM((samples * len(x) * C, n), F32)],
        ),
        out_shape=slow((shards, modes, width), BF16),
        compiler_params=params(28),
        cost_estimate=cost(),
        name="forward",
    )(*stay(ids, inv, *x, small, small))


def row_scratch(modes, shards, width):
    return pltpu.VMEM((width // PACK, modes * shards, PACK), F32)


def gather_rows(blocks, sc):
    shards, modes = blocks[0].shape[:2]
    first = 0
    for block in blocks:
        for n in range(block.shape[2] // PACK):
            for x in range(shards):
                rows = block[x, :, n * PACK : (n + 1) * PACK].astype(F32)
                sc[first + n, pl.ds(x, modes, stride=shards), :] = rows
        first += block.shape[2] // PACK


def scatter_rows(ysc, out):
    shards, modes = out.shape[:2]
    for x in range(shards):
        for n in range(ysc.shape[0]):
            piece = ysc[n, pl.ds(x, modes, stride=shards), :]
            out[x, :, n * PACK : (n + 1) * PACK] = piece.astype(BF16)


def blade_rows(sc, mode, shards, groups):
    at = pl.ds(pl.multiple_of(mode * shards, shards), shards)
    found = [[] for _ in range(4)]
    for tile, pairs in groups:
        tiles = [sc[tile + n, at, :] for n in range(-(-len(pairs) * LANES // PACK))]
        pieces = split_lanes(tiles[0], tiles[min(1, len(tiles) - 1)], tiles[-1])
        for piece, (_, t) in zip(pieces, pairs):
            found[t].append(piece)
    return [jnp.concatenate(found[t], axis=0) for t in range(4)]


def groups_of(samples, *blades):
    groups = []
    tile = 0
    for some in blades:
        pairs = [(s, t) for s in range(samples) for t in some]
        for n in range(0, len(pairs), 4):
            part = pairs[n : n + 4]
            groups.append((tile, part))
            tile += -(-len(part) * LANES // PACK)
    return groups


EARLY = (0, 3)
LATE = (1, 2)


def mix_modes(xsc, ysc, pq_ref, groups, shards, first_mode, back):
    modes = xsc.shape[1] // shards
    samples = ysc.shape[0] // 3
    group = samples * shards

    def step(m, carry):
        low = jnp.concatenate(blade_rows(xsc, m, shards, groups), axis=0)
        low = low[:, :LANES].astype(BF16)
        total = [None] * 4
        if not back:
            parts = dot(low, pq_ref[m])
        for k in range(4):
            if back:
                part = dot(low, pq_ref[m, :, k * PACK : k * PACK + LANES], ((1,), (1,)))
            else:
                part = parts[:, k * PACK : (k + 1) * PACK]
            for t in range(4):
                u = t ^ k
                piece = part[t * group : (t + 1) * group]
                sign = sgn(u, k) if back else sgn(t, k)
                if total[u] is None:
                    total[u] = piece if sign > 0 else -piece
                else:
                    total[u] = total[u] + piece if sign > 0 else total[u] - piece
        factor = mode_factor(first_mode + m)
        at = pl.ds(pl.multiple_of(m * shards, shards), shards)
        for s in range(samples):
            rows = []
            for u in range(4):
                piece = total[u][s * shards : (s + 1) * shards] * factor
                if back:
                    piece = jnp.concatenate([piece, jnp.zeros((shards, PACK - LANES), F32)], axis=1)
                rows.append(piece)
            for n, tile in enumerate(join_lanes(*rows)):
                ysc[s * 3 + n, at, :] = tile
        return carry

    lax.fori_loop(0, modes, step, 0, unroll=min(32, modes))


def mix_kernel(ids_ref, xa, xb, pq_ref, y_ref, xsc, ysc):
    shards, modes, width = y_ref.shape
    gather_rows((xa, xb), xsc)
    groups = groups_of(width // (4 * LANES), EARLY, LATE)
    mix_modes(xsc, ysc, pq_ref, groups, shards, ids_ref[1] * modes, False)
    scatter_rows(ysc, y_ref)


def mix(ids, xa, xb, pq, samples):
    shards, modes = xa.shape[:2]
    width = samples * 4 * LANES
    return pl.pallas_call(
        mix_kernel,
        in_specs=[pl.BlockSpec(memory_space=SMEM)] + in_vmem(3),
        out_specs=in_vmem(1)[0],
        out_shape=slow((shards, modes, width), BF16),
        scratch_shapes=[
            row_scratch(modes, shards, xa.shape[2] + xb.shape[2]),
            row_scratch(modes, shards, width),
        ],
        compiler_params=params(28),
        cost_estimate=cost(),
        name="mix",
    )(*stay(ids), xa, xb, *pin(pq))


def mix_back_kernel(ids_ref, g_ref, pq_ref, out_ref, gsc, ysc):
    shards, modes, width = g_ref.shape
    gather_rows((g_ref,), gsc)
    groups = groups_of(width // (4 * LANES), range(4))
    mix_modes(gsc, ysc, pq_ref, groups, shards, ids_ref[1] * modes, True)
    scatter_rows(ysc, out_ref)


def mix_back(ids, g, pq):
    shards, modes, width = g.shape
    return pl.pallas_call(
        mix_back_kernel,
        in_specs=[pl.BlockSpec(memory_space=SMEM)] + in_vmem(2),
        out_specs=in_vmem(1)[0],
        out_shape=slow(g.shape, BF16),
        scratch_shapes=[row_scratch(modes, shards, width)] * 2,
        compiler_params=params(28),
        cost_estimate=cost(),
        name="mix_back",
    )(*stay(ids), g, *pin(pq))


def turn_kernel(xa, xb, xt_ref, xsc):
    shards, modes = xa.shape[:2]
    samples = xt_ref.shape[2] // (8 * shards)
    groups = groups_of(samples, EARLY, LATE)
    gather_rows((xa, xb), xsc)

    def step(m, carry):
        x = blade_rows(xsc, m, shards, groups)
        x = x + [pltpu.roll(rows, PACK - C, 1) for rows in x]
        xt_ref[m] = jnp.concatenate(x, axis=0).T[:C].astype(BF16)
        return carry

    lax.fori_loop(0, modes, step, 0, unroll=4)


def turn_modes(xa, xb, samples):
    shards, modes = xa.shape[:2]
    return pl.pallas_call(
        turn_kernel,
        in_specs=in_vmem(2),
        out_specs=in_vmem(1)[0],
        out_shape=slow((modes, C, 8 * samples * shards), BF16),
        scratch_shapes=[row_scratch(modes, shards, xa.shape[2] + xb.shape[2])],
        compiler_params=params(28),
        cost_estimate=cost(),
        name="turn_modes",
    )(xa, xb)


def grad_kernel(ids_ref, xt_ref, g_ref, lin_ref, o0, o1, o2, o3, gsc, osc):
    shards, modes, width = g_ref.shape
    samples = width // (4 * LANES)
    own = ids_ref[0]
    first_mode = ids_ref[1] * modes
    groups = groups_of(samples, range(4))
    gather_rows((g_ref,), gsc)
    lane = lanes_of((samples * shards, PACK))

    def step(g, carry):
        found = [[] for _ in range(4)]
        for q in range(QUAD):
            m = g * QUAD + q
            factor = mode_factor(first_mode + m)
            plain = [rows * factor for rows in blade_rows(gsc, m, shards, groups)]
            turned = [
                jnp.where(lane < C, pltpu.roll(rows, PACK - C, 1), -pltpu.roll(rows, C, 1))
                for rows in plain
            ]
            plus = [rows.astype(BF16) for rows in plain + turned]
            minus = [(-rows).astype(BF16) for rows in plain + turned]
            right = []
            for k in range(4):
                rows = []
                for r in range(2):
                    for t in range(4):
                        rows.append((plus if sgn(t, k) > 0 else minus)[4 * r + (t ^ k)])
                right.append(jnp.concatenate(rows, axis=0))
            grad = dot(xt_ref[m], jnp.concatenate(right, axis=1))
            for k in range(4):
                found[k].append(grad[:, k * PACK : (k + 1) * PACK])
        for k in range(4):
            for n, tile in enumerate(join_lanes(*found[k])):
                at = pl.ds(pl.multiple_of(g * QUAD * LANES + n * PACK, PACK), PACK)
                osc[k, :, at] = tile.astype(BF16)
        return carry

    quads = modes // QUAD
    lax.fori_loop(0, quads, step, 0, unroll=min(2, quads))
    for k in range(4):
        line = jnp.concatenate([lin_ref[k], jnp.zeros((C, PACK - C), F32)], axis=1)
        osc[k, :, modes * LANES :] = line.astype(BF16)
    for t, out in enumerate((o0, o1, o2, o3)):
        out[...] = osc[jnp.bitwise_xor(own, t)]


def weight_grads(ids, xt, g, lin):
    shards, modes, width = g.shape
    shape = (C, modes * LANES + PACK)
    return pl.pallas_call(
        grad_kernel,
        in_specs=[pl.BlockSpec(memory_space=SMEM)] + in_vmem(3),
        out_specs=in_vmem(4),
        out_shape=[slow(shape, BF16)] * 4,
        scratch_shapes=[row_scratch(modes, shards, width), pltpu.VMEM((4,) + shape, BF16)],
        compiler_params=params(28),
        cost_estimate=cost(),
        name="weight_grads",
    )(*stay(ids, xt), g, *stay(lin))


CDF_AT = 0.28
CDF = (0.11652094, 0.06749571, 0.2689128, -0.23699677, 0.38987606, -0.10580875)
SERIES = [value / CDF_AT ** (i + 1) for i, value in enumerate(CDF)]


def gelu_parts(v):
    z = jnp.abs(v)
    t = 1.0 / (z + 1.0 / CDF_AT)
    bell = jnp.exp2(v * v * (-0.5 * math.log2(math.e)))
    series = jnp.float32(SERIES[-1])
    for value in SERIES[-2::-1]:
        series = series * t + value
    tail = series * t * bell
    cdf = jnp.where(v < 0.0, tail, 1.0 - tail)
    return v * cdf, cdf + v * (bell * (1.0 / math.sqrt(2.0 * math.pi)))


def pixel_kernel(ids_ref, inv_ref, *refs):
    x = refs[:4]
    y_ref, ft_ref, lt_ref = refs[4:7]
    outs = refs[7:11]
    slope_ref = refs[11]
    ysc, pre, lts = refs[12:]
    samples = x[1].shape[0]
    rows = 4 * C

    @pl.when(pl.program_id(0) == 0)
    def _():
        collect(y_ref, ysc)
        for s in range(samples):
            lts[s] = (lt_ref[...].astype(F32) * inv_ref[s]).astype(BF16)

    for s in range(samples):
        at = slice(s * rows, (s + 1) * rows)
        fields = jnp.concatenate([x[t][s, 0] for t in range(4)], axis=0)
        left = jnp.concatenate([ysc[at], lts[s]], axis=1)
        pre[at] = dot(left, jnp.concatenate([ft_ref[...], fields], axis=0))
    for s in range(samples):
        for t in range(4):
            for c in range(0, C, ROWS):
                at = s * rows + t * C + c
                value, slope = gelu_parts(pre[at : at + ROWS])
                normed = x[t][s, 0, c : c + ROWS].astype(F32) * inv_ref[s]
                outs[t][s, 0, c : c + ROWS] = (normed + value).astype(BF16)
                slope_ref[at : at + ROWS] = slope.astype(BF16)


def pixels(ids, inv, x, y, turned, lt):
    samples = inv.shape[0]
    n = 2 * MODES
    tile = 512
    mine = pl.BlockSpec((samples, 1, C, tile), lambda i, ids, inv: (ids[0], 0, 0, i))
    block = pl.BlockSpec((samples, 1, C, tile), lambda i, ids, inv: (0, 0, 0, i))
    rows = samples * 4 * C
    flat = pl.BlockSpec((rows, tile), lambda i, ids, inv: (0, i))
    return pl.pallas_call(
        pixel_kernel,
        grid_spec=pltpu.PrefetchScalarGridSpec(
            num_scalar_prefetch=2,
            grid=(NPIX // tile,),
            in_specs=[mine]
            + [block] * 3
            + [
                whole(y.shape),
                pl.BlockSpec((n, tile), lambda i, ids, inv: (0, i)),
                whole((4 * C, 4 * C)),
            ],
            out_specs=[mine] + [block] * 3 + [flat],
            scratch_shapes=[
                pltpu.VMEM((rows, n), BF16),
                pltpu.VMEM((rows, tile), F32),
                pltpu.VMEM((samples, 4 * C, 4 * C), BF16),
            ],
        ),
        out_shape=[slow(x[0].shape, BF16)]
        + [slow((samples, 1, C, NPIX), BF16)] * 3
        + [fast((rows, NPIX), BF16)],
        compiler_params=params(28),
        cost_estimate=cost(),
        name="pixels",
    )(*stay(ids, inv, *x), y, *stay(turned), *pin(lt))


def slope_kernel(ids_ref, inv_ref, *refs):
    x, cot = refs[:4], refs[4:8]
    slope, row_ref, col_ref, g_ref, g_out, lin_ref, gacc, lacc = refs[8:]
    samples = cot[1].shape[0]
    rows = 4 * C
    i = pl.program_id(0)

    @pl.when(i == 0)
    def _():
        gacc[...] = jnp.zeros_like(gacc)
        lacc[...] = jnp.zeros_like(lacc)

    for s in range(samples):
        for t in range(4):
            at = s * rows + t * C
            grad = cot[t][s, 0].astype(F32) * slope[at : at + C].astype(F32)
            g_ref[at : at + C] = grad.astype(BF16)
    table = table_rows(row_ref, col_ref, 0, row_ref.shape[1])
    gacc[...] += dot(g_ref[...], table)
    for s in range(samples):
        at = slice(s * rows, (s + 1) * rows)
        g = g_ref[at]
        fields = jnp.concatenate([x[t][s, 0] for t in range(4)], axis=0)
        lacc[...] += dot(fields, g, ((1,), (1,))) * inv_ref[s]

    @pl.when(i == pl.num_programs(0) - 1)
    def _():
        spread(gacc, g_out)
        for k in range(4):
            total = None
            for t in range(4):
                u = t ^ k
                piece = lacc[t * C : (t + 1) * C, u * C : (u + 1) * C] * sgn(t, k)
                total = piece if total is None else total + piece
            lin_ref[k] = total


def pixel_grads(ids, inv, x, cot, slope, small, spectrum):
    rows = slope.shape[0]
    samples = rows // (4 * C)
    n = 2 * MODES
    tile = 2048
    mine = pl.BlockSpec((samples, 1, C, tile), lambda i, ids, inv: (ids[0], 0, 0, i))
    block = pl.BlockSpec((samples, 1, C, tile), lambda i, ids, inv: (0, 0, 0, i))
    flat = pl.BlockSpec((rows, tile), lambda i, ids, inv: (0, i))
    return pl.pallas_call(
        slope_kernel,
        grid_spec=pltpu.PrefetchScalarGridSpec(
            num_scalar_prefetch=2,
            grid=(NPIX // tile,),
            in_specs=([mine] + [block] * 3) * 2
            + [flat]
            + small_specs(tile),
            out_specs=[flat, whole(spectrum), whole((4, C, C))],
            scratch_shapes=[pltpu.VMEM((rows, n), F32), pltpu.VMEM((4 * C, 4 * C), F32)],
        ),
        out_shape=[
            slow((rows, NPIX), BF16),
            slow(spectrum, BF16),
            slow((4, C, C), F32),
        ],
        compiler_params=params(28),
        cost_estimate=cost(),
        name="pixel_grads",
    )(*stay(ids, inv, *x, *cot), *pin(slope), *stay(small, small))


def inner_kernel(ids_ref, inv_ref, y_ref, g_ref, row_ref, col_ref, lb_ref, cot_ref, mine_ref, *refs):
    o1, o2, o3, ysc = refs
    samples = cot_ref.shape[0]
    rows = 4 * C

    @pl.when(pl.program_id(0) == 0)
    def _():
        collect(y_ref, ysc)

    table = table_rows(row_ref, col_ref, 0, row_ref.shape[1])
    spatial = dot(ysc[...], table, ((1,), (1,)))
    for s in range(samples):
        at = slice(s * rows, (s + 1) * rows)
        total = spatial[at] + dot(lb_ref[...], g_ref[at])
        mine_ref[s, 0] = (cot_ref[s, 0].astype(F32) + total[:C]) * inv_ref[s]
        for t, out in ((1, o1), (2, o2), (3, o3)):
            out[s, 0] = total[t * C : (t + 1) * C].astype(BF16)


def inner_grads(ids, inv, y, g, small, lb, cotangent):
    samples = inv.shape[0]
    n = 2 * MODES
    tile = 2048
    rows = samples * 4 * C
    mine = pl.BlockSpec((samples, 1, C, tile), lambda i, ids, inv: (ids[0], 0, 0, i))
    block = pl.BlockSpec((samples, 1, C, tile), lambda i, ids, inv: (0, 0, 0, i))
    return pl.pallas_call(
        inner_kernel,
        grid_spec=pltpu.PrefetchScalarGridSpec(
            num_scalar_prefetch=2,
            grid=(NPIX // tile,),
            in_specs=[
                whole(y.shape),
                pl.BlockSpec((rows, tile), lambda i, ids, inv: (0, i)),
                *small_specs(tile),
                whole((4 * C, 4 * C)),
                mine,
            ],
            out_specs=[mine] + [block] * 3,
            scratch_shapes=[pltpu.VMEM((rows, n), BF16)],
        ),
        out_shape=[slow(cotangent.shape, F32)] + [slow((samples, 1, C, NPIX), BF16)] * 3,
        compiler_params=params(28),
        cost_estimate=cost(),
        name="inner_grads",
    )(*stay(ids, inv), y, *stay(g, small, small, lb, cotangent))


def place_kernel(ids_ref, a_ref, b_ref, c_ref, old_ref, out_ref):
    for n, part in enumerate((a_ref, b_ref, c_ref)):

        @pl.when(pl.program_id(0) == n)
        def _():
            out_ref[...] = part[...]


def place_output(ids, parts, result):
    samples = parts[0].shape[0]
    shape = (1, 1, C, NPIX)

    def spec(n):
        def at(j, s, ids):
            return (jnp.where(j == n, s, jnp.where(j < n, 0, samples - 1)), 0, 0, 0)

        return pl.BlockSpec(shape, at)

    return pl.pallas_call(
        place_kernel,
        grid_spec=pltpu.PrefetchScalarGridSpec(
            num_scalar_prefetch=1,
            grid=(3, samples),
            in_specs=[spec(0), spec(1), spec(2), pl.BlockSpec(memory_space=pl.ANY)],
            out_specs=pl.BlockSpec(
                shape, lambda j, s, ids: (jnp.bitwise_xor(ids[0], j + 1) * samples + s, 0, 0, 0)
            ),
        ),
        out_shape=jax.ShapeDtypeStruct(result.shape, BF16),
        input_output_aliases={4: 0},
        compiler_params=params(28),
        cost_estimate=cost(),
        name="place",
    )(ids, *parts, result)


def final_kernel(count, codes, ids_ref, inv_ref, cot_ref, *refs):
    samples = pl.num_programs(1)
    j = pl.program_id(0)
    for n in range(count):

        @pl.when(j == n)
        def _():
            inv = inv_ref[jnp.bitwise_xor(ids_ref[0], codes[n]) * samples + pl.program_id(1)]
            refs[-1][...] = (cot_ref[...].astype(F32) + refs[n][...].astype(F32)) * inv


def final_grads(ids, inv, cotangent, parts, codes, result):
    samples = parts[0].shape[0]
    count = len(parts)
    shape = (1, 1, C, NPIX)

    def code(j):
        value = codes[0]
        for n in range(1, count):
            value = jnp.where(j == n, codes[n], value)
        return value

    def spec(n):
        def at(j, s, ids, inv):
            return (jnp.where(j == n, s, jnp.where(j < n, 0, samples - 1)), 0, 0, 0)

        return pl.BlockSpec(shape, at)

    place = pl.BlockSpec(
        shape, lambda j, s, ids, inv: (jnp.bitwise_xor(ids[0], code(j)) * samples + s, 0, 0, 0)
    )
    return pl.pallas_call(
        partial(final_kernel, count, codes),
        grid_spec=pltpu.PrefetchScalarGridSpec(
            num_scalar_prefetch=2,
            grid=(count, samples),
            in_specs=[place]
            + [spec(n) for n in range(count)]
            + [pl.BlockSpec(memory_space=pl.ANY)],
            out_specs=place,
        ),
        out_shape=jax.ShapeDtypeStruct(cotangent.shape, F32),
        input_output_aliases={3 + count: 0},
        compiler_params=params(28),
        cost_estimate=cost(),
        name="final",
    )(ids, inv, cotangent, *parts, result)


def adamw(weight, first, second, grad):
    first_new = BETA_ONE * first + (1.0 - BETA_ONE) * grad
    second_new = BETA_TWO * second + (1.0 - BETA_TWO) * grad * grad
    corr_one = 1.0 - BETA_ONE**STEP_COUNT
    corr_two = 1.0 - BETA_TWO**STEP_COUNT
    update = first_new / corr_one / (jnp.sqrt(second_new / corr_two) + EPSILON)
    return (weight - RATE * (update + DECAY * weight), first_new, second_new)


def adam_kernel(flips, d0, d1, d2, d3, w_ref, first_ref, second_ref, w_out, first_out, second_out):
    grad = d0[...].astype(F32) * flips[0]
    for t, d in ((1, d1), (2, d2), (3, d3)):
        grad = grad + d[...].astype(F32) * flips[t]
    for q in range(QUAD):
        for r in range(2):
            lane = q * LANES + r * C
            at = (0, q, r)
            new = adamw(w_ref[at], first_ref[at], second_ref[at], grad[:, lane : lane + C])
            w_out[at], first_out[at], second_out[at] = new


def adam_spec(flips, grads, weight, first, second):
    modes = weight.shape[1]
    packed = pl.BlockSpec((C, QUAD * LANES), lambda g: (0, g))
    block = pl.BlockSpec((1, QUAD, 2, C, C), lambda g: (0, g, 0, 0, 0))
    return pl.pallas_call(
        adam_kernel,
        grid=(modes // QUAD,),
        in_specs=[pl.BlockSpec(memory_space=SMEM)] + [packed] * 4 + [block] * 3,
        out_specs=[block] * 3,
        out_shape=[jax.ShapeDtypeStruct(weight.shape, F32)] * 3,
        compiler_params=params(28),
        cost_estimate=cost(),
        name="adam",
    )(flips, *grads, weight, first, second)


def swap(value, axis, size, x):
    return lax.ppermute(value, axis, [(i, i ^ x) for i in range(size)])


def to_modes(value):
    return lax.all_to_all(value, "dp", split_axis=0, concat_axis=0, tiled=True)


def after(values, first):
    values, _ = lax.optimization_barrier((values, first))
    return values


def body(
    shards,
    inputs,
    cotangent,
    norm_table,
    sample_index,
    spec_weight,
    spec_first,
    spec_second,
    lin_weight,
    lin_first,
    lin_second,
):
    own = lax.axis_index("blade")
    shard = lax.axis_index("dp")
    ids = jnp.stack([own, shard]).astype(jnp.int32)
    samples = inputs.shape[0] // 4

    def cut(array, t):
        return lax.dynamic_slice_in_dim(array, jnp.bitwise_xor(own, t) * samples, samples, 0)

    def send(array, t):
        block = cut(array, t)
        return block, swap(block, "blade", 4, t)

    sent, x3 = send(inputs, 3)
    rest = after(inputs, sent)
    sent, x1 = send(rest, 1)
    rest = after(rest, sent)
    _, x2 = send(rest, 2)

    matches = sample_index[:, None] == jnp.arange(NTAB, dtype=jnp.int32)[None, :]
    normalizer = jnp.sum(jnp.where(matches, norm_table[None, :], 0.0), axis=1)
    inv_all = 1.0 / normalizer
    inv = lax.dynamic_slice_in_dim(inv_all, own * samples, samples, 0)

    small = lax.optimization_barrier(small_tables())
    turned = turned_table(small)
    packed = pack_weights(spec_weight, lin_weight)
    packs = [packed] + [swap(packed, "blade", 4, t) for t in (1, 2, 3)]

    x3 = after(x3, (packed, turned))
    sent = forward_spectrum(ids, inv, (inputs, x3), small, shards)
    x1, x2 = after((x1, x2), sent)
    xa = to_modes(sent)
    blocks = after([cut(cotangent, t) for t in (1, 2, 3)], (x1, x2))
    cot = (cotangent,) + tuple(swap(blocks[t - 1], "blade", 4, t) for t in (1, 2, 3))
    xb = to_modes(forward_spectrum(ids, inv, (x1, x2), small, shards))
    pq, lt, lb = unpack(ids, packs, True)
    y = to_modes(mix(ids, xa, xb, pq, samples))

    x = (inputs, x1, x2, x3)
    result = pixels(ids, inv, x, y, turned, lt)
    output, slope = result[0], result[4]
    last, cot = lax.optimization_barrier((result[3], cot))
    parts = (result[1], result[2], last)
    out_parts = [swap(parts[t - 1], "blade", 4, t) for t in (1, 2, 3)]

    grad_pre, sent, lin = pixel_grads(ids, inv, x, cot, slope, small, y.shape)
    xt = turn_modes(after(xa, lin), xb, samples)
    g = after(to_modes(sent), (out_parts[2], xt))
    mixed = mix_back(ids, g, unpack(after(ids, lin), packs, False))
    back = to_modes(mixed)
    spec_grads = weight_grads(ids, xt, g, lin)
    spec_grads = [spec_grads[0]] + [swap(spec_grads[t], "blade", 4, t) for t in (1, 2, 3)]

    inner = inner_grads(ids, inv, back, grad_pre, small, lb, cotangent)
    inner = after(inner, out_parts)
    grad_parts = [swap(inner[t], "blade", 4, t) for t in (1, 2, 3)]

    output = place_output(ids, out_parts, output)
    spec_grads = after(spec_grads, output)
    flips = jnp.stack(
        [jnp.where(own % 2 == 1, flip_of(jnp.bitwise_xor(own, t), 1), 1.0) for t in range(4)]
    )
    lin_grad = 0.0
    first = spec_weight.shape[1] * LANES
    for t in range(4):
        lin_grad = lin_grad + spec_grads[t][:, first : first + C].astype(F32) * flips[t]
    step = 1
    while step < shards:
        lin_grad = lin_grad + swap(lin_grad, "dp", shards, step)
        step *= 2

    spec_out = adam_spec(flips, spec_grads, spec_weight, spec_first, spec_second)
    lin_out = adamw(lin_weight, lin_first, lin_second, lin_grad[None])
    input_grad = final_grads(ids, inv_all, cotangent, grad_parts[2:], (3,), inner[0])
    input_grad = final_grads(ids, inv_all, cotangent, grad_parts[:2], (1, 2), input_grad)
    return (output, input_grad, *spec_out, *lin_out)


def solution(mesh):
    fields = P("dp", "blade", None, None)
    spec = P("blade", "dp", None, None, None)
    lin = P("blade", None, None)
    return jax.shard_map(
        partial(body, mesh.shape["dp"]),
        mesh=mesh,
        in_specs=(fields, fields, P(), P("dp"), spec, spec, spec, lin, lin, lin),
        out_specs=(fields, fields, spec, spec, spec, lin, lin, lin),
        check_vma=False,
    )
```

```python
from functools import partial
import math

import jax
import jax.numpy as jnp
from jax import lax
from jax.experimental import pallas as pl
from jax.experimental.pallas import tpu as pltpu
from jax.sharding import PartitionSpec as P

GRID = 64
MSIDE = 16
NTAB = 16
STEP_COUNT = 5
NPIX = 4096
MODES = 256
C = 48
LANES = 2 * C
QUAD = 4
PACK = 128

BETA_ONE = 0.9
BETA_TWO = 0.999
EPSILON = 1e-08
RATE = 0.1
DECAY = 0.01

F32 = jnp.float32
BF16 = jnp.bfloat16
SMEM = pltpu.MemorySpace.SMEM


def sgn(left, right):
    return -1.0 if (left & 2) and (right & 1) else 1.0


def flip_of(own, k):
    if k & 1:
        return (1 - 2 * ((own // 2) % 2)).astype(F32)
    return jnp.float32(1.0)


def mode_factor(mode):
    return jnp.where(mode % MSIDE == 0, 1.0, 2.0).astype(F32)


def dot(left, right, dims=((1,), (0,))):
    return lax.dot_general(left, right, (dims, ((), ())), preferred_element_type=F32)


def whole(shape):
    zeros = (0,) * len(shape)
    return pl.BlockSpec(tuple(shape), lambda *_: zeros)


def params(mib):
    return pltpu.CompilerParams(vmem_limit_bytes=mib * 1024 * 1024)


def fast(shape, kind):
    return pltpu.VMEM(tuple(shape), kind)


def slow(shape, kind):
    return pltpu.HBM(tuple(shape), kind)


def pin(*arrays):
    return [pltpu.with_memory_space_constraint(array, pltpu.VMEM) for array in arrays]


def stay(*arrays):
    return [pltpu.with_memory_space_constraint(array, pltpu.HBM) for array in arrays]


def in_vmem(count):
    return [pl.BlockSpec(memory_space=pltpu.MemorySpace.VMEM)] * count


def cost():
    return pl.CostEstimate(flops=1, bytes_accessed=1, transcendentals=0)


def small_tables():
    mode_ids = jnp.arange(2 * MODES, dtype=jnp.int32)
    imag = mode_ids >= MODES
    mode_ids = mode_ids % MODES
    row_index = mode_ids // MSIDE
    col_freq = mode_ids % MSIDE
    row_freq = jnp.where(row_index < MSIDE // 2, row_index, GRID - MSIDE + row_index)
    place = jnp.arange(GRID, dtype=jnp.int32)[:, None]
    row_angle = ((place * row_freq[None, :]) % GRID).astype(F32) * (2.0 * math.pi / GRID)
    col_angle = ((place * col_freq[None, :]) % GRID).astype(F32) * (2.0 * math.pi / GRID)
    row_cos, row_sin = jnp.cos(row_angle) / GRID, jnp.sin(row_angle) / GRID
    first = jnp.where(imag[None, :], -row_sin, row_cos)
    second = jnp.where(imag[None, :], -row_cos, -row_sin)
    return jnp.stack([first, second, jnp.cos(col_angle), jnp.sin(col_angle)])


def table_rows(row_ref, col_ref, start, stop):
    tiles = []
    for h in range(start, stop):
        tile = row_ref[0, h : h + 1] * col_ref[0] + row_ref[1, h : h + 1] * col_ref[1]
        tiles.append(tile.astype(BF16))
    return jnp.concatenate(tiles, axis=0)


def small_specs(tile):
    n = 2 * MODES
    return [
        pl.BlockSpec((2, tile // GRID, n), lambda i, *_: (0, i, 0)),
        pl.BlockSpec((2, GRID, n), lambda i, *_: (1, 0, 0)),
    ]


def turned_kernel(row_ref, col_ref, ft_ref):
    for h in range(0, row_ref.shape[1], 2):
        tile = table_rows(row_ref, col_ref, h, h + 2)
        ft_ref[:, h * GRID : (h + 2) * GRID] = tile.astype(F32).T.astype(BF16)


def turned_table(small):
    rows = 8
    n = 2 * MODES
    return pl.pallas_call(
        turned_kernel,
        grid=(GRID // rows,),
        in_specs=small_specs(rows * GRID),
        out_specs=pl.BlockSpec((n, rows * GRID), lambda i: (0, i)),
        out_shape=slow((n, NPIX), BF16),
        compiler_params=params(28),
        cost_estimate=cost(),
        name="turned",
    )(*stay(small, small))


def pack_kernel(w_ref, l_ref, o_ref):
    def step(g, carry):
        parts = [w_ref[0, g * QUAD + q, r] for q in range(QUAD) for r in range(2)]
        at = pl.ds(pl.multiple_of(g * QUAD * LANES, PACK), QUAD * LANES)
        o_ref[:, at] = jnp.concatenate(parts, axis=1).astype(BF16)
        return carry

    modes = w_ref.shape[1]
    lax.fori_loop(0, modes // QUAD, step, 0)
    line = jnp.concatenate([l_ref[0], jnp.zeros((C, PACK - C), F32)], axis=1)
    o_ref[:, modes * LANES :] = line.astype(BF16)


def pack_weights(spec_weight, lin_weight):
    modes = spec_weight.shape[1]
    return pl.pallas_call(
        pack_kernel,
        in_specs=in_vmem(2),
        out_specs=in_vmem(1)[0],
        out_shape=jax.ShapeDtypeStruct((C, modes * LANES + PACK), BF16),
        compiler_params=params(28),
        cost_estimate=cost(),
        name="pack",
    )(spec_weight, lin_weight)


def lanes_of(shape):
    return lax.broadcasted_iota(jnp.int32, shape, len(shape) - 1)


def split_lanes(a, b, c):
    lane = lanes_of(a.shape)
    second = jnp.where(lane < 32, pltpu.roll(a, 32, 1), pltpu.roll(b, 32, 1))
    third = jnp.where(lane < 64, pltpu.roll(b, 64, 1), pltpu.roll(c, 64, 1))
    return a, second, third, pltpu.roll(c, 96, 1)


def join_lanes(first, second, third, fourth):
    lane = lanes_of(first.shape)
    a = jnp.where(lane < 96, first, pltpu.roll(second, 96, 1))
    b = jnp.where(lane < 64, pltpu.roll(second, 96, 1), pltpu.roll(third, 64, 1))
    c = jnp.where(lane < 32, pltpu.roll(third, 64, 1), pltpu.roll(fourth, 32, 1))
    return a, b, c


def quad_tiles(ref, g):
    tiles = []
    for n in range(3):
        at = pl.ds(pl.multiple_of(g * QUAD * LANES + n * PACK, PACK), PACK)
        tiles.append(ref[:, at].astype(F32))
    return tiles


def unpack_kernel(ids_ref, w0, w1, w2, w3, pq_ref, *lines):
    own = ids_ref[0]
    modes = pq_ref.shape[0]
    lane = lanes_of((C, PACK))
    flip = flip_of(own, 1)

    def step(g, carry):
        for t, w in enumerate((w0, w1, w2, w3)):
            slot = jnp.bitwise_xor(own, t)
            scale = jnp.where(slot % 2 == 1, flip, 1.0)
            at = pl.ds(pl.multiple_of(slot * PACK, PACK), PACK)
            tiles = [tile * scale for tile in quad_tiles(w, g)]
            for q, p in enumerate(split_lanes(*tiles)):
                p = jnp.where(lane < LANES, p, 0.0)
                low = jnp.where(lane < C, -pltpu.roll(p, PACK - C, 1), pltpu.roll(p, C, 1))
                low = jnp.where(lane < LANES, low, 0.0)
                pq_ref[g * QUAD + q, :C, at] = p.astype(BF16)
                pq_ref[g * QUAD + q, C:, at] = low.astype(BF16)
        return carry

    quads = modes // QUAD
    lax.fori_loop(0, quads, step, 0, unroll=min(4, quads))
    if not lines:
        return
    lt_ref, lb_ref, lsc = lines
    for t, w in enumerate((w0, w1, w2, w3)):
        slot = jnp.bitwise_xor(own, t)
        lsc[slot] = w[:, modes * LANES :].astype(F32) * jnp.where(slot % 2 == 1, flip, 1.0)
    for k in range(4):
        line = lsc[k]
        turned = line.T
        for t in range(4):
            u = t ^ k
            lb_ref[t * C : (t + 1) * C, u * C : (u + 1) * C] = (line[:, :C] * sgn(t, k)).astype(BF16)
            lt_ref[u * C : (u + 1) * C, t * C : (t + 1) * C] = (turned[:C] * sgn(t, k)).astype(BF16)


def unpack(ids, packs, lines):
    modes = (packs[0].shape[1] - PACK) // LANES
    weights = fast((modes, LANES, 4 * PACK), BF16)
    shape = (4 * C, 4 * C)
    result = pl.pallas_call(
        unpack_kernel,
        in_specs=[pl.BlockSpec(memory_space=SMEM)] + in_vmem(4),
        out_specs=in_vmem(3 if lines else 1),
        out_shape=[weights] + ([slow(shape, BF16)] * 2 if lines else []),
        scratch_shapes=[pltpu.VMEM((4, C, PACK), F32)] if lines else [],
        compiler_params=params(28),
        cost_estimate=cost(),
        name="unpack",
    )(*stay(ids, *packs))
    return result if lines else result[0]


def spread(acc, out_ref, scales=None):
    rows = []
    for n in range(acc.shape[0] // C):
        for r in range(2):
            row = acc[n * C : (n + 1) * C, r * MODES : (r + 1) * MODES]
            rows.append(row if scales is None else row * scales[n])
    extra = out_ref.shape[2] - len(rows) * C
    if extra:
        rows.append(jnp.zeros((extra, MODES), F32))
    turned = jnp.concatenate(rows, axis=0).T
    out_ref[...] = turned.reshape(out_ref.shape).astype(BF16)


def collect(block, ysc):
    turned = block[...].astype(F32).reshape(MODES, block.shape[2]).T
    for n in range(ysc.shape[0] // C):
        for r in range(2):
            row = (n * 2 + r) * C
            piece = turned[row : row + C].astype(BF16)
            ysc[n * C : (n + 1) * C, r * MODES : (r + 1) * MODES] = piece


def forward_kernel(ids_ref, inv_ref, *refs):
    x = refs[:-4]
    row_ref, col_ref, out_ref, acc = refs[-4:]
    i = pl.program_id(0)
    samples = x[0].shape[0]
    rows = [part[s, 0] for s in range(samples) for part in x]
    table = table_rows(row_ref, col_ref, 0, row_ref.shape[1])
    part = dot(jnp.concatenate(rows, axis=0), table)

    @pl.when(i == 0)
    def _():
        acc[...] = part

    @pl.when(i > 0)
    def _():
        acc[...] += part

    @pl.when(i == pl.num_programs(0) - 1)
    def _():
        spread(acc, out_ref, [inv_ref[s] for s in range(samples) for _ in x])


def forward_spectrum(ids, inv, x, small, shards):
    samples = inv.shape[0]
    modes = MODES // shards
    width = -(-samples * len(x) * LANES // PACK) * PACK
    n = 2 * MODES
    tile = 2048

    def spec(array):
        if array.shape[0] == samples:
            return pl.BlockSpec((samples, 1, C, tile), lambda i, ids, inv: (0, 0, 0, i))
        return pl.BlockSpec((samples, 1, C, tile), lambda i, ids, inv: (ids[0], 0, 0, i))

    return pl.pallas_call(
        forward_kernel,
        grid_spec=pltpu.PrefetchScalarGridSpec(
            num_scalar_prefetch=2,
            grid=(NPIX // tile,),
            in_specs=[spec(part) for part in x] + small_specs(tile),
            out_specs=whole((shards, modes, width)),
            scratch_shapes=[pltpu.VMEM((samples * len(x) * C, n), F32)],
        ),
        out_shape=slow((shards, modes, width), BF16),
        compiler_params=params(28),
        cost_estimate=cost(),
        name="forward",
    )(*stay(ids, inv, *x, small, small))


def row_scratch(modes, shards, width):
    return pltpu.VMEM((width // PACK, modes * shards, PACK), F32)


def gather_rows(blocks, sc):
    shards, modes = blocks[0].shape[:2]
    first = 0
    for block in blocks:
        for n in range(block.shape[2] // PACK):
            for x in range(shards):
                rows = block[x, :, n * PACK : (n + 1) * PACK].astype(F32)
                sc[first + n, pl.ds(x, modes, stride=shards), :] = rows
        first += block.shape[2] // PACK


def scatter_rows(ysc, out):
    shards, modes = out.shape[:2]
    for x in range(shards):
        for n in range(ysc.shape[0]):
            piece = ysc[n, pl.ds(x, modes, stride=shards), :]
            out[x, :, n * PACK : (n + 1) * PACK] = piece.astype(BF16)


def blade_rows(sc, mode, shards, groups):
    at = pl.ds(pl.multiple_of(mode * shards, shards), shards)
    found = [[] for _ in range(4)]
    for tile, pairs in groups:
        tiles = [sc[tile + n, at, :] for n in range(-(-len(pairs) * LANES // PACK))]
        pieces = split_lanes(tiles[0], tiles[min(1, len(tiles) - 1)], tiles[-1])
        for piece, (_, t) in zip(pieces, pairs):
            found[t].append(piece)
    return [jnp.concatenate(found[t], axis=0) for t in range(4)]


def groups_of(samples, *blades):
    groups = []
    tile = 0
    for some in blades:
        pairs = [(s, t) for s in range(samples) for t in some]
        for n in range(0, len(pairs), 4):
            part = pairs[n : n + 4]
            groups.append((tile, part))
            tile += -(-len(part) * LANES // PACK)
    return groups


EARLY = (0, 3)
LATE = (1, 2)


def mix_modes(xsc, ysc, pq_ref, groups, shards, first_mode, back):
    modes = xsc.shape[1] // shards
    samples = ysc.shape[0] // 3
    group = samples * shards

    def step(m, carry):
        low = jnp.concatenate(blade_rows(xsc, m, shards, groups), axis=0)
        low = low[:, :LANES].astype(BF16)
        total = [None] * 4
        parts = dot(low, pq_ref[m])
        for k in range(4):
            part = parts[:, k * PACK : (k + 1) * PACK]
            for t in range(4):
                u = t ^ k
                piece = part[t * group : (t + 1) * group]
                sign = sgn(u, k) if back else sgn(t, k)
                if total[u] is None:
                    total[u] = piece if sign > 0 else -piece
                else:
                    total[u] = total[u] + piece if sign > 0 else total[u] - piece
        factor = mode_factor(first_mode + m)
        at = pl.ds(pl.multiple_of(m * shards, shards), shards)
        for s in range(samples):
            rows = []
            for u in range(4):
                rows.append(total[u][s * shards : (s + 1) * shards] * factor)
            for n, tile in enumerate(join_lanes(*rows)):
                ysc[s * 3 + n, at, :] = tile
        return carry

    lax.fori_loop(0, modes, step, 0, unroll=min(32, modes))


def mix_kernel(ids_ref, xa, xb, pq_ref, y_ref, xsc, ysc):
    shards, modes, width = y_ref.shape
    gather_rows((xa, xb), xsc)
    groups = groups_of(width // (4 * LANES), EARLY, LATE)
    mix_modes(xsc, ysc, pq_ref, groups, shards, ids_ref[1] * modes, False)
    scatter_rows(ysc, y_ref)


def mix(ids, xa, xb, pq, samples):
    shards, modes = xa.shape[:2]
    width = samples * 4 * LANES
    return pl.pallas_call(
        mix_kernel,
        in_specs=[pl.BlockSpec(memory_space=SMEM)] + in_vmem(3),
        out_specs=in_vmem(1)[0],
        out_shape=slow((shards, modes, width), BF16),
        scratch_shapes=[
            row_scratch(modes, shards, xa.shape[2] + xb.shape[2]),
            row_scratch(modes, shards, width),
        ],
        compiler_params=params(28),
        cost_estimate=cost(),
        name="mix",
    )(*stay(ids, xa, xb), *pin(pq))


def turn_blocks_kernel(pq_ref, out_ref, held):
    modes = pq_ref.shape[0]
    shape = (LANES, LANES)
    diagonal = lax.broadcasted_iota(jnp.int32, shape, 0) == lax.broadcasted_iota(jnp.int32, shape, 1)
    unit = jnp.where(diagonal, 1.0, 0.0).astype(BF16)

    def step(m, carry):
        for k in range(4):
            at = slice(k * PACK, k * PACK + LANES)
            held[m, :, at] = dot(unit, pq_ref[m, :, at], ((1,), (1,))).astype(BF16)
        return carry

    lax.fori_loop(0, modes, step, 0, unroll=min(16, modes))
    out_ref[...] = held[...]


def turn_blocks(pq):
    return pl.pallas_call(
        turn_blocks_kernel,
        in_specs=in_vmem(1),
        out_specs=in_vmem(1)[0],
        out_shape=fast(pq.shape, BF16),
        input_output_aliases={0: 0},
        scratch_shapes=[pltpu.VMEM(pq.shape, BF16)],
        compiler_params=params(28),
        cost_estimate=cost(),
        name="turn_blocks",
    )(*pin(pq))


def mix_back_kernel(ids_ref, g_ref, pq_ref, out_ref, gsc, ysc):
    shards, modes, width = g_ref.shape
    gather_rows((g_ref,), gsc)
    groups = groups_of(width // (4 * LANES), range(4))
    mix_modes(gsc, ysc, pq_ref, groups, shards, ids_ref[1] * modes, True)
    scatter_rows(ysc, out_ref)


def mix_back(ids, g, pq):
    shards, modes, width = g.shape
    return pl.pallas_call(
        mix_back_kernel,
        in_specs=[pl.BlockSpec(memory_space=SMEM)] + in_vmem(2),
        out_specs=in_vmem(1)[0],
        out_shape=slow(g.shape, BF16),
        scratch_shapes=[row_scratch(modes, shards, width)] * 2,
        compiler_params=params(28),
        cost_estimate=cost(),
        name="mix_back",
    )(*stay(ids), g, *pin(pq))


def turn_kernel(xa, xb, xt_ref, xsc):
    shards, modes = xa.shape[:2]
    samples = xt_ref.shape[2] // (8 * shards)
    groups = groups_of(samples, EARLY, LATE)
    gather_rows((xa, xb), xsc)

    def step(m, carry):
        x = blade_rows(xsc, m, shards, groups)
        x = x + [pltpu.roll(rows, PACK - C, 1) for rows in x]
        xt_ref[m] = jnp.concatenate(x, axis=0).T[:C].astype(BF16)
        return carry

    lax.fori_loop(0, modes, step, 0, unroll=4)


def turn_modes(xa, xb, samples):
    shards, modes = xa.shape[:2]
    return pl.pallas_call(
        turn_kernel,
        in_specs=in_vmem(2),
        out_specs=in_vmem(1)[0],
        out_shape=slow((modes, C, 8 * samples * shards), BF16),
        scratch_shapes=[row_scratch(modes, shards, xa.shape[2] + xb.shape[2])],
        compiler_params=params(28),
        cost_estimate=cost(),
        name="turn_modes",
    )(*stay(xa, xb))


def grad_kernel(ids_ref, xt_ref, g_ref, lin_ref, o0, o1, o2, o3, gsc, osc):
    shards, modes, width = g_ref.shape
    samples = width // (4 * LANES)
    own = ids_ref[0]
    first_mode = ids_ref[1] * modes
    groups = groups_of(samples, range(4))
    gather_rows((g_ref,), gsc)
    lane = lanes_of((samples * shards, PACK))

    def step(g, carry):
        found = [[] for _ in range(4)]
        for q in range(QUAD):
            m = g * QUAD + q
            factor = mode_factor(first_mode + m)
            plain = [rows * factor for rows in blade_rows(gsc, m, shards, groups)]
            turned = [
                jnp.where(lane < C, pltpu.roll(rows, PACK - C, 1), -pltpu.roll(rows, C, 1))
                for rows in plain
            ]
            plus = [rows.astype(BF16) for rows in plain + turned]
            minus = [(-rows).astype(BF16) for rows in plain + turned]
            right = []
            for k in range(4):
                rows = []
                for r in range(2):
                    for t in range(4):
                        rows.append((plus if sgn(t, k) > 0 else minus)[4 * r + (t ^ k)])
                right.append(jnp.concatenate(rows, axis=0))
            grad = dot(xt_ref[m], jnp.concatenate(right, axis=1))
            for k in range(4):
                found[k].append(grad[:, k * PACK : (k + 1) * PACK])
        for k in range(4):
            for n, tile in enumerate(join_lanes(*found[k])):
                at = pl.ds(pl.multiple_of(g * QUAD * LANES + n * PACK, PACK), PACK)
                osc[k, :, at] = tile.astype(BF16)
        return carry

    quads = modes // QUAD
    lax.fori_loop(0, quads, step, 0, unroll=min(2, quads))
    for k in range(4):
        line = jnp.concatenate([lin_ref[k], jnp.zeros((C, PACK - C), F32)], axis=1)
        osc[k, :, modes * LANES :] = line.astype(BF16)
    for t, out in enumerate((o0, o1, o2, o3)):
        out[...] = osc[jnp.bitwise_xor(own, t)]


def weight_grads(ids, xt, g, lin):
    shards, modes, width = g.shape
    shape = (C, modes * LANES + PACK)
    return pl.pallas_call(
        grad_kernel,
        in_specs=[pl.BlockSpec(memory_space=SMEM)] + in_vmem(3),
        out_specs=in_vmem(4),
        out_shape=[slow(shape, BF16)] * 4,
        scratch_shapes=[row_scratch(modes, shards, width), pltpu.VMEM((4,) + shape, BF16)],
        compiler_params=params(28),
        cost_estimate=cost(),
        name="weight_grads",
    )(*stay(ids, xt), g, *stay(lin))


CDF_AT = 0.28
CDF = (0.11652094, 0.06749571, 0.2689128, -0.23699677, 0.38987606, -0.10580875)
SERIES = [value / CDF_AT ** (i + 1) for i, value in enumerate(CDF)]


def gelu_parts(v):
    z = jnp.abs(v)
    t = 1.0 / (z + 1.0 / CDF_AT)
    bell = jnp.exp2(v * v * (-0.5 * math.log2(math.e)))
    series = jnp.float32(SERIES[-1])
    for value in SERIES[-2::-1]:
        series = series * t + value
    tail = series * t * bell
    cdf = jnp.where(v < 0.0, tail, 1.0 - tail)
    return v * cdf, cdf + v * (bell * (1.0 / math.sqrt(2.0 * math.pi)))


def pixel_kernel(ids_ref, inv_ref, *refs):
    x = refs[:4]
    y_ref, ft_ref, lt_ref = refs[4:7]
    outs = refs[8:12]
    slope_ref = refs[12]
    left, ysc, even, odd = refs[14:]
    samples = x[1].shape[0]
    rows = 4 * C
    n = 2 * MODES
    width = even.shape[1]

    @pl.when(pl.program_id(0) == 0)
    def _():
        collect(y_ref, ysc)
        for s in range(samples):
            left[s, :, :n] = ysc[s * rows : (s + 1) * rows]
            left[s, :, n:] = (lt_ref[...].astype(F32) * inv_ref[s]).astype(BF16)

    def product(s, at, pre):
        fields = [x[t][s, 0, :, at] for t in range(4)]
        pre[...] = dot(left[s], jnp.concatenate([ft_ref[:, at]] + fields, axis=0))

    def activate(s, at, pre):
        for t in range(4):
            value, slope = gelu_parts(pre[t * C : (t + 1) * C])
            normed = x[t][s, 0, :, at].astype(F32) * inv_ref[s]
            outs[t][s, 0, :, at] = (normed + value).astype(BF16)
            row = s * rows + t * C
            slope_ref[row : row + C, at] = slope.astype(BF16)

    tile = ft_ref.shape[1]
    blocks = [(s, slice(k, k + width)) for k in range(0, tile, width) for s in range(samples)]
    buffers = [even, odd]
    product(*blocks[0], buffers[0])
    for k, block in enumerate(blocks):
        if k + 1 < len(blocks):
            product(*blocks[k + 1], buffers[(k + 1) % 2])
        activate(*block, buffers[k % 2])


def pixels(ids, inv, x, y, turned, lt, pq):
    samples = inv.shape[0]
    n = 2 * MODES
    tile = 1024
    mine = pl.BlockSpec((samples, 1, C, tile), lambda i, ids, inv: (ids[0], 0, 0, i))
    block = pl.BlockSpec((samples, 1, C, tile), lambda i, ids, inv: (0, 0, 0, i))
    rows = samples * 4 * C
    flat = pl.BlockSpec((rows, tile), lambda i, ids, inv: (0, i))
    return pl.pallas_call(
        pixel_kernel,
        grid_spec=pltpu.PrefetchScalarGridSpec(
            num_scalar_prefetch=2,
            grid=(NPIX // tile,),
            in_specs=[mine]
            + [block] * 3
            + [
                whole(y.shape),
                pl.BlockSpec((n, tile), lambda i, ids, inv: (0, i)),
                whole((4 * C, 4 * C)),
                pl.BlockSpec(memory_space=pl.ANY),
            ],
            out_specs=[mine] + [block] * 3 + [flat, pl.BlockSpec(memory_space=pl.ANY)],
            scratch_shapes=[
                pltpu.VMEM((samples, 4 * C, n + 4 * C), BF16),
                pltpu.VMEM((rows, n), BF16),
                pltpu.VMEM((4 * C, 256), F32),
                pltpu.VMEM((4 * C, 256), F32),
            ],
        ),
        out_shape=[slow(x[0].shape, BF16)]
        + [slow((samples, 1, C, NPIX), BF16)] * 3
        + [fast((rows, NPIX), BF16), fast(pq.shape, BF16)],
        input_output_aliases={9: 5},
        compiler_params=params(28),
        cost_estimate=cost(),
        name="pixels",
    )(*stay(ids, inv, *x), y, *stay(turned, lt), *pin(pq))


def slope_kernel(ids_ref, inv_ref, *refs):
    x, cot = refs[:4], refs[4:8]
    slope, row_ref, col_ref, _, g_ref, g_out, lin_ref, _, gacc, lacc = refs[8:]
    samples = cot[1].shape[0]
    rows = 4 * C
    i = pl.program_id(0)

    @pl.when(i == 0)
    def _():
        gacc[...] = jnp.zeros_like(gacc)
        lacc[...] = jnp.zeros_like(lacc)

    for s in range(samples):
        for t in range(4):
            at = s * rows + t * C
            grad = cot[t][s, 0].astype(F32) * slope[at : at + C].astype(F32)
            g_ref[at : at + C] = grad.astype(BF16)
    table = table_rows(row_ref, col_ref, 0, row_ref.shape[1])
    gacc[...] += dot(g_ref[...], table)
    for s in range(samples):
        at = slice(s * rows, (s + 1) * rows)
        g = g_ref[at]
        fields = jnp.concatenate([x[t][s, 0] for t in range(4)], axis=0)
        lacc[...] += dot(fields, g, ((1,), (1,))) * inv_ref[s]

    @pl.when(i == pl.num_programs(0) - 1)
    def _():
        spread(gacc, g_out)
        for k in range(4):
            total = None
            for t in range(4):
                u = t ^ k
                piece = lacc[t * C : (t + 1) * C, u * C : (u + 1) * C] * sgn(t, k)
                total = piece if total is None else total + piece
            lin_ref[k] = total


def pixel_grads(ids, inv, x, cot, slope, small, spectrum, pq):
    rows = slope.shape[0]
    samples = rows // (4 * C)
    n = 2 * MODES
    tile = 2048
    mine = pl.BlockSpec((samples, 1, C, tile), lambda i, ids, inv: (ids[0], 0, 0, i))
    block = pl.BlockSpec((samples, 1, C, tile), lambda i, ids, inv: (0, 0, 0, i))
    flat = pl.BlockSpec((rows, tile), lambda i, ids, inv: (0, i))
    return pl.pallas_call(
        slope_kernel,
        grid_spec=pltpu.PrefetchScalarGridSpec(
            num_scalar_prefetch=2,
            grid=(NPIX // tile,),
            in_specs=([mine] + [block] * 3) * 2
            + [flat]
            + small_specs(tile)
            + [pl.BlockSpec(memory_space=pl.ANY)],
            out_specs=[
                flat,
                whole(spectrum),
                whole((4, C, C)),
                pl.BlockSpec(memory_space=pl.ANY),
            ],
            scratch_shapes=[pltpu.VMEM((rows, n), F32), pltpu.VMEM((4 * C, 4 * C), F32)],
        ),
        out_shape=[
            slow((rows, NPIX), BF16),
            slow(spectrum, BF16),
            slow((4, C, C), F32),
            fast(pq.shape, BF16),
        ],
        input_output_aliases={13: 3},
        compiler_params=params(28),
        cost_estimate=cost(),
        name="pixel_grads",
    )(*stay(ids, inv, *x, *cot), *pin(slope), *stay(small, small), *pin(pq))


def inner_kernel(ids_ref, inv_ref, y_ref, g_ref, row_ref, col_ref, lb_ref, cot_ref, mine_ref, *refs):
    o1, o2, o3, ysc = refs
    samples = cot_ref.shape[0]
    rows = 4 * C

    @pl.when(pl.program_id(0) == 0)
    def _():
        collect(y_ref, ysc)

    table = table_rows(row_ref, col_ref, 0, row_ref.shape[1])
    spatial = dot(ysc[...], table, ((1,), (1,)))
    for s in range(samples):
        at = slice(s * rows, (s + 1) * rows)
        total = spatial[at] + dot(lb_ref[...], g_ref[at])
        mine_ref[s, 0] = (cot_ref[s, 0].astype(F32) + total[:C]) * inv_ref[s]
        for t, out in ((1, o1), (2, o2), (3, o3)):
            out[s, 0] = total[t * C : (t + 1) * C].astype(BF16)


def inner_grads(ids, inv, y, g, small, lb, cotangent):
    samples = inv.shape[0]
    n = 2 * MODES
    tile = 2048
    rows = samples * 4 * C
    mine = pl.BlockSpec((samples, 1, C, tile), lambda i, ids, inv: (ids[0], 0, 0, i))
    block = pl.BlockSpec((samples, 1, C, tile), lambda i, ids, inv: (0, 0, 0, i))
    return pl.pallas_call(
        inner_kernel,
        grid_spec=pltpu.PrefetchScalarGridSpec(
            num_scalar_prefetch=2,
            grid=(NPIX // tile,),
            in_specs=[
                whole(y.shape),
                pl.BlockSpec((rows, tile), lambda i, ids, inv: (0, i)),
                *small_specs(tile),
                whole((4 * C, 4 * C)),
                mine,
            ],
            out_specs=[mine] + [block] * 3,
            scratch_shapes=[pltpu.VMEM((rows, n), BF16)],
        ),
        out_shape=[slow(cotangent.shape, F32)] + [slow((samples, 1, C, NPIX), BF16)] * 3,
        compiler_params=params(28),
        cost_estimate=cost(),
        name="inner_grads",
    )(*stay(ids, inv), y, *stay(g, small, small, lb, cotangent))


def place_kernel(ids_ref, a_ref, b_ref, c_ref, old_ref, out_ref):
    for n, part in enumerate((a_ref, b_ref, c_ref)):

        @pl.when(pl.program_id(0) == n)
        def _():
            out_ref[...] = part[...]


def place_output(ids, parts, result):
    samples = parts[0].shape[0]
    shape = (1, 1, C, NPIX)

    def spec(n):
        def at(j, s, ids):
            return (jnp.where(j == n, s, jnp.where(j < n, 0, samples - 1)), 0, 0, 0)

        return pl.BlockSpec(shape, at)

    return pl.pallas_call(
        place_kernel,
        grid_spec=pltpu.PrefetchScalarGridSpec(
            num_scalar_prefetch=1,
            grid=(3, samples),
            in_specs=[spec(0), spec(1), spec(2), pl.BlockSpec(memory_space=pl.ANY)],
            out_specs=pl.BlockSpec(
                shape, lambda j, s, ids: (jnp.bitwise_xor(ids[0], j + 1) * samples + s, 0, 0, 0)
            ),
        ),
        out_shape=jax.ShapeDtypeStruct(result.shape, BF16),
        input_output_aliases={4: 0},
        compiler_params=params(28),
        cost_estimate=cost(),
        name="place",
    )(ids, *parts, result)


def final_kernel(count, codes, ids_ref, inv_ref, cot_ref, *refs):
    samples = pl.num_programs(1)
    j = pl.program_id(0)
    for n in range(count):

        @pl.when(j == n)
        def _():
            inv = inv_ref[jnp.bitwise_xor(ids_ref[0], codes[n]) * samples + pl.program_id(1)]
            refs[-1][...] = (cot_ref[...].astype(F32) + refs[n][...].astype(F32)) * inv


def final_grads(ids, inv, cotangent, parts, codes, result):
    samples = parts[0].shape[0]
    count = len(parts)
    shape = (1, 1, C, NPIX)

    def code(j):
        value = codes[0]
        for n in range(1, count):
            value = jnp.where(j == n, codes[n], value)
        return value

    def spec(n):
        def at(j, s, ids, inv):
            return (jnp.where(j == n, s, jnp.where(j < n, 0, samples - 1)), 0, 0, 0)

        return pl.BlockSpec(shape, at)

    place = pl.BlockSpec(
        shape, lambda j, s, ids, inv: (jnp.bitwise_xor(ids[0], code(j)) * samples + s, 0, 0, 0)
    )
    return pl.pallas_call(
        partial(final_kernel, count, codes),
        grid_spec=pltpu.PrefetchScalarGridSpec(
            num_scalar_prefetch=2,
            grid=(count, samples),
            in_specs=[place]
            + [spec(n) for n in range(count)]
            + [pl.BlockSpec(memory_space=pl.ANY)],
            out_specs=place,
        ),
        out_shape=jax.ShapeDtypeStruct(cotangent.shape, F32),
        input_output_aliases={3 + count: 0},
        compiler_params=params(28),
        cost_estimate=cost(),
        name="final",
    )(ids, inv, cotangent, *parts, result)


def adamw(weight, first, second, grad):
    first_new = BETA_ONE * first + (1.0 - BETA_ONE) * grad
    second_new = BETA_TWO * second + (1.0 - BETA_TWO) * grad * grad
    corr_one = 1.0 - BETA_ONE**STEP_COUNT
    corr_two = 1.0 - BETA_TWO**STEP_COUNT
    update = first_new / corr_one / (jnp.sqrt(second_new / corr_two) + EPSILON)
    return (weight - RATE * (update + DECAY * weight), first_new, second_new)


def adam_kernel(flips, d0, d1, d2, d3, w_ref, first_ref, second_ref, w_out, first_out, second_out):
    grad = d0[...].astype(F32) * flips[0]
    for t, d in ((1, d1), (2, d2), (3, d3)):
        grad = grad + d[...].astype(F32) * flips[t]
    for q in range(QUAD):
        for r in range(2):
            lane = q * LANES + r * C
            at = (0, q, r)
            new = adamw(w_ref[at], first_ref[at], second_ref[at], grad[:, lane : lane + C])
            w_out[at], first_out[at], second_out[at] = new


def adam_spec(flips, grads, weight, first, second):
    modes = weight.shape[1]
    packed = pl.BlockSpec((C, QUAD * LANES), lambda g: (0, g))
    block = pl.BlockSpec((1, QUAD, 2, C, C), lambda g: (0, g, 0, 0, 0))
    return pl.pallas_call(
        adam_kernel,
        grid=(modes // QUAD,),
        in_specs=[pl.BlockSpec(memory_space=SMEM)] + [packed] * 4 + [block] * 3,
        out_specs=[block] * 3,
        out_shape=[jax.ShapeDtypeStruct(weight.shape, F32)] * 3,
        compiler_params=params(28),
        cost_estimate=cost(),
        name="adam",
    )(flips, *grads, weight, first, second)


def swap(value, axis, size, x):
    return lax.ppermute(value, axis, [(i, i ^ x) for i in range(size)])


def to_modes(value):
    return lax.all_to_all(value, "dp", split_axis=0, concat_axis=0, tiled=True)


def after(values, first):
    values, _ = lax.optimization_barrier((values, first))
    return values


def body(
    shards,
    inputs,
    cotangent,
    norm_table,
    sample_index,
    spec_weight,
    spec_first,
    spec_second,
    lin_weight,
    lin_first,
    lin_second,
):
    own = lax.axis_index("blade")
    shard = lax.axis_index("dp")
    ids = jnp.stack([own, shard]).astype(jnp.int32)
    samples = inputs.shape[0] // 4

    def cut(array, t):
        return lax.dynamic_slice_in_dim(array, jnp.bitwise_xor(own, t) * samples, samples, 0)

    def send(array, t):
        block = cut(array, t)
        return block, swap(block, "blade", 4, t)

    sent, x3 = send(inputs, 3)
    rest = after(inputs, sent)
    sent, x1 = send(rest, 1)
    rest = after(rest, sent)
    _, x2 = send(rest, 2)

    matches = sample_index[:, None] == jnp.arange(NTAB, dtype=jnp.int32)[None, :]
    normalizer = jnp.sum(jnp.where(matches, norm_table[None, :], 0.0), axis=1)
    inv_all = 1.0 / normalizer
    inv = lax.dynamic_slice_in_dim(inv_all, own * samples, samples, 0)

    small = lax.optimization_barrier(small_tables())
    turned = turned_table(small)
    packed = pack_weights(spec_weight, lin_weight)
    packs = [packed] + [swap(packed, "blade", 4, t) for t in (1, 2, 3)]

    x3 = after(x3, (packed, turned))
    sent = forward_spectrum(ids, inv, (inputs, x3), small, shards)
    x1, x2 = after((x1, x2), sent)
    xa = to_modes(sent)
    blocks = after([cut(cotangent, t) for t in (1, 2, 3)], (x1, x2))
    cot = (cotangent,) + tuple(swap(blocks[t - 1], "blade", 4, t) for t in (1, 2, 3))
    xb = to_modes(forward_spectrum(ids, inv, (x1, x2), small, shards))
    pq, lt, lb = unpack(ids, packs, True)
    y = to_modes(mix(ids, xa, xb, pq, samples))

    x = (inputs, x1, x2, x3)
    result = pixels(ids, inv, x, y, turned, lt, pq)
    output, slope, pq = result[0], result[4], result[5]
    last, cot = lax.optimization_barrier((result[3], cot))
    parts = (result[1], result[2], last)
    out_parts = [swap(parts[t - 1], "blade", 4, t) for t in (1, 2, 3)]

    grad_pre, sent, lin, pq = pixel_grads(ids, inv, x, cot, slope, small, y.shape, pq)
    xt = turn_modes(after(xa, lin), xb, samples)
    pq = turn_blocks(pq)
    g = after(to_modes(sent), (out_parts[2], xt, pq))
    mixed = mix_back(ids, g, pq)
    back = to_modes(mixed)
    spec_grads = weight_grads(ids, xt, g, lin)
    spec_grads = [spec_grads[0]] + [swap(spec_grads[t], "blade", 4, t) for t in (1, 2, 3)]

    inner = inner_grads(ids, inv, back, grad_pre, small, lb, cotangent)
    inner = after(inner, out_parts)
    grad_parts = [swap(inner[t], "blade", 4, t) for t in (1, 2, 3)]

    output = place_output(ids, out_parts, output)
    spec_grads = after(spec_grads, output)
    flips = jnp.stack(
        [jnp.where(own % 2 == 1, flip_of(jnp.bitwise_xor(own, t), 1), 1.0) for t in range(4)]
    )
    lin_grad = 0.0
    first = spec_weight.shape[1] * LANES
    for t in range(4):
        lin_grad = lin_grad + spec_grads[t][:, first : first + C].astype(F32) * flips[t]
    step = 1
    while step < shards:
        lin_grad = lin_grad + swap(lin_grad, "dp", shards, step)
        step *= 2

    spec_out = adam_spec(flips, spec_grads, spec_weight, spec_first, spec_second)
    lin_out = adamw(lin_weight, lin_first, lin_second, lin_grad[None])
    input_grad = final_grads(ids, inv_all, cotangent, grad_parts[2:], (3,), inner[0])
    input_grad = final_grads(ids, inv_all, cotangent, grad_parts[:2], (1, 2), input_grad)
    return (output, input_grad, *spec_out, *lin_out)


def solution(mesh):
    fields = P("dp", "blade", None, None)
    spec = P("blade", "dp", None, None, None)
    lin = P("blade", None, None)
    return jax.shard_map(
        partial(body, mesh.shape["dp"]),
        mesh=mesh,
        in_specs=(fields, fields, P(), P("dp"), spec, spec, spec, lin, lin, lin),
        out_specs=(fields, fields, spec, spec, spec, lin, lin, lin),
        check_vma=False,
    )
```

```python
from functools import partial
import math

import jax
import jax.numpy as jnp
from jax import lax
from jax.experimental import pallas as pl
from jax.experimental.pallas import tpu as pltpu
from jax.sharding import PartitionSpec as P

GRID = 64
MSIDE = 16
NTAB = 16
STEP_COUNT = 5
NPIX = 4096
MODES = 256
C = 48
LANES = 2 * C
QUAD = 4
PACK = 128

BETA_ONE = 0.9
BETA_TWO = 0.999
EPSILON = 1e-08
RATE = 0.1
DECAY = 0.01

F32 = jnp.float32
BF16 = jnp.bfloat16
SMEM = pltpu.MemorySpace.SMEM


def sgn(left, right):
    return -1.0 if (left & 2) and (right & 1) else 1.0


def flip_of(own, k):
    if k & 1:
        return (1 - 2 * ((own // 2) % 2)).astype(F32)
    return jnp.float32(1.0)


def mode_factor(mode):
    return jnp.where(mode % MSIDE == 0, 1.0, 2.0).astype(F32)


def dot(left, right, dims=((1,), (0,))):
    return lax.dot_general(left, right, (dims, ((), ())), preferred_element_type=F32)


def whole(shape):
    zeros = (0,) * len(shape)
    return pl.BlockSpec(tuple(shape), lambda *_: zeros)


def params(mib):
    return pltpu.CompilerParams(vmem_limit_bytes=mib * 1024 * 1024)


def fast(shape, kind):
    return pltpu.VMEM(tuple(shape), kind)


def slow(shape, kind):
    return pltpu.HBM(tuple(shape), kind)


def pin(*arrays):
    return [pltpu.with_memory_space_constraint(array, pltpu.VMEM) for array in arrays]


def stay(*arrays):
    return [pltpu.with_memory_space_constraint(array, pltpu.HBM) for array in arrays]


def in_vmem(count):
    return [pl.BlockSpec(memory_space=pltpu.MemorySpace.VMEM)] * count


def cost():
    return pl.CostEstimate(flops=1, bytes_accessed=1, transcendentals=0)


def small_tables():
    mode_ids = jnp.arange(2 * MODES, dtype=jnp.int32)
    imag = mode_ids >= MODES
    mode_ids = mode_ids % MODES
    row_index = mode_ids // MSIDE
    col_freq = mode_ids % MSIDE
    row_freq = jnp.where(row_index < MSIDE // 2, row_index, GRID - MSIDE + row_index)
    place = jnp.arange(GRID, dtype=jnp.int32)[:, None]
    row_angle = ((place * row_freq[None, :]) % GRID).astype(F32) * (2.0 * math.pi / GRID)
    col_angle = ((place * col_freq[None, :]) % GRID).astype(F32) * (2.0 * math.pi / GRID)
    row_cos, row_sin = jnp.cos(row_angle) / GRID, jnp.sin(row_angle) / GRID
    first = jnp.where(imag[None, :], -row_sin, row_cos)
    second = jnp.where(imag[None, :], -row_cos, -row_sin)
    return jnp.stack([first, second, jnp.cos(col_angle), jnp.sin(col_angle)])


def table_rows(row_ref, col_ref, start, stop):
    tiles = []
    for h in range(start, stop):
        tile = row_ref[0, h : h + 1] * col_ref[0] + row_ref[1, h : h + 1] * col_ref[1]
        tiles.append(tile.astype(BF16))
    return jnp.concatenate(tiles, axis=0)


def small_specs(tile):
    n = 2 * MODES
    return [
        pl.BlockSpec((2, tile // GRID, n), lambda i, *_: (0, i, 0)),
        pl.BlockSpec((2, GRID, n), lambda i, *_: (1, 0, 0)),
    ]


def turned_kernel(row_ref, col_ref, ft_ref):
    for h in range(0, row_ref.shape[1], 2):
        tile = table_rows(row_ref, col_ref, h, h + 2)
        ft_ref[:, h * GRID : (h + 2) * GRID] = tile.astype(F32).T.astype(BF16)


def turned_table(small):
    rows = 8
    n = 2 * MODES
    return pl.pallas_call(
        turned_kernel,
        grid=(GRID // rows,),
        in_specs=small_specs(rows * GRID),
        out_specs=pl.BlockSpec((n, rows * GRID), lambda i: (0, i)),
        out_shape=slow((n, NPIX), BF16),
        compiler_params=params(28),
        cost_estimate=cost(),
        name="turned",
    )(*stay(small, small))


def pack_kernel(w_ref, l_ref, o_ref):
    def step(g, carry):
        parts = [w_ref[0, g * QUAD + q, r] for q in range(QUAD) for r in range(2)]
        at = pl.ds(pl.multiple_of(g * QUAD * LANES, PACK), QUAD * LANES)
        o_ref[:, at] = jnp.concatenate(parts, axis=1).astype(BF16)
        return carry

    modes = w_ref.shape[1]
    lax.fori_loop(0, modes // QUAD, step, 0)
    line = jnp.concatenate([l_ref[0], jnp.zeros((C, PACK - C), F32)], axis=1)
    o_ref[:, modes * LANES :] = line.astype(BF16)


def pack_weights(spec_weight, lin_weight):
    modes = spec_weight.shape[1]
    return pl.pallas_call(
        pack_kernel,
        in_specs=in_vmem(2),
        out_specs=in_vmem(1)[0],
        out_shape=jax.ShapeDtypeStruct((C, modes * LANES + PACK), BF16),
        compiler_params=params(28),
        cost_estimate=cost(),
        name="pack",
    )(spec_weight, lin_weight)


def lanes_of(shape):
    return lax.broadcasted_iota(jnp.int32, shape, len(shape) - 1)


def split_lanes(a, b, c):
    lane = lanes_of(a.shape)
    second = jnp.where(lane < 32, pltpu.roll(a, 32, 1), pltpu.roll(b, 32, 1))
    third = jnp.where(lane < 64, pltpu.roll(b, 64, 1), pltpu.roll(c, 64, 1))
    return a, second, third, pltpu.roll(c, 96, 1)


def join_lanes(first, second, third, fourth):
    lane = lanes_of(first.shape)
    a = jnp.where(lane < 96, first, pltpu.roll(second, 96, 1))
    b = jnp.where(lane < 64, pltpu.roll(second, 96, 1), pltpu.roll(third, 64, 1))
    c = jnp.where(lane < 32, pltpu.roll(third, 64, 1), pltpu.roll(fourth, 32, 1))
    return a, b, c


def quad_tiles(ref, g):
    tiles = []
    for n in range(3):
        at = pl.ds(pl.multiple_of(g * QUAD * LANES + n * PACK, PACK), PACK)
        tiles.append(ref[:, at].astype(F32))
    return tiles


def unpack_kernel(ids_ref, w0, w1, w2, w3, pq_ref, *lines):
    own = ids_ref[0]
    modes = pq_ref.shape[0]
    lane = lanes_of((C, PACK))
    flip = flip_of(own, 1)

    def step(g, carry):
        for t, w in enumerate((w0, w1, w2, w3)):
            slot = jnp.bitwise_xor(own, t)
            scale = jnp.where(slot % 2 == 1, flip, 1.0)
            at = pl.ds(pl.multiple_of(slot * PACK, PACK), PACK)
            tiles = [tile * scale for tile in quad_tiles(w, g)]
            for q, p in enumerate(split_lanes(*tiles)):
                p = jnp.where(lane < LANES, p, 0.0)
                low = jnp.where(lane < C, -pltpu.roll(p, PACK - C, 1), pltpu.roll(p, C, 1))
                low = jnp.where(lane < LANES, low, 0.0)
                pq_ref[g * QUAD + q, :C, at] = p.astype(BF16)
                pq_ref[g * QUAD + q, C:, at] = low.astype(BF16)
        return carry

    quads = modes // QUAD
    lax.fori_loop(0, quads, step, 0, unroll=min(4, quads))
    if not lines:
        return
    lt_ref, lb_ref, lsc = lines
    for t, w in enumerate((w0, w1, w2, w3)):
        slot = jnp.bitwise_xor(own, t)
        lsc[slot] = w[:, modes * LANES :].astype(F32) * jnp.where(slot % 2 == 1, flip, 1.0)
    for k in range(4):
        line = lsc[k]
        turned = line.T
        for t in range(4):
            u = t ^ k
            lb_ref[t * C : (t + 1) * C, u * C : (u + 1) * C] = (line[:, :C] * sgn(t, k)).astype(BF16)
            lt_ref[u * C : (u + 1) * C, t * C : (t + 1) * C] = (turned[:C] * sgn(t, k)).astype(BF16)


def unpack(ids, packs, lines):
    modes = (packs[0].shape[1] - PACK) // LANES
    weights = fast((modes, LANES, 4 * PACK), BF16)
    shape = (4 * C, 4 * C)
    result = pl.pallas_call(
        unpack_kernel,
        in_specs=[pl.BlockSpec(memory_space=SMEM)] + in_vmem(4),
        out_specs=in_vmem(3 if lines else 1),
        out_shape=[weights] + ([slow(shape, BF16)] * 2 if lines else []),
        scratch_shapes=[pltpu.VMEM((4, C, PACK), F32)] if lines else [],
        compiler_params=params(28),
        cost_estimate=cost(),
        name="unpack",
    )(*stay(ids, *packs))
    return result if lines else result[0]


def spread(acc, out_ref, scales=None):
    rows = []
    for n in range(acc.shape[0] // C):
        for r in range(2):
            row = acc[n * C : (n + 1) * C, r * MODES : (r + 1) * MODES]
            rows.append(row if scales is None else row * scales[n])
    extra = out_ref.shape[2] - len(rows) * C
    if extra:
        rows.append(jnp.zeros((extra, MODES), F32))
    turned = jnp.concatenate(rows, axis=0).T
    out_ref[...] = turned.reshape(out_ref.shape).astype(BF16)


def collect(block, ysc):
    turned = block[...].astype(F32).reshape(MODES, block.shape[2]).T
    for n in range(ysc.shape[0] // C):
        for r in range(2):
            row = (n * 2 + r) * C
            piece = turned[row : row + C].astype(BF16)
            ysc[n * C : (n + 1) * C, r * MODES : (r + 1) * MODES] = piece


def forward_kernel(ids_ref, inv_ref, *refs):
    x = refs[:-4]
    row_ref, col_ref, out_ref, acc = refs[-4:]
    i = pl.program_id(0)
    samples = x[0].shape[0]
    rows = [part[s, 0] for s in range(samples) for part in x]
    table = table_rows(row_ref, col_ref, 0, row_ref.shape[1])
    part = dot(jnp.concatenate(rows, axis=0), table)

    @pl.when(i == 0)
    def _():
        acc[...] = part

    @pl.when(i > 0)
    def _():
        acc[...] += part

    @pl.when(i == pl.num_programs(0) - 1)
    def _():
        spread(acc, out_ref, [inv_ref[s] for s in range(samples) for _ in x])


def forward_spectrum(ids, inv, x, small, shards):
    samples = inv.shape[0]
    modes = MODES // shards
    width = -(-samples * len(x) * LANES // PACK) * PACK
    n = 2 * MODES
    tile = 2048

    def spec(array):
        if array.shape[0] == samples:
            return pl.BlockSpec((samples, 1, C, tile), lambda i, ids, inv: (0, 0, 0, i))
        return pl.BlockSpec((samples, 1, C, tile), lambda i, ids, inv: (ids[0], 0, 0, i))

    return pl.pallas_call(
        forward_kernel,
        grid_spec=pltpu.PrefetchScalarGridSpec(
            num_scalar_prefetch=2,
            grid=(NPIX // tile,),
            in_specs=[spec(part) for part in x] + small_specs(tile),
            out_specs=whole((shards, modes, width)),
            scratch_shapes=[pltpu.VMEM((samples * len(x) * C, n), F32)],
        ),
        out_shape=slow((shards, modes, width), BF16),
        compiler_params=params(28),
        cost_estimate=cost(),
        name="forward",
    )(*stay(ids, inv, *x, small, small))


def row_scratch(modes, shards, width):
    return pltpu.VMEM((width // PACK, modes * shards, PACK), F32)


def gather_rows(blocks, sc):
    shards, modes = blocks[0].shape[:2]
    first = 0
    for block in blocks:
        for n in range(block.shape[2] // PACK):
            for x in range(shards):
                rows = block[x, :, n * PACK : (n + 1) * PACK].astype(F32)
                sc[first + n, pl.ds(x, modes, stride=shards), :] = rows
        first += block.shape[2] // PACK


def scatter_rows(ysc, out):
    shards, modes = out.shape[:2]
    for x in range(shards):
        for n in range(ysc.shape[0]):
            piece = ysc[n, pl.ds(x, modes, stride=shards), :]
            out[x, :, n * PACK : (n + 1) * PACK] = piece.astype(BF16)


def blade_rows(sc, mode, shards, groups):
    at = pl.ds(pl.multiple_of(mode * shards, shards), shards)
    found = [[] for _ in range(4)]
    for tile, pairs in groups:
        tiles = [sc[tile + n, at, :] for n in range(-(-len(pairs) * LANES // PACK))]
        pieces = split_lanes(tiles[0], tiles[min(1, len(tiles) - 1)], tiles[-1])
        for piece, (_, t) in zip(pieces, pairs):
            found[t].append(piece)
    return [jnp.concatenate(found[t], axis=0) for t in range(4)]


def groups_of(samples, *blades):
    groups = []
    tile = 0
    for some in blades:
        pairs = [(s, t) for s in range(samples) for t in some]
        for n in range(0, len(pairs), 4):
            part = pairs[n : n + 4]
            groups.append((tile, part))
            tile += -(-len(part) * LANES // PACK)
    return groups


EARLY = (0, 3)
LATE = (1, 2)


def mix_modes(xsc, ysc, pq_ref, groups, shards, first_mode, back):
    modes = xsc.shape[1] // shards
    samples = ysc.shape[0] // 3
    group = samples * shards

    def step(m, carry):
        low = jnp.concatenate(blade_rows(xsc, m, shards, groups), axis=0)
        low = low[:, :LANES].astype(BF16)
        total = [None] * 4
        parts = dot(low, pq_ref[m])
        for k in range(4):
            part = parts[:, k * PACK : (k + 1) * PACK]
            for t in range(4):
                u = t ^ k
                piece = part[t * group : (t + 1) * group]
                sign = sgn(u, k) if back else sgn(t, k)
                if total[u] is None:
                    total[u] = piece if sign > 0 else -piece
                else:
                    total[u] = total[u] + piece if sign > 0 else total[u] - piece
        factor = mode_factor(first_mode + m)
        at = pl.ds(pl.multiple_of(m * shards, shards), shards)
        for s in range(samples):
            rows = []
            for u in range(4):
                rows.append(total[u][s * shards : (s + 1) * shards] * factor)
            for n, tile in enumerate(join_lanes(*rows)):
                ysc[s * 3 + n, at, :] = tile
        return carry

    lax.fori_loop(0, modes, step, 0, unroll=min(32, modes))


def mix_kernel(ids_ref, xa, xb, pq_ref, y_ref, xsc, ysc):
    shards, modes, width = y_ref.shape
    gather_rows((xa, xb), xsc)
    groups = groups_of(width // (4 * LANES), EARLY, LATE)
    mix_modes(xsc, ysc, pq_ref, groups, shards, ids_ref[1] * modes, False)
    scatter_rows(ysc, y_ref)


def mix(ids, xa, xb, pq, samples):
    shards, modes = xa.shape[:2]
    width = samples * 4 * LANES
    return pl.pallas_call(
        mix_kernel,
        in_specs=[pl.BlockSpec(memory_space=SMEM)] + in_vmem(3),
        out_specs=in_vmem(1)[0],
        out_shape=slow((shards, modes, width), BF16),
        scratch_shapes=[
            row_scratch(modes, shards, xa.shape[2] + xb.shape[2]),
            row_scratch(modes, shards, width),
        ],
        compiler_params=params(28),
        cost_estimate=cost(),
        name="mix",
    )(*stay(ids, xa, xb), *pin(pq))


def mix_back_kernel(ids_ref, g_ref, pq_ref, out_ref, gsc, ysc):
    shards, modes, width = g_ref.shape
    gather_rows((g_ref,), gsc)
    groups = groups_of(width // (4 * LANES), range(4))
    mix_modes(gsc, ysc, pq_ref, groups, shards, ids_ref[1] * modes, True)
    scatter_rows(ysc, out_ref)


def mix_back(ids, g, pq):
    shards, modes, width = g.shape
    return pl.pallas_call(
        mix_back_kernel,
        in_specs=[pl.BlockSpec(memory_space=SMEM)] + in_vmem(2),
        out_specs=in_vmem(1)[0],
        out_shape=slow(g.shape, BF16),
        scratch_shapes=[row_scratch(modes, shards, width)] * 2,
        compiler_params=params(28),
        cost_estimate=cost(),
        name="mix_back",
    )(*stay(ids), g, *pin(pq))


def turn_kernel(pq_ref, xa, xb, out_ref, xt_ref, held, xsc):
    shards, modes = xa.shape[:2]
    samples = xt_ref.shape[2] // (8 * shards)
    groups = groups_of(samples, EARLY, LATE)
    shape = (LANES, LANES)
    diagonal = lax.broadcasted_iota(jnp.int32, shape, 0) == lax.broadcasted_iota(jnp.int32, shape, 1)
    unit = jnp.where(diagonal, 1.0, 0.0).astype(BF16)
    gather_rows((xa, xb), xsc)

    def step(m, carry):
        for k in range(4):
            at = slice(k * PACK, k * PACK + LANES)
            held[m, :, at] = dot(unit, pq_ref[m, :, at], ((1,), (1,))).astype(BF16)
        x = blade_rows(xsc, m, shards, groups)
        x = x + [pltpu.roll(rows, PACK - C, 1) for rows in x]
        xt_ref[m] = jnp.concatenate(x, axis=0).T[:C].astype(BF16)
        return carry

    lax.fori_loop(0, modes, step, 0, unroll=min(16, modes))
    out_ref[...] = held[...]


def turn(pq, xa, xb, samples):
    shards, modes = xa.shape[:2]
    return pl.pallas_call(
        turn_kernel,
        in_specs=in_vmem(3),
        out_specs=in_vmem(2),
        out_shape=[fast(pq.shape, BF16), slow((modes, C, 8 * samples * shards), BF16)],
        input_output_aliases={0: 0},
        scratch_shapes=[
            pltpu.VMEM(pq.shape, BF16),
            row_scratch(modes, shards, xa.shape[2] + xb.shape[2]),
        ],
        compiler_params=params(28),
        cost_estimate=cost(),
        name="turn",
    )(*pin(pq), *stay(xa, xb))


def grad_kernel(ids_ref, xt_ref, g_ref, lin_ref, o0, o1, o2, o3, gsc, osc):
    shards, modes, width = g_ref.shape
    samples = width // (4 * LANES)
    own = ids_ref[0]
    first_mode = ids_ref[1] * modes
    groups = groups_of(samples, range(4))
    gather_rows((g_ref,), gsc)
    lane = lanes_of((samples * shards, PACK))

    def step(g, carry):
        found = [[] for _ in range(4)]
        for q in range(QUAD):
            m = g * QUAD + q
            factor = mode_factor(first_mode + m)
            plain = [rows * factor for rows in blade_rows(gsc, m, shards, groups)]
            turned = [
                jnp.where(lane < C, pltpu.roll(rows, PACK - C, 1), -pltpu.roll(rows, C, 1))
                for rows in plain
            ]
            plus = [rows.astype(BF16) for rows in plain + turned]
            minus = [(-rows).astype(BF16) for rows in plain + turned]
            right = []
            for k in range(4):
                rows = []
                for r in range(2):
                    for t in range(4):
                        rows.append((plus if sgn(t, k) > 0 else minus)[4 * r + (t ^ k)])
                right.append(jnp.concatenate(rows, axis=0))
            grad = dot(xt_ref[m], jnp.concatenate(right, axis=1))
            for k in range(4):
                found[k].append(grad[:, k * PACK : (k + 1) * PACK])
        for k in range(4):
            for n, tile in enumerate(join_lanes(*found[k])):
                at = pl.ds(pl.multiple_of(g * QUAD * LANES + n * PACK, PACK), PACK)
                osc[k, :, at] = tile.astype(BF16)
        return carry

    quads = modes // QUAD
    lax.fori_loop(0, quads, step, 0, unroll=min(2, quads))
    for k in range(4):
        line = jnp.concatenate([lin_ref[k], jnp.zeros((C, PACK - C), F32)], axis=1)
        osc[k, :, modes * LANES :] = line.astype(BF16)
    for t, out in enumerate((o0, o1, o2, o3)):
        out[...] = osc[jnp.bitwise_xor(own, t)]


def weight_grads(ids, xt, g, lin):
    shards, modes, width = g.shape
    shape = (C, modes * LANES + PACK)
    return pl.pallas_call(
        grad_kernel,
        in_specs=[pl.BlockSpec(memory_space=SMEM)] + in_vmem(3),
        out_specs=in_vmem(4),
        out_shape=[slow(shape, BF16)] * 4,
        scratch_shapes=[row_scratch(modes, shards, width), pltpu.VMEM((4,) + shape, BF16)],
        compiler_params=params(28),
        cost_estimate=cost(),
        name="weight_grads",
    )(*stay(ids, xt), g, *stay(lin))


CDF_AT = 0.28
CDF = (0.11652094, 0.06749571, 0.2689128, -0.23699677, 0.38987606, -0.10580875)
SERIES = [value / CDF_AT ** (i + 1) for i, value in enumerate(CDF)]


def gelu_parts(v):
    z = jnp.abs(v)
    t = 1.0 / (z + 1.0 / CDF_AT)
    bell = jnp.exp2(v * v * (-0.5 * math.log2(math.e)))
    series = jnp.float32(SERIES[-1])
    for value in SERIES[-2::-1]:
        series = series * t + value
    tail = series * t * bell
    cdf = jnp.where(v < 0.0, tail, 1.0 - tail)
    return v * cdf, cdf + v * (bell * (1.0 / math.sqrt(2.0 * math.pi)))


def pixel_kernel(ids_ref, inv_ref, *refs):
    x = refs[:4]
    y_ref, ft_ref, lt_ref = refs[4:7]
    outs = refs[8:12]
    slope_ref = refs[12]
    left, ysc, even, odd = refs[14:]
    samples = x[1].shape[0]
    rows = 4 * C
    n = 2 * MODES
    width = even.shape[1]

    @pl.when(pl.program_id(0) == 0)
    def _():
        collect(y_ref, ysc)
        for s in range(samples):
            left[s, :, :n] = ysc[s * rows : (s + 1) * rows]
            left[s, :, n:] = (lt_ref[...].astype(F32) * inv_ref[s]).astype(BF16)

    def product(s, at, pre):
        fields = [x[t][s, 0, :, at] for t in range(4)]
        pre[...] = dot(left[s], jnp.concatenate([ft_ref[:, at]] + fields, axis=0))

    def activate(s, at, pre):
        for t in range(4):
            value, slope = gelu_parts(pre[t * C : (t + 1) * C])
            normed = x[t][s, 0, :, at].astype(F32) * inv_ref[s]
            outs[t][s, 0, :, at] = (normed + value).astype(BF16)
            row = s * rows + t * C
            slope_ref[row : row + C, at] = slope.astype(BF16)

    tile = ft_ref.shape[1]
    blocks = [(s, slice(k, k + width)) for k in range(0, tile, width) for s in range(samples)]
    buffers = [even, odd]
    product(*blocks[0], buffers[0])
    for k, block in enumerate(blocks):
        if k + 1 < len(blocks):
            product(*blocks[k + 1], buffers[(k + 1) % 2])
        activate(*block, buffers[k % 2])


def pixels(ids, inv, x, y, turned, lt, pq):
    samples = inv.shape[0]
    n = 2 * MODES
    tile = 1024
    mine = pl.BlockSpec((samples, 1, C, tile), lambda i, ids, inv: (ids[0], 0, 0, i))
    block = pl.BlockSpec((samples, 1, C, tile), lambda i, ids, inv: (0, 0, 0, i))
    rows = samples * 4 * C
    flat = pl.BlockSpec((rows, tile), lambda i, ids, inv: (0, i))
    return pl.pallas_call(
        pixel_kernel,
        grid_spec=pltpu.PrefetchScalarGridSpec(
            num_scalar_prefetch=2,
            grid=(NPIX // tile,),
            in_specs=[mine]
            + [block] * 3
            + [
                whole(y.shape),
                pl.BlockSpec((n, tile), lambda i, ids, inv: (0, i)),
                whole((4 * C, 4 * C)),
                pl.BlockSpec(memory_space=pl.ANY),
            ],
            out_specs=[mine] + [block] * 3 + [flat, pl.BlockSpec(memory_space=pl.ANY)],
            scratch_shapes=[
                pltpu.VMEM((samples, 4 * C, n + 4 * C), BF16),
                pltpu.VMEM((rows, n), BF16),
                pltpu.VMEM((4 * C, 256), F32),
                pltpu.VMEM((4 * C, 256), F32),
            ],
        ),
        out_shape=[slow(x[0].shape, BF16)]
        + [slow((samples, 1, C, NPIX), BF16)] * 3
        + [fast((rows, NPIX), BF16), fast(pq.shape, BF16)],
        input_output_aliases={9: 5},
        compiler_params=params(28),
        cost_estimate=cost(),
        name="pixels",
    )(*stay(ids, inv, *x), y, *stay(turned, lt), *pin(pq))


def slope_kernel(ids_ref, *refs):
    cot = refs[:4]
    slope, row_ref, col_ref, _, g_ref, g_out, _, gacc = refs[4:]
    samples = cot[1].shape[0]
    rows = 4 * C
    i = pl.program_id(0)

    @pl.when(i == 0)
    def _():
        gacc[...] = jnp.zeros_like(gacc)

    for s in range(samples):
        for t in range(4):
            at = s * rows + t * C
            grad = cot[t][s, 0].astype(F32) * slope[at : at + C].astype(F32)
            g_ref[at : at + C] = grad.astype(BF16)
    table = table_rows(row_ref, col_ref, 0, row_ref.shape[1])
    gacc[...] += dot(g_ref[...], table)

    @pl.when(i == pl.num_programs(0) - 1)
    def _():
        spread(gacc, g_out)


def pixel_grads(ids, cot, slope, small, spectrum, pq):
    rows = slope.shape[0]
    samples = rows // (4 * C)
    n = 2 * MODES
    tile = 2048
    mine = pl.BlockSpec((samples, 1, C, tile), lambda i, ids: (ids[0], 0, 0, i))
    block = pl.BlockSpec((samples, 1, C, tile), lambda i, ids: (0, 0, 0, i))
    flat = pl.BlockSpec((rows, tile), lambda i, ids: (0, i))
    kept = pl.BlockSpec(memory_space=pl.ANY)
    return pl.pallas_call(
        slope_kernel,
        grid_spec=pltpu.PrefetchScalarGridSpec(
            num_scalar_prefetch=1,
            grid=(NPIX // tile,),
            in_specs=[mine] + [block] * 3 + [flat] + small_specs(tile) + [kept],
            out_specs=[flat, whole(spectrum), kept],
            scratch_shapes=[pltpu.VMEM((rows, n), F32)],
        ),
        out_shape=[slow((rows, NPIX), BF16), slow(spectrum, BF16), fast(pq.shape, BF16)],
        input_output_aliases={8: 2},
        compiler_params=params(28),
        cost_estimate=cost(),
        name="pixel_grads",
    )(*stay(ids, *cot), *pin(slope), *stay(small, small), *pin(pq))


def lin_kernel(ids_ref, inv_ref, *refs):
    x = refs[:4]
    g_ref, lin_ref, lacc = refs[4:]
    samples = x[1].shape[0]
    rows = 4 * C

    @pl.when(pl.program_id(0) == 0)
    def _():
        lacc[...] = jnp.zeros_like(lacc)

    for s in range(samples):
        fields = jnp.concatenate([x[t][s, 0] for t in range(4)], axis=0)
        g = g_ref[s * rows : (s + 1) * rows]
        lacc[...] += dot(fields, g, ((1,), (1,))) * inv_ref[s]

    @pl.when(pl.program_id(0) == pl.num_programs(0) - 1)
    def _():
        for k in range(4):
            total = None
            for t in range(4):
                u = t ^ k
                piece = lacc[t * C : (t + 1) * C, u * C : (u + 1) * C] * sgn(t, k)
                total = piece if total is None else total + piece
            lin_ref[k] = total


def lin_grads(ids, inv, x, g):
    rows = g.shape[0]
    samples = rows // (4 * C)
    tile = 2048
    mine = pl.BlockSpec((samples, 1, C, tile), lambda i, ids, inv: (ids[0], 0, 0, i))
    block = pl.BlockSpec((samples, 1, C, tile), lambda i, ids, inv: (0, 0, 0, i))
    flat = pl.BlockSpec((rows, tile), lambda i, ids, inv: (0, i))
    return pl.pallas_call(
        lin_kernel,
        grid_spec=pltpu.PrefetchScalarGridSpec(
            num_scalar_prefetch=2,
            grid=(NPIX // tile,),
            in_specs=[mine] + [block] * 3 + [flat],
            out_specs=whole((4, C, C)),
            scratch_shapes=[pltpu.VMEM((4 * C, 4 * C), F32)],
        ),
        out_shape=slow((4, C, C), F32),
        compiler_params=params(28),
        cost_estimate=cost(),
        name="lin_grads",
    )(*stay(ids, inv, *x, g))


def inner_kernel(ids_ref, inv_ref, y_ref, g_ref, row_ref, col_ref, lb_ref, cot_ref, mine_ref, *refs):
    o1, o2, o3, ysc = refs
    samples = cot_ref.shape[0]
    rows = 4 * C

    @pl.when(pl.program_id(0) == 0)
    def _():
        collect(y_ref, ysc)

    table = table_rows(row_ref, col_ref, 0, row_ref.shape[1])
    spatial = dot(ysc[...], table, ((1,), (1,)))
    for s in range(samples):
        at = slice(s * rows, (s + 1) * rows)
        total = spatial[at] + dot(lb_ref[...], g_ref[at])
        mine_ref[s, 0] = (cot_ref[s, 0].astype(F32) + total[:C]) * inv_ref[s]
        for t, out in ((1, o1), (2, o2), (3, o3)):
            out[s, 0] = total[t * C : (t + 1) * C].astype(BF16)


def inner_grads(ids, inv, y, g, small, lb, cotangent):
    samples = inv.shape[0]
    n = 2 * MODES
    tile = 2048
    rows = samples * 4 * C
    mine = pl.BlockSpec((samples, 1, C, tile), lambda i, ids, inv: (ids[0], 0, 0, i))
    block = pl.BlockSpec((samples, 1, C, tile), lambda i, ids, inv: (0, 0, 0, i))
    return pl.pallas_call(
        inner_kernel,
        grid_spec=pltpu.PrefetchScalarGridSpec(
            num_scalar_prefetch=2,
            grid=(NPIX // tile,),
            in_specs=[
                whole(y.shape),
                pl.BlockSpec((rows, tile), lambda i, ids, inv: (0, i)),
                *small_specs(tile),
                whole((4 * C, 4 * C)),
                mine,
            ],
            out_specs=[mine] + [block] * 3,
            scratch_shapes=[pltpu.VMEM((rows, n), BF16)],
        ),
        out_shape=[slow(cotangent.shape, F32)] + [slow((samples, 1, C, NPIX), BF16)] * 3,
        compiler_params=params(28),
        cost_estimate=cost(),
        name="inner_grads",
    )(*stay(ids, inv), y, *stay(g, small, small, lb, cotangent))


def place_kernel(ids_ref, a_ref, b_ref, c_ref, old_ref, out_ref):
    for n, part in enumerate((a_ref, b_ref, c_ref)):

        @pl.when(pl.program_id(0) == n)
        def _():
            out_ref[...] = part[...]


def place_output(ids, parts, result):
    samples = parts[0].shape[0]
    shape = (1, 1, C, NPIX)

    def spec(n):
        def at(j, s, ids):
            return (jnp.where(j == n, s, jnp.where(j < n, 0, samples - 1)), 0, 0, 0)

        return pl.BlockSpec(shape, at)

    return pl.pallas_call(
        place_kernel,
        grid_spec=pltpu.PrefetchScalarGridSpec(
            num_scalar_prefetch=1,
            grid=(3, samples),
            in_specs=[spec(0), spec(1), spec(2), pl.BlockSpec(memory_space=pl.ANY)],
            out_specs=pl.BlockSpec(
                shape, lambda j, s, ids: (jnp.bitwise_xor(ids[0], j + 1) * samples + s, 0, 0, 0)
            ),
        ),
        out_shape=jax.ShapeDtypeStruct(result.shape, BF16),
        input_output_aliases={4: 0},
        compiler_params=params(28),
        cost_estimate=cost(),
        name="place",
    )(ids, *parts, result)


def final_kernel(count, codes, ids_ref, inv_ref, cot_ref, *refs):
    samples = pl.num_programs(1)
    j = pl.program_id(0)
    for n in range(count):

        @pl.when(j == n)
        def _():
            inv = inv_ref[jnp.bitwise_xor(ids_ref[0], codes[n]) * samples + pl.program_id(1)]
            refs[-1][...] = (cot_ref[...].astype(F32) + refs[n][...].astype(F32)) * inv


def final_grads(ids, inv, cotangent, parts, codes, result):
    samples = parts[0].shape[0]
    count = len(parts)
    shape = (1, 1, C, NPIX)

    def code(j):
        value = codes[0]
        for n in range(1, count):
            value = jnp.where(j == n, codes[n], value)
        return value

    def spec(n):
        def at(j, s, ids, inv):
            return (jnp.where(j == n, s, jnp.where(j < n, 0, samples - 1)), 0, 0, 0)

        return pl.BlockSpec(shape, at)

    place = pl.BlockSpec(
        shape, lambda j, s, ids, inv: (jnp.bitwise_xor(ids[0], code(j)) * samples + s, 0, 0, 0)
    )
    return pl.pallas_call(
        partial(final_kernel, count, codes),
        grid_spec=pltpu.PrefetchScalarGridSpec(
            num_scalar_prefetch=2,
            grid=(count, samples),
            in_specs=[place]
            + [spec(n) for n in range(count)]
            + [pl.BlockSpec(memory_space=pl.ANY)],
            out_specs=place,
        ),
        out_shape=jax.ShapeDtypeStruct(cotangent.shape, F32),
        input_output_aliases={3 + count: 0},
        compiler_params=params(28),
        cost_estimate=cost(),
        name="final",
    )(ids, inv, cotangent, *parts, result)


def adamw(weight, first, second, grad):
    first_new = BETA_ONE * first + (1.0 - BETA_ONE) * grad
    second_new = BETA_TWO * second + (1.0 - BETA_TWO) * grad * grad
    corr_one = 1.0 - BETA_ONE**STEP_COUNT
    corr_two = 1.0 - BETA_TWO**STEP_COUNT
    update = first_new / corr_one / (jnp.sqrt(second_new / corr_two) + EPSILON)
    return (weight - RATE * (update + DECAY * weight), first_new, second_new)


def adam_kernel(flips, d0, d1, d2, d3, w_ref, first_ref, second_ref, w_out, first_out, second_out):
    grad = d0[...].astype(F32) * flips[0]
    for t, d in ((1, d1), (2, d2), (3, d3)):
        grad = grad + d[...].astype(F32) * flips[t]
    for q in range(QUAD):
        for r in range(2):
            lane = q * LANES + r * C
            at = (0, q, r)
            new = adamw(w_ref[at], first_ref[at], second_ref[at], grad[:, lane : lane + C])
            w_out[at], first_out[at], second_out[at] = new


def adam_spec(flips, grads, weight, first, second):
    modes = weight.shape[1]
    packed = pl.BlockSpec((C, QUAD * LANES), lambda g: (0, g))
    block = pl.BlockSpec((1, QUAD, 2, C, C), lambda g: (0, g, 0, 0, 0))
    return pl.pallas_call(
        adam_kernel,
        grid=(modes // QUAD,),
        in_specs=[pl.BlockSpec(memory_space=SMEM)] + [packed] * 4 + [block] * 3,
        out_specs=[block] * 3,
        out_shape=[jax.ShapeDtypeStruct(weight.shape, F32)] * 3,
        compiler_params=params(28),
        cost_estimate=cost(),
        name="adam",
    )(flips, *grads, weight, first, second)


def swap(value, axis, size, x):
    return lax.ppermute(value, axis, [(i, i ^ x) for i in range(size)])


def to_modes(value):
    return lax.all_to_all(value, "dp", split_axis=0, concat_axis=0, tiled=True)


def after(values, first):
    values, _ = lax.optimization_barrier((values, first))
    return values


def body(
    shards,
    inputs,
    cotangent,
    norm_table,
    sample_index,
    spec_weight,
    spec_first,
    spec_second,
    lin_weight,
    lin_first,
    lin_second,
):
    own = lax.axis_index("blade")
    shard = lax.axis_index("dp")
    ids = jnp.stack([own, shard]).astype(jnp.int32)
    samples = inputs.shape[0] // 4

    def cut(array, t):
        return lax.dynamic_slice_in_dim(array, jnp.bitwise_xor(own, t) * samples, samples, 0)

    def send(array, t):
        block = cut(array, t)
        return block, swap(block, "blade", 4, t)

    sent, x3 = send(inputs, 3)
    rest = after(inputs, sent)
    sent, x1 = send(rest, 1)
    rest = after(rest, sent)
    _, x2 = send(rest, 2)

    matches = sample_index[:, None] == jnp.arange(NTAB, dtype=jnp.int32)[None, :]
    normalizer = jnp.sum(jnp.where(matches, norm_table[None, :], 0.0), axis=1)
    inv_all = 1.0 / normalizer
    inv = lax.dynamic_slice_in_dim(inv_all, own * samples, samples, 0)

    small = lax.optimization_barrier(small_tables())
    turned = turned_table(small)
    packed = pack_weights(spec_weight, lin_weight)
    packs = [packed] + [swap(packed, "blade", 4, t) for t in (1, 2, 3)]

    x3 = after(x3, (packed, turned))
    sent = forward_spectrum(ids, inv, (inputs, x3), small, shards)
    x1, x2 = after((x1, x2), sent)
    xa = to_modes(sent)
    blocks = after([cut(cotangent, t) for t in (1, 2, 3)], (x1, x2))
    cot = (cotangent,) + tuple(swap(blocks[t - 1], "blade", 4, t) for t in (1, 2, 3))
    xb = to_modes(forward_spectrum(ids, inv, (x1, x2), small, shards))
    pq, lt, lb = unpack(ids, packs, True)
    y = to_modes(mix(ids, xa, xb, pq, samples))

    x = (inputs, x1, x2, x3)
    result = pixels(ids, inv, x, y, turned, lt, pq)
    output, slope, pq = result[0], result[4], result[5]
    last, cot = lax.optimization_barrier((result[3], cot))
    parts = (result[1], result[2], last)
    out_parts = [swap(parts[t - 1], "blade", 4, t) for t in (1, 2, 3)]

    grad_pre, sent, pq = pixel_grads(ids, cot, slope, small, y.shape, pq)
    lin = lin_grads(ids, inv, x, grad_pre)
    pq, xt = turn(pq, after(xa, sent), xb, samples)
    g = after(to_modes(sent), (out_parts[2], xt, pq, lin))
    mixed = mix_back(ids, g, pq)
    back = to_modes(mixed)
    spec_grads = weight_grads(ids, xt, g, lin)
    spec_grads = [spec_grads[0]] + [swap(spec_grads[t], "blade", 4, t) for t in (1, 2, 3)]

    inner = inner_grads(ids, inv, back, grad_pre, small, lb, cotangent)
    inner = after(inner, out_parts)
    grad_parts = [swap(inner[t], "blade", 4, t) for t in (1, 2, 3)]

    output = place_output(ids, out_parts, output)
    spec_grads = after(spec_grads, output)
    flips = jnp.stack(
        [jnp.where(own % 2 == 1, flip_of(jnp.bitwise_xor(own, t), 1), 1.0) for t in range(4)]
    )
    lin_grad = 0.0
    first = spec_weight.shape[1] * LANES
    for t in range(4):
        lin_grad = lin_grad + spec_grads[t][:, first : first + C].astype(F32) * flips[t]
    step = 1
    while step < shards:
        lin_grad = lin_grad + swap(lin_grad, "dp", shards, step)
        step *= 2

    spec_out = adam_spec(flips, spec_grads, spec_weight, spec_first, spec_second)
    lin_out = adamw(lin_weight, lin_first, lin_second, lin_grad[None])
    input_grad = final_grads(ids, inv_all, cotangent, grad_parts[2:], (3,), inner[0])
    input_grad = final_grads(ids, inv_all, cotangent, grad_parts[:2], (1, 2), input_grad)
    return (output, input_grad, *spec_out, *lin_out)


def solution(mesh):
    fields = P("dp", "blade", None, None)
    spec = P("blade", "dp", None, None, None)
    lin = P("blade", None, None)
    return jax.shard_map(
        partial(body, mesh.shape["dp"]),
        mesh=mesh,
        in_specs=(fields, fields, P(), P("dp"), spec, spec, spec, lin, lin, lin),
        out_specs=(fields, fields, spec, spec, spec, lin, lin, lin),
        check_vma=False,
    )
```

```python
from functools import partial
import math

import jax
import jax.numpy as jnp
from jax import lax
from jax.experimental import pallas as pl
from jax.experimental.pallas import tpu as pltpu
from jax.sharding import PartitionSpec as P

GRID = 64
MSIDE = 16
NTAB = 16
STEP_COUNT = 5
NPIX = 4096
MODES = 256
C = 48
LANES = 2 * C
QUAD = 4
PACK = 128

BETA_ONE = 0.9
BETA_TWO = 0.999
EPSILON = 1e-08
RATE = 0.1
DECAY = 0.01

F32 = jnp.float32
BF16 = jnp.bfloat16
SMEM = pltpu.MemorySpace.SMEM


def sgn(left, right):
    return -1.0 if (left & 2) and (right & 1) else 1.0


def flip_of(own, k):
    if k & 1:
        return (1 - 2 * ((own // 2) % 2)).astype(F32)
    return jnp.float32(1.0)


def mode_factor(mode):
    return jnp.where(mode % MSIDE == 0, 1.0, 2.0).astype(F32)


def dot(left, right, dims=((1,), (0,))):
    return lax.dot_general(left, right, (dims, ((), ())), preferred_element_type=F32)


def whole(shape):
    zeros = (0,) * len(shape)
    return pl.BlockSpec(tuple(shape), lambda *_: zeros)


def params(mib):
    return pltpu.CompilerParams(vmem_limit_bytes=mib * 1024 * 1024)


def fast(shape, kind):
    return pltpu.VMEM(tuple(shape), kind)


def slow(shape, kind):
    return pltpu.HBM(tuple(shape), kind)


def pin(*arrays):
    return [pltpu.with_memory_space_constraint(array, pltpu.VMEM) for array in arrays]


def stay(*arrays):
    return [pltpu.with_memory_space_constraint(array, pltpu.HBM) for array in arrays]


def in_vmem(count):
    return [pl.BlockSpec(memory_space=pltpu.MemorySpace.VMEM)] * count


def cost():
    return pl.CostEstimate(flops=1, bytes_accessed=1, transcendentals=0)


def small_tables():
    mode_ids = jnp.arange(2 * MODES, dtype=jnp.int32)
    imag = mode_ids >= MODES
    mode_ids = mode_ids % MODES
    row_index = mode_ids // MSIDE
    col_freq = mode_ids % MSIDE
    row_freq = jnp.where(row_index < MSIDE // 2, row_index, GRID - MSIDE + row_index)
    place = jnp.arange(GRID, dtype=jnp.int32)[:, None]
    row_angle = ((place * row_freq[None, :]) % GRID).astype(F32) * (2.0 * math.pi / GRID)
    col_angle = ((place * col_freq[None, :]) % GRID).astype(F32) * (2.0 * math.pi / GRID)
    row_cos, row_sin = jnp.cos(row_angle) / GRID, jnp.sin(row_angle) / GRID
    first = jnp.where(imag[None, :], -row_sin, row_cos)
    second = jnp.where(imag[None, :], -row_cos, -row_sin)
    return jnp.stack([first, second, jnp.cos(col_angle), jnp.sin(col_angle)])


def table_rows(row_ref, col_ref, start, stop):
    tiles = []
    for h in range(start, stop):
        tile = row_ref[0, h : h + 1] * col_ref[0] + row_ref[1, h : h + 1] * col_ref[1]
        tiles.append(tile.astype(BF16))
    return jnp.concatenate(tiles, axis=0)


def small_specs(tile):
    n = 2 * MODES
    return [
        pl.BlockSpec((2, tile // GRID, n), lambda i, *_: (0, i, 0)),
        pl.BlockSpec((2, GRID, n), lambda i, *_: (1, 0, 0)),
    ]


def turned_kernel(row_ref, col_ref, ft_ref):
    for h in range(0, row_ref.shape[1], 2):
        tile = table_rows(row_ref, col_ref, h, h + 2)
        ft_ref[:, h * GRID : (h + 2) * GRID] = tile.astype(F32).T.astype(BF16)


def turned_table(small):
    rows = 8
    n = 2 * MODES
    return pl.pallas_call(
        turned_kernel,
        grid=(GRID // rows,),
        in_specs=small_specs(rows * GRID),
        out_specs=pl.BlockSpec((n, rows * GRID), lambda i: (0, i)),
        out_shape=slow((n, NPIX), BF16),
        compiler_params=params(28),
        cost_estimate=cost(),
        name="turned",
    )(*stay(small, small))


def pack_kernel(w_ref, l_ref, o_ref):
    def step(g, carry):
        parts = [w_ref[0, g * QUAD + q, r] for q in range(QUAD) for r in range(2)]
        at = pl.ds(pl.multiple_of(g * QUAD * LANES, PACK), QUAD * LANES)
        o_ref[:, at] = jnp.concatenate(parts, axis=1).astype(BF16)
        return carry

    modes = w_ref.shape[1]
    lax.fori_loop(0, modes // QUAD, step, 0)
    line = jnp.concatenate([l_ref[0], jnp.zeros((C, PACK - C), F32)], axis=1)
    o_ref[:, modes * LANES :] = line.astype(BF16)


def pack_weights(spec_weight, lin_weight):
    modes = spec_weight.shape[1]
    return pl.pallas_call(
        pack_kernel,
        in_specs=in_vmem(2),
        out_specs=in_vmem(1)[0],
        out_shape=jax.ShapeDtypeStruct((C, modes * LANES + PACK), BF16),
        compiler_params=params(28),
        cost_estimate=cost(),
        name="pack",
    )(spec_weight, lin_weight)


def lanes_of(shape):
    return lax.broadcasted_iota(jnp.int32, shape, len(shape) - 1)


def split_lanes(a, b, c):
    lane = lanes_of(a.shape)
    second = jnp.where(lane < 32, pltpu.roll(a, 32, 1), pltpu.roll(b, 32, 1))
    third = jnp.where(lane < 64, pltpu.roll(b, 64, 1), pltpu.roll(c, 64, 1))
    return a, second, third, pltpu.roll(c, 96, 1)


def join_lanes(first, second, third, fourth):
    lane = lanes_of(first.shape)
    a = jnp.where(lane < 96, first, pltpu.roll(second, 96, 1))
    b = jnp.where(lane < 64, pltpu.roll(second, 96, 1), pltpu.roll(third, 64, 1))
    c = jnp.where(lane < 32, pltpu.roll(third, 64, 1), pltpu.roll(fourth, 32, 1))
    return a, b, c


def quad_tiles(ref, g):
    tiles = []
    for n in range(3):
        at = pl.ds(pl.multiple_of(g * QUAD * LANES + n * PACK, PACK), PACK)
        tiles.append(ref[:, at])
    return tiles


def unpack_kernel(ids_ref, w0, w1, w2, w3, pq_ref):
    own = ids_ref[0]
    modes = pq_ref.shape[0]
    lane = lanes_of((C, PACK))
    flip = flip_of(own, 1)

    def step(g, carry):
        for t, w in enumerate((w0, w1, w2, w3)):
            slot = jnp.bitwise_xor(own, t)
            scale = jnp.where(slot % 2 == 1, flip, 1.0)
            at = pl.ds(pl.multiple_of(slot * PACK, PACK), PACK)
            tiles = [tile * scale.astype(BF16) for tile in quad_tiles(w, g)]
            for q, p in enumerate(split_lanes(*tiles)):
                low = jnp.where(lane < C, -pltpu.roll(p, PACK - C, 1), pltpu.roll(p, C, 1))
                pq_ref[g * QUAD + q, :C, at] = p
                pq_ref[g * QUAD + q, C:, at] = low
        return carry

    quads = modes // QUAD
    lax.fori_loop(0, quads, step, 0, unroll=min(4, quads))


def unpack(ids, packs):
    modes = (packs[0].shape[1] - PACK) // LANES
    return pl.pallas_call(
        unpack_kernel,
        in_specs=[pl.BlockSpec(memory_space=SMEM)] + in_vmem(4),
        out_specs=in_vmem(1)[0],
        out_shape=fast((modes, LANES, 4 * PACK), BF16),
        compiler_params=params(28),
        cost_estimate=cost(),
        name="unpack",
    )(*stay(ids, *packs))


def spread(acc, out_ref, scales=None):
    rows = []
    for n in range(acc.shape[0] // C):
        for r in range(2):
            row = acc[n * C : (n + 1) * C, r * MODES : (r + 1) * MODES]
            rows.append(row if scales is None else row * scales[n])
    extra = out_ref.shape[2] - len(rows) * C
    if extra:
        rows.append(jnp.zeros((extra, MODES), F32))
    turned = jnp.concatenate(rows, axis=0).T
    out_ref[...] = turned.reshape(out_ref.shape).astype(BF16)


def collect(block, ysc):
    turned = block[...].astype(F32).reshape(MODES, block.shape[2]).T
    for n in range(ysc.shape[0] // C):
        for r in range(2):
            row = (n * 2 + r) * C
            piece = turned[row : row + C].astype(BF16)
            ysc[n * C : (n + 1) * C, r * MODES : (r + 1) * MODES] = piece


def forward_kernel(ids_ref, inv_ref, *refs):
    x = refs[:-4]
    row_ref, col_ref, out_ref, acc = refs[-4:]
    i = pl.program_id(0)
    samples = x[0].shape[0]
    rows = [part[s, 0] for s in range(samples) for part in x]
    table = table_rows(row_ref, col_ref, 0, row_ref.shape[1])
    part = dot(jnp.concatenate(rows, axis=0), table)

    @pl.when(i == 0)
    def _():
        acc[...] = part

    @pl.when(i > 0)
    def _():
        acc[...] += part

    @pl.when(i == pl.num_programs(0) - 1)
    def _():
        spread(acc, out_ref, [inv_ref[s] for s in range(samples) for _ in x])


def forward_spectrum(ids, inv, x, small, shards):
    samples = inv.shape[0]
    modes = MODES // shards
    width = -(-samples * len(x) * LANES // PACK) * PACK
    n = 2 * MODES
    tile = 2048

    def spec(array):
        if array.shape[0] == samples:
            return pl.BlockSpec((samples, 1, C, tile), lambda i, ids, inv: (0, 0, 0, i))
        return pl.BlockSpec((samples, 1, C, tile), lambda i, ids, inv: (ids[0], 0, 0, i))

    return pl.pallas_call(
        forward_kernel,
        grid_spec=pltpu.PrefetchScalarGridSpec(
            num_scalar_prefetch=2,
            grid=(NPIX // tile,),
            in_specs=[spec(part) for part in x] + small_specs(tile),
            out_specs=whole((shards, modes, width)),
            scratch_shapes=[pltpu.VMEM((samples * len(x) * C, n), F32)],
        ),
        out_shape=slow((shards, modes, width), BF16),
        compiler_params=params(28),
        cost_estimate=cost(),
        name="forward",
    )(*stay(ids, inv, *x, small, small))


def row_scratch(modes, shards, width):
    return pltpu.VMEM((width // PACK, modes * shards, PACK), F32)


def gather_rows(blocks, sc):
    shards, modes = blocks[0].shape[:2]
    first = 0
    for block in blocks:
        for n in range(block.shape[2] // PACK):
            for x in range(shards):
                rows = block[x, :, n * PACK : (n + 1) * PACK].astype(F32)
                sc[first + n, pl.ds(x, modes, stride=shards), :] = rows
        first += block.shape[2] // PACK


def scatter_rows(ysc, out):
    shards, modes = out.shape[:2]
    for x in range(shards):
        for n in range(ysc.shape[0]):
            piece = ysc[n, pl.ds(x, modes, stride=shards), :]
            out[x, :, n * PACK : (n + 1) * PACK] = piece.astype(BF16)


def blade_rows(sc, mode, shards, groups):
    at = pl.ds(pl.multiple_of(mode * shards, shards), shards)
    found = [[] for _ in range(4)]
    for tile, pairs in groups:
        tiles = [sc[tile + n, at, :] for n in range(-(-len(pairs) * LANES // PACK))]
        pieces = split_lanes(tiles[0], tiles[min(1, len(tiles) - 1)], tiles[-1])
        for piece, (_, t) in zip(pieces, pairs):
            found[t].append(piece)
    return [jnp.concatenate(found[t], axis=0) for t in range(4)]


def groups_of(samples, *blades):
    groups = []
    tile = 0
    for some in blades:
        pairs = [(s, t) for s in range(samples) for t in some]
        for n in range(0, len(pairs), 4):
            part = pairs[n : n + 4]
            groups.append((tile, part))
            tile += -(-len(part) * LANES // PACK)
    return groups


EARLY = (0, 3)
LATE = (1, 2)


def mix_modes(xsc, ysc, pq_ref, groups, shards, first_mode, back):
    modes = xsc.shape[1] // shards
    samples = ysc.shape[0] // 3
    group = samples * shards

    def step(m, carry):
        low = jnp.concatenate(blade_rows(xsc, m, shards, groups), axis=0)
        low = low[:, :LANES].astype(BF16)
        total = [None] * 4
        parts = dot(low, pq_ref[m])
        for k in range(4):
            part = parts[:, k * PACK : (k + 1) * PACK]
            for t in range(4):
                u = t ^ k
                piece = part[t * group : (t + 1) * group]
                sign = sgn(u, k) if back else sgn(t, k)
                if total[u] is None:
                    total[u] = piece if sign > 0 else -piece
                else:
                    total[u] = total[u] + piece if sign > 0 else total[u] - piece
        factor = mode_factor(first_mode + m)
        at = pl.ds(pl.multiple_of(m * shards, shards), shards)
        for s in range(samples):
            rows = []
            for u in range(4):
                rows.append(total[u][s * shards : (s + 1) * shards] * factor)
            for n, tile in enumerate(join_lanes(*rows)):
                ysc[s * 3 + n, at, :] = tile
        return carry

    lax.fori_loop(0, modes, step, 0, unroll=min(32, modes))


def mix_kernel(ids_ref, xa, xb, pq_ref, y_ref, xsc, ysc):
    shards, modes, width = y_ref.shape
    gather_rows((xa, xb), xsc)
    groups = groups_of(width // (4 * LANES), EARLY, LATE)
    mix_modes(xsc, ysc, pq_ref, groups, shards, ids_ref[1] * modes, False)
    scatter_rows(ysc, y_ref)


def mix(ids, xa, xb, pq, samples):
    shards, modes = xa.shape[:2]
    width = samples * 4 * LANES
    return pl.pallas_call(
        mix_kernel,
        in_specs=[pl.BlockSpec(memory_space=SMEM)] + in_vmem(3),
        out_specs=in_vmem(1)[0],
        out_shape=slow((shards, modes, width), BF16),
        scratch_shapes=[
            row_scratch(modes, shards, xa.shape[2] + xb.shape[2]),
            row_scratch(modes, shards, width),
        ],
        compiler_params=params(28),
        cost_estimate=cost(),
        name="mix",
    )(*stay(ids, xa, xb), *pin(pq))


def mix_back_kernel(ids_ref, g_ref, pq_ref, out_ref, gsc, ysc):
    shards, modes, width = g_ref.shape
    gather_rows((g_ref,), gsc)
    groups = groups_of(width // (4 * LANES), range(4))
    mix_modes(gsc, ysc, pq_ref, groups, shards, ids_ref[1] * modes, True)
    scatter_rows(ysc, out_ref)


def mix_back(ids, g, pq):
    shards, modes, width = g.shape
    return pl.pallas_call(
        mix_back_kernel,
        in_specs=[pl.BlockSpec(memory_space=SMEM)] + in_vmem(2),
        out_specs=in_vmem(1)[0],
        out_shape=slow(g.shape, BF16),
        scratch_shapes=[row_scratch(modes, shards, width)] * 2,
        compiler_params=params(28),
        cost_estimate=cost(),
        name="mix_back",
    )(*stay(ids), g, *pin(pq))


def turn_kernel(ids_ref, pq_ref, xa, xb, l0, l1, l2, l3, out_ref, xt_ref, lt_ref, lb_ref, held, xsc, lsc):
    shards, modes = xa.shape[:2]
    samples = xt_ref.shape[2] // (8 * shards)
    groups = groups_of(samples, EARLY, LATE)
    shape = (LANES, LANES)
    diagonal = lax.broadcasted_iota(jnp.int32, shape, 0) == lax.broadcasted_iota(jnp.int32, shape, 1)
    unit = jnp.where(diagonal, 1.0, 0.0).astype(BF16)
    gather_rows((xa, xb), xsc)

    def step(m, carry):
        for k in range(4):
            at = slice(k * PACK, k * PACK + LANES)
            held[m, :, at] = dot(unit, pq_ref[m, :, at], ((1,), (1,))).astype(BF16)
        x = blade_rows(xsc, m, shards, groups)
        x = x + [pltpu.roll(rows, PACK - C, 1) for rows in x]
        xt_ref[m] = jnp.concatenate(x, axis=0).T[:C].astype(BF16)
        return carry

    lax.fori_loop(0, modes, step, 0, unroll=min(16, modes))
    out_ref[...] = held[...]
    own = ids_ref[0]
    for t, line in enumerate((l0, l1, l2, l3)):
        slot = jnp.bitwise_xor(own, t)
        lsc[slot] = line[...].astype(F32) * jnp.where(slot % 2 == 1, flip_of(own, 1), 1.0)
    for k in range(4):
        line = lsc[k]
        turned = line.T
        for t in range(4):
            u = t ^ k
            lb_ref[t * C : (t + 1) * C, u * C : (u + 1) * C] = (line[:, :C] * sgn(t, k)).astype(BF16)
            lt_ref[u * C : (u + 1) * C, t * C : (t + 1) * C] = (turned[:C] * sgn(t, k)).astype(BF16)


def turn(ids, pq, xa, xb, packs, samples):
    shards, modes = xa.shape[:2]
    last = packs[0].shape[1] // PACK - 1
    shape = (4 * C, 4 * C)
    turned_shape = (modes, C, 8 * samples * shards)
    return pl.pallas_call(
        turn_kernel,
        grid=(1,),
        in_specs=[pl.BlockSpec(memory_space=SMEM), whole(pq.shape), whole(xa.shape), whole(xb.shape)]
        + [pl.BlockSpec((C, PACK), lambda i: (0, last))] * 4,
        out_specs=[whole(pq.shape), whole(turned_shape)] + [whole(shape)] * 2,
        out_shape=[fast(pq.shape, BF16), slow(turned_shape, BF16)] + [slow(shape, BF16)] * 2,
        input_output_aliases={1: 0},
        scratch_shapes=[
            pltpu.VMEM(pq.shape, BF16),
            row_scratch(modes, shards, xa.shape[2] + xb.shape[2]),
            pltpu.VMEM((4, C, PACK), F32),
        ],
        compiler_params=params(28),
        cost_estimate=cost(),
        name="turn",
    )(*stay(ids), *pin(pq), *stay(xa, xb, *packs))


def grad_kernel(ids_ref, xt_ref, g_ref, lin_ref, o0, o1, o2, o3, gsc, osc):
    shards, modes, width = g_ref.shape
    samples = width // (4 * LANES)
    own = ids_ref[0]
    first_mode = ids_ref[1] * modes
    groups = groups_of(samples, range(4))
    gather_rows((g_ref,), gsc)
    lane = lanes_of((samples * shards, PACK))

    def step(g, carry):
        found = [[] for _ in range(4)]
        for q in range(QUAD):
            m = g * QUAD + q
            factor = mode_factor(first_mode + m)
            plain = [rows * factor for rows in blade_rows(gsc, m, shards, groups)]
            turned = [
                jnp.where(lane < C, pltpu.roll(rows, PACK - C, 1), -pltpu.roll(rows, C, 1))
                for rows in plain
            ]
            plus = [rows.astype(BF16) for rows in plain + turned]
            minus = [(-rows).astype(BF16) for rows in plain + turned]
            right = []
            for k in range(4):
                rows = []
                for r in range(2):
                    for t in range(4):
                        rows.append((plus if sgn(t, k) > 0 else minus)[4 * r + (t ^ k)])
                right.append(jnp.concatenate(rows, axis=0))
            grad = dot(xt_ref[m], jnp.concatenate(right, axis=1))
            for k in range(4):
                found[k].append(grad[:, k * PACK : (k + 1) * PACK])
        for k in range(4):
            for n, tile in enumerate(join_lanes(*found[k])):
                at = pl.ds(pl.multiple_of(g * QUAD * LANES + n * PACK, PACK), PACK)
                osc[k, :, at] = tile.astype(BF16)
        return carry

    quads = modes // QUAD
    lax.fori_loop(0, quads, step, 0, unroll=min(2, quads))
    for k in range(4):
        line = jnp.concatenate([lin_ref[k], jnp.zeros((C, PACK - C), F32)], axis=1)
        osc[k, :, modes * LANES :] = line.astype(BF16)
    for t, out in enumerate((o0, o1, o2, o3)):
        out[...] = osc[jnp.bitwise_xor(own, t)]


def weight_grads(ids, xt, g, lin):
    shards, modes, width = g.shape
    shape = (C, modes * LANES + PACK)
    return pl.pallas_call(
        grad_kernel,
        in_specs=[pl.BlockSpec(memory_space=SMEM)] + in_vmem(3),
        out_specs=in_vmem(4),
        out_shape=[slow(shape, BF16)] * 4,
        scratch_shapes=[row_scratch(modes, shards, width), pltpu.VMEM((4,) + shape, BF16)],
        compiler_params=params(28),
        cost_estimate=cost(),
        name="weight_grads",
    )(*stay(ids, xt), g, *stay(lin))


CDF_AT = 0.28
CDF = (0.11652094, 0.06749571, 0.2689128, -0.23699677, 0.38987606, -0.10580875)
SERIES = [value / CDF_AT ** (i + 1) for i, value in enumerate(CDF)]


def gelu_parts(v):
    z = jnp.abs(v)
    t = 1.0 / (z + 1.0 / CDF_AT)
    bell = jnp.exp2(v * v * (-0.5 * math.log2(math.e)))
    series = jnp.float32(SERIES[-1])
    for value in SERIES[-2::-1]:
        series = series * t + value
    tail = series * t * bell
    cdf = jnp.where(v < 0.0, tail, 1.0 - tail)
    return v * cdf, cdf + v * (bell * (1.0 / math.sqrt(2.0 * math.pi)))


def pixel_kernel(ids_ref, inv_ref, *refs):
    x = refs[:4]
    y_ref, ft_ref, lt_ref = refs[4:7]
    outs = refs[8:12]
    slope_ref = refs[12]
    left, ysc, even, odd = refs[14:]
    samples = x[1].shape[0]
    rows = 4 * C
    n = 2 * MODES
    width = even.shape[1]

    @pl.when(pl.program_id(0) == 0)
    def _():
        collect(y_ref, ysc)
        for s in range(samples):
            left[s, :, :n] = ysc[s * rows : (s + 1) * rows]
            left[s, :, n:] = (lt_ref[...].astype(F32) * inv_ref[s]).astype(BF16)

    def product(s, at, pre):
        fields = [x[t][s, 0, :, at] for t in range(4)]
        pre[...] = dot(left[s], jnp.concatenate([ft_ref[:, at]] + fields, axis=0))

    def activate(s, at, pre):
        for t in range(4):
            value, slope = gelu_parts(pre[t * C : (t + 1) * C])
            normed = x[t][s, 0, :, at].astype(F32) * inv_ref[s]
            outs[t][s, 0, :, at] = (normed + value).astype(BF16)
            row = s * rows + t * C
            slope_ref[row : row + C, at] = slope.astype(BF16)

    tile = ft_ref.shape[1]
    blocks = [(s, slice(k, k + width)) for k in range(0, tile, width) for s in range(samples)]
    buffers = [even, odd]
    product(*blocks[0], buffers[0])
    for k, block in enumerate(blocks):
        if k + 1 < len(blocks):
            product(*blocks[k + 1], buffers[(k + 1) % 2])
        activate(*block, buffers[k % 2])


def pixels(ids, inv, x, y, turned, lt, pq):
    samples = inv.shape[0]
    n = 2 * MODES
    tile = 1024
    mine = pl.BlockSpec((samples, 1, C, tile), lambda i, ids, inv: (ids[0], 0, 0, i))
    block = pl.BlockSpec((samples, 1, C, tile), lambda i, ids, inv: (0, 0, 0, i))
    rows = samples * 4 * C
    flat = pl.BlockSpec((rows, tile), lambda i, ids, inv: (0, i))
    return pl.pallas_call(
        pixel_kernel,
        grid_spec=pltpu.PrefetchScalarGridSpec(
            num_scalar_prefetch=2,
            grid=(NPIX // tile,),
            in_specs=[mine]
            + [block] * 3
            + [
                whole(y.shape),
                pl.BlockSpec((n, tile), lambda i, ids, inv: (0, i)),
                whole((4 * C, 4 * C)),
                pl.BlockSpec(memory_space=pl.ANY),
            ],
            out_specs=[mine] + [block] * 3 + [flat, pl.BlockSpec(memory_space=pl.ANY)],
            scratch_shapes=[
                pltpu.VMEM((samples, 4 * C, n + 4 * C), BF16),
                pltpu.VMEM((rows, n), BF16),
                pltpu.VMEM((4 * C, 256), F32),
                pltpu.VMEM((4 * C, 256), F32),
            ],
        ),
        out_shape=[slow(x[0].shape, BF16)]
        + [slow((samples, 1, C, NPIX), BF16)] * 3
        + [fast((rows, NPIX), BF16), fast(pq.shape, BF16)],
        input_output_aliases={9: 5},
        compiler_params=params(28),
        cost_estimate=cost(),
        name="pixels",
    )(*stay(ids, inv, *x), y, *stay(turned, lt), *pin(pq))


def slope_kernel(ids_ref, *refs):
    cot = refs[:4]
    slope, row_ref, col_ref, _, g_ref, g_out, _, gacc = refs[4:]
    samples = cot[1].shape[0]
    rows = 4 * C
    i = pl.program_id(0)

    @pl.when(i == 0)
    def _():
        gacc[...] = jnp.zeros_like(gacc)

    for s in range(samples):
        for t in range(4):
            at = s * rows + t * C
            grad = cot[t][s, 0].astype(F32) * slope[at : at + C].astype(F32)
            g_ref[at : at + C] = grad.astype(BF16)
    table = table_rows(row_ref, col_ref, 0, row_ref.shape[1])
    gacc[...] += dot(g_ref[...], table)

    @pl.when(i == pl.num_programs(0) - 1)
    def _():
        spread(gacc, g_out)


def pixel_grads(ids, cot, slope, small, spectrum, pq):
    rows = slope.shape[0]
    samples = rows // (4 * C)
    n = 2 * MODES
    tile = 2048
    mine = pl.BlockSpec((samples, 1, C, tile), lambda i, ids: (ids[0], 0, 0, i))
    block = pl.BlockSpec((samples, 1, C, tile), lambda i, ids: (0, 0, 0, i))
    flat = pl.BlockSpec((rows, tile), lambda i, ids: (0, i))
    kept = pl.BlockSpec(memory_space=pl.ANY)
    return pl.pallas_call(
        slope_kernel,
        grid_spec=pltpu.PrefetchScalarGridSpec(
            num_scalar_prefetch=1,
            grid=(NPIX // tile,),
            in_specs=[mine] + [block] * 3 + [flat] + small_specs(tile) + [kept],
            out_specs=[flat, whole(spectrum), kept],
            scratch_shapes=[pltpu.VMEM((rows, n), F32)],
        ),
        out_shape=[slow((rows, NPIX), BF16), slow(spectrum, BF16), fast(pq.shape, BF16)],
        input_output_aliases={8: 2},
        compiler_params=params(28),
        cost_estimate=cost(),
        name="pixel_grads",
    )(*stay(ids, *cot), *pin(slope), *stay(small, small), *pin(pq))


def lin_kernel(ids_ref, inv_ref, *refs):
    x = refs[:4]
    g_ref, lin_ref, lacc = refs[4:]
    samples = x[1].shape[0]
    rows = 4 * C

    @pl.when(pl.program_id(0) == 0)
    def _():
        lacc[...] = jnp.zeros_like(lacc)

    for s in range(samples):
        fields = jnp.concatenate([x[t][s, 0] for t in range(4)], axis=0)
        g = g_ref[s * rows : (s + 1) * rows]
        lacc[...] += dot(fields, g, ((1,), (1,))) * inv_ref[s]

    @pl.when(pl.program_id(0) == pl.num_programs(0) - 1)
    def _():
        for k in range(4):
            total = None
            for t in range(4):
                u = t ^ k
                piece = lacc[t * C : (t + 1) * C, u * C : (u + 1) * C] * sgn(t, k)
                total = piece if total is None else total + piece
            lin_ref[k] = total


def lin_grads(ids, inv, x, g):
    rows = g.shape[0]
    samples = rows // (4 * C)
    tile = 2048
    mine = pl.BlockSpec((samples, 1, C, tile), lambda i, ids, inv: (ids[0], 0, 0, i))
    block = pl.BlockSpec((samples, 1, C, tile), lambda i, ids, inv: (0, 0, 0, i))
    flat = pl.BlockSpec((rows, tile), lambda i, ids, inv: (0, i))
    return pl.pallas_call(
        lin_kernel,
        grid_spec=pltpu.PrefetchScalarGridSpec(
            num_scalar_prefetch=2,
            grid=(NPIX // tile,),
            in_specs=[mine] + [block] * 3 + [flat],
            out_specs=whole((4, C, C)),
            scratch_shapes=[pltpu.VMEM((4 * C, 4 * C), F32)],
        ),
        out_shape=slow((4, C, C), F32),
        compiler_params=params(28),
        cost_estimate=cost(),
        name="lin_grads",
    )(*stay(ids, inv, *x, g))


def inner_kernel(ids_ref, inv_ref, y_ref, g_ref, row_ref, col_ref, lb_ref, cot_ref, mine_ref, *refs):
    o1, o2, o3, ysc = refs
    samples = cot_ref.shape[0]
    rows = 4 * C

    @pl.when(pl.program_id(0) == 0)
    def _():
        collect(y_ref, ysc)

    table = table_rows(row_ref, col_ref, 0, row_ref.shape[1])
    spatial = dot(ysc[...], table, ((1,), (1,)))
    for s in range(samples):
        at = slice(s * rows, (s + 1) * rows)
        total = spatial[at] + dot(lb_ref[...], g_ref[at])
        mine_ref[s, 0] = (cot_ref[s, 0].astype(F32) + total[:C]) * inv_ref[s]
        for t, out in ((1, o1), (2, o2), (3, o3)):
            out[s, 0] = total[t * C : (t + 1) * C].astype(BF16)


def inner_grads(ids, inv, y, g, small, lb, cotangent):
    samples = inv.shape[0]
    n = 2 * MODES
    tile = 2048
    rows = samples * 4 * C
    mine = pl.BlockSpec((samples, 1, C, tile), lambda i, ids, inv: (ids[0], 0, 0, i))
    block = pl.BlockSpec((samples, 1, C, tile), lambda i, ids, inv: (0, 0, 0, i))
    return pl.pallas_call(
        inner_kernel,
        grid_spec=pltpu.PrefetchScalarGridSpec(
            num_scalar_prefetch=2,
            grid=(NPIX // tile,),
            in_specs=[
                whole(y.shape),
                pl.BlockSpec((rows, tile), lambda i, ids, inv: (0, i)),
                *small_specs(tile),
                whole((4 * C, 4 * C)),
                mine,
            ],
            out_specs=[mine] + [block] * 3,
            scratch_shapes=[pltpu.VMEM((rows, n), BF16)],
        ),
        out_shape=[slow(cotangent.shape, F32)] + [slow((samples, 1, C, NPIX), BF16)] * 3,
        compiler_params=params(28),
        cost_estimate=cost(),
        name="inner_grads",
    )(*stay(ids, inv), y, *stay(g, small, small, lb, cotangent))


def place_kernel(ids_ref, a_ref, b_ref, c_ref, old_ref, out_ref):
    for n, part in enumerate((a_ref, b_ref, c_ref)):

        @pl.when(pl.program_id(0) == n)
        def _():
            out_ref[...] = part[...]


def place_output(ids, parts, result):
    samples = parts[0].shape[0]
    shape = (1, 1, C, NPIX)

    def spec(n):
        def at(j, s, ids):
            return (jnp.where(j == n, s, jnp.where(j < n, 0, samples - 1)), 0, 0, 0)

        return pl.BlockSpec(shape, at)

    return pl.pallas_call(
        place_kernel,
        grid_spec=pltpu.PrefetchScalarGridSpec(
            num_scalar_prefetch=1,
            grid=(3, samples),
            in_specs=[spec(0), spec(1), spec(2), pl.BlockSpec(memory_space=pl.ANY)],
            out_specs=pl.BlockSpec(
                shape, lambda j, s, ids: (jnp.bitwise_xor(ids[0], j + 1) * samples + s, 0, 0, 0)
            ),
        ),
        out_shape=jax.ShapeDtypeStruct(result.shape, BF16),
        input_output_aliases={4: 0},
        compiler_params=params(28),
        cost_estimate=cost(),
        name="place",
    )(ids, *parts, result)


def final_kernel(count, codes, ids_ref, inv_ref, cot_ref, *refs):
    samples = pl.num_programs(1)
    j = pl.program_id(0)
    for n in range(count):

        @pl.when(j == n)
        def _():
            inv = inv_ref[jnp.bitwise_xor(ids_ref[0], codes[n]) * samples + pl.program_id(1)]
            refs[-1][...] = (cot_ref[...].astype(F32) + refs[n][...].astype(F32)) * inv


def final_grads(ids, inv, cotangent, parts, codes, result):
    samples = parts[0].shape[0]
    count = len(parts)
    shape = (1, 1, C, NPIX)

    def code(j):
        value = codes[0]
        for n in range(1, count):
            value = jnp.where(j == n, codes[n], value)
        return value

    def spec(n):
        def at(j, s, ids, inv):
            return (jnp.where(j == n, s, jnp.where(j < n, 0, samples - 1)), 0, 0, 0)

        return pl.BlockSpec(shape, at)

    place = pl.BlockSpec(
        shape, lambda j, s, ids, inv: (jnp.bitwise_xor(ids[0], code(j)) * samples + s, 0, 0, 0)
    )
    return pl.pallas_call(
        partial(final_kernel, count, codes),
        grid_spec=pltpu.PrefetchScalarGridSpec(
            num_scalar_prefetch=2,
            grid=(count, samples),
            in_specs=[place]
            + [spec(n) for n in range(count)]
            + [pl.BlockSpec(memory_space=pl.ANY)],
            out_specs=place,
        ),
        out_shape=jax.ShapeDtypeStruct(cotangent.shape, F32),
        input_output_aliases={3 + count: 0},
        compiler_params=params(28),
        cost_estimate=cost(),
        name="final",
    )(ids, inv, cotangent, *parts, result)


def adamw(weight, first, second, grad):
    first_new = BETA_ONE * first + (1.0 - BETA_ONE) * grad
    second_new = BETA_TWO * second + (1.0 - BETA_TWO) * grad * grad
    corr_one = 1.0 - BETA_ONE**STEP_COUNT
    corr_two = 1.0 - BETA_TWO**STEP_COUNT
    update = first_new / corr_one / (jnp.sqrt(second_new / corr_two) + EPSILON)
    return (weight - RATE * (update + DECAY * weight), first_new, second_new)


def adam_kernel(flips, d0, d1, d2, d3, w_ref, first_ref, second_ref, w_out, first_out, second_out):
    grad = d0[...].astype(F32) * flips[0]
    for t, d in ((1, d1), (2, d2), (3, d3)):
        grad = grad + d[...].astype(F32) * flips[t]
    for q in range(w_ref.shape[1]):
        for r in range(2):
            lane = q * LANES + r * C
            at = (0, q, r)
            new = adamw(w_ref[at], first_ref[at], second_ref[at], grad[:, lane : lane + C])
            w_out[at], first_out[at], second_out[at] = new


def adam_spec(flips, grads, weight, first, second):
    modes = weight.shape[1]
    part = min(modes, 4 * QUAD)
    packed = pl.BlockSpec((C, part * LANES), lambda g: (0, g))
    block = pl.BlockSpec((1, part, 2, C, C), lambda g: (0, g, 0, 0, 0))
    return pl.pallas_call(
        adam_kernel,
        grid=(modes // part,),
        in_specs=[pl.BlockSpec(memory_space=SMEM)] + [packed] * 4 + [block] * 3,
        out_specs=[block] * 3,
        out_shape=[jax.ShapeDtypeStruct(weight.shape, F32)] * 3,
        compiler_params=params(28),
        cost_estimate=cost(),
        name="adam",
    )(flips, *grads, weight, first, second)


def swap(value, axis, size, x):
    return lax.ppermute(value, axis, [(i, i ^ x) for i in range(size)])


def to_modes(value):
    return lax.all_to_all(value, "dp", split_axis=0, concat_axis=0, tiled=True)


def after(values, first):
    values, _ = lax.optimization_barrier((values, first))
    return values


def body(
    shards,
    inputs,
    cotangent,
    norm_table,
    sample_index,
    spec_weight,
    spec_first,
    spec_second,
    lin_weight,
    lin_first,
    lin_second,
):
    own = lax.axis_index("blade")
    shard = lax.axis_index("dp")
    ids = jnp.stack([own, shard]).astype(jnp.int32)
    samples = inputs.shape[0] // 4

    def cut(array, t):
        return lax.dynamic_slice_in_dim(array, jnp.bitwise_xor(own, t) * samples, samples, 0)

    def send(array, t):
        block = cut(array, t)
        return block, swap(block, "blade", 4, t)

    sent, x3 = send(inputs, 3)
    rest = after(inputs, sent)
    sent, x1 = send(rest, 1)
    rest = after(rest, sent)
    _, x2 = send(rest, 2)

    matches = sample_index[:, None] == jnp.arange(NTAB, dtype=jnp.int32)[None, :]
    normalizer = jnp.sum(jnp.where(matches, norm_table[None, :], 0.0), axis=1)
    inv_all = 1.0 / normalizer
    inv = lax.dynamic_slice_in_dim(inv_all, own * samples, samples, 0)

    small = lax.optimization_barrier(small_tables())
    turned = turned_table(small)
    packed = pack_weights(spec_weight, lin_weight)
    packs = [packed] + [swap(packed, "blade", 4, t) for t in (1, 2, 3)]

    x3 = after(x3, (packed, turned))
    sent = forward_spectrum(ids, inv, (inputs, x3), small, shards)
    x1, x2 = after((x1, x2), sent)
    xa = to_modes(sent)
    blocks = after([cut(cotangent, t) for t in (1, 2, 3)], (x1, x2))
    cot = (cotangent,) + tuple(swap(blocks[t - 1], "blade", 4, t) for t in (1, 2, 3))
    xb = to_modes(forward_spectrum(ids, inv, (x1, x2), small, shards))
    pq = unpack(ids, packs)
    mixed = mix(ids, xa, xb, pq, samples)
    pq, xt, lt, lb = turn(ids, after(pq, mixed), xa, xb, packs, samples)
    y = to_modes(mixed)

    x = (inputs, x1, x2, x3)
    result = pixels(ids, inv, x, y, turned, lt, pq)
    output, slope, pq = result[0], result[4], result[5]
    last, cot = lax.optimization_barrier((result[3], cot))
    parts = (result[1], result[2], last)
    out_parts = [swap(parts[t - 1], "blade", 4, t) for t in (1, 2, 3)]

    grad_pre, sent, pq = pixel_grads(ids, cot, slope, small, y.shape, pq)
    lin = lin_grads(ids, inv, x, grad_pre)
    g = after(to_modes(sent), (out_parts[2], xt, pq, lin))
    mixed = mix_back(ids, g, pq)
    back = to_modes(mixed)
    spec_grads = weight_grads(ids, xt, g, lin)
    spec_grads = [spec_grads[0]] + [swap(spec_grads[t], "blade", 4, t) for t in (1, 2, 3)]

    inner = inner_grads(ids, inv, back, grad_pre, small, lb, cotangent)
    inner = after(inner, out_parts)
    grad_parts = [swap(inner[t], "blade", 4, t) for t in (1, 2, 3)]

    output = place_output(ids, out_parts, output)
    spec_grads = after(spec_grads, output)
    flips = jnp.stack(
        [jnp.where(own % 2 == 1, flip_of(jnp.bitwise_xor(own, t), 1), 1.0) for t in range(4)]
    )
    lin_grad = 0.0
    first = spec_weight.shape[1] * LANES
    for t in range(4):
        lin_grad = lin_grad + spec_grads[t][:, first : first + C].astype(F32) * flips[t]
    step = 1
    while step < shards:
        lin_grad = lin_grad + swap(lin_grad, "dp", shards, step)
        step *= 2

    spec_out = adam_spec(flips, spec_grads, spec_weight, spec_first, spec_second)
    lin_out = adamw(lin_weight, lin_first, lin_second, lin_grad[None])
    input_grad = final_grads(ids, inv_all, cotangent, grad_parts[2:], (3,), inner[0])
    input_grad = final_grads(ids, inv_all, cotangent, grad_parts[:2], (1, 2), input_grad)
    return (output, input_grad, *spec_out, *lin_out)


def solution(mesh):
    fields = P("dp", "blade", None, None)
    spec = P("blade", "dp", None, None, None)
    lin = P("blade", None, None)
    return jax.shard_map(
        partial(body, mesh.shape["dp"]),
        mesh=mesh,
        in_specs=(fields, fields, P(), P("dp"), spec, spec, spec, lin, lin, lin),
        out_specs=(fields, fields, spec, spec, spec, lin, lin, lin),
        check_vma=False,
    )
```

```python
from functools import partial
import math

import jax
import jax.numpy as jnp
from jax import lax
from jax.experimental import pallas as pl
from jax.experimental.pallas import tpu as pltpu
from jax.sharding import PartitionSpec as P

GRID = 64
MSIDE = 16
NTAB = 16
STEP_COUNT = 5
NPIX = 4096
MODES = 256
C = 48
LANES = 2 * C
QUAD = 4
PACK = 128

BETA_ONE = 0.9
BETA_TWO = 0.999
EPSILON = 1e-08
RATE = 0.1
DECAY = 0.01

F32 = jnp.float32
BF16 = jnp.bfloat16
SMEM = pltpu.MemorySpace.SMEM


def sgn(left, right):
    return -1.0 if (left & 2) and (right & 1) else 1.0


def flip_of(own, k):
    if k & 1:
        return (1 - 2 * ((own // 2) % 2)).astype(F32)
    return jnp.float32(1.0)


def mode_factor(mode):
    return jnp.where(mode % MSIDE == 0, 1.0, 2.0).astype(F32)


def dot(left, right, dims=((1,), (0,))):
    return lax.dot_general(left, right, (dims, ((), ())), preferred_element_type=F32)


def whole(shape):
    zeros = (0,) * len(shape)
    return pl.BlockSpec(tuple(shape), lambda *_: zeros)


def params(mib):
    return pltpu.CompilerParams(vmem_limit_bytes=mib * 1024 * 1024)


def fast(shape, kind):
    return pltpu.VMEM(tuple(shape), kind)


def slow(shape, kind):
    return pltpu.HBM(tuple(shape), kind)


def pin(*arrays):
    return [pltpu.with_memory_space_constraint(array, pltpu.VMEM) for array in arrays]


def stay(*arrays):
    return [pltpu.with_memory_space_constraint(array, pltpu.HBM) for array in arrays]


def in_vmem(count):
    return [pl.BlockSpec(memory_space=pltpu.MemorySpace.VMEM)] * count


def cost():
    return pl.CostEstimate(flops=1, bytes_accessed=1, transcendentals=0)


def small_tables():
    mode_ids = jnp.arange(2 * MODES, dtype=jnp.int32)
    imag = mode_ids >= MODES
    mode_ids = mode_ids % MODES
    row_index = mode_ids // MSIDE
    col_freq = mode_ids % MSIDE
    row_freq = jnp.where(row_index < MSIDE // 2, row_index, GRID - MSIDE + row_index)
    place = jnp.arange(GRID, dtype=jnp.int32)[:, None]
    row_angle = ((place * row_freq[None, :]) % GRID).astype(F32) * (2.0 * math.pi / GRID)
    col_angle = ((place * col_freq[None, :]) % GRID).astype(F32) * (2.0 * math.pi / GRID)
    row_cos, row_sin = jnp.cos(row_angle) / GRID, jnp.sin(row_angle) / GRID
    first = jnp.where(imag[None, :], -row_sin, row_cos)
    second = jnp.where(imag[None, :], -row_cos, -row_sin)
    return jnp.stack([first, second, jnp.cos(col_angle), jnp.sin(col_angle)])


def table_rows(row_ref, col_ref, start, stop):
    tiles = []
    for h in range(start, stop):
        tile = row_ref[0, h : h + 1] * col_ref[0] + row_ref[1, h : h + 1] * col_ref[1]
        tiles.append(tile.astype(BF16))
    return jnp.concatenate(tiles, axis=0)


def small_specs(tile):
    n = 2 * MODES
    return [
        pl.BlockSpec((2, tile // GRID, n), lambda i, *_: (0, i, 0)),
        pl.BlockSpec((2, GRID, n), lambda i, *_: (1, 0, 0)),
    ]


def turned_kernel(row_ref, col_ref, ft_ref):
    for h in range(0, row_ref.shape[1], 2):
        tile = table_rows(row_ref, col_ref, h, h + 2)
        ft_ref[:, h * GRID : (h + 2) * GRID] = tile.astype(F32).T.astype(BF16)


def turned_table(small):
    rows = 8
    n = 2 * MODES
    return pl.pallas_call(
        turned_kernel,
        grid=(GRID // rows,),
        in_specs=small_specs(rows * GRID),
        out_specs=pl.BlockSpec((n, rows * GRID), lambda i: (0, i)),
        out_shape=slow((n, NPIX), BF16),
        compiler_params=params(28),
        cost_estimate=cost(),
        name="turned",
    )(*stay(small, small))


def pack_kernel(w_ref, l_ref, o_ref):
    def step(g, carry):
        parts = [w_ref[0, g * QUAD + q, r] for q in range(QUAD) for r in range(2)]
        at = pl.ds(pl.multiple_of(g * QUAD * LANES, PACK), QUAD * LANES)
        o_ref[:, at] = jnp.concatenate(parts, axis=1).astype(BF16)
        return carry

    modes = w_ref.shape[1]
    lax.fori_loop(0, modes // QUAD, step, 0)
    line = jnp.concatenate([l_ref[0], jnp.zeros((C, PACK - C), F32)], axis=1)
    o_ref[:, modes * LANES :] = line.astype(BF16)


def pack_weights(spec_weight, lin_weight):
    modes = spec_weight.shape[1]
    return pl.pallas_call(
        pack_kernel,
        in_specs=in_vmem(2),
        out_specs=in_vmem(1)[0],
        out_shape=jax.ShapeDtypeStruct((C, modes * LANES + PACK), BF16),
        compiler_params=params(28),
        cost_estimate=cost(),
        name="pack",
    )(spec_weight, lin_weight)


def lanes_of(shape):
    return lax.broadcasted_iota(jnp.int32, shape, len(shape) - 1)


def split_lanes(a, b, c):
    lane = lanes_of(a.shape)
    second = jnp.where(lane < 32, pltpu.roll(a, 32, 1), pltpu.roll(b, 32, 1))
    third = jnp.where(lane < 64, pltpu.roll(b, 64, 1), pltpu.roll(c, 64, 1))
    return a, second, third, pltpu.roll(c, 96, 1)


def join_lanes(first, second, third, fourth):
    lane = lanes_of(first.shape)
    a = jnp.where(lane < 96, first, pltpu.roll(second, 96, 1))
    b = jnp.where(lane < 64, pltpu.roll(second, 96, 1), pltpu.roll(third, 64, 1))
    c = jnp.where(lane < 32, pltpu.roll(third, 64, 1), pltpu.roll(fourth, 32, 1))
    return a, b, c


def quad_tiles(ref, g):
    tiles = []
    for n in range(3):
        at = pl.ds(pl.multiple_of(g * QUAD * LANES + n * PACK, PACK), PACK)
        tiles.append(ref[:, at])
    return tiles


def unpack_kernel(ids_ref, w0, w1, w2, w3, pq_ref):
    own = ids_ref[0]
    modes = pq_ref.shape[0]
    lane = lanes_of((C, PACK))
    flip = flip_of(own, 1)

    def step(g, carry):
        for t, w in enumerate((w0, w1, w2, w3)):
            slot = jnp.bitwise_xor(own, t)
            scale = jnp.where(slot % 2 == 1, flip, 1.0)
            at = pl.ds(pl.multiple_of(slot * PACK, PACK), PACK)
            tiles = [tile * scale.astype(BF16) for tile in quad_tiles(w, g)]
            for q, p in enumerate(split_lanes(*tiles)):
                low = jnp.where(lane < C, -pltpu.roll(p, PACK - C, 1), pltpu.roll(p, C, 1))
                pq_ref[g * QUAD + q, :C, at] = p
                pq_ref[g * QUAD + q, C:, at] = low
        return carry

    quads = modes // QUAD
    lax.fori_loop(0, quads, step, 0, unroll=min(4, quads))


def unpack(ids, packs):
    modes = (packs[0].shape[1] - PACK) // LANES
    return pl.pallas_call(
        unpack_kernel,
        in_specs=[pl.BlockSpec(memory_space=SMEM)] + in_vmem(4),
        out_specs=in_vmem(1)[0],
        out_shape=fast((modes, LANES, 4 * PACK), BF16),
        compiler_params=params(28),
        cost_estimate=cost(),
        name="unpack",
    )(*stay(ids, *packs))


def spread(acc, out_ref, scales=None):
    rows = []
    for n in range(acc.shape[0] // C):
        for r in range(2):
            row = acc[n * C : (n + 1) * C, r * MODES : (r + 1) * MODES]
            rows.append(row if scales is None else row * scales[n])
    extra = out_ref.shape[2] - len(rows) * C
    if extra:
        rows.append(jnp.zeros((extra, MODES), F32))
    turned = jnp.concatenate(rows, axis=0).T
    out_ref[...] = turned.reshape(out_ref.shape).astype(BF16)


def collect(block, ysc):
    turned = block[...].astype(F32).reshape(MODES, block.shape[2]).T
    for n in range(ysc.shape[0] // C):
        for r in range(2):
            row = (n * 2 + r) * C
            piece = turned[row : row + C].astype(BF16)
            ysc[n * C : (n + 1) * C, r * MODES : (r + 1) * MODES] = piece


def forward_kernel(ids_ref, inv_ref, *refs):
    x = refs[:-4]
    row_ref, col_ref, out_ref, acc = refs[-4:]
    i = pl.program_id(0)
    samples = x[0].shape[0]
    rows = [part[s, 0] for s in range(samples) for part in x]
    table = table_rows(row_ref, col_ref, 0, row_ref.shape[1])
    part = dot(jnp.concatenate(rows, axis=0), table)

    @pl.when(i == 0)
    def _():
        acc[...] = part

    @pl.when(i > 0)
    def _():
        acc[...] += part

    @pl.when(i == pl.num_programs(0) - 1)
    def _():
        spread(acc, out_ref, [inv_ref[s] for s in range(samples) for _ in x])


def forward_spectrum(ids, inv, x, small, shards):
    samples = inv.shape[0]
    modes = MODES // shards
    width = -(-samples * len(x) * LANES // PACK) * PACK
    n = 2 * MODES
    tile = 2048

    def spec(array):
        if array.shape[0] == samples:
            return pl.BlockSpec((samples, 1, C, tile), lambda i, ids, inv: (0, 0, 0, i))
        return pl.BlockSpec((samples, 1, C, tile), lambda i, ids, inv: (ids[0], 0, 0, i))

    return pl.pallas_call(
        forward_kernel,
        grid_spec=pltpu.PrefetchScalarGridSpec(
            num_scalar_prefetch=2,
            grid=(NPIX // tile,),
            in_specs=[spec(part) for part in x] + small_specs(tile),
            out_specs=whole((shards, modes, width)),
            scratch_shapes=[pltpu.VMEM((samples * len(x) * C, n), F32)],
        ),
        out_shape=slow((shards, modes, width), BF16),
        compiler_params=params(28),
        cost_estimate=cost(),
        name="forward",
    )(*stay(ids, inv, *x, small, small))


def row_scratch(modes, shards, width):
    return pltpu.VMEM((width // PACK, modes * shards, PACK), F32)


def gather_rows(blocks, sc):
    shards, modes = blocks[0].shape[:2]
    first = 0
    for block in blocks:
        for n in range(block.shape[2] // PACK):
            for x in range(shards):
                rows = block[x, :, n * PACK : (n + 1) * PACK].astype(F32)
                sc[first + n, pl.ds(x, modes, stride=shards), :] = rows
        first += block.shape[2] // PACK


def scatter_rows(ysc, out):
    shards, modes = out.shape[:2]
    for x in range(shards):
        for n in range(ysc.shape[0]):
            piece = ysc[n, pl.ds(x, modes, stride=shards), :]
            out[x, :, n * PACK : (n + 1) * PACK] = piece.astype(BF16)


def blade_rows(sc, mode, shards, groups):
    at = pl.ds(pl.multiple_of(mode * shards, shards), shards)
    found = [[] for _ in range(4)]
    for tile, pairs in groups:
        tiles = [sc[tile + n, at, :] for n in range(-(-len(pairs) * LANES // PACK))]
        pieces = split_lanes(tiles[0], tiles[min(1, len(tiles) - 1)], tiles[-1])
        for piece, (_, t) in zip(pieces, pairs):
            found[t].append(piece)
    return [jnp.concatenate(found[t], axis=0) for t in range(4)]


def groups_of(samples, *blades):
    groups = []
    tile = 0
    for some in blades:
        pairs = [(s, t) for s in range(samples) for t in some]
        for n in range(0, len(pairs), 4):
            part = pairs[n : n + 4]
            groups.append((tile, part))
            tile += -(-len(part) * LANES // PACK)
    return groups


EARLY = (0, 3)
LATE = (1, 2)


def mix_modes(xsc, ysc, pq_ref, groups, shards, first_mode, back):
    modes = xsc.shape[1] // shards
    samples = ysc.shape[0] // 3
    group = samples * shards

    def step(m, carry):
        low = jnp.concatenate(blade_rows(xsc, m, shards, groups), axis=0)
        low = low[:, :LANES].astype(BF16)
        total = [None] * 4
        parts = dot(low, pq_ref[m])
        for k in range(4):
            part = parts[:, k * PACK : (k + 1) * PACK]
            for t in range(4):
                u = t ^ k
                piece = part[t * group : (t + 1) * group]
                sign = sgn(u, k) if back else sgn(t, k)
                if total[u] is None:
                    total[u] = piece if sign > 0 else -piece
                else:
                    total[u] = total[u] + piece if sign > 0 else total[u] - piece
        factor = mode_factor(first_mode + m)
        at = pl.ds(pl.multiple_of(m * shards, shards), shards)
        for s in range(samples):
            rows = []
            for u in range(4):
                rows.append(total[u][s * shards : (s + 1) * shards] * factor)
            for n, tile in enumerate(join_lanes(*rows)):
                ysc[s * 3 + n, at, :] = tile
        return carry

    lax.fori_loop(0, modes, step, 0, unroll=min(32, modes))


def mix_kernel(ids_ref, xa, xb, pq_ref, y_ref, xsc, ysc):
    shards, modes, width = y_ref.shape
    gather_rows((xa, xb), xsc)
    groups = groups_of(width // (4 * LANES), EARLY, LATE)
    mix_modes(xsc, ysc, pq_ref, groups, shards, ids_ref[1] * modes, False)
    scatter_rows(ysc, y_ref)


def mix(ids, xa, xb, pq, samples):
    shards, modes = xa.shape[:2]
    width = samples * 4 * LANES
    return pl.pallas_call(
        mix_kernel,
        in_specs=[pl.BlockSpec(memory_space=SMEM)] + in_vmem(3),
        out_specs=in_vmem(1)[0],
        out_shape=slow((shards, modes, width), BF16),
        scratch_shapes=[
            row_scratch(modes, shards, xa.shape[2] + xb.shape[2]),
            row_scratch(modes, shards, width),
        ],
        compiler_params=params(28),
        cost_estimate=cost(),
        name="mix",
    )(*stay(ids, xa, xb), *pin(pq))


def mix_back_kernel(ids_ref, g_ref, pq_ref, out_ref, gsc, ysc):
    shards, modes, width = g_ref.shape
    gather_rows((g_ref,), gsc)
    groups = groups_of(width // (4 * LANES), range(4))
    mix_modes(gsc, ysc, pq_ref, groups, shards, ids_ref[1] * modes, True)
    scatter_rows(ysc, out_ref)


def mix_back(ids, g, pq):
    shards, modes, width = g.shape
    return pl.pallas_call(
        mix_back_kernel,
        in_specs=[pl.BlockSpec(memory_space=SMEM)] + in_vmem(2),
        out_specs=in_vmem(1)[0],
        out_shape=slow(g.shape, BF16),
        scratch_shapes=[row_scratch(modes, shards, width)] * 2,
        compiler_params=params(28),
        cost_estimate=cost(),
        name="mix_back",
    )(*stay(ids), g, *pin(pq))


def turn_kernel(ids_ref, pq_ref, xa, xb, l0, l1, l2, l3, out_ref, xt_ref, lt_ref, lb_ref, held, xsc, lsc):
    shards, modes = xa.shape[:2]
    samples = xt_ref.shape[2] // (8 * shards)
    groups = groups_of(samples, EARLY, LATE)
    shape = (LANES, LANES)
    diagonal = lax.broadcasted_iota(jnp.int32, shape, 0) == lax.broadcasted_iota(jnp.int32, shape, 1)
    unit = jnp.where(diagonal, 1.0, 0.0).astype(BF16)
    gather_rows((xa, xb), xsc)

    def step(m, carry):
        for k in range(4):
            at = slice(k * PACK, k * PACK + LANES)
            held[m, :, at] = dot(unit, pq_ref[m, :, at], ((1,), (1,))).astype(BF16)
        x = blade_rows(xsc, m, shards, groups)
        x = x + [pltpu.roll(rows, PACK - C, 1) for rows in x]
        xt_ref[m] = jnp.concatenate(x, axis=0).T[:C].astype(BF16)
        return carry

    lax.fori_loop(0, modes, step, 0, unroll=min(16, modes))
    out_ref[...] = held[...]
    own = ids_ref[0]
    for t, line in enumerate((l0, l1, l2, l3)):
        slot = jnp.bitwise_xor(own, t)
        lsc[slot] = line[...].astype(F32) * jnp.where(slot % 2 == 1, flip_of(own, 1), 1.0)
    for k in range(4):
        line = lsc[k]
        turned = line.T
        for t in range(4):
            u = t ^ k
            lb_ref[t * C : (t + 1) * C, u * C : (u + 1) * C] = (line[:, :C] * sgn(t, k)).astype(BF16)
            lt_ref[u * C : (u + 1) * C, t * C : (t + 1) * C] = (turned[:C] * sgn(t, k)).astype(BF16)


def turn(ids, pq, xa, xb, packs, samples):
    shards, modes = xa.shape[:2]
    last = packs[0].shape[1] // PACK - 1
    shape = (4 * C, 4 * C)
    turned_shape = (modes, C, 8 * samples * shards)
    return pl.pallas_call(
        turn_kernel,
        grid=(1,),
        in_specs=[pl.BlockSpec(memory_space=SMEM), whole(pq.shape), whole(xa.shape), whole(xb.shape)]
        + [pl.BlockSpec((C, PACK), lambda i: (0, last))] * 4,
        out_specs=[whole(pq.shape), whole(turned_shape)] + [whole(shape)] * 2,
        out_shape=[fast(pq.shape, BF16), slow(turned_shape, BF16)] + [slow(shape, BF16)] * 2,
        input_output_aliases={1: 0},
        scratch_shapes=[
            pltpu.VMEM(pq.shape, BF16),
            row_scratch(modes, shards, xa.shape[2] + xb.shape[2]),
            pltpu.VMEM((4, C, PACK), F32),
        ],
        compiler_params=params(28),
        cost_estimate=cost(),
        name="turn",
    )(*stay(ids), *pin(pq), *stay(xa, xb, *packs))


def grad_kernel(ids_ref, xt_ref, g_ref, lin_ref, o0, o1, o2, o3, gsc, osc):
    shards, modes, width = g_ref.shape
    samples = width // (4 * LANES)
    own = ids_ref[0]
    first_mode = ids_ref[1] * modes
    groups = groups_of(samples, range(4))
    gather_rows((g_ref,), gsc)
    lane = lanes_of((samples * shards, PACK))

    def step(g, carry):
        found = [[] for _ in range(4)]
        for q in range(QUAD):
            m = g * QUAD + q
            factor = mode_factor(first_mode + m)
            plain = [rows * factor for rows in blade_rows(gsc, m, shards, groups)]
            turned = [
                jnp.where(lane < C, pltpu.roll(rows, PACK - C, 1), -pltpu.roll(rows, C, 1))
                for rows in plain
            ]
            plus = [rows.astype(BF16) for rows in plain + turned]
            minus = [(-rows).astype(BF16) for rows in plain + turned]
            right = []
            for k in range(4):
                rows = []
                for r in range(2):
                    for t in range(4):
                        rows.append((plus if sgn(t, k) > 0 else minus)[4 * r + (t ^ k)])
                right.append(jnp.concatenate(rows, axis=0))
            grad = dot(xt_ref[m], jnp.concatenate(right, axis=1))
            for k in range(4):
                found[k].append(grad[:, k * PACK : (k + 1) * PACK])
        for k in range(4):
            for n, tile in enumerate(join_lanes(*found[k])):
                at = pl.ds(pl.multiple_of(g * QUAD * LANES + n * PACK, PACK), PACK)
                osc[k, :, at] = tile.astype(BF16)
        return carry

    quads = modes // QUAD
    lax.fori_loop(0, quads, step, 0, unroll=min(2, quads))
    for k in range(4):
        line = jnp.concatenate([lin_ref[k], jnp.zeros((C, PACK - C), F32)], axis=1)
        osc[k, :, modes * LANES :] = line.astype(BF16)
    for t, out in enumerate((o0, o1, o2, o3)):
        out[...] = osc[jnp.bitwise_xor(own, t)]


def weight_grads(ids, xt, g, lin):
    shards, modes, width = g.shape
    shape = (C, modes * LANES + PACK)
    return pl.pallas_call(
        grad_kernel,
        in_specs=[pl.BlockSpec(memory_space=SMEM)] + in_vmem(3),
        out_specs=in_vmem(4),
        out_shape=[slow(shape, BF16)] * 4,
        scratch_shapes=[row_scratch(modes, shards, width), pltpu.VMEM((4,) + shape, BF16)],
        compiler_params=params(28),
        cost_estimate=cost(),
        name="weight_grads",
    )(*stay(ids, xt), g, *stay(lin))


CDF_AT = 0.28
CDF = (0.11652094, 0.06749571, 0.2689128, -0.23699677, 0.38987606, -0.10580875)
SERIES = [value / CDF_AT ** (i + 1) for i, value in enumerate(CDF)]


def gelu_parts(v):
    z = jnp.abs(v)
    t = 1.0 / (z + 1.0 / CDF_AT)
    bell = jnp.exp2(v * v * (-0.5 * math.log2(math.e)))
    series = jnp.float32(SERIES[-1])
    for value in SERIES[-2::-1]:
        series = series * t + value
    tail = series * t * bell
    cdf = jnp.where(v < 0.0, tail, 1.0 - tail)
    return v * cdf, cdf + v * (bell * (1.0 / math.sqrt(2.0 * math.pi)))


def pixel_kernel(ids_ref, inv_ref, *refs):
    x = refs[:4]
    y_ref, ft_ref, lt_ref = refs[4:7]
    outs = refs[8:12]
    slope_ref = refs[12]
    left, ysc, even, odd = refs[14:]
    samples = x[1].shape[0]
    rows = 4 * C
    n = 2 * MODES
    width = even.shape[1]

    @pl.when(pl.program_id(0) == 0)
    def _():
        collect(y_ref, ysc)
        for s in range(samples):
            left[s, :, :n] = ysc[s * rows : (s + 1) * rows]
            left[s, :, n:] = (lt_ref[...].astype(F32) * inv_ref[s]).astype(BF16)

    def product(s, at, pre):
        fields = [x[t][s, 0, :, at] for t in range(4)]
        pre[...] = dot(left[s], jnp.concatenate([ft_ref[:, at]] + fields, axis=0))

    def activate(s, at, pre):
        for t in range(4):
            value, slope = gelu_parts(pre[t * C : (t + 1) * C])
            normed = x[t][s, 0, :, at].astype(F32) * inv_ref[s]
            outs[t][s, 0, :, at] = (normed + value).astype(BF16)
            row = s * rows + t * C
            slope_ref[row : row + C, at] = slope.astype(BF16)

    tile = ft_ref.shape[1]
    blocks = [(s, slice(k, k + width)) for k in range(0, tile, width) for s in range(samples)]
    buffers = [even, odd]
    product(*blocks[0], buffers[0])
    for k, block in enumerate(blocks):
        if k + 1 < len(blocks):
            product(*blocks[k + 1], buffers[(k + 1) % 2])
        activate(*block, buffers[k % 2])


def pixels(ids, inv, x, y, turned, lt, pq):
    samples = inv.shape[0]
    n = 2 * MODES
    tile = 1024
    mine = pl.BlockSpec((samples, 1, C, tile), lambda i, ids, inv: (ids[0], 0, 0, i))
    block = pl.BlockSpec((samples, 1, C, tile), lambda i, ids, inv: (0, 0, 0, i))
    rows = samples * 4 * C
    flat = pl.BlockSpec((rows, tile), lambda i, ids, inv: (0, i))
    return pl.pallas_call(
        pixel_kernel,
        grid_spec=pltpu.PrefetchScalarGridSpec(
            num_scalar_prefetch=2,
            grid=(NPIX // tile,),
            in_specs=[mine]
            + [block] * 3
            + [
                whole(y.shape),
                pl.BlockSpec((n, tile), lambda i, ids, inv: (0, i)),
                whole((4 * C, 4 * C)),
                pl.BlockSpec(memory_space=pl.ANY),
            ],
            out_specs=[mine] + [block] * 3 + [flat, pl.BlockSpec(memory_space=pl.ANY)],
            scratch_shapes=[
                pltpu.VMEM((samples, 4 * C, n + 4 * C), BF16),
                pltpu.VMEM((rows, n), BF16),
                pltpu.VMEM((4 * C, 256), F32),
                pltpu.VMEM((4 * C, 256), F32),
            ],
        ),
        out_shape=[slow(x[0].shape, BF16)]
        + [slow((samples, 1, C, NPIX), BF16)] * 3
        + [fast((rows, NPIX), BF16), fast(pq.shape, BF16)],
        input_output_aliases={9: 5},
        compiler_params=params(28),
        cost_estimate=cost(),
        name="pixels",
    )(*stay(ids, inv, *x), y, *stay(turned, lt), *pin(pq))


def slope_kernel(ids_ref, *refs):
    cot = refs[:4]
    slope, row_ref, col_ref, _, g_ref, g_out, _, gacc = refs[4:]
    samples = cot[1].shape[0]
    rows = 4 * C
    i = pl.program_id(0)

    @pl.when(i == 0)
    def _():
        gacc[...] = jnp.zeros_like(gacc)

    for s in range(samples):
        for t in range(4):
            at = s * rows + t * C
            grad = cot[t][s, 0].astype(F32) * slope[at : at + C].astype(F32)
            g_ref[at : at + C] = grad.astype(BF16)
    table = table_rows(row_ref, col_ref, 0, row_ref.shape[1])
    gacc[...] += dot(g_ref[...], table)

    @pl.when(i == pl.num_programs(0) - 1)
    def _():
        spread(gacc, g_out)


def pixel_grads(ids, cot, slope, small, spectrum, pq):
    rows = slope.shape[0]
    samples = rows // (4 * C)
    n = 2 * MODES
    tile = 2048
    mine = pl.BlockSpec((samples, 1, C, tile), lambda i, ids: (ids[0], 0, 0, i))
    block = pl.BlockSpec((samples, 1, C, tile), lambda i, ids: (0, 0, 0, i))
    flat = pl.BlockSpec((rows, tile), lambda i, ids: (0, i))
    kept = pl.BlockSpec(memory_space=pl.ANY)
    return pl.pallas_call(
        slope_kernel,
        grid_spec=pltpu.PrefetchScalarGridSpec(
            num_scalar_prefetch=1,
            grid=(NPIX // tile,),
            in_specs=[mine] + [block] * 3 + [flat] + small_specs(tile) + [kept],
            out_specs=[flat, whole(spectrum), kept],
            scratch_shapes=[pltpu.VMEM((rows, n), F32)],
        ),
        out_shape=[slow((rows, NPIX), BF16), slow(spectrum, BF16), fast(pq.shape, BF16)],
        input_output_aliases={8: 2},
        compiler_params=params(28),
        cost_estimate=cost(),
        name="pixel_grads",
    )(*stay(ids, *cot), *pin(slope), *stay(small, small), *pin(pq))


def lin_kernel(ids_ref, inv_ref, *refs):
    x = refs[:4]
    g_ref, lb_ref, lin_ref, back_ref, lacc = refs[4:]
    samples = x[1].shape[0]
    rows = 4 * C

    @pl.when(pl.program_id(0) == 0)
    def _():
        lacc[...] = jnp.zeros_like(lacc)

    for s in range(samples):
        fields = jnp.concatenate([x[t][s, 0] for t in range(4)], axis=0)
        g = g_ref[s * rows : (s + 1) * rows]
        lacc[...] += dot(fields, g, ((1,), (1,))) * inv_ref[s]
        back_ref[s * rows : (s + 1) * rows] = dot(lb_ref[...], g).astype(BF16)

    @pl.when(pl.program_id(0) == pl.num_programs(0) - 1)
    def _():
        for k in range(4):
            total = None
            for t in range(4):
                u = t ^ k
                piece = lacc[t * C : (t + 1) * C, u * C : (u + 1) * C] * sgn(t, k)
                total = piece if total is None else total + piece
            lin_ref[k] = total


def lin_grads(ids, inv, x, g, lb):
    rows = g.shape[0]
    samples = rows // (4 * C)
    tile = 2048
    mine = pl.BlockSpec((samples, 1, C, tile), lambda i, ids, inv: (ids[0], 0, 0, i))
    block = pl.BlockSpec((samples, 1, C, tile), lambda i, ids, inv: (0, 0, 0, i))
    flat = pl.BlockSpec((rows, tile), lambda i, ids, inv: (0, i))
    return pl.pallas_call(
        lin_kernel,
        grid_spec=pltpu.PrefetchScalarGridSpec(
            num_scalar_prefetch=2,
            grid=(NPIX // tile,),
            in_specs=[mine] + [block] * 3 + [flat, whole((4 * C, 4 * C))],
            out_specs=[whole((4, C, C)), flat],
            scratch_shapes=[pltpu.VMEM((4 * C, 4 * C), F32)],
        ),
        out_shape=[slow((4, C, C), F32), slow(g.shape, BF16)],
        compiler_params=params(28),
        cost_estimate=cost(),
        name="lin_grads",
    )(*stay(ids, inv, *x, g, lb))


def inner_kernel(ids_ref, inv_ref, y_ref, back_ref, row_ref, col_ref, cot_ref, mine_ref, *refs):
    o1, o2, o3, ysc = refs
    samples = cot_ref.shape[0]
    rows = 4 * C

    @pl.when(pl.program_id(0) == 0)
    def _():
        collect(y_ref, ysc)

    table = table_rows(row_ref, col_ref, 0, row_ref.shape[1])
    spatial = dot(ysc[...], table, ((1,), (1,)))
    for s in range(samples):
        at = slice(s * rows, (s + 1) * rows)
        total = spatial[at] + back_ref[at].astype(F32)
        mine_ref[s, 0] = (cot_ref[s, 0].astype(F32) + total[:C]) * inv_ref[s]
        for t, out in ((1, o1), (2, o2), (3, o3)):
            out[s, 0] = total[t * C : (t + 1) * C].astype(BF16)


def inner_grads(ids, inv, y, back, small, cotangent):
    samples = inv.shape[0]
    n = 2 * MODES
    tile = 2048
    rows = samples * 4 * C
    mine = pl.BlockSpec((samples, 1, C, tile), lambda i, ids, inv: (ids[0], 0, 0, i))
    block = pl.BlockSpec((samples, 1, C, tile), lambda i, ids, inv: (0, 0, 0, i))
    return pl.pallas_call(
        inner_kernel,
        grid_spec=pltpu.PrefetchScalarGridSpec(
            num_scalar_prefetch=2,
            grid=(NPIX // tile,),
            in_specs=[
                whole(y.shape),
                pl.BlockSpec((rows, tile), lambda i, ids, inv: (0, i)),
                *small_specs(tile),
                mine,
            ],
            out_specs=[mine] + [block] * 3,
            scratch_shapes=[pltpu.VMEM((rows, n), BF16)],
        ),
        out_shape=[slow(cotangent.shape, F32)] + [slow((samples, 1, C, NPIX), BF16)] * 3,
        compiler_params=params(28),
        cost_estimate=cost(),
        name="inner_grads",
    )(*stay(ids, inv), y, *stay(back, small, small, cotangent))


def place_kernel(ids_ref, a_ref, b_ref, c_ref, old_ref, out_ref):
    for n, part in enumerate((a_ref, b_ref, c_ref)):

        @pl.when(pl.program_id(0) == n)
        def _():
            out_ref[...] = part[...]


def place_output(ids, parts, result):
    samples = parts[0].shape[0]
    shape = (1, 1, C, NPIX)

    def spec(n):
        def at(j, s, ids):
            return (jnp.where(j == n, s, jnp.where(j < n, 0, samples - 1)), 0, 0, 0)

        return pl.BlockSpec(shape, at)

    return pl.pallas_call(
        place_kernel,
        grid_spec=pltpu.PrefetchScalarGridSpec(
            num_scalar_prefetch=1,
            grid=(3, samples),
            in_specs=[spec(0), spec(1), spec(2), pl.BlockSpec(memory_space=pl.ANY)],
            out_specs=pl.BlockSpec(
                shape, lambda j, s, ids: (jnp.bitwise_xor(ids[0], j + 1) * samples + s, 0, 0, 0)
            ),
        ),
        out_shape=jax.ShapeDtypeStruct(result.shape, BF16),
        input_output_aliases={4: 0},
        compiler_params=params(28),
        cost_estimate=cost(),
        name="place",
    )(ids, *parts, result)


def final_kernel(count, codes, ids_ref, inv_ref, cot_ref, *refs):
    samples = pl.num_programs(1)
    j = pl.program_id(0)
    for n in range(count):

        @pl.when(j == n)
        def _():
            inv = inv_ref[jnp.bitwise_xor(ids_ref[0], codes[n]) * samples + pl.program_id(1)]
            refs[-1][...] = (cot_ref[...].astype(F32) + refs[n][...].astype(F32)) * inv


def final_grads(ids, inv, cotangent, parts, codes, result):
    samples = parts[0].shape[0]
    count = len(parts)
    shape = (1, 1, C, NPIX)

    def code(j):
        value = codes[0]
        for n in range(1, count):
            value = jnp.where(j == n, codes[n], value)
        return value

    def spec(n):
        def at(j, s, ids, inv):
            return (jnp.where(j == n, s, jnp.where(j < n, 0, samples - 1)), 0, 0, 0)

        return pl.BlockSpec(shape, at)

    place = pl.BlockSpec(
        shape, lambda j, s, ids, inv: (jnp.bitwise_xor(ids[0], code(j)) * samples + s, 0, 0, 0)
    )
    return pl.pallas_call(
        partial(final_kernel, count, codes),
        grid_spec=pltpu.PrefetchScalarGridSpec(
            num_scalar_prefetch=2,
            grid=(count, samples),
            in_specs=[place]
            + [spec(n) for n in range(count)]
            + [pl.BlockSpec(memory_space=pl.ANY)],
            out_specs=place,
        ),
        out_shape=jax.ShapeDtypeStruct(cotangent.shape, F32),
        input_output_aliases={3 + count: 0},
        compiler_params=params(28),
        cost_estimate=cost(),
        name="final",
    )(ids, inv, cotangent, *parts, result)


def adamw(weight, first, second, grad):
    first_new = BETA_ONE * first + (1.0 - BETA_ONE) * grad
    second_new = BETA_TWO * second + (1.0 - BETA_TWO) * grad * grad
    corr_one = 1.0 - BETA_ONE**STEP_COUNT
    corr_two = 1.0 - BETA_TWO**STEP_COUNT
    update = first_new / corr_one / (jnp.sqrt(second_new / corr_two) + EPSILON)
    return (weight - RATE * (update + DECAY * weight), first_new, second_new)


def adam_kernel(flips, d0, d1, d2, d3, w_ref, first_ref, second_ref, w_out, first_out, second_out):
    grad = d0[...].astype(F32) * flips[0]
    for t, d in ((1, d1), (2, d2), (3, d3)):
        grad = grad + d[...].astype(F32) * flips[t]
    for q in range(w_ref.shape[1]):
        for r in range(2):
            lane = q * LANES + r * C
            at = (0, q, r)
            new = adamw(w_ref[at], first_ref[at], second_ref[at], grad[:, lane : lane + C])
            w_out[at], first_out[at], second_out[at] = new


def adam_spec(flips, grads, weight, first, second):
    modes = weight.shape[1]
    part = min(modes, 4 * QUAD)
    packed = pl.BlockSpec((C, part * LANES), lambda g: (0, g))
    block = pl.BlockSpec((1, part, 2, C, C), lambda g: (0, g, 0, 0, 0))
    return pl.pallas_call(
        adam_kernel,
        grid=(modes // part,),
        in_specs=[pl.BlockSpec(memory_space=SMEM)] + [packed] * 4 + [block] * 3,
        out_specs=[block] * 3,
        out_shape=[jax.ShapeDtypeStruct(weight.shape, F32)] * 3,
        compiler_params=params(28),
        cost_estimate=cost(),
        name="adam",
    )(flips, *grads, weight, first, second)


def swap(value, axis, size, x):
    return lax.ppermute(value, axis, [(i, i ^ x) for i in range(size)])


def to_modes(value):
    return lax.all_to_all(value, "dp", split_axis=0, concat_axis=0, tiled=True)


def after(values, first):
    values, _ = lax.optimization_barrier((values, first))
    return values


def body(
    shards,
    inputs,
    cotangent,
    norm_table,
    sample_index,
    spec_weight,
    spec_first,
    spec_second,
    lin_weight,
    lin_first,
    lin_second,
):
    own = lax.axis_index("blade")
    shard = lax.axis_index("dp")
    ids = jnp.stack([own, shard]).astype(jnp.int32)
    samples = inputs.shape[0] // 4

    def cut(array, t):
        return lax.dynamic_slice_in_dim(array, jnp.bitwise_xor(own, t) * samples, samples, 0)

    def send(array, t):
        block = cut(array, t)
        return block, swap(block, "blade", 4, t)

    sent, x3 = send(inputs, 3)
    rest = after(inputs, sent)
    sent, x1 = send(rest, 1)
    rest = after(rest, sent)
    _, x2 = send(rest, 2)

    matches = sample_index[:, None] == jnp.arange(NTAB, dtype=jnp.int32)[None, :]
    normalizer = jnp.sum(jnp.where(matches, norm_table[None, :], 0.0), axis=1)
    inv_all = 1.0 / normalizer
    inv = lax.dynamic_slice_in_dim(inv_all, own * samples, samples, 0)

    small = lax.optimization_barrier(small_tables())
    turned = turned_table(small)
    packed = pack_weights(spec_weight, lin_weight)
    packs = [packed] + [swap(packed, "blade", 4, t) for t in (1, 2, 3)]

    x3 = after(x3, (packed, turned))
    sent = forward_spectrum(ids, inv, (inputs, x3), small, shards)
    x1, x2 = after((x1, x2), sent)
    xa = to_modes(sent)
    blocks = after([cut(cotangent, t) for t in (1, 2, 3)], (x1, x2))
    cot = (cotangent,) + tuple(swap(blocks[t - 1], "blade", 4, t) for t in (1, 2, 3))
    xb = to_modes(forward_spectrum(ids, inv, (x1, x2), small, shards))
    pq = unpack(ids, packs)
    mixed = mix(ids, xa, xb, pq, samples)
    pq, xt, lt, lb = turn(ids, after(pq, mixed), xa, xb, packs, samples)
    y = to_modes(mixed)

    x = (inputs, x1, x2, x3)
    result = pixels(ids, inv, x, y, turned, lt, pq)
    output, slope, pq = result[0], result[4], result[5]
    last, cot = lax.optimization_barrier((result[3], cot))
    parts = (result[1], result[2], last)
    out_parts = [swap(parts[t - 1], "blade", 4, t) for t in (1, 2, 3)]

    grad_pre, sent, pq = pixel_grads(ids, cot, slope, small, y.shape, pq)
    lin, from_lin = lin_grads(ids, inv, x, grad_pre, lb)
    g = after(to_modes(sent), (out_parts[2], xt, pq, lin))
    mixed = mix_back(ids, g, pq)
    back = to_modes(mixed)
    spec_grads = weight_grads(ids, xt, g, lin)
    spec_grads = [spec_grads[0]] + [swap(spec_grads[t], "blade", 4, t) for t in (1, 2, 3)]

    inner = inner_grads(ids, inv, back, from_lin, small, cotangent)
    inner = after(inner, out_parts)
    grad_parts = [swap(inner[t], "blade", 4, t) for t in (1, 2, 3)]

    output = place_output(ids, out_parts, output)
    spec_grads = after(spec_grads, output)
    flips = jnp.stack(
        [jnp.where(own % 2 == 1, flip_of(jnp.bitwise_xor(own, t), 1), 1.0) for t in range(4)]
    )
    lin_grad = 0.0
    first = spec_weight.shape[1] * LANES
    for t in range(4):
        lin_grad = lin_grad + spec_grads[t][:, first : first + C].astype(F32) * flips[t]
    step = 1
    while step < shards:
        lin_grad = lin_grad + swap(lin_grad, "dp", shards, step)
        step *= 2

    spec_out = adam_spec(flips, spec_grads, spec_weight, spec_first, spec_second)
    lin_out = adamw(lin_weight, lin_first, lin_second, lin_grad[None])
    input_grad = final_grads(ids, inv_all, cotangent, grad_parts[2:], (3,), inner[0])
    input_grad = final_grads(ids, inv_all, cotangent, grad_parts[:2], (1, 2), input_grad)
    return (output, input_grad, *spec_out, *lin_out)


def solution(mesh):
    fields = P("dp", "blade", None, None)
    spec = P("blade", "dp", None, None, None)
    lin = P("blade", None, None)
    return jax.shard_map(
        partial(body, mesh.shape["dp"]),
        mesh=mesh,
        in_specs=(fields, fields, P(), P("dp"), spec, spec, spec, lin, lin, lin),
        out_specs=(fields, fields, spec, spec, spec, lin, lin, lin),
        check_vma=False,
    )
```

```python
from functools import partial
import math

import jax
import jax.numpy as jnp
from jax import lax
from jax.experimental import pallas as pl
from jax.experimental.pallas import tpu as pltpu
from jax.sharding import PartitionSpec as P

GRID = 64
MSIDE = 16
NTAB = 16
STEP_COUNT = 5
NPIX = 4096
MODES = 256
C = 48
LANES = 2 * C
QUAD = 4
PACK = 128

BETA_ONE = 0.9
BETA_TWO = 0.999
EPSILON = 1e-08
RATE = 0.1
DECAY = 0.01

F32 = jnp.float32
BF16 = jnp.bfloat16
SMEM = pltpu.MemorySpace.SMEM


def sgn(left, right):
    return -1.0 if (left & 2) and (right & 1) else 1.0


def flip_of(own, k):
    if k & 1:
        return (1 - 2 * ((own // 2) % 2)).astype(F32)
    return jnp.float32(1.0)


def mode_factor(mode):
    return jnp.where(mode % MSIDE == 0, 1.0, 2.0).astype(F32)


def dot(left, right, dims=((1,), (0,))):
    return lax.dot_general(left, right, (dims, ((), ())), preferred_element_type=F32)


def whole(shape):
    zeros = (0,) * len(shape)
    return pl.BlockSpec(tuple(shape), lambda *_: zeros)


def params(mib):
    return pltpu.CompilerParams(vmem_limit_bytes=mib * 1024 * 1024)


def fast(shape, kind):
    return pltpu.VMEM(tuple(shape), kind)


def slow(shape, kind):
    return pltpu.HBM(tuple(shape), kind)


def pin(*arrays):
    return [pltpu.with_memory_space_constraint(array, pltpu.VMEM) for array in arrays]


def stay(*arrays):
    return [pltpu.with_memory_space_constraint(array, pltpu.HBM) for array in arrays]


def in_vmem(count):
    return [pl.BlockSpec(memory_space=pltpu.MemorySpace.VMEM)] * count


def cost():
    return pl.CostEstimate(flops=1, bytes_accessed=1, transcendentals=0)


def small_tables():
    mode_ids = jnp.arange(2 * MODES, dtype=jnp.int32)
    imag = mode_ids >= MODES
    mode_ids = mode_ids % MODES
    row_index = mode_ids // MSIDE
    col_freq = mode_ids % MSIDE
    row_freq = jnp.where(row_index < MSIDE // 2, row_index, GRID - MSIDE + row_index)
    place = jnp.arange(GRID, dtype=jnp.int32)[:, None]
    row_angle = ((place * row_freq[None, :]) % GRID).astype(F32) * (2.0 * math.pi / GRID)
    col_angle = ((place * col_freq[None, :]) % GRID).astype(F32) * (2.0 * math.pi / GRID)
    row_cos, row_sin = jnp.cos(row_angle) / GRID, jnp.sin(row_angle) / GRID
    first = jnp.where(imag[None, :], -row_sin, row_cos)
    second = jnp.where(imag[None, :], -row_cos, -row_sin)
    return jnp.stack([first, second, jnp.cos(col_angle), jnp.sin(col_angle)])


def table_rows(row_ref, col_ref, start, stop):
    tiles = []
    for h in range(start, stop):
        tile = row_ref[0, h : h + 1] * col_ref[0] + row_ref[1, h : h + 1] * col_ref[1]
        tiles.append(tile.astype(BF16))
    return jnp.concatenate(tiles, axis=0)


def small_specs(tile):
    n = 2 * MODES
    return [
        pl.BlockSpec((2, tile // GRID, n), lambda i, *_: (0, i, 0)),
        pl.BlockSpec((2, GRID, n), lambda i, *_: (1, 0, 0)),
    ]


def turned_kernel(row_ref, col_ref, ft_ref):
    for h in range(0, row_ref.shape[1], 2):
        tile = table_rows(row_ref, col_ref, h, h + 2)
        ft_ref[:, h * GRID : (h + 2) * GRID] = tile.astype(F32).T.astype(BF16)


def turned_table(small):
    rows = 8
    n = 2 * MODES
    return pl.pallas_call(
        turned_kernel,
        grid=(GRID // rows,),
        in_specs=small_specs(rows * GRID),
        out_specs=pl.BlockSpec((n, rows * GRID), lambda i: (0, i)),
        out_shape=slow((n, NPIX), BF16),
        compiler_params=params(28),
        cost_estimate=cost(),
        name="turned",
    )(*stay(small, small))


def pack_kernel(w_ref, l_ref, o_ref):
    def step(g, carry):
        rest = jnp.zeros((C, PACK - LANES), F32)
        pieces = []
        for q in range(QUAD):
            parts = [w_ref[0, g * QUAD + q, 0], w_ref[0, g * QUAD + q, 1], rest]
            pieces.append(jnp.concatenate(parts, axis=1))
        for n, tile in enumerate(join_lanes(*pieces)):
            at = pl.ds(pl.multiple_of(g * QUAD * LANES + n * PACK, PACK), PACK)
            o_ref[:, at] = tile.astype(BF16)
        return carry

    modes = w_ref.shape[1]
    lax.fori_loop(0, modes // QUAD, step, 0)
    line = jnp.concatenate([l_ref[0], jnp.zeros((C, PACK - C), F32)], axis=1)
    o_ref[:, modes * LANES :] = line.astype(BF16)


def pack_weights(spec_weight, lin_weight):
    modes = spec_weight.shape[1]
    return pl.pallas_call(
        pack_kernel,
        in_specs=in_vmem(2),
        out_specs=in_vmem(1)[0],
        out_shape=jax.ShapeDtypeStruct((C, modes * LANES + PACK), BF16),
        compiler_params=params(28),
        cost_estimate=cost(),
        name="pack",
    )(spec_weight, lin_weight)


def lanes_of(shape):
    return lax.broadcasted_iota(jnp.int32, shape, len(shape) - 1)


def split_lanes(a, b, c):
    lane = lanes_of(a.shape)
    last = jnp.where(lane < 64, pltpu.roll(b, 64, 1), pltpu.roll(c, 96, 1))
    return a, b, c, jnp.where(lane < 32, pltpu.roll(a, 32, 1), last)


def join_lanes(first, second, third, fourth):
    near = lanes_of(first.shape) < LANES
    a = jnp.where(near, first, pltpu.roll(fourth, 96, 1))
    b = jnp.where(near, second, pltpu.roll(fourth, 64, 1))
    c = jnp.where(near, third, pltpu.roll(fourth, 32, 1))
    return a, b, c


def quad_tiles(ref, g):
    tiles = []
    for n in range(3):
        at = pl.ds(pl.multiple_of(g * QUAD * LANES + n * PACK, PACK), PACK)
        tiles.append(ref[:, at])
    return tiles


def unpack_kernel(ids_ref, w0, w1, w2, w3, pq_ref):
    own = ids_ref[0]
    modes = pq_ref.shape[0]
    lane = lanes_of((C, PACK))
    flip = flip_of(own, 1)

    def step(g, carry):
        for t, w in enumerate((w0, w1, w2, w3)):
            slot = jnp.bitwise_xor(own, t)
            scale = jnp.where(slot % 2 == 1, flip, 1.0)
            at = pl.ds(pl.multiple_of(slot * PACK, PACK), PACK)
            tiles = [tile * scale.astype(BF16) for tile in quad_tiles(w, g)]
            for q, p in enumerate(split_lanes(*tiles)):
                low = jnp.where(lane < C, -pltpu.roll(p, PACK - C, 1), pltpu.roll(p, C, 1))
                pq_ref[g * QUAD + q, :C, at] = p
                pq_ref[g * QUAD + q, C:, at] = low
        return carry

    quads = modes // QUAD
    lax.fori_loop(0, quads, step, 0, unroll=min(4, quads))


def unpack(ids, packs):
    modes = (packs[0].shape[1] - PACK) // LANES
    return pl.pallas_call(
        unpack_kernel,
        in_specs=[pl.BlockSpec(memory_space=SMEM)] + in_vmem(4),
        out_specs=in_vmem(1)[0],
        out_shape=fast((modes, LANES, 4 * PACK), BF16),
        compiler_params=params(28),
        cost_estimate=cost(),
        name="unpack",
    )(*stay(ids, *packs))


def spread(acc, out_ref, scales=None):
    def piece(n):
        parts = [acc[n * C : (n + 1) * C, r * MODES : (r + 1) * MODES] for r in range(2)]
        row = jnp.concatenate(parts, axis=0)
        return row if scales is None else row * scales[n]

    rows = []
    third = LANES // 3
    for n in range(0, acc.shape[0] // C, 4):
        last = piece(n + 3)
        for k in range(3):
            rows += [piece(n + k), last[k * third : (k + 1) * third]]
    turned = jnp.concatenate(rows, axis=0).T
    out_ref[...] = turned.reshape(out_ref.shape).astype(BF16)


def collect(block, ysc):
    turned = block[...].astype(F32).reshape(MODES, block.shape[2]).T
    for n in range(0, ysc.shape[0] // C, 4):
        tiles = [turned[(n // 4 * 3 + k) * PACK :][:PACK] for k in range(3)]
        pieces = [tile[:LANES] for tile in tiles]
        pieces.append(jnp.concatenate([tile[LANES:] for tile in tiles], axis=0))
        for k, piece in enumerate(pieces):
            row = (n + k) * C
            for r in range(2):
                part = piece[r * C : (r + 1) * C].astype(BF16)
                ysc[row : row + C, r * MODES : (r + 1) * MODES] = part


def forward_kernel(ids_ref, inv_ref, *refs):
    x = refs[:-4]
    row_ref, col_ref, out_ref, acc = refs[-4:]
    i = pl.program_id(0)
    samples = x[0].shape[0]
    rows = [part[s, 0] for s in range(samples) for part in x]
    table = table_rows(row_ref, col_ref, 0, row_ref.shape[1])
    part = dot(jnp.concatenate(rows, axis=0), table)

    @pl.when(i == 0)
    def _():
        acc[...] = part

    @pl.when(i > 0)
    def _():
        acc[...] += part

    @pl.when(i == pl.num_programs(0) - 1)
    def _():
        spread(acc, out_ref, [inv_ref[s] for s in range(samples) for _ in x])


def forward_spectrum(ids, inv, x, small, shards):
    samples = inv.shape[0]
    modes = MODES // shards
    width = -(-samples * len(x) * LANES // PACK) * PACK
    n = 2 * MODES
    tile = 2048

    def spec(array):
        if array.shape[0] == samples:
            return pl.BlockSpec((samples, 1, C, tile), lambda i, ids, inv: (0, 0, 0, i))
        return pl.BlockSpec((samples, 1, C, tile), lambda i, ids, inv: (ids[0], 0, 0, i))

    return pl.pallas_call(
        forward_kernel,
        grid_spec=pltpu.PrefetchScalarGridSpec(
            num_scalar_prefetch=2,
            grid=(NPIX // tile,),
            in_specs=[spec(part) for part in x] + small_specs(tile),
            out_specs=whole((shards, modes, width)),
            scratch_shapes=[pltpu.VMEM((samples * len(x) * C, n), F32)],
        ),
        out_shape=slow((shards, modes, width), BF16),
        compiler_params=params(28),
        cost_estimate=cost(),
        name="forward",
    )(*stay(ids, inv, *x, small, small))


def row_scratch(modes, shards, width):
    return pltpu.VMEM((width // PACK, modes * shards, PACK), F32)


def gather_rows(blocks, sc):
    shards, modes = blocks[0].shape[:2]
    first = 0
    for block in blocks:
        for n in range(block.shape[2] // PACK):
            for x in range(shards):
                rows = block[x, :, n * PACK : (n + 1) * PACK].astype(F32)
                sc[first + n, pl.ds(x, modes, stride=shards), :] = rows
        first += block.shape[2] // PACK


def scatter_rows(ysc, out):
    shards, modes = out.shape[:2]
    for x in range(shards):
        for n in range(ysc.shape[0]):
            piece = ysc[n, pl.ds(x, modes, stride=shards), :]
            out[x, :, n * PACK : (n + 1) * PACK] = piece.astype(BF16)


def blade_rows(sc, mode, shards, groups):
    at = pl.ds(pl.multiple_of(mode * shards, shards), shards)
    found = [[] for _ in range(4)]
    for tile, pairs in groups:
        tiles = [sc[tile + n, at, :] for n in range(-(-len(pairs) * LANES // PACK))]
        pieces = split_lanes(tiles[0], tiles[min(1, len(tiles) - 1)], tiles[-1])
        for piece, (_, t) in zip(pieces, pairs):
            found[t].append(piece)
    return [jnp.concatenate(found[t], axis=0) for t in range(4)]


def groups_of(samples, *blades):
    groups = []
    tile = 0
    for some in blades:
        pairs = [(s, t) for s in range(samples) for t in some]
        for n in range(0, len(pairs), 4):
            part = pairs[n : n + 4]
            groups.append((tile, part))
            tile += -(-len(part) * LANES // PACK)
    return groups


EARLY = (0, 3)
LATE = (1, 2)


def mix_modes(xsc, ysc, pq_ref, groups, shards, first_mode, back):
    modes = xsc.shape[1] // shards
    samples = ysc.shape[0] // 3
    group = samples * shards

    def step(m, carry):
        low = jnp.concatenate(blade_rows(xsc, m, shards, groups), axis=0)
        low = low[:, :LANES].astype(BF16)
        total = [None] * 4
        parts = dot(low, pq_ref[m])
        for k in range(4):
            part = parts[:, k * PACK : (k + 1) * PACK]
            for t in range(4):
                u = t ^ k
                piece = part[t * group : (t + 1) * group]
                sign = sgn(u, k) if back else sgn(t, k)
                if total[u] is None:
                    total[u] = piece if sign > 0 else -piece
                else:
                    total[u] = total[u] + piece if sign > 0 else total[u] - piece
        factor = mode_factor(first_mode + m)
        at = pl.ds(pl.multiple_of(m * shards, shards), shards)
        for s in range(samples):
            rows = []
            for u in range(4):
                rows.append(total[u][s * shards : (s + 1) * shards] * factor)
            for n, tile in enumerate(join_lanes(*rows)):
                ysc[s * 3 + n, at, :] = tile
        return carry

    lax.fori_loop(0, modes, step, 0, unroll=min(32, modes))


def mix_kernel(ids_ref, xa, xb, pq_ref, y_ref, xsc, ysc):
    shards, modes, width = y_ref.shape
    gather_rows((xa, xb), xsc)
    groups = groups_of(width // (4 * LANES), EARLY, LATE)
    mix_modes(xsc, ysc, pq_ref, groups, shards, ids_ref[1] * modes, False)
    scatter_rows(ysc, y_ref)


def mix(ids, xa, xb, pq, samples):
    shards, modes = xa.shape[:2]
    width = samples * 4 * LANES
    return pl.pallas_call(
        mix_kernel,
        in_specs=[pl.BlockSpec(memory_space=SMEM)] + in_vmem(3),
        out_specs=in_vmem(1)[0],
        out_shape=slow((shards, modes, width), BF16),
        scratch_shapes=[
            row_scratch(modes, shards, xa.shape[2] + xb.shape[2]),
            row_scratch(modes, shards, width),
        ],
        compiler_params=params(28),
        cost_estimate=cost(),
        name="mix",
    )(*stay(ids, xa, xb), *pin(pq))


def mix_back_kernel(ids_ref, g_ref, pq_ref, out_ref, gsc, ysc):
    shards, modes, width = g_ref.shape
    gather_rows((g_ref,), gsc)
    groups = groups_of(width // (4 * LANES), range(4))
    mix_modes(gsc, ysc, pq_ref, groups, shards, ids_ref[1] * modes, True)
    scatter_rows(ysc, out_ref)


def mix_back(ids, g, pq):
    shards, modes, width = g.shape
    return pl.pallas_call(
        mix_back_kernel,
        in_specs=[pl.BlockSpec(memory_space=SMEM)] + in_vmem(2),
        out_specs=in_vmem(1)[0],
        out_shape=slow(g.shape, BF16),
        scratch_shapes=[row_scratch(modes, shards, width)] * 2,
        compiler_params=params(28),
        cost_estimate=cost(),
        name="mix_back",
    )(*stay(ids), g, *pin(pq))


def turn_kernel(ids_ref, pq_ref, xa, xb, l0, l1, l2, l3, out_ref, xt_ref, lt_ref, lb_ref, held, xsc, lsc):
    shards, modes = xa.shape[:2]
    samples = xt_ref.shape[2] // (8 * shards)
    groups = groups_of(samples, EARLY, LATE)
    shape = (LANES, LANES)
    diagonal = lax.broadcasted_iota(jnp.int32, shape, 0) == lax.broadcasted_iota(jnp.int32, shape, 1)
    unit = jnp.where(diagonal, 1.0, 0.0).astype(BF16)
    gather_rows((xa, xb), xsc)

    def step(m, carry):
        for k in range(4):
            at = slice(k * PACK, k * PACK + LANES)
            held[m, :, at] = dot(unit, pq_ref[m, :, at], ((1,), (1,))).astype(BF16)
        x = blade_rows(xsc, m, shards, groups)
        x = x + [pltpu.roll(rows, PACK - C, 1) for rows in x]
        xt_ref[m] = jnp.concatenate(x, axis=0).T[:C].astype(BF16)
        return carry

    lax.fori_loop(0, modes, step, 0, unroll=min(16, modes))
    out_ref[...] = held[...]
    own = ids_ref[0]
    for t, line in enumerate((l0, l1, l2, l3)):
        slot = jnp.bitwise_xor(own, t)
        lsc[slot] = line[...].astype(F32) * jnp.where(slot % 2 == 1, flip_of(own, 1), 1.0)
    for k in range(4):
        line = lsc[k]
        turned = line.T
        for t in range(4):
            u = t ^ k
            lb_ref[t * C : (t + 1) * C, u * C : (u + 1) * C] = (line[:, :C] * sgn(t, k)).astype(BF16)
            lt_ref[u * C : (u + 1) * C, t * C : (t + 1) * C] = (turned[:C] * sgn(t, k)).astype(BF16)


def turn(ids, pq, xa, xb, packs, samples):
    shards, modes = xa.shape[:2]
    last = packs[0].shape[1] // PACK - 1
    shape = (4 * C, 4 * C)
    turned_shape = (modes, C, 8 * samples * shards)
    return pl.pallas_call(
        turn_kernel,
        grid=(1,),
        in_specs=[pl.BlockSpec(memory_space=SMEM), whole(pq.shape), whole(xa.shape), whole(xb.shape)]
        + [pl.BlockSpec((C, PACK), lambda i: (0, last))] * 4,
        out_specs=[whole(pq.shape), whole(turned_shape)] + [whole(shape)] * 2,
        out_shape=[fast(pq.shape, BF16), slow(turned_shape, BF16)] + [slow(shape, BF16)] * 2,
        input_output_aliases={1: 0},
        scratch_shapes=[
            pltpu.VMEM(pq.shape, BF16),
            row_scratch(modes, shards, xa.shape[2] + xb.shape[2]),
            pltpu.VMEM((4, C, PACK), F32),
        ],
        compiler_params=params(28),
        cost_estimate=cost(),
        name="turn",
    )(*stay(ids), *pin(pq), *stay(xa, xb, *packs))


def grad_kernel(ids_ref, xt_ref, g_ref, lin_ref, o0, o1, o2, o3, gsc, osc):
    shards, modes, width = g_ref.shape
    samples = width // (4 * LANES)
    own = ids_ref[0]
    first_mode = ids_ref[1] * modes
    groups = groups_of(samples, range(4))
    gather_rows((g_ref,), gsc)
    lane = lanes_of((samples * shards, PACK))

    def step(g, carry):
        found = [[] for _ in range(4)]
        for q in range(QUAD):
            m = g * QUAD + q
            factor = mode_factor(first_mode + m)
            plain = [(rows * factor).astype(BF16) for rows in blade_rows(gsc, m, shards, groups)]
            turned = [
                jnp.where(lane < C, pltpu.roll(rows, PACK - C, 1), -pltpu.roll(rows, C, 1))
                for rows in plain
            ]
            plus = plain + turned
            minus = [-rows for rows in plus]
            right = []
            for k in range(4):
                rows = []
                for r in range(2):
                    for t in range(4):
                        rows.append((plus if sgn(t, k) > 0 else minus)[4 * r + (t ^ k)])
                right.append(jnp.concatenate(rows, axis=0))
            grad = dot(xt_ref[m], jnp.concatenate(right, axis=1))
            for k in range(4):
                found[k].append(grad[:, k * PACK : (k + 1) * PACK])
        for k in range(4):
            for n, tile in enumerate(join_lanes(*found[k])):
                at = pl.ds(pl.multiple_of(g * QUAD * LANES + n * PACK, PACK), PACK)
                osc[k, :, at] = tile.astype(BF16)
        return carry

    quads = modes // QUAD
    lax.fori_loop(0, quads, step, 0, unroll=min(2, quads))
    for k in range(4):
        line = jnp.concatenate([lin_ref[k], jnp.zeros((C, PACK - C), F32)], axis=1)
        osc[k, :, modes * LANES :] = line.astype(BF16)
    for t, out in enumerate((o0, o1, o2, o3)):
        out[...] = osc[jnp.bitwise_xor(own, t)]


def weight_grads(ids, xt, g, lin):
    shards, modes, width = g.shape
    shape = (C, modes * LANES + PACK)
    return pl.pallas_call(
        grad_kernel,
        in_specs=[pl.BlockSpec(memory_space=SMEM)] + in_vmem(3),
        out_specs=in_vmem(4),
        out_shape=[slow(shape, BF16)] * 4,
        scratch_shapes=[row_scratch(modes, shards, width), pltpu.VMEM((4,) + shape, BF16)],
        compiler_params=params(28),
        cost_estimate=cost(),
        name="weight_grads",
    )(*stay(ids, xt), g, *stay(lin))


CDF_AT = 0.28
CDF = (0.11652094, 0.06749571, 0.2689128, -0.23699677, 0.38987606, -0.10580875)
SERIES = [value / CDF_AT ** (i + 1) for i, value in enumerate(CDF)]


def gelu_parts(v):
    z = jnp.abs(v)
    t = 1.0 / (z + 1.0 / CDF_AT)
    bell = jnp.exp2(v * v * (-0.5 * math.log2(math.e)))
    series = jnp.float32(SERIES[-1])
    for value in SERIES[-2::-1]:
        series = series * t + value
    tail = series * t * bell
    cdf = jnp.where(v < 0.0, tail, 1.0 - tail)
    return v * cdf, cdf + v * (bell * (1.0 / math.sqrt(2.0 * math.pi)))


def pixel_kernel(ids_ref, inv_ref, *refs):
    x = refs[:4]
    y_ref, ft_ref, lt_ref = refs[4:7]
    outs = refs[8:12]
    slope_ref = refs[12]
    left, ysc, even, odd = refs[14:]
    samples = x[1].shape[0]
    rows = 4 * C
    n = 2 * MODES
    width = even.shape[1]

    @pl.when(pl.program_id(0) == 0)
    def _():
        collect(y_ref, ysc)
        for s in range(samples):
            left[s, :, :n] = ysc[s * rows : (s + 1) * rows]
            left[s, :, n:] = (lt_ref[...].astype(F32) * inv_ref[s]).astype(BF16)

    def product(s, at, pre):
        fields = [x[t][s, 0, :, at] for t in range(4)]
        pre[...] = dot(left[s], jnp.concatenate([ft_ref[:, at]] + fields, axis=0))

    def activate(s, at, pre):
        for t in range(4):
            value, slope = gelu_parts(pre[t * C : (t + 1) * C])
            normed = x[t][s, 0, :, at].astype(F32) * inv_ref[s]
            outs[t][s, 0, :, at] = (normed + value).astype(BF16)
            row = s * rows + t * C
            slope_ref[row : row + C, at] = slope.astype(BF16)

    tile = ft_ref.shape[1]
    blocks = [(s, slice(k, k + width)) for k in range(0, tile, width) for s in range(samples)]
    buffers = [even, odd]
    product(*blocks[0], buffers[0])
    for k, block in enumerate(blocks):
        if k + 1 < len(blocks):
            product(*blocks[k + 1], buffers[(k + 1) % 2])
        activate(*block, buffers[k % 2])


def pixels(ids, inv, x, y, turned, lt, pq):
    samples = inv.shape[0]
    n = 2 * MODES
    tile = 1024
    mine = pl.BlockSpec((samples, 1, C, tile), lambda i, ids, inv: (ids[0], 0, 0, i))
    block = pl.BlockSpec((samples, 1, C, tile), lambda i, ids, inv: (0, 0, 0, i))
    rows = samples * 4 * C
    flat = pl.BlockSpec((rows, tile), lambda i, ids, inv: (0, i))
    return pl.pallas_call(
        pixel_kernel,
        grid_spec=pltpu.PrefetchScalarGridSpec(
            num_scalar_prefetch=2,
            grid=(NPIX // tile,),
            in_specs=[mine]
            + [block] * 3
            + [
                whole(y.shape),
                pl.BlockSpec((n, tile), lambda i, ids, inv: (0, i)),
                whole((4 * C, 4 * C)),
                pl.BlockSpec(memory_space=pl.ANY),
            ],
            out_specs=[mine] + [block] * 3 + [flat, pl.BlockSpec(memory_space=pl.ANY)],
            scratch_shapes=[
                pltpu.VMEM((samples, 4 * C, n + 4 * C), BF16),
                pltpu.VMEM((rows, n), BF16),
                pltpu.VMEM((4 * C, 256), F32),
                pltpu.VMEM((4 * C, 256), F32),
            ],
        ),
        out_shape=[slow(x[0].shape, BF16)]
        + [slow((samples, 1, C, NPIX), BF16)] * 3
        + [fast((rows, NPIX), BF16), fast(pq.shape, BF16)],
        input_output_aliases={9: 5},
        compiler_params=params(28),
        cost_estimate=cost(),
        name="pixels",
    )(*stay(ids, inv, *x), y, *stay(turned, lt), *pin(pq))


def slope_kernel(ids_ref, *refs):
    cot = refs[:4]
    slope, row_ref, col_ref, _, g_ref, g_out, _, gacc = refs[4:]
    samples = cot[1].shape[0]
    rows = 4 * C
    i = pl.program_id(0)

    @pl.when(i == 0)
    def _():
        gacc[...] = jnp.zeros_like(gacc)

    for s in range(samples):
        for t in range(4):
            at = s * rows + t * C
            grad = cot[t][s, 0].astype(F32) * slope[at : at + C].astype(F32)
            g_ref[at : at + C] = grad.astype(BF16)
    table = table_rows(row_ref, col_ref, 0, row_ref.shape[1])
    gacc[...] += dot(g_ref[...], table)

    @pl.when(i == pl.num_programs(0) - 1)
    def _():
        spread(gacc, g_out)


def pixel_grads(ids, cot, slope, small, spectrum, pq):
    rows = slope.shape[0]
    samples = rows // (4 * C)
    n = 2 * MODES
    tile = 2048
    mine = pl.BlockSpec((samples, 1, C, tile), lambda i, ids: (ids[0], 0, 0, i))
    block = pl.BlockSpec((samples, 1, C, tile), lambda i, ids: (0, 0, 0, i))
    flat = pl.BlockSpec((rows, tile), lambda i, ids: (0, i))
    kept = pl.BlockSpec(memory_space=pl.ANY)
    return pl.pallas_call(
        slope_kernel,
        grid_spec=pltpu.PrefetchScalarGridSpec(
            num_scalar_prefetch=1,
            grid=(NPIX // tile,),
            in_specs=[mine] + [block] * 3 + [flat] + small_specs(tile) + [kept],
            out_specs=[flat, whole(spectrum), kept],
            scratch_shapes=[pltpu.VMEM((rows, n), F32)],
        ),
        out_shape=[slow((rows, NPIX), BF16), slow(spectrum, BF16), fast(pq.shape, BF16)],
        input_output_aliases={8: 2},
        compiler_params=params(28),
        cost_estimate=cost(),
        name="pixel_grads",
    )(*stay(ids, *cot), *pin(slope), *stay(small, small), *pin(pq))


def lin_kernel(ids_ref, inv_ref, *refs):
    x = refs[:4]
    g_ref, lb_ref, lin_ref, back_ref, lacc = refs[4:]
    samples = x[1].shape[0]
    rows = 4 * C

    @pl.when(pl.program_id(0) == 0)
    def _():
        lacc[...] = jnp.zeros_like(lacc)

    for s in range(samples):
        fields = jnp.concatenate([x[t][s, 0] for t in range(4)], axis=0)
        g = g_ref[s * rows : (s + 1) * rows]
        lacc[...] += dot(fields, g, ((1,), (1,))) * inv_ref[s]
        back_ref[s * rows : (s + 1) * rows] = dot(lb_ref[...], g).astype(BF16)

    @pl.when(pl.program_id(0) == pl.num_programs(0) - 1)
    def _():
        for k in range(4):
            total = None
            for t in range(4):
                u = t ^ k
                piece = lacc[t * C : (t + 1) * C, u * C : (u + 1) * C] * sgn(t, k)
                total = piece if total is None else total + piece
            lin_ref[k] = total


def lin_grads(ids, inv, x, g, lb):
    rows = g.shape[0]
    samples = rows // (4 * C)
    tile = 2048
    mine = pl.BlockSpec((samples, 1, C, tile), lambda i, ids, inv: (ids[0], 0, 0, i))
    block = pl.BlockSpec((samples, 1, C, tile), lambda i, ids, inv: (0, 0, 0, i))
    flat = pl.BlockSpec((rows, tile), lambda i, ids, inv: (0, i))
    return pl.pallas_call(
        lin_kernel,
        grid_spec=pltpu.PrefetchScalarGridSpec(
            num_scalar_prefetch=2,
            grid=(NPIX // tile,),
            in_specs=[mine] + [block] * 3 + [flat, whole((4 * C, 4 * C))],
            out_specs=[whole((4, C, C)), flat],
            scratch_shapes=[pltpu.VMEM((4 * C, 4 * C), F32)],
        ),
        out_shape=[slow((4, C, C), F32), slow(g.shape, BF16)],
        compiler_params=params(28),
        cost_estimate=cost(),
        name="lin_grads",
    )(*stay(ids, inv, *x, g, lb))


def inner_kernel(ids_ref, inv_ref, y_ref, back_ref, row_ref, col_ref, cot_ref, mine_ref, *refs):
    o1, o2, o3, ysc = refs
    samples = cot_ref.shape[0]
    rows = 4 * C

    @pl.when(pl.program_id(0) == 0)
    def _():
        collect(y_ref, ysc)

    table = table_rows(row_ref, col_ref, 0, row_ref.shape[1])
    spatial = dot(ysc[...], table, ((1,), (1,)))
    for s in range(samples):
        at = slice(s * rows, (s + 1) * rows)
        total = spatial[at] + back_ref[at].astype(F32)
        mine_ref[s, 0] = (cot_ref[s, 0].astype(F32) + total[:C]) * inv_ref[s]
        for t, out in ((1, o1), (2, o2), (3, o3)):
            out[s, 0] = total[t * C : (t + 1) * C].astype(BF16)


def inner_grads(ids, inv, y, back, small, cotangent):
    samples = inv.shape[0]
    n = 2 * MODES
    tile = 2048
    rows = samples * 4 * C
    mine = pl.BlockSpec((samples, 1, C, tile), lambda i, ids, inv: (ids[0], 0, 0, i))
    block = pl.BlockSpec((samples, 1, C, tile), lambda i, ids, inv: (0, 0, 0, i))
    return pl.pallas_call(
        inner_kernel,
        grid_spec=pltpu.PrefetchScalarGridSpec(
            num_scalar_prefetch=2,
            grid=(NPIX // tile,),
            in_specs=[
                whole(y.shape),
                pl.BlockSpec((rows, tile), lambda i, ids, inv: (0, i)),
                *small_specs(tile),
                mine,
            ],
            out_specs=[mine] + [block] * 3,
            scratch_shapes=[pltpu.VMEM((rows, n), BF16)],
        ),
        out_shape=[slow(cotangent.shape, F32)] + [slow((samples, 1, C, NPIX), BF16)] * 3,
        compiler_params=params(28),
        cost_estimate=cost(),
        name="inner_grads",
    )(*stay(ids, inv), y, *stay(back, small, small, cotangent))


def place_kernel(ids_ref, a_ref, b_ref, c_ref, old_ref, out_ref):
    for n, part in enumerate((a_ref, b_ref, c_ref)):

        @pl.when(pl.program_id(0) == n)
        def _():
            out_ref[...] = part[...]


def place_output(ids, parts, result):
    samples = parts[0].shape[0]
    shape = (1, 1, C, NPIX)

    def spec(n):
        def at(j, s, ids):
            return (jnp.where(j == n, s, jnp.where(j < n, 0, samples - 1)), 0, 0, 0)

        return pl.BlockSpec(shape, at)

    return pl.pallas_call(
        place_kernel,
        grid_spec=pltpu.PrefetchScalarGridSpec(
            num_scalar_prefetch=1,
            grid=(3, samples),
            in_specs=[spec(0), spec(1), spec(2), pl.BlockSpec(memory_space=pl.ANY)],
            out_specs=pl.BlockSpec(
                shape, lambda j, s, ids: (jnp.bitwise_xor(ids[0], j + 1) * samples + s, 0, 0, 0)
            ),
        ),
        out_shape=jax.ShapeDtypeStruct(result.shape, BF16),
        input_output_aliases={4: 0},
        compiler_params=params(28),
        cost_estimate=cost(),
        name="place",
    )(ids, *parts, result)


def final_kernel(count, codes, ids_ref, inv_ref, cot_ref, *refs):
    samples = pl.num_programs(1)
    j = pl.program_id(0)
    for n in range(count):

        @pl.when(j == n)
        def _():
            inv = inv_ref[jnp.bitwise_xor(ids_ref[0], codes[n]) * samples + pl.program_id(1)]
            refs[-1][...] = (cot_ref[...].astype(F32) + refs[n][...].astype(F32)) * inv


def final_grads(ids, inv, cotangent, parts, codes, result):
    samples = parts[0].shape[0]
    count = len(parts)
    shape = (1, 1, C, NPIX)

    def code(j):
        value = codes[0]
        for n in range(1, count):
            value = jnp.where(j == n, codes[n], value)
        return value

    def spec(n):
        def at(j, s, ids, inv):
            return (jnp.where(j == n, s, jnp.where(j < n, 0, samples - 1)), 0, 0, 0)

        return pl.BlockSpec(shape, at)

    place = pl.BlockSpec(
        shape, lambda j, s, ids, inv: (jnp.bitwise_xor(ids[0], code(j)) * samples + s, 0, 0, 0)
    )
    return pl.pallas_call(
        partial(final_kernel, count, codes),
        grid_spec=pltpu.PrefetchScalarGridSpec(
            num_scalar_prefetch=2,
            grid=(count, samples),
            in_specs=[place]
            + [spec(n) for n in range(count)]
            + [pl.BlockSpec(memory_space=pl.ANY)],
            out_specs=place,
        ),
        out_shape=jax.ShapeDtypeStruct(cotangent.shape, F32),
        input_output_aliases={3 + count: 0},
        compiler_params=params(28),
        cost_estimate=cost(),
        name="final",
    )(ids, inv, cotangent, *parts, result)


def adamw(weight, first, second, grad):
    first_new = BETA_ONE * first + (1.0 - BETA_ONE) * grad
    second_new = BETA_TWO * second + (1.0 - BETA_TWO) * grad * grad
    corr_one = 1.0 - BETA_ONE**STEP_COUNT
    corr_two = 1.0 - BETA_TWO**STEP_COUNT
    update = first_new / corr_one / (jnp.sqrt(second_new / corr_two) + EPSILON)
    return (weight - RATE * (update + DECAY * weight), first_new, second_new)


def adam_kernel(flips, d0, d1, d2, d3, w_ref, first_ref, second_ref, w_out, first_out, second_out):
    grad = d0[...].astype(F32) * flips[0]
    for t, d in ((1, d1), (2, d2), (3, d3)):
        grad = grad + d[...].astype(F32) * flips[t]
    for g in range(w_ref.shape[1] // QUAD):
        tiles = [grad[:, (3 * g + n) * PACK : (3 * g + n + 1) * PACK] for n in range(3)]
        for q, piece in enumerate(split_lanes(*tiles)):
            for r in range(2):
                at = (0, g * QUAD + q, r)
                new = adamw(w_ref[at], first_ref[at], second_ref[at], piece[:, r * C : (r + 1) * C])
                w_out[at], first_out[at], second_out[at] = new


def adam_spec(flips, grads, weight, first, second):
    modes = weight.shape[1]
    part = min(modes, 4 * QUAD)
    packed = pl.BlockSpec((C, part * LANES), lambda g: (0, g))
    block = pl.BlockSpec((1, part, 2, C, C), lambda g: (0, g, 0, 0, 0))
    return pl.pallas_call(
        adam_kernel,
        grid=(modes // part,),
        in_specs=[pl.BlockSpec(memory_space=SMEM)] + [packed] * 4 + [block] * 3,
        out_specs=[block] * 3,
        out_shape=[jax.ShapeDtypeStruct(weight.shape, F32)] * 3,
        compiler_params=params(28),
        cost_estimate=cost(),
        name="adam",
    )(flips, *grads, weight, first, second)


def swap(value, axis, size, x):
    return lax.ppermute(value, axis, [(i, i ^ x) for i in range(size)])


def to_modes(value):
    return lax.all_to_all(value, "dp", split_axis=0, concat_axis=0, tiled=True)


def after(values, first):
    values, _ = lax.optimization_barrier((values, first))
    return values


def body(
    shards,
    inputs,
    cotangent,
    norm_table,
    sample_index,
    spec_weight,
    spec_first,
    spec_second,
    lin_weight,
    lin_first,
    lin_second,
):
    own = lax.axis_index("blade")
    shard = lax.axis_index("dp")
    ids = jnp.stack([own, shard]).astype(jnp.int32)
    samples = inputs.shape[0] // 4

    def cut(array, t):
        return lax.dynamic_slice_in_dim(array, jnp.bitwise_xor(own, t) * samples, samples, 0)

    def send(array, t):
        block = cut(array, t)
        return block, swap(block, "blade", 4, t)

    sent, x3 = send(inputs, 3)
    rest = after(inputs, sent)
    sent, x1 = send(rest, 1)
    rest = after(rest, sent)
    _, x2 = send(rest, 2)

    matches = sample_index[:, None] == jnp.arange(NTAB, dtype=jnp.int32)[None, :]
    normalizer = jnp.sum(jnp.where(matches, norm_table[None, :], 0.0), axis=1)
    inv_all = 1.0 / normalizer
    inv = lax.dynamic_slice_in_dim(inv_all, own * samples, samples, 0)

    small = lax.optimization_barrier(small_tables())
    turned = turned_table(small)
    packed = pack_weights(spec_weight, lin_weight)
    packs = [packed] + [swap(packed, "blade", 4, t) for t in (1, 2, 3)]

    x3 = after(x3, (packed, turned))
    sent = forward_spectrum(ids, inv, (inputs, x3), small, shards)
    x1, x2 = after((x1, x2), sent)
    xa = to_modes(sent)
    blocks = after([cut(cotangent, t) for t in (1, 2, 3)], (x1, x2))
    cot = (cotangent,) + tuple(swap(blocks[t - 1], "blade", 4, t) for t in (1, 2, 3))
    xb = to_modes(forward_spectrum(ids, inv, (x1, x2), small, shards))
    pq = unpack(ids, packs)
    mixed = mix(ids, xa, xb, pq, samples)
    pq, xt, lt, lb = turn(ids, after(pq, mixed), xa, xb, packs, samples)
    y = to_modes(mixed)

    x = (inputs, x1, x2, x3)
    result = pixels(ids, inv, x, y, turned, lt, pq)
    output, slope, pq = result[0], result[4], result[5]
    last, cot = lax.optimization_barrier((result[3], cot))
    parts = (result[1], result[2], last)
    out_parts = [swap(parts[t - 1], "blade", 4, t) for t in (1, 2, 3)]

    grad_pre, sent, pq = pixel_grads(ids, cot, slope, small, y.shape, pq)
    lin, from_lin = lin_grads(ids, inv, x, grad_pre, lb)
    g = after(to_modes(sent), (out_parts[2], xt, pq, lin))
    mixed = mix_back(ids, g, pq)
    back = to_modes(mixed)
    spec_grads = weight_grads(ids, xt, g, lin)
    spec_grads = [spec_grads[0]] + [swap(spec_grads[t], "blade", 4, t) for t in (1, 2, 3)]

    inner = inner_grads(ids, inv, back, from_lin, small, cotangent)
    inner = after(inner, out_parts)
    grad_parts = [swap(inner[t], "blade", 4, t) for t in (1, 2, 3)]

    output = place_output(ids, out_parts, output)
    spec_grads = after(spec_grads, output)
    flips = jnp.stack(
        [jnp.where(own % 2 == 1, flip_of(jnp.bitwise_xor(own, t), 1), 1.0) for t in range(4)]
    )
    lin_grad = 0.0
    first = spec_weight.shape[1] * LANES
    for t in range(4):
        lin_grad = lin_grad + spec_grads[t][:, first : first + C].astype(F32) * flips[t]
    step = 1
    while step < shards:
        lin_grad = lin_grad + swap(lin_grad, "dp", shards, step)
        step *= 2

    spec_out = adam_spec(flips, spec_grads, spec_weight, spec_first, spec_second)
    lin_out = adamw(lin_weight, lin_first, lin_second, lin_grad[None])
    input_grad = final_grads(ids, inv_all, cotangent, grad_parts[2:], (3,), inner[0])
    input_grad = final_grads(ids, inv_all, cotangent, grad_parts[:2], (1, 2), input_grad)
    return (output, input_grad, *spec_out, *lin_out)


def solution(mesh):
    fields = P("dp", "blade", None, None)
    spec = P("blade", "dp", None, None, None)
    lin = P("blade", None, None)
    return jax.shard_map(
        partial(body, mesh.shape["dp"]),
        mesh=mesh,
        in_specs=(fields, fields, P(), P("dp"), spec, spec, spec, lin, lin, lin),
        out_specs=(fields, fields, spec, spec, spec, lin, lin, lin),
        check_vma=False,
    )
```

```python
from functools import partial
import math

import jax
import jax.numpy as jnp
from jax import lax
from jax.experimental import pallas as pl
from jax.experimental.pallas import tpu as pltpu
from jax.sharding import PartitionSpec as P

GRID = 64
MSIDE = 16
NTAB = 16
STEP_COUNT = 5
NPIX = 4096
MODES = 256
C = 48
LANES = 2 * C
QUAD = 4
PACK = 128

BETA_ONE = 0.9
BETA_TWO = 0.999
EPSILON = 1e-08
RATE = 0.1
DECAY = 0.01

F32 = jnp.float32
BF16 = jnp.bfloat16
SMEM = pltpu.MemorySpace.SMEM


def sgn(left, right):
    return -1.0 if (left & 2) and (right & 1) else 1.0


def flip_of(own, k):
    if k & 1:
        return (1 - 2 * ((own // 2) % 2)).astype(F32)
    return jnp.float32(1.0)


def mode_factor(mode):
    return jnp.where(mode % MSIDE == 0, 1.0, 2.0).astype(F32)


def dot(left, right, dims=((1,), (0,))):
    return lax.dot_general(left, right, (dims, ((), ())), preferred_element_type=F32)


def whole(shape):
    zeros = (0,) * len(shape)
    return pl.BlockSpec(tuple(shape), lambda *_: zeros)


def params(mib):
    return pltpu.CompilerParams(vmem_limit_bytes=mib * 1024 * 1024)


def fast(shape, kind):
    return pltpu.VMEM(tuple(shape), kind)


def slow(shape, kind):
    return pltpu.HBM(tuple(shape), kind)


def pin(*arrays):
    return [pltpu.with_memory_space_constraint(array, pltpu.VMEM) for array in arrays]


def stay(*arrays):
    return [pltpu.with_memory_space_constraint(array, pltpu.HBM) for array in arrays]


def in_vmem(count):
    return [pl.BlockSpec(memory_space=pltpu.MemorySpace.VMEM)] * count


def cost():
    return pl.CostEstimate(flops=1, bytes_accessed=1, transcendentals=0)


def small_tables():
    mode_ids = jnp.arange(2 * MODES, dtype=jnp.int32)
    imag = mode_ids >= MODES
    mode_ids = mode_ids % MODES
    row_index = mode_ids // MSIDE
    col_freq = mode_ids % MSIDE
    row_freq = jnp.where(row_index < MSIDE // 2, row_index, GRID - MSIDE + row_index)
    place = jnp.arange(GRID, dtype=jnp.int32)[:, None]
    row_angle = ((place * row_freq[None, :]) % GRID).astype(F32) * (2.0 * math.pi / GRID)
    col_angle = ((place * col_freq[None, :]) % GRID).astype(F32) * (2.0 * math.pi / GRID)
    row_cos, row_sin = jnp.cos(row_angle) / GRID, jnp.sin(row_angle) / GRID
    first = jnp.where(imag[None, :], -row_sin, row_cos)
    second = jnp.where(imag[None, :], -row_cos, -row_sin)
    return jnp.stack([first, second, jnp.cos(col_angle), jnp.sin(col_angle)])


def table_rows(row_ref, col_ref, start, stop):
    tiles = []
    for h in range(start, stop):
        tile = row_ref[0, h : h + 1] * col_ref[0] + row_ref[1, h : h + 1] * col_ref[1]
        tiles.append(tile.astype(BF16))
    return jnp.concatenate(tiles, axis=0)


def small_specs(tile):
    n = 2 * MODES
    return [
        pl.BlockSpec((2, tile // GRID, n), lambda i, *_: (0, i, 0)),
        pl.BlockSpec((2, GRID, n), lambda i, *_: (1, 0, 0)),
    ]


def turned_kernel(row_ref, col_ref, ft_ref):
    for h in range(0, row_ref.shape[1], 2):
        tile = table_rows(row_ref, col_ref, h, h + 2)
        ft_ref[:, h * GRID : (h + 2) * GRID] = tile.astype(F32).T.astype(BF16)


def turned_table(small):
    rows = 8
    n = 2 * MODES
    return pl.pallas_call(
        turned_kernel,
        grid=(GRID // rows,),
        in_specs=small_specs(rows * GRID),
        out_specs=pl.BlockSpec((n, rows * GRID), lambda i: (0, i)),
        out_shape=slow((n, NPIX), BF16),
        compiler_params=params(28),
        cost_estimate=cost(),
        name="turned",
    )(*stay(small, small))


def pack_kernel(w_ref, l_ref, o_ref):
    def step(g, carry):
        parts = [w_ref[0, g * QUAD + q, r] for q in range(QUAD) for r in range(2)]
        at = pl.ds(pl.multiple_of(g * QUAD * LANES, PACK), QUAD * LANES)
        o_ref[:, at] = jnp.concatenate(parts, axis=1).astype(BF16)
        return carry

    modes = w_ref.shape[1]
    lax.fori_loop(0, modes // QUAD, step, 0)
    line = jnp.concatenate([l_ref[0], jnp.zeros((C, PACK - C), F32)], axis=1)
    o_ref[:, modes * LANES :] = line.astype(BF16)


def pack_weights(spec_weight, lin_weight):
    modes = spec_weight.shape[1]
    return pl.pallas_call(
        pack_kernel,
        in_specs=in_vmem(2),
        out_specs=in_vmem(1)[0],
        out_shape=jax.ShapeDtypeStruct((C, modes * LANES + PACK), BF16),
        compiler_params=params(28),
        cost_estimate=cost(),
        name="pack",
    )(spec_weight, lin_weight)


def lanes_of(shape):
    return lax.broadcasted_iota(jnp.int32, shape, len(shape) - 1)


def split_lanes(a, b, c):
    lane = lanes_of(a.shape)
    second = jnp.where(lane < 32, pltpu.roll(a, 32, 1), pltpu.roll(b, 32, 1))
    third = jnp.where(lane < 64, pltpu.roll(b, 64, 1), pltpu.roll(c, 64, 1))
    return a, second, third, pltpu.roll(c, 96, 1)


def join_lanes(first, second, third, fourth):
    lane = lanes_of(first.shape)
    a = jnp.where(lane < 96, first, pltpu.roll(second, 96, 1))
    b = jnp.where(lane < 64, pltpu.roll(second, 96, 1), pltpu.roll(third, 64, 1))
    c = jnp.where(lane < 32, pltpu.roll(third, 64, 1), pltpu.roll(fourth, 32, 1))
    return a, b, c


def quad_tiles(ref, g):
    tiles = []
    for n in range(3):
        at = pl.ds(pl.multiple_of(g * QUAD * LANES + n * PACK, PACK), PACK)
        tiles.append(ref[:, at])
    return tiles


def unpack_kernel(ids_ref, w0, w1, w2, w3, pq_ref):
    own = ids_ref[0]
    modes = pq_ref.shape[0]
    lane = lanes_of((C, PACK))
    flip = flip_of(own, 1)

    def step(g, carry):
        for t, w in enumerate((w0, w1, w2, w3)):
            slot = jnp.bitwise_xor(own, t)
            scale = jnp.where(slot % 2 == 1, flip, 1.0)
            at = pl.ds(pl.multiple_of(slot * PACK, PACK), PACK)
            tiles = [tile * scale.astype(BF16) for tile in quad_tiles(w, g)]
            for q, p in enumerate(split_lanes(*tiles)):
                low = jnp.where(lane < C, -pltpu.roll(p, PACK - C, 1), pltpu.roll(p, C, 1))
                pq_ref[g * QUAD + q, :C, at] = p
                pq_ref[g * QUAD + q, C:, at] = low
        return carry

    quads = modes // QUAD
    lax.fori_loop(0, quads, step, 0, unroll=min(4, quads))


def unpack(ids, packs):
    modes = (packs[0].shape[1] - PACK) // LANES
    return pl.pallas_call(
        unpack_kernel,
        in_specs=[pl.BlockSpec(memory_space=SMEM)] + in_vmem(4),
        out_specs=in_vmem(1)[0],
        out_shape=fast((modes, LANES, 4 * PACK), BF16),
        compiler_params=params(28),
        cost_estimate=cost(),
        name="unpack",
    )(*stay(ids, *packs))


def spread(acc, out_ref, scales=None):
    rows = []
    for n in range(acc.shape[0] // C):
        for r in range(2):
            row = acc[n * C : (n + 1) * C, r * MODES : (r + 1) * MODES]
            rows.append(row if scales is None else row * scales[n])
    extra = out_ref.shape[2] - len(rows) * C
    if extra:
        rows.append(jnp.zeros((extra, MODES), F32))
    turned = jnp.concatenate(rows, axis=0).T
    out_ref[...] = turned.reshape(out_ref.shape).astype(BF16)


def collect(block, ysc):
    turned = block[...].astype(F32).reshape(MODES, block.shape[2]).T
    for n in range(ysc.shape[0] // C):
        for r in range(2):
            row = (n * 2 + r) * C
            piece = turned[row : row + C].astype(BF16)
            ysc[n * C : (n + 1) * C, r * MODES : (r + 1) * MODES] = piece


def forward_kernel(ids_ref, inv_ref, *refs):
    x = refs[:-4]
    row_ref, col_ref, out_ref, acc = refs[-4:]
    i = pl.program_id(0)
    samples = x[0].shape[0]
    rows = [part[s, 0] for s in range(samples) for part in x]
    table = table_rows(row_ref, col_ref, 0, row_ref.shape[1])
    part = dot(jnp.concatenate(rows, axis=0), table)

    @pl.when(i == 0)
    def _():
        acc[...] = part

    @pl.when(i > 0)
    def _():
        acc[...] += part

    @pl.when(i == pl.num_programs(0) - 1)
    def _():
        spread(acc, out_ref, [inv_ref[s] for s in range(samples) for _ in x])


def forward_spectrum(ids, inv, x, small, shards):
    samples = inv.shape[0]
    modes = MODES // shards
    width = -(-samples * len(x) * LANES // PACK) * PACK
    n = 2 * MODES
    tile = 2048

    def spec(array):
        if array.shape[0] == samples:
            return pl.BlockSpec((samples, 1, C, tile), lambda i, ids, inv: (0, 0, 0, i))
        return pl.BlockSpec((samples, 1, C, tile), lambda i, ids, inv: (ids[0], 0, 0, i))

    return pl.pallas_call(
        forward_kernel,
        grid_spec=pltpu.PrefetchScalarGridSpec(
            num_scalar_prefetch=2,
            grid=(NPIX // tile,),
            in_specs=[spec(part) for part in x] + small_specs(tile),
            out_specs=whole((shards, modes, width)),
            scratch_shapes=[pltpu.VMEM((samples * len(x) * C, n), F32)],
        ),
        out_shape=slow((shards, modes, width), BF16),
        compiler_params=params(28),
        cost_estimate=cost(),
        name="forward",
    )(*stay(ids, inv, *x, small, small))


def row_scratch(modes, shards, width):
    return pltpu.VMEM((width // PACK, modes * shards, PACK), F32)


def gather_rows(blocks, sc):
    shards, modes = blocks[0].shape[:2]
    first = 0
    for block in blocks:
        for n in range(block.shape[2] // PACK):
            for x in range(shards):
                rows = block[x, :, n * PACK : (n + 1) * PACK].astype(F32)
                sc[first + n, pl.ds(x, modes, stride=shards), :] = rows
        first += block.shape[2] // PACK


def scatter_rows(ysc, out):
    shards, modes = out.shape[:2]
    for x in range(shards):
        for n in range(ysc.shape[0]):
            piece = ysc[n, pl.ds(x, modes, stride=shards), :]
            out[x, :, n * PACK : (n + 1) * PACK] = piece.astype(BF16)


def blade_rows(sc, mode, shards, groups):
    at = pl.ds(pl.multiple_of(mode * shards, shards), shards)
    found = [[] for _ in range(4)]
    for tile, pairs in groups:
        tiles = [sc[tile + n, at, :] for n in range(-(-len(pairs) * LANES // PACK))]
        pieces = split_lanes(tiles[0], tiles[min(1, len(tiles) - 1)], tiles[-1])
        for piece, (_, t) in zip(pieces, pairs):
            found[t].append(piece)
    return [jnp.concatenate(found[t], axis=0) for t in range(4)]


def groups_of(samples, *blades):
    groups = []
    tile = 0
    for some in blades:
        pairs = [(s, t) for s in range(samples) for t in some]
        for n in range(0, len(pairs), 4):
            part = pairs[n : n + 4]
            groups.append((tile, part))
            tile += -(-len(part) * LANES // PACK)
    return groups


EARLY = (0, 3)
LATE = (1, 2)


def mix_modes(xsc, ysc, pq_ref, groups, shards, first_mode, back):
    modes = xsc.shape[1] // shards
    samples = ysc.shape[0] // 3
    group = samples * shards

    def step(m, carry):
        low = jnp.concatenate(blade_rows(xsc, m, shards, groups), axis=0)
        low = low[:, :LANES].astype(BF16)
        total = [None] * 4
        parts = dot(low, pq_ref[m])
        for k in range(4):
            part = parts[:, k * PACK : (k + 1) * PACK]
            for t in range(4):
                u = t ^ k
                piece = part[t * group : (t + 1) * group]
                sign = sgn(u, k) if back else sgn(t, k)
                if total[u] is None:
                    total[u] = piece if sign > 0 else -piece
                else:
                    total[u] = total[u] + piece if sign > 0 else total[u] - piece
        factor = mode_factor(first_mode + m)
        at = pl.ds(pl.multiple_of(m * shards, shards), shards)
        for s in range(samples):
            rows = []
            for u in range(4):
                rows.append(total[u][s * shards : (s + 1) * shards] * factor)
            for n, tile in enumerate(join_lanes(*rows)):
                ysc[s * 3 + n, at, :] = tile
        return carry

    lax.fori_loop(0, modes, step, 0, unroll=min(32, modes))


def mix_kernel(ids_ref, xa, xb, pq_ref, y_ref, xsc, ysc):
    shards, modes, width = y_ref.shape
    gather_rows((xa, xb), xsc)
    groups = groups_of(width // (4 * LANES), EARLY, LATE)
    mix_modes(xsc, ysc, pq_ref, groups, shards, ids_ref[1] * modes, False)
    scatter_rows(ysc, y_ref)


def mix(ids, xa, xb, pq, samples):
    shards, modes = xa.shape[:2]
    width = samples * 4 * LANES
    return pl.pallas_call(
        mix_kernel,
        in_specs=[pl.BlockSpec(memory_space=SMEM)] + in_vmem(3),
        out_specs=in_vmem(1)[0],
        out_shape=slow((shards, modes, width), BF16),
        scratch_shapes=[
            row_scratch(modes, shards, xa.shape[2] + xb.shape[2]),
            row_scratch(modes, shards, width),
        ],
        compiler_params=params(28),
        cost_estimate=cost(),
        name="mix",
    )(*stay(ids, xa, xb), *pin(pq))


def mix_back_kernel(ids_ref, g_ref, pq_ref, out_ref, gsc, ysc):
    shards, modes, width = g_ref.shape
    gather_rows((g_ref,), gsc)
    groups = groups_of(width // (4 * LANES), range(4))
    mix_modes(gsc, ysc, pq_ref, groups, shards, ids_ref[1] * modes, True)
    scatter_rows(ysc, out_ref)


def mix_back(ids, g, pq):
    shards, modes, width = g.shape
    return pl.pallas_call(
        mix_back_kernel,
        in_specs=[pl.BlockSpec(memory_space=SMEM)] + in_vmem(2),
        out_specs=in_vmem(1)[0],
        out_shape=slow(g.shape, BF16),
        scratch_shapes=[row_scratch(modes, shards, width)] * 2,
        compiler_params=params(28),
        cost_estimate=cost(),
        name="mix_back",
    )(*stay(ids), g, *pin(pq))


def turn_kernel(ids_ref, pq_ref, xa, xb, l0, l1, l2, l3, out_ref, xt_ref, lt_ref, lb_ref, held, xsc, lsc):
    shards, modes = xa.shape[:2]
    samples = xt_ref.shape[2] // (8 * shards)
    groups = groups_of(samples, EARLY, LATE)
    shape = (LANES, LANES)
    diagonal = lax.broadcasted_iota(jnp.int32, shape, 0) == lax.broadcasted_iota(jnp.int32, shape, 1)
    unit = jnp.where(diagonal, 1.0, 0.0).astype(BF16)
    gather_rows((xa, xb), xsc)

    def step(m, carry):
        for k in range(4):
            at = slice(k * PACK, k * PACK + LANES)
            held[m, :, at] = dot(unit, pq_ref[m, :, at], ((1,), (1,))).astype(BF16)
        x = blade_rows(xsc, m, shards, groups)
        x = x + [pltpu.roll(rows, PACK - C, 1) for rows in x]
        xt_ref[m] = jnp.concatenate(x, axis=0).T[:C].astype(BF16)
        return carry

    lax.fori_loop(0, modes, step, 0, unroll=min(16, modes))
    out_ref[...] = held[...]
    own = ids_ref[0]
    for t, line in enumerate((l0, l1, l2, l3)):
        slot = jnp.bitwise_xor(own, t)
        lsc[slot] = line[...].astype(F32) * jnp.where(slot % 2 == 1, flip_of(own, 1), 1.0)
    for k in range(4):
        line = lsc[k]
        turned = line.T
        for t in range(4):
            u = t ^ k
            lb_ref[t * C : (t + 1) * C, u * C : (u + 1) * C] = (line[:, :C] * sgn(t, k)).astype(BF16)
            lt_ref[u * C : (u + 1) * C, t * C : (t + 1) * C] = (turned[:C] * sgn(t, k)).astype(BF16)


def turn(ids, pq, xa, xb, packs, samples):
    shards, modes = xa.shape[:2]
    last = packs[0].shape[1] // PACK - 1
    shape = (4 * C, 4 * C)
    turned_shape = (modes, C, 8 * samples * shards)
    return pl.pallas_call(
        turn_kernel,
        grid=(1,),
        in_specs=[pl.BlockSpec(memory_space=SMEM), whole(pq.shape), whole(xa.shape), whole(xb.shape)]
        + [pl.BlockSpec((C, PACK), lambda i: (0, last))] * 4,
        out_specs=[whole(pq.shape), whole(turned_shape)] + [whole(shape)] * 2,
        out_shape=[fast(pq.shape, BF16), slow(turned_shape, BF16)] + [slow(shape, BF16)] * 2,
        input_output_aliases={1: 0},
        scratch_shapes=[
            pltpu.VMEM(pq.shape, BF16),
            row_scratch(modes, shards, xa.shape[2] + xb.shape[2]),
            pltpu.VMEM((4, C, PACK), F32),
        ],
        compiler_params=params(28),
        cost_estimate=cost(),
        name="turn",
    )(*stay(ids), *pin(pq), *stay(xa, xb, *packs))


def grad_kernel(ids_ref, xt_ref, g_ref, lin_ref, o0, o1, o2, o3, gsc, osc):
    shards, modes, width = g_ref.shape
    samples = width // (4 * LANES)
    own = ids_ref[0]
    first_mode = ids_ref[1] * modes
    groups = groups_of(samples, range(4))
    gather_rows((g_ref,), gsc)
    lane = lanes_of((samples * shards, PACK))

    def step(g, carry):
        found = [[] for _ in range(4)]
        for q in range(QUAD):
            m = g * QUAD + q
            factor = mode_factor(first_mode + m)
            plain = [rows * factor for rows in blade_rows(gsc, m, shards, groups)]
            turned = [
                jnp.where(lane < C, pltpu.roll(rows, PACK - C, 1), -pltpu.roll(rows, C, 1))
                for rows in plain
            ]
            plus = [rows.astype(BF16) for rows in plain + turned]
            minus = [(-rows).astype(BF16) for rows in plain + turned]
            right = []
            for k in range(4):
                rows = []
                for r in range(2):
                    for t in range(4):
                        rows.append((plus if sgn(t, k) > 0 else minus)[4 * r + (t ^ k)])
                right.append(jnp.concatenate(rows, axis=0))
            grad = dot(xt_ref[m], jnp.concatenate(right, axis=1))
            for k in range(4):
                found[k].append(grad[:, k * PACK : (k + 1) * PACK])
        for k in range(4):
            for n, tile in enumerate(join_lanes(*found[k])):
                at = pl.ds(pl.multiple_of(g * QUAD * LANES + n * PACK, PACK), PACK)
                osc[k, :, at] = tile.astype(BF16)
        return carry

    quads = modes // QUAD
    lax.fori_loop(0, quads, step, 0, unroll=min(2, quads))
    for k in range(4):
        line = jnp.concatenate([lin_ref[k], jnp.zeros((C, PACK - C), F32)], axis=1)
        osc[k, :, modes * LANES :] = line.astype(BF16)
    for t, out in enumerate((o0, o1, o2, o3)):
        out[...] = osc[jnp.bitwise_xor(own, t)]


def weight_grads(ids, xt, g, lin):
    shards, modes, width = g.shape
    shape = (C, modes * LANES + PACK)
    return pl.pallas_call(
        grad_kernel,
        in_specs=[pl.BlockSpec(memory_space=SMEM)] + in_vmem(3),
        out_specs=in_vmem(4),
        out_shape=[slow(shape, BF16)] * 4,
        scratch_shapes=[row_scratch(modes, shards, width), pltpu.VMEM((4,) + shape, BF16)],
        compiler_params=params(28),
        cost_estimate=cost(),
        name="weight_grads",
    )(*stay(ids, xt), g, *stay(lin))


CDF_AT = 0.28
CDF = (0.11652094, 0.06749571, 0.2689128, -0.23699677, 0.38987606, -0.10580875)
SERIES = [value / CDF_AT ** (i + 1) for i, value in enumerate(CDF)]


def gelu_parts(v):
    z = jnp.abs(v)
    t = 1.0 / (z + 1.0 / CDF_AT)
    bell = jnp.exp2(v * v * (-0.5 * math.log2(math.e)))
    series = jnp.float32(SERIES[-1])
    for value in SERIES[-2::-1]:
        series = series * t + value
    tail = series * t * bell
    cdf = jnp.where(v < 0.0, tail, 1.0 - tail)
    return v * cdf, cdf + v * (bell * (1.0 / math.sqrt(2.0 * math.pi)))


def pixel_kernel(ids_ref, inv_ref, *refs):
    x = refs[:4]
    y_ref, ft_ref, lt_ref = refs[4:7]
    outs = refs[8:12]
    slope_ref = refs[12]
    left, ysc, even, odd = refs[14:]
    samples = x[1].shape[0]
    rows = 4 * C
    n = 2 * MODES
    width = even.shape[1]

    @pl.when(pl.program_id(0) == 0)
    def _():
        collect(y_ref, ysc)
        for s in range(samples):
            left[s, :, :n] = ysc[s * rows : (s + 1) * rows]
            left[s, :, n:] = (lt_ref[...].astype(F32) * inv_ref[s]).astype(BF16)

    def product(s, at, pre):
        fields = [x[t][s, 0, :, at] for t in range(4)]
        pre[...] = dot(left[s], jnp.concatenate([ft_ref[:, at]] + fields, axis=0))

    def activate(s, at, pre):
        for t in range(4):
            value, slope = gelu_parts(pre[t * C : (t + 1) * C])
            normed = x[t][s, 0, :, at].astype(F32) * inv_ref[s]
            outs[t][s, 0, :, at] = (normed + value).astype(BF16)
            row = s * rows + t * C
            slope_ref[row : row + C, at] = slope.astype(BF16)

    tile = ft_ref.shape[1]
    blocks = [(s, slice(k, k + width)) for k in range(0, tile, width) for s in range(samples)]
    buffers = [even, odd]
    product(*blocks[0], buffers[0])
    for k, block in enumerate(blocks):
        if k + 1 < len(blocks):
            product(*blocks[k + 1], buffers[(k + 1) % 2])
        activate(*block, buffers[k % 2])


def pixels(ids, inv, x, y, turned, lt, pq):
    samples = inv.shape[0]
    n = 2 * MODES
    tile = 1024
    mine = pl.BlockSpec((samples, 1, C, tile), lambda i, ids, inv: (ids[0], 0, 0, i))
    block = pl.BlockSpec((samples, 1, C, tile), lambda i, ids, inv: (0, 0, 0, i))
    rows = samples * 4 * C
    flat = pl.BlockSpec((rows, tile), lambda i, ids, inv: (0, i))
    return pl.pallas_call(
        pixel_kernel,
        grid_spec=pltpu.PrefetchScalarGridSpec(
            num_scalar_prefetch=2,
            grid=(NPIX // tile,),
            in_specs=[mine]
            + [block] * 3
            + [
                whole(y.shape),
                pl.BlockSpec((n, tile), lambda i, ids, inv: (0, i)),
                whole((4 * C, 4 * C)),
                pl.BlockSpec(memory_space=pl.ANY),
            ],
            out_specs=[mine] + [block] * 3 + [flat, pl.BlockSpec(memory_space=pl.ANY)],
            scratch_shapes=[
                pltpu.VMEM((samples, 4 * C, n + 4 * C), BF16),
                pltpu.VMEM((rows, n), BF16),
                pltpu.VMEM((4 * C, 256), F32),
                pltpu.VMEM((4 * C, 256), F32),
            ],
        ),
        out_shape=[slow(x[0].shape, BF16)]
        + [slow((samples, 1, C, NPIX), BF16)] * 3
        + [fast((rows, NPIX), BF16), fast(pq.shape, BF16)],
        input_output_aliases={9: 5},
        compiler_params=params(28),
        cost_estimate=cost(),
        name="pixels",
    )(*stay(ids, inv, *x), y, *stay(turned, lt), *pin(pq))


def slope_kernel(ids_ref, *refs):
    cot = refs[:4]
    slope, row_ref, col_ref, _, g_ref, g_out, _, gacc = refs[4:]
    samples = cot[1].shape[0]
    rows = 4 * C
    i = pl.program_id(0)

    @pl.when(i == 0)
    def _():
        gacc[...] = jnp.zeros_like(gacc)

    for s in range(samples):
        for t in range(4):
            at = s * rows + t * C
            grad = cot[t][s, 0].astype(F32) * slope[at : at + C].astype(F32)
            g_ref[at : at + C] = grad.astype(BF16)
    table = table_rows(row_ref, col_ref, 0, row_ref.shape[1])
    gacc[...] += dot(g_ref[...], table)

    @pl.when(i == pl.num_programs(0) - 1)
    def _():
        spread(gacc, g_out)


def pixel_grads(ids, cot, slope, small, spectrum, pq):
    rows = slope.shape[0]
    samples = rows // (4 * C)
    n = 2 * MODES
    tile = 2048
    mine = pl.BlockSpec((samples, 1, C, tile), lambda i, ids: (ids[0], 0, 0, i))
    block = pl.BlockSpec((samples, 1, C, tile), lambda i, ids: (0, 0, 0, i))
    flat = pl.BlockSpec((rows, tile), lambda i, ids: (0, i))
    kept = pl.BlockSpec(memory_space=pl.ANY)
    return pl.pallas_call(
        slope_kernel,
        grid_spec=pltpu.PrefetchScalarGridSpec(
            num_scalar_prefetch=1,
            grid=(NPIX // tile,),
            in_specs=[mine] + [block] * 3 + [flat] + small_specs(tile) + [kept],
            out_specs=[flat, whole(spectrum), kept],
            scratch_shapes=[pltpu.VMEM((rows, n), F32)],
        ),
        out_shape=[slow((rows, NPIX), BF16), slow(spectrum, BF16), fast(pq.shape, BF16)],
        input_output_aliases={8: 2},
        compiler_params=params(28),
        cost_estimate=cost(),
        name="pixel_grads",
    )(*stay(ids, *cot), *pin(slope), *stay(small, small), *pin(pq))


def lin_kernel(ids_ref, inv_ref, *refs):
    x = refs[:4]
    g_ref, lb_ref, lin_ref, back_ref, lacc = refs[4:]
    samples = x[1].shape[0]
    rows = 4 * C

    @pl.when(pl.program_id(0) == 0)
    def _():
        lacc[...] = jnp.zeros_like(lacc)

    for s in range(samples):
        fields = jnp.concatenate([x[t][s, 0] for t in range(4)], axis=0)
        g = g_ref[s * rows : (s + 1) * rows]
        lacc[...] += dot(fields, g, ((1,), (1,))) * inv_ref[s]
        back_ref[s * rows : (s + 1) * rows] = dot(lb_ref[...], g).astype(BF16)

    @pl.when(pl.program_id(0) == pl.num_programs(0) - 1)
    def _():
        for k in range(4):
            total = None
            for t in range(4):
                u = t ^ k
                piece = lacc[t * C : (t + 1) * C, u * C : (u + 1) * C] * sgn(t, k)
                total = piece if total is None else total + piece
            lin_ref[k] = total


def lin_grads(ids, inv, x, g, lb):
    rows = g.shape[0]
    samples = rows // (4 * C)
    tile = 2048
    mine = pl.BlockSpec((samples, 1, C, tile), lambda i, ids, inv: (ids[0], 0, 0, i))
    block = pl.BlockSpec((samples, 1, C, tile), lambda i, ids, inv: (0, 0, 0, i))
    flat = pl.BlockSpec((rows, tile), lambda i, ids, inv: (0, i))
    return pl.pallas_call(
        lin_kernel,
        grid_spec=pltpu.PrefetchScalarGridSpec(
            num_scalar_prefetch=2,
            grid=(NPIX // tile,),
            in_specs=[mine] + [block] * 3 + [flat, whole((4 * C, 4 * C))],
            out_specs=[whole((4, C, C)), flat],
            scratch_shapes=[pltpu.VMEM((4 * C, 4 * C), F32)],
        ),
        out_shape=[slow((4, C, C), F32), slow(g.shape, BF16)],
        compiler_params=params(28),
        cost_estimate=cost(),
        name="lin_grads",
    )(*stay(ids, inv, *x, g, lb))


def inner_kernel(ids_ref, inv_ref, y_ref, back_ref, row_ref, col_ref, cot_ref, mine_ref, *refs):
    o1, o2, o3, ysc = refs
    samples = cot_ref.shape[0]
    rows = 4 * C

    @pl.when(pl.program_id(0) == 0)
    def _():
        collect(y_ref, ysc)

    table = table_rows(row_ref, col_ref, 0, row_ref.shape[1])
    spatial = dot(ysc[...], table, ((1,), (1,)))
    for s in range(samples):
        at = slice(s * rows, (s + 1) * rows)
        total = spatial[at] + back_ref[at].astype(F32)
        mine_ref[s, 0] = (cot_ref[s, 0].astype(F32) + total[:C]) * inv_ref[s]
        for t, out in ((1, o1), (2, o2), (3, o3)):
            out[s, 0] = total[t * C : (t + 1) * C].astype(BF16)


def inner_grads(ids, inv, y, back, small, cotangent):
    samples = inv.shape[0]
    n = 2 * MODES
    tile = 2048
    rows = samples * 4 * C
    mine = pl.BlockSpec((samples, 1, C, tile), lambda i, ids, inv: (ids[0], 0, 0, i))
    block = pl.BlockSpec((samples, 1, C, tile), lambda i, ids, inv: (0, 0, 0, i))
    return pl.pallas_call(
        inner_kernel,
        grid_spec=pltpu.PrefetchScalarGridSpec(
            num_scalar_prefetch=2,
            grid=(NPIX // tile,),
            in_specs=[
                whole(y.shape),
                pl.BlockSpec((rows, tile), lambda i, ids, inv: (0, i)),
                *small_specs(tile),
                mine,
            ],
            out_specs=[mine] + [block] * 3,
            scratch_shapes=[pltpu.VMEM((rows, n), BF16)],
        ),
        out_shape=[slow(cotangent.shape, F32)] + [slow((samples, 1, C, NPIX), BF16)] * 3,
        compiler_params=params(28),
        cost_estimate=cost(),
        name="inner_grads",
    )(*stay(ids, inv), y, *stay(back, small, small, cotangent))


def place_kernel(ids_ref, a_ref, b_ref, c_ref, old_ref, out_ref):
    for n, part in enumerate((a_ref, b_ref, c_ref)):

        @pl.when(pl.program_id(0) == n)
        def _():
            out_ref[...] = part[...]


def place_output(ids, parts, result):
    samples = parts[0].shape[0]
    shape = (1, 1, C, NPIX)

    def spec(n):
        def at(j, s, ids):
            return (jnp.where(j == n, s, jnp.where(j < n, 0, samples - 1)), 0, 0, 0)

        return pl.BlockSpec(shape, at)

    return pl.pallas_call(
        place_kernel,
        grid_spec=pltpu.PrefetchScalarGridSpec(
            num_scalar_prefetch=1,
            grid=(3, samples),
            in_specs=[spec(0), spec(1), spec(2), pl.BlockSpec(memory_space=pl.ANY)],
            out_specs=pl.BlockSpec(
                shape, lambda j, s, ids: (jnp.bitwise_xor(ids[0], j + 1) * samples + s, 0, 0, 0)
            ),
        ),
        out_shape=jax.ShapeDtypeStruct(result.shape, BF16),
        input_output_aliases={4: 0},
        compiler_params=params(28),
        cost_estimate=cost(),
        name="place",
    )(ids, *parts, result)


def final_kernel(count, codes, ids_ref, inv_ref, cot_ref, *refs):
    samples = cot_ref.shape[0]
    j = pl.program_id(0)
    for n in range(count):

        @pl.when(j == n)
        def _():
            for s in range(samples):
                inv = inv_ref[jnp.bitwise_xor(ids_ref[0], codes[n]) * samples + s]
                refs[-1][s] = (cot_ref[s].astype(F32) + refs[n][s].astype(F32)) * inv


def final_grads(ids, inv, cotangent, parts, codes, result):
    samples = parts[0].shape[0]
    count = len(parts)
    shape = (samples, 1, C, NPIX)

    def code(j):
        value = codes[0]
        for n in range(1, count):
            value = jnp.where(j == n, codes[n], value)
        return value

    def spec(n):
        return pl.BlockSpec(shape, lambda j, ids, inv: (0, 0, 0, 0))

    place = pl.BlockSpec(
        shape, lambda j, ids, inv: (jnp.bitwise_xor(ids[0], code(j)), 0, 0, 0)
    )
    return pl.pallas_call(
        partial(final_kernel, count, codes),
        grid_spec=pltpu.PrefetchScalarGridSpec(
            num_scalar_prefetch=2,
            grid=(count,),
            in_specs=[place]
            + [spec(n) for n in range(count)]
            + [pl.BlockSpec(memory_space=pl.ANY)],
            out_specs=place,
        ),
        out_shape=jax.ShapeDtypeStruct(cotangent.shape, F32),
        input_output_aliases={3 + count: 0},
        compiler_params=params(28),
        cost_estimate=cost(),
        name="final",
    )(ids, inv, cotangent, *parts, result)


def adamw(weight, first, second, grad):
    first_new = BETA_ONE * first + (1.0 - BETA_ONE) * grad
    second_new = BETA_TWO * second + (1.0 - BETA_TWO) * grad * grad
    corr_one = 1.0 - BETA_ONE**STEP_COUNT
    corr_two = 1.0 - BETA_TWO**STEP_COUNT
    update = first_new / corr_one / (jnp.sqrt(second_new / corr_two) + EPSILON)
    return (weight - RATE * (update + DECAY * weight), first_new, second_new)


def adam_kernel(flips, d0, d1, d2, d3, w_ref, first_ref, second_ref, w_out, first_out, second_out):
    grad = d0[...].astype(F32) * flips[0]
    for t, d in ((1, d1), (2, d2), (3, d3)):
        grad = grad + d[...].astype(F32) * flips[t]
    for q in range(w_ref.shape[1]):
        for r in range(2):
            lane = q * LANES + r * C
            at = (0, q, r)
            new = adamw(w_ref[at], first_ref[at], second_ref[at], grad[:, lane : lane + C])
            w_out[at], first_out[at], second_out[at] = new


def adam_spec(flips, grads, weight, first, second):
    modes = weight.shape[1]
    part = min(modes, 4 * QUAD)
    packed = pl.BlockSpec((C, part * LANES), lambda g: (0, g))
    block = pl.BlockSpec((1, part, 2, C, C), lambda g: (0, g, 0, 0, 0))
    return pl.pallas_call(
        adam_kernel,
        grid=(modes // part,),
        in_specs=[pl.BlockSpec(memory_space=SMEM)] + [packed] * 4 + [block] * 3,
        out_specs=[block] * 3,
        out_shape=[jax.ShapeDtypeStruct(weight.shape, F32)] * 3,
        compiler_params=params(28),
        cost_estimate=cost(),
        name="adam",
    )(flips, *grads, weight, first, second)


def swap(value, axis, size, x):
    return lax.ppermute(value, axis, [(i, i ^ x) for i in range(size)])


def to_modes(value):
    return lax.all_to_all(value, "dp", split_axis=0, concat_axis=0, tiled=True)


def after(values, first):
    values, _ = lax.optimization_barrier((values, first))
    return values


def body(
    shards,
    inputs,
    cotangent,
    norm_table,
    sample_index,
    spec_weight,
    spec_first,
    spec_second,
    lin_weight,
    lin_first,
    lin_second,
):
    own = lax.axis_index("blade")
    shard = lax.axis_index("dp")
    ids = jnp.stack([own, shard]).astype(jnp.int32)
    samples = inputs.shape[0] // 4

    def cut(array, t):
        return lax.dynamic_slice_in_dim(array, jnp.bitwise_xor(own, t) * samples, samples, 0)

    def send(array, t):
        block = cut(array, t)
        return block, swap(block, "blade", 4, t)

    sent, x3 = send(inputs, 3)
    rest = after(inputs, sent)
    sent, x1 = send(rest, 1)
    rest = after(rest, sent)
    _, x2 = send(rest, 2)

    matches = sample_index[:, None] == jnp.arange(NTAB, dtype=jnp.int32)[None, :]
    normalizer = jnp.sum(jnp.where(matches, norm_table[None, :], 0.0), axis=1)
    inv_all = 1.0 / normalizer
    inv = lax.dynamic_slice_in_dim(inv_all, own * samples, samples, 0)

    small = lax.optimization_barrier(small_tables())
    turned = turned_table(small)
    packed = pack_weights(spec_weight, lin_weight)
    packs = [packed] + [swap(packed, "blade", 4, t) for t in (1, 2, 3)]

    x3 = after(x3, (packed, turned))
    sent = forward_spectrum(ids, inv, (inputs, x3), small, shards)
    x1, x2 = after((x1, x2), sent)
    xa = to_modes(sent)
    blocks = after([cut(cotangent, t) for t in (1, 2, 3)], (x1, x2))
    cot = (cotangent,) + tuple(swap(blocks[t - 1], "blade", 4, t) for t in (1, 2, 3))
    xb = to_modes(forward_spectrum(ids, inv, (x1, x2), small, shards))
    pq = unpack(ids, packs)
    mixed = mix(ids, xa, xb, pq, samples)
    pq, xt, lt, lb = turn(ids, after(pq, mixed), xa, xb, packs, samples)
    y = to_modes(mixed)

    x = (inputs, x1, x2, x3)
    result = pixels(ids, inv, x, y, turned, lt, pq)
    output, slope, pq = result[0], result[4], result[5]
    last, cot = lax.optimization_barrier((result[3], cot))
    parts = (result[1], result[2], last)
    out_parts = [swap(parts[t - 1], "blade", 4, t) for t in (1, 2, 3)]

    grad_pre, sent, pq = pixel_grads(ids, cot, slope, small, y.shape, pq)
    lin, from_lin = lin_grads(ids, inv, x, grad_pre, lb)
    g = after(to_modes(sent), (out_parts[2], xt, pq, lin))
    mixed = mix_back(ids, g, pq)
    back = to_modes(mixed)
    spec_grads = weight_grads(ids, xt, g, lin)
    spec_grads = [spec_grads[0]] + [swap(spec_grads[t], "blade", 4, t) for t in (1, 2, 3)]

    inner = inner_grads(ids, inv, back, from_lin, small, cotangent)
    inner = after(inner, out_parts)
    grad_parts = [swap(inner[t], "blade", 4, t) for t in (1, 2, 3)]

    output = place_output(ids, out_parts, output)
    spec_grads = after(spec_grads, output)
    flips = jnp.stack(
        [jnp.where(own % 2 == 1, flip_of(jnp.bitwise_xor(own, t), 1), 1.0) for t in range(4)]
    )
    lin_grad = 0.0
    first = spec_weight.shape[1] * LANES
    for t in range(4):
        lin_grad = lin_grad + spec_grads[t][:, first : first + C].astype(F32) * flips[t]
    step = 1
    while step < shards:
        lin_grad = lin_grad + swap(lin_grad, "dp", shards, step)
        step *= 2

    spec_out = adam_spec(flips, spec_grads, spec_weight, spec_first, spec_second)
    lin_out = adamw(lin_weight, lin_first, lin_second, lin_grad[None])
    input_grad = final_grads(ids, inv_all, cotangent, grad_parts[2:], (3,), inner[0])
    input_grad = final_grads(ids, inv_all, cotangent, grad_parts[:2], (1, 2), input_grad)
    return (output, input_grad, *spec_out, *lin_out)


def solution(mesh):
    fields = P("dp", "blade", None, None)
    spec = P("blade", "dp", None, None, None)
    lin = P("blade", None, None)
    return jax.shard_map(
        partial(body, mesh.shape["dp"]),
        mesh=mesh,
        in_specs=(fields, fields, P(), P("dp"), spec, spec, spec, lin, lin, lin),
        out_specs=(fields, fields, spec, spec, spec, lin, lin, lin),
        check_vma=False,
    )
```
